32 devices in a mesh: dp: 8 (over y, x, core), tensor: 4 (over z).
Axes of the slice: x: 2, y: 2, z: 4, core: 2. Of those that a mesh axis runs over, the one named last changes fastest.
Arguments:
- x_in: float32 [4096, 1024], P(('dp', 'tensor')), may hold values from -6 to 6
- d_out: float32 [4096, 1024], P(('dp', 'tensor')), may hold values from -6 to 6
- seq_lengths: int32 [8, 2], P('dp'), may hold values from 128 to 384, as said below
- w_qkv: bfloat16 [2, 1024, 3, 1024], P(None, 'dp', None, 'tensor'), may hold values from -0.1875 to 0.1875
- b_qv: bfloat16 [2, 2, 1024], P(None, None, ('tensor', 'dp')), may hold values from -3 to 3
- w_o: bfloat16 [2, 1024, 1024], P(None, 'tensor', 'dp'), may hold values from -0.5 to 0.5
- w_1: bfloat16 [2, 1024, 4096], P(None, 'dp', 'tensor'), may hold values from -0.1875 to 0.1875
- b_ffn: bfloat16 [2, 4096], P(None, ('tensor', 'dp')), may hold values from -3 to 3
- w_2: bfloat16 [2, 4096, 1024], P(None, 'tensor', 'dp'), may hold values from -0.09375 to 0.09375
- norm_gains: bfloat16 [2, 2, 1024], P(None, None, 'dp'), may hold values from 0.5 to 1.5
- vec_biases: bfloat16 [2, 4, 1024], P(None, None, 'dp'), may hold values from -3 to 3
Outputs:
- output: float32 [4096, 1024], P(('dp', 'tensor'))
- grad_x: float32 [4096, 1024], P(('dp', 'tensor'))
- grad_w_qkv: float32 [2, 1024, 3, 1024], P(None, 'dp', None, 'tensor')
- grad_b_qv: float32 [2, 2, 1024], P(None, None, ('tensor', 'dp'))
- grad_w_o: float32 [2, 1024, 1024], P(None, 'tensor', 'dp')
- grad_w_1: float32 [2, 1024, 4096], P(None, 'dp', 'tensor')
- grad_b_ffn: float32 [2, 4096], P(None, ('tensor', 'dp'))
- grad_w_2: float32 [2, 4096, 1024], P(None, 'tensor', 'dp')
- grad_norm_gains: float32 [2, 2, 1024], P(None, None, 'dp')
- grad_vec_biases: float32 [2, 4, 1024], P(None, None, 'dp')
The draws below stay inside these ranges and needn't reach their ends.
Inputs may be any that keep to these rules, and one draw needn't show every extreme that they name: `seq_lengths`: each row lists the lengths of the 2 sequences of one group in packing order; they sum to 512. Some group holds a sequence of length exactly 384.
All inputs are finite; a program needn't handle non-finite values.
Results may differ from the reference program's by a relative error of at most 0.02.
Values may be sent and summed in bfloat16 or wider, within the bound.
A program may use at most 128 MiB of HBM per device.

```python
import math
import jax
import jax.numpy as jnp
from jax import lax

D = 1024
HEAD_DIM = 64
FF = 4096
LAYERS = 2
TOK_DEV = 512
MOST = 384
TOKENS = 4096
N_DP = 8


def draw_seq_lengths(key, part):
    first_key = jax.random.fold_in(key, 11)
    pick_key = jax.random.fold_in(key, 12)
    flip_key = jax.random.fold_in(key, 13)
    first_len = jax.random.randint(first_key, (N_DP,), TOK_DEV - MOST, MOST + 1, dtype=jnp.int32)
    chosen = jax.random.randint(pick_key, (), 0, N_DP, dtype=jnp.int32)
    group_ids = jnp.arange(N_DP, dtype=jnp.int32)
    first_len = jnp.where(group_ids == chosen, jnp.int32(MOST), first_len).astype(jnp.int32)
    second_len = (TOK_DEV - first_len).astype(jnp.int32)
    flipped = jax.random.randint(flip_key, (N_DP,), 0, 2, dtype=jnp.int32) == 1
    lead = jnp.where(flipped, second_len, first_len)
    trail = jnp.where(flipped, first_len, second_len)
    return jnp.stack([lead, trail], axis=1).astype(jnp.int32)


def spiked(result, key, source, target, blocks, factor):
    owner, partner = [(jnp.arange(result.shape[dim]) // (result.shape[dim] // blocks)).reshape([-1 if axis == dim else 1 for axis in range(result.ndim)]) for dim in (source, target)]
    chosen = jax.random.permutation(key, blocks)[partner]
    strong = (owner == chosen) | (owner == (partner + blocks // 2) % blocks)
    return jnp.where(strong, factor * result, result)


def block_scale(rng, shape, split, least, high):
    loudness = 1.0
    for axis_at, blocks in split:
        steps = jax.random.uniform(jax.random.fold_in(jax.random.fold_in(rng, 6), axis_at), (blocks,), jnp.float32, least / len(split), high / len(split))
        loudness = loudness * jnp.repeat(jnp.exp(steps), shape[axis_at] // blocks).reshape((-1,) + (1,) * (len(shape) - 1 - axis_at))
    return loudness


def noise(key, shape, spread, most, split=(), held_as=jnp.bfloat16):
    factor_of = block_scale(key, shape, split, -0.22, 0.18) if split else 1.0
    values = jax.random.normal(key, shape, jnp.float32) * spread * factor_of
    return jnp.minimum(jnp.maximum(values, -most), most).astype(held_as)


def bell_draw_with(stream_key, shape, scale, reach, split, heavy, kind=jnp.bfloat16):
    result = scale * jax.random.normal(stream_key, shape, jnp.float32)
    if split:
        result = result * block_scale(stream_key, shape, split, -0.22, 0.18)
    return jnp.clip(spiked(result, jax.random.fold_in(stream_key, 3), *heavy), -reach, reach).astype(kind)


def setup_inputs(seed: int = 0) -> dict:
    key_list = jax.random.split(jax.random.key(seed), 12)
    return {
        "x_in": noise(key_list[0], (TOKENS, D), 1.0, 6.0, ((0, 32),), jnp.float32),
        "d_out": bell_draw_with(key_list[1], (TOKENS, D), 1.0, 6.0, ((0, 32),), (0, 1, 32, 2.75), jnp.float32),
        "seq_lengths": draw_seq_lengths(jax.random.fold_in(key_list[11], 71), 0),
        "w_qkv": noise(key_list[3], (LAYERS, D, 3, D), D ** -0.5, 0.1875, ((1, 8), (3, 4))),
        "b_qv": noise(key_list[4], (LAYERS, 2, D), 0.5, 3.0, ((2, 32),)),
        "w_o": noise(key_list[5], (LAYERS, D, D), (D // 8) ** -0.5, 0.5, ((1, 4), (2, 8))),
        "w_1": noise(key_list[6], (LAYERS, D, FF), D ** -0.5, 0.1875, ((1, 8), (2, 4))),
        "b_ffn": noise(key_list[7], (LAYERS, FF), 0.5, 3.0, ((1, 32),)),
        "w_2": noise(key_list[8], (LAYERS, FF, D), FF ** -0.5, 0.09375, ((1, 4), (2, 8))),
        "norm_gains": jnp.clip(1.0 + 0.1 * jax.random.normal(key_list[9], (LAYERS, 2, D), jnp.float32), 0.5, 1.5).astype(jnp.bfloat16),
        "vec_biases": noise(key_list[10], (LAYERS, 4, D), 0.5, 3.0, ((2, 8),)),
    }


NORM_EPS = 1e-05
GELU_COEFF = 0.7978845608028654
GELU_CUBIC = 0.044715

def layer_norm(inputs, gain_row, bias_row):
    row_mean = lax.optimization_barrier(jnp.mean(inputs, axis=-1, keepdims=True))
    centered = inputs - row_mean
    inv_std = lax.rsqrt(lax.optimization_barrier(jnp.mean(centered * centered, axis=-1, keepdims=True)) + NORM_EPS)
    normed = centered * inv_std
    return (normed * gain_row + bias_row, normed, inv_std)

def norm_back(grad_in, normed, inv_std, gain_row):
    scaled = grad_in * gain_row
    return inv_std * (scaled - lax.optimization_barrier(jnp.mean(scaled, axis=-1, keepdims=True)) - normed * lax.optimization_barrier(jnp.mean(scaled * normed, axis=-1, keepdims=True)))

def gelu_pair(pre_act):
    squared = pre_act * pre_act
    tangent = jnp.tanh(GELU_COEFF * (pre_act + GELU_CUBIC * squared * pre_act))
    gelu_value = 0.5 * pre_act * (1.0 + tangent)
    gelu_slope = 0.5 * (1.0 + tangent) + 0.5 * pre_act * (1.0 - tangent * tangent) * GELU_COEFF * (1.0 + 3.0 * GELU_CUBIC * squared)
    return (gelu_value, gelu_slope)

def segment_ids(lengths, total_rows):
    sequence_ends = jnp.cumsum(lengths.astype(jnp.int32)).astype(jnp.int32)
    positions = jnp.arange(total_rows, dtype=jnp.int32)
    return lax.optimization_barrier(jnp.sum((positions[:, None] >= sequence_ends[None, :]).astype(jnp.int32), axis=1, dtype=jnp.int32))

def group_pass(x_group, grad_group, lengths, params):
    w_qkv, b_qv, w_o, w_1, b_ffn, w_2, norm_gains, vec_biases = params
    group_rows = x_group.shape[0]
    width = x_group.shape[1]
    head_count = width // HEAD_DIM
    score_scale = 1.0 / math.sqrt(HEAD_DIM)
    segments = segment_ids(lengths, group_rows)
    positions = jnp.arange(group_rows, dtype=jnp.int32)
    allowed = (segments[:, None] == segments[None, :]) & (positions[None, :] <= positions[:, None])
    caches = []
    hidden_in = x_group
    for layer_index in range(LAYERS):
        gain_rows = norm_gains[layer_index].astype(jnp.float32)
        bias_rows = vec_biases[layer_index].astype(jnp.float32)
        normed_one, unit_one, inv_one = layer_norm(hidden_in, gain_rows[0], bias_rows[0])
        normed_one = normed_one.astype(jnp.bfloat16)
        qkv_matrix = w_qkv[layer_index].reshape(width, 3 * width)
        projected = jnp.dot(normed_one, qkv_matrix, preferred_element_type=jnp.float32).reshape(group_rows, 3, width)
        qv_bias = b_qv[layer_index].astype(jnp.float32)
        queries = (projected[:, 0] + qv_bias[0]).astype(jnp.bfloat16).reshape(group_rows, head_count, HEAD_DIM)
        key_vecs = projected[:, 1].astype(jnp.bfloat16).reshape(group_rows, head_count, HEAD_DIM)
        val_vecs = (projected[:, 2] + qv_bias[1]).astype(jnp.bfloat16).reshape(group_rows, head_count, HEAD_DIM)
        scores = jnp.einsum('qhd,khd->hqk', queries.astype(jnp.float32), key_vecs.astype(jnp.float32)) * score_scale
        scores = jnp.where(allowed[None], scores, -jnp.inf)
        row_max = lax.optimization_barrier(jnp.max(scores, axis=-1, keepdims=True))
        log_total = row_max + jnp.log(lax.optimization_barrier(jnp.sum(jnp.exp(scores - row_max), axis=-1, keepdims=True)))
        soft_probs = jnp.exp(scores - log_total)
        probs_half = soft_probs.astype(jnp.bfloat16)
        attended = jnp.einsum('hqk,khd->qhd', probs_half.astype(jnp.float32), val_vecs.astype(jnp.float32))
        attended = attended.astype(jnp.bfloat16).reshape(group_rows, width)
        residual_mid = hidden_in + jnp.dot(attended, w_o[layer_index], preferred_element_type=jnp.float32) + bias_rows[2]
        normed_two, unit_two, inv_two = layer_norm(residual_mid, gain_rows[1], bias_rows[1])
        normed_two = normed_two.astype(jnp.bfloat16)
        pre_act = jnp.dot(normed_two, w_1[layer_index], preferred_element_type=jnp.float32) + b_ffn[layer_index].astype(jnp.float32)
        gelu_value, gelu_slope = gelu_pair(pre_act)
        activated = gelu_value.astype(jnp.bfloat16)
        hidden_out = residual_mid + jnp.dot(activated, w_2[layer_index], preferred_element_type=jnp.float32) + bias_rows[3]
        caches.append((unit_one, inv_one, normed_one, queries, key_vecs, val_vecs, soft_probs, probs_half, attended, unit_two, inv_two, normed_two, activated, gelu_slope))
        hidden_in = hidden_out
    output_rows = hidden_in
    back = grad_group
    layer_grads = [None] * LAYERS
    for layer_index in reversed(range(LAYERS)):
        unit_one, inv_one, normed_one, queries, key_vecs, val_vecs, soft_probs, probs_half, attended, unit_two, inv_two, normed_two, activated, gelu_slope = caches[layer_index]
        gain_rows = norm_gains[layer_index].astype(jnp.float32)
        grad_half = back.astype(jnp.bfloat16)
        grad_w2 = jnp.dot(activated.T, grad_half, preferred_element_type=jnp.float32)
        grad_pre = jnp.dot(grad_half, w_2[layer_index].T, preferred_element_type=jnp.float32) * gelu_slope
        grad_pre_half = grad_pre.astype(jnp.bfloat16)
        grad_w1 = jnp.dot(normed_two.T, grad_pre_half, preferred_element_type=jnp.float32)
        grad_normed_two = jnp.dot(grad_pre_half, w_1[layer_index].T, preferred_element_type=jnp.float32)
        grad_mid = back + norm_back(grad_normed_two, unit_two, inv_two, gain_rows[1])
        grad_mid_half = grad_mid.astype(jnp.bfloat16)
        grad_wo = jnp.dot(attended.T, grad_mid_half, preferred_element_type=jnp.float32)
        grad_attended = jnp.dot(grad_mid_half, w_o[layer_index].T, preferred_element_type=jnp.float32)
        grad_attended = grad_attended.astype(jnp.bfloat16).reshape(group_rows, head_count, HEAD_DIM)
        grad_probs = jnp.einsum('qhd,khd->hqk', grad_attended.astype(jnp.float32), val_vecs.astype(jnp.float32))
        row_dot = lax.optimization_barrier(jnp.sum(grad_probs * soft_probs, axis=-1, keepdims=True))
        score_grad = (soft_probs * (grad_probs - row_dot) * score_scale).astype(jnp.bfloat16)
        query_grad = jnp.einsum('hqk,khd->qhd', score_grad.astype(jnp.float32), key_vecs.astype(jnp.float32))
        key_grad = jnp.einsum('hqk,qhd->khd', score_grad.astype(jnp.float32), queries.astype(jnp.float32))
        val_grad = jnp.einsum('hqk,qhd->khd', probs_half.astype(jnp.float32), grad_attended.astype(jnp.float32))
        grad_qkv = jnp.stack([query_grad, key_grad, val_grad], axis=1).astype(jnp.bfloat16).reshape(group_rows, 3 * width)
        grad_bqv = jnp.stack([lax.optimization_barrier(jnp.sum(query_grad, axis=0)).reshape(width), lax.optimization_barrier(jnp.sum(val_grad, axis=0)).reshape(width)])
        qkv_matrix = w_qkv[layer_index].reshape(width, 3 * width)
        grad_wqkv = jnp.dot(normed_one.T, grad_qkv, preferred_element_type=jnp.float32).reshape(width, 3, width)
        grad_normed_one = jnp.dot(grad_qkv, qkv_matrix.T, preferred_element_type=jnp.float32)
        next_back = grad_mid + norm_back(grad_normed_one, unit_one, inv_one, gain_rows[0])
        grad_gains = jnp.stack([lax.optimization_barrier(jnp.sum(grad_normed_one * unit_one, axis=0)), lax.optimization_barrier(jnp.sum(grad_normed_two * unit_two, axis=0))])
        grad_vbias = jnp.stack([lax.optimization_barrier(jnp.sum(grad_normed_one, axis=0)), lax.optimization_barrier(jnp.sum(grad_normed_two, axis=0)), lax.optimization_barrier(jnp.sum(grad_mid, axis=0)), lax.optimization_barrier(jnp.sum(back, axis=0))])
        layer_grads[layer_index] = (grad_wqkv, grad_bqv, grad_wo, grad_w1, lax.optimization_barrier(jnp.sum(grad_pre, axis=0)), grad_w2, grad_gains, grad_vbias)
        back = next_back
    stacked = tuple((jnp.stack([layer_grads[index][member] for index in range(LAYERS)]) for member in range(8)))
    return (output_rows, back, stacked)

def reference(x_in, d_out, seq_lengths, w_qkv, b_qv, w_o, w_1, b_ffn, w_2, norm_gains, vec_biases):
    params = (w_qkv, b_qv, w_o, w_1, b_ffn, w_2, norm_gains, vec_biases)
    x_groups = x_in.reshape(-1, TOK_DEV, D)
    grad_groups = d_out.reshape(-1, TOK_DEV, D)
    zero_grads = tuple((jnp.zeros(weight.shape, jnp.float32) for weight in params))

    def group_step(totals, items):
        x_group, grad_group, lengths = items
        output_rows, grad_rows, grads = group_pass(x_group, grad_group, lengths, params)
        return (tuple((total + grad for total, grad in zip(totals, grads))), (output_rows, grad_rows))
    totals, (outputs, grads_x) = lax.scan(group_step, zero_grads, (x_groups, grad_groups, seq_lengths))
    return (outputs.reshape(-1, D), grads_x.reshape(-1, D), totals[0], totals[1], totals[2], totals[3], totals[4], totals[5], totals[6], totals[7])
```

```python
import math

import jax
import jax.numpy as jnp
from jax import lax
from jax.experimental import pallas as pl
from jax.experimental.pallas import tpu as pltpu
from jax.sharding import PartitionSpec as P

HEAD_DIM = 64


NORM_EPS = 1e-05
GELU_COEFF = 0.7978845608028654
GELU_CUBIC = 0.044715


def layer_norm(inputs, gain_row, bias_row):
    row_mean = jnp.mean(inputs, axis=-1, keepdims=True)
    centered = inputs - row_mean
    inv_std = lax.rsqrt(jnp.mean(centered * centered, axis=-1, keepdims=True) + NORM_EPS)
    normed = centered * inv_std
    return (normed * gain_row + bias_row, normed, inv_std)


def norm_back(grad_in, normed, inv_std, gain_row):
    scaled = grad_in * gain_row
    return inv_std * (
        scaled
        - jnp.mean(scaled, axis=-1, keepdims=True)
        - normed * jnp.mean(scaled * normed, axis=-1, keepdims=True)
    )


def gelu_pair(pre_act):
    squared = pre_act * pre_act
    tangent = jnp.tanh(GELU_COEFF * (pre_act + GELU_CUBIC * squared * pre_act))
    gelu_value = 0.5 * pre_act * (1.0 + tangent)
    gelu_slope = 0.5 * (1.0 + tangent) + 0.5 * pre_act * (1.0 - tangent * tangent) * GELU_COEFF * (
        1.0 + 3.0 * GELU_CUBIC * squared
    )
    return (gelu_value, gelu_slope)


def segment_ids(lengths, total_rows):
    positions = jnp.arange(total_rows, dtype=jnp.int32)
    found = jnp.zeros_like(positions)
    end = jnp.int32(0)
    for index in range(lengths.shape[0]):
        end = end + lengths[index]
        found = found + (positions >= end).astype(jnp.int32)
    return found


def contract_first(left, right):
    return lax.dot_general(
        left, right, (((0,), (0,)), ((), ())), preferred_element_type=jnp.float32
    )


def contract_last(left, right):
    return lax.dot_general(
        left, right, (((1,), (1,)), ((), ())), preferred_element_type=jnp.float32
    )

def exchange_kernel(plan, *refs):
    count = len(plan)
    ins = refs[:count]
    outs = refs[count : 2 * count]
    send_sem, recv_sem, own_sem = refs[2 * count : 2 * count + 3]
    spare = list(refs[2 * count + 3 :])

    greeted = []
    for axis in sorted({axis for axis, _, _ in plan}):
        kinds = {kind for name, kind, _ in plan if name == axis}
        size = [n for name, _, n in plan if name == axis][0]
        me = lax.axis_index(axis)
        if kinds == {"paired"}:
            greeted.append({axis: me + 1 - 2 * (me % 2)})
            greeted += [{axis: (me + k) % size} for k in range(2, size, 2)]
        else:
            greeted += [{axis: (me + k) % size} for k in range(1, size)]
    barrier = pltpu.get_barrier_semaphore()
    for device in greeted:
        pl.semaphore_signal(
            barrier, inc=1, device_id=device, device_id_type=pl.DeviceIdType.MESH
        )
    pl.semaphore_wait(barrier, len(greeted))

    used = [0]

    def remote(src, dst, device):
        slot = used[0]
        used[0] += 1
        copy = pltpu.make_async_remote_copy(
            src_ref=src,
            dst_ref=dst,
            send_sem=send_sem.at[slot],
            recv_sem=recv_sem.at[slot],
            device_id=device,
            device_id_type=pl.DeviceIdType.MESH,
        )
        copy.start()
        return copy

    def in_line(axis, src, dst, base, place, target, arrival):
        return pltpu.make_async_remote_copy(
            src_ref=src,
            dst_ref=dst,
            send_sem=send_sem.at[base + place],
            recv_sem=recv_sem.at[base + arrival],
            device_id={axis: jnp.int32(target)},
            device_id_type=pl.DeviceIdType.MESH,
        )

    def line_start(axis, kind, src, dst, base, held):
        me = lax.axis_index(axis)
        for m in range(4):

            @pl.when(me == m)
            def _(m=m):
                if kind == "sum" and m in (0, 3):
                    far = 3 - m
                    near = 1 if m == 0 else 2
                    in_line(axis, src.at[far], held, base, far, near, 4).start()
                for target in ((2, 1), (3, 2, 0), (0, 1, 3), (1, 2))[m]:
                    if kind == "sum" and (m, target) in ((1, 3), (2, 0)):
                        continue
                    block = src.at[target] if kind == "sum" else src
                    in_line(axis, block, dst.at[m], base, target, target, m).start()

    def line_relay(axis, kind, src, dst, base, held, mixed):
        me = lax.axis_index(axis)
        for m in (1, 2):

            @pl.when(me == m)
            def _(m=m):
                far = 3 if m == 1 else 0
                near = 3 - far
                if kind == "line":
                    in_line(axis, src, dst.at[far], base, far, far, far).wait_recv()
                    in_line(axis, dst.at[far], dst.at[far], base, 4, near, far).start()
                else:
                    in_line(axis, held, held, base, far, far, 4).wait_recv()

                    def add(row, carry):
                        rows = pl.ds(row * 16, 16)
                        mixed[rows] = (
                            held[rows].astype(jnp.float32)
                            + src[far, rows].astype(jnp.float32)
                        ).astype(mixed.dtype)
                        return carry

                    lax.fori_loop(0, mixed.shape[0] // 16, add, 0)
                    in_line(axis, mixed, dst.at[m], base, far, far, m).start()

        if kind == "sum":
            for m in (0, 3):

                @pl.when(me == m)
                def _(m=m):
                    dst[3 - m] = jnp.zeros(dst.shape[1:], dst.dtype)

    def line_finish(axis, kind, src, dst, base, held, mixed):
        me = lax.axis_index(axis)
        for m in range(4):

            @pl.when(me == m)
            def _(m=m):
                block = src.at[0] if kind == "sum" else src
                for other in range(4):
                    if other == m:
                        continue
                    ends = (m, other) in ((0, 3), (3, 0))
                    relayed = (m, other) in ((1, 3), (2, 0))
                    copy = in_line(axis, block, dst.at[other], base, other, other, other)
                    if not (kind == "sum" and ends) and not (kind == "line" and relayed):
                        copy.wait_recv()
                    if not (kind == "line" and ends):
                        copy.wait_send()
                if kind == "line" and m in (1, 2):
                    in_line(axis, block, dst.at[0], base, 4, 0, 0).wait_send()

    started = []
    relays = []
    own = []
    lines = []
    for index, (axis, kind, size) in enumerate(plan):
        me = lax.axis_index(axis)
        src, dst = ins[index], outs[index]
        if kind in ("line", "sum"):
            held = spare.pop(0) if kind == "sum" else None
            mixed = spare.pop(0) if kind == "sum" else None
            line_start(axis, kind, src, dst, used[0], held)
            lines.append((axis, kind, src, dst, used[0], held, mixed))
            used[0] += 5
        elif kind == "paired":
            for k in range(2, size, 2):
                copy = remote(src, dst.at[me], {axis: (me + k) % size})
                relays.append((copy, dst, axis, (me + size - k) % size))
            started.append(remote(src, dst.at[me], {axis: me + 1 - 2 * (me % 2)}))
        else:
            for k in range(1, size):
                peer = (me + k) % size
                block = src if kind == "gather" else src.at[peer]
                started.append(remote(block, dst.at[me], {axis: peer}))
    for index, (axis, kind, size) in enumerate(plan):
        me = lax.axis_index(axis)
        block = ins[index].at[me] if kind in ("swap", "sum") else ins[index]
        copy = pltpu.make_async_copy(block, outs[index].at[me], own_sem.at[index])
        copy.start()
        own.append(copy)
    for line in lines:
        line_relay(*line)
    for copy, dst, axis, slot in relays:
        copy.wait_recv()
        me = lax.axis_index(axis)
        started.append(
            remote(dst.at[slot], dst.at[slot], {axis: me + 1 - 2 * (me % 2)})
        )
    for copy, _, _, _ in relays:
        copy.wait_send()
    for copy in own:
        copy.wait()
    for copy in started:
        copy.wait()
    for line in lines:
        line_finish(*line)


def make_exchange():
    calls = [0]

    def exchange(*items):
        plan = []
        shapes = []
        copies = 0
        sent = 0
        spare = []
        for axis, kind, value in items:
            size = lax.axis_size(axis)
            if kind == "paired" and size % 2:
                kind = "gather"
            block = value.shape[1:] if kind == "swap" else value.shape
            if axis == "tensor" and size == 4 and value.dtype == jnp.bfloat16:
                kind = {"swap": "sum", "gather": "line"}[kind]
                if kind == "sum":
                    spare += [pltpu.VMEM(block, value.dtype)] * 2
            plan.append((axis, kind, size))
            copies += 5 if kind in ("line", "sum") else size - 1
            shapes.append(jax.ShapeDtypeStruct((size,) + block, value.dtype))
            sent += (size - 1) * math.prod(block) * value.dtype.itemsize
        collective_id = calls[0]
        calls[0] += 1
        return pl.pallas_call(
            lambda *refs: exchange_kernel(tuple(plan), *refs),
            out_shape=tuple(shapes),
            in_specs=[pl.BlockSpec(memory_space=pltpu.VMEM)] * len(plan),
            out_specs=tuple([pl.BlockSpec(memory_space=pltpu.VMEM)] * len(plan)),
            scratch_shapes=[
                pltpu.SemaphoreType.DMA((copies,)),
                pltpu.SemaphoreType.DMA((copies,)),
                pltpu.SemaphoreType.DMA((len(plan),)),
                *spare,
            ],
            compiler_params=pltpu.CompilerParams(
                collective_id=collective_id,
                has_side_effects=True,
                vmem_limit_bytes=48 * 1024 * 1024,
            ),
            cost_estimate=pl.CostEstimate(flops=0, bytes_accessed=sent, transcendentals=0),
            name=f"exchange_{collective_id}",
        )(*[value for _, _, value in items])

    return exchange


MESH = pl.DeviceIdType.MESH


class Place:
    def __init__(self):
        self.dp = lax.axis_index("dp")
        self.z = lax.axis_index("tensor")
        self.core = lax.rem(self.dp, 2)
        self.pair = lax.div(self.z, 2)
        self.low = lax.rem(self.z, 2)
        self.rank = 2 * self.core + self.low
        self.native = self.core == self.pair
        self.block = lax.div(self.dp, 2)
        self.x = lax.rem(self.block, 2)
        self.y = lax.div(self.block, 2)
        self.base = self.dp - self.core

    def sibling(self):
        return {"dp": self.base + 1 - self.core, "tensor": self.z}

    def cross(self, core):
        return {"dp": self.base + core, "tensor": self.z + 1 - 2 * self.low}

    def far(self, core):
        return {"dp": self.base + core, "tensor": self.z + 2 - 4 * self.pair}

    def beside(self):
        return {"dp": self.dp + 2 - 4 * self.x, "tensor": self.z}

    def above(self):
        return {"dp": self.dp + 4 - 8 * self.y, "tensor": self.z}

    def in_line(self, index):
        return {"dp": self.base + lax.rem(index, 2), "tensor": lax.div(index, 2)}

    def rank_at(self, core, low):
        return 2 * core + low

    def block_at(self, dy, dx):
        y = 1 - self.y if dy else self.y
        x = 1 - self.x if dx else self.x
        return 2 * y + x


class Wires:
    def __init__(self, send_sem, recv_sem, own_sem):
        self.send_sem, self.recv_sem, self.own_sem = send_sem, recv_sem, own_sem
        self.used = 0
        self.own_used = 0

    def take(self, count):
        at = self.used
        self.used += count
        return at

    def take_own(self, count=1):
        at = self.own_used
        self.own_used += count
        return at

    def copy(self, src, dst, device, send, recv):
        return pltpu.make_async_remote_copy(
            src_ref=src,
            dst_ref=dst,
            send_sem=self.send_sem.at[send],
            recv_sem=self.recv_sem.at[recv],
            device_id=device,
            device_id_type=MESH,
        )

    def local(self, src, dst, slot):
        return pltpu.make_async_copy(src, dst, self.own_sem.at[slot])


def add_rows(dst, *parts):
    rows = dst.shape[0]
    step = 16 if rows % 16 == 0 else 8

    def body(index, carry):
        at = pl.ds(index * step, step)
        total = parts[0][at].astype(jnp.float32)
        for part in parts[1:]:
            total = total + part[at].astype(jnp.float32)
        dst[at] = total.astype(dst.dtype)
        return carry

    lax.fori_loop(0, rows // step, body, 0)


class Gather:
    peers = ("sibling", "cross")
    copies = 5
    owns = 1

    @staticmethod
    def shape(value):
        return (4,) + value.shape

    @staticmethod
    def scratch(value):
        return []

    def __init__(self, place, wires, src, dst, spare):
        self.p, self.w, self.src, self.dst = place, wires, src, dst
        self.at = wires.take(self.copies)
        self.own = wires.take_own()

    def _copies(self):
        p, w, src, dst, at = self.p, self.w, self.src, self.dst, self.at
        other = 1 - p.core
        near = p.rank_at(p.core, 1 - p.low)
        skew = p.rank_at(other, 1 - p.low)
        sib = p.sibling()
        return [
            lambda: w.copy(src, dst.at[p.rank], sib, at, at),
            lambda: w.copy(src.at[p.core], dst.at[p.rank, p.core], p.cross(p.core), at + 1, at + 1),
            lambda: w.copy(src.at[other], dst.at[p.rank, other], p.cross(other), at + 2, at + 2),
            lambda: w.copy(dst.at[near, p.core], dst.at[near, p.core], sib, at + 3, at + 4),
            lambda: w.copy(dst.at[skew, p.core], dst.at[skew, p.core], sib, at + 4, at + 3),
        ]

    def start(self):
        made = self._copies()
        for copy in (made[1], made[2], made[0]):
            copy().start()
        self.w.local(self.src, self.dst.at[self.p.rank], self.own).start()

    def relay(self):
        made = self._copies()
        made[1]().wait_recv()
        made[3]().start()
        made[2]().wait_recv()
        made[4]().start()

    def relay_more(self):
        pass

    def finish(self):
        made = self._copies()
        for index in (0, 3, 4):
            made[index]().wait_recv()
        for copy in made:
            copy().wait_send()
        self.w.local(self.src, self.dst.at[self.p.rank], self.own).wait()


class Reduce:
    peers = ("sibling", "cross")
    copies = 3
    owns = 1

    @staticmethod
    def shape(value):
        return (3,) + value.shape[1:]

    @staticmethod
    def scratch(value):
        return [pltpu.VMEM(value.shape[1:], value.dtype)] * 2

    def __init__(self, place, wires, src, dst, spare):
        self.p, self.w, self.src, self.dst = place, wires, src, dst
        self.held, self.mixed = spare
        self.at = wires.take(self.copies)
        self.own = wires.take_own()

    def _copies(self):
        p, w, src, dst, at = self.p, self.w, self.src, self.dst, self.at
        other = 1 - p.core
        sib = p.sibling()
        return [
            lambda: w.copy(src.at[p.rank_at(other, p.low)], dst.at[1], sib, at, at),
            lambda: w.copy(src.at[p.rank_at(other, 1 - p.low)], self.held, sib, at + 1, at + 1),
            lambda: w.copy(self.mixed, dst.at[2], p.cross(p.core), at + 2, at + 2),
        ]

    def start(self):
        made = self._copies()
        made[1]().start()
        made[0]().start()
        self.w.local(self.src.at[self.p.rank], self.dst.at[0], self.own).start()

    def relay(self):
        made = self._copies()
        made[1]().wait_recv()
        add_rows(self.mixed, self.held, self.src.at[self.p.rank_at(self.p.core, 1 - self.p.low)])
        made[2]().start()

    def relay_more(self):
        pass

    def finish(self):
        made = self._copies()
        made[0]().wait_recv()
        made[2]().wait_recv()
        for copy in made:
            copy().wait_send()
        self.w.local(self.src.at[self.p.rank], self.dst.at[0], self.own).wait()


class Pairing:
    peers = ("sibling", "far")
    copies = 3
    owns = 1

    @staticmethod
    def shape(value):
        return (2,) + value.shape

    @staticmethod
    def scratch(value):
        return []

    def __init__(self, place, wires, src, dst, spare):
        self.p, self.w, self.src, self.dst = place, wires, src, dst
        self.at = wires.take(self.copies)
        self.own = wires.take_own()

    def _near(self):
        p, at = self.p, self.at
        return self.w.copy(self.src, self.dst.at[p.core], p.sibling(), at, at)

    def _far(self, recv):
        p, at = self.p, self.at
        return self.w.copy(self.src, self.dst.at[p.core], p.far(p.pair), at + 1, recv)

    def start(self):
        p = self.p
        self._far(self.at + 1 + p.core).start()

        @pl.when(p.native)
        def _():
            self.w.local(self.src, self.dst.at[p.core], self.own).start()

        @pl.when(jnp.logical_not(p.native))
        def _():
            self._near().start()

    def settle(self):
        p = self.p

        @pl.when(p.native)
        def _():
            self._near().wait_recv()
            self.w.local(self.src, self.dst.at[p.core], self.own).wait()

        @pl.when(jnp.logical_not(p.native))
        def _():
            self._far(self.at + 1).wait_recv()
            self._far(self.at + 2).wait_recv()

    def sent(self):
        p = self.p
        self._far(self.at + 1).wait_send()

        @pl.when(jnp.logical_not(p.native))
        def _():
            self._near().wait_send()

    def relay(self):
        pass

    def relay_more(self):
        pass

    def finish(self):
        self.settle()
        self.sent()


class Spread:
    peers = ("beside", "above")
    copies = 4
    owns = 1

    @staticmethod
    def shape(value):
        return (4,) + value.shape

    @staticmethod
    def scratch(value):
        return []

    def __init__(self, place, wires, src, dst, spare):
        self.p, self.w, self.src, self.dst = place, wires, src, dst
        self.at = wires.take(self.copies)
        self.own = wires.take_own()

    def _copies(self):
        p, w, src, dst, at = self.p, self.w, self.src, self.dst, self.at
        row, column = p.block_at(0, 1), p.block_at(1, 0)
        return [
            lambda: w.copy(src, dst.at[p.block], p.beside(), at, at),
            lambda: w.copy(src, dst.at[p.block], p.above(), at + 1, at + 1),
            lambda: w.copy(dst.at[row, 0], dst.at[row, 0], p.above(), at + 2, at + 2),
            lambda: w.copy(dst.at[column, 1], dst.at[column, 1], p.beside(), at + 3, at + 3),
        ]

    def start(self):
        made = self._copies()
        made[0]().start()
        made[1]().start()
        self.w.local(self.src, self.dst.at[self.p.block], self.own).start()

    def relay(self):
        pass

    def relay_more(self):
        made = self._copies()
        made[0]().wait_recv()
        made[2]().start()
        made[1]().wait_recv()
        made[3]().start()

    def finish(self):
        made = self._copies()
        made[2]().wait_recv()
        made[3]().wait_recv()
        for copy in made:
            copy().wait_send()
        self.w.local(self.src, self.dst.at[self.p.block], self.own).wait()


class Fetch:
    peers = ("sibling", "far", "beside", "above")
    copies = 7
    owns = 2

    @staticmethod
    def shape(value):
        return (4, 2) + value.shape

    @staticmethod
    def scratch(value):
        return [pltpu.VMEM((2,) + value.shape, value.dtype)]

    def __init__(self, place, wires, src, dst, spare):
        self.one = Pairing(place, wires, src, spare[0], [])
        self.two = Spread(place, wires, spare[0], dst, [])

    def start(self):
        self.one.start()

    def relay(self):
        self.one.settle()
        self.two.start()

    def relay_more(self):
        self.two.relay_more()

    def finish(self):
        self.one.sent()
        self.two.finish()


class Total:
    peers = ("beside", "above")
    copies = 6
    owns = 0

    @staticmethod
    def shape(value):
        return value.shape[1:]

    @staticmethod
    def scratch(value):
        one = pltpu.VMEM(value.shape[2:], value.dtype)
        two = pltpu.VMEM(value.shape[1:], value.dtype)
        return [two, two, two, one, one]

    def __init__(self, place, wires, src, dst, spare):
        self.p, self.w, self.src, self.dst = place, wires, src, dst
        self.from_x, self.from_y, self.last, self.to_y, self.to_x = spare
        self.at = wires.take(self.copies)

    def _copies(self):
        p, w, src, at = self.p, self.w, self.src, self.at
        here_x, here_y, skew = p.block_at(0, 1), p.block_at(1, 0), p.block_at(1, 1)
        return [
            lambda: w.copy(src.at[here_x, 0], self.from_x.at[0], p.beside(), at, at),
            lambda: w.copy(src.at[skew, 0], self.from_x.at[1], p.beside(), at + 1, at + 1),
            lambda: w.copy(src.at[here_y, 1], self.from_y.at[0], p.above(), at + 2, at + 2),
            lambda: w.copy(src.at[skew, 1], self.from_y.at[1], p.above(), at + 3, at + 3),
            lambda: w.copy(self.to_y, self.last.at[0], p.above(), at + 4, at + 4),
            lambda: w.copy(self.to_x, self.last.at[1], p.beside(), at + 5, at + 5),
        ]

    def start(self):
        made = self._copies()
        for index in (1, 3, 0, 2):
            made[index]().start()

    def relay(self):
        pass

    def relay_more(self):
        made = self._copies()
        p = self.p
        made[1]().wait_recv()
        add_rows(self.to_y, self.src.at[p.block_at(1, 0), 0], self.from_x.at[1])
        made[4]().start()
        made[3]().wait_recv()
        add_rows(self.to_x, self.src.at[p.block_at(0, 1), 1], self.from_y.at[1])
        made[5]().start()

    def finish(self):
        made = self._copies()
        p = self.p
        for index in (0, 2, 4, 5):
            made[index]().wait_recv()
        add_rows(self.dst.at[0], self.src.at[p.block, 0], self.from_x.at[0], self.last.at[0])
        add_rows(self.dst.at[1], self.src.at[p.block, 1], self.from_y.at[0], self.last.at[1])
        for copy in made:
            copy().wait_send()


class Deliver:
    peers = ("sibling", "far")
    copies = 4
    owns = 1

    @staticmethod
    def shape(value):
        return value.shape

    @staticmethod
    def scratch(value):
        return []

    def __init__(self, place, wires, src, dst, spare):
        self.p, self.w, self.src, self.dst = place, wires, src, dst
        self.at = wires.take(self.copies)
        self.own = wires.take_own()

    def _near(self):
        p, at = self.p, self.at
        return self.w.copy(self.src.at[1 - p.core], self.dst.at[0], p.sibling(), at, at)

    def _far(self, core):
        p, at = self.p, self.at
        return self.w.copy(
            self.src.at[core], self.dst.at[1], p.far(jnp.int32(core)), at + 1 + core, at + 1
        )

    def start(self):
        p = self.p

        @pl.when(p.native)
        def _():
            self._near().start()
            self.w.local(self.src.at[p.core], self.dst.at[0], self.own).start()

        @pl.when(jnp.logical_not(p.native))
        def _():
            self._far(0).start()
            self._far(1).start()

    def relay(self):
        pass

    def relay_more(self):
        pass

    def finish(self):
        p = self.p
        self._far(0).wait_recv()

        @pl.when(p.native)
        def _():
            self._near().wait_send()
            self.w.local(self.src.at[p.core], self.dst.at[0], self.own).wait()

        @pl.when(jnp.logical_not(p.native))
        def _():
            self._near().wait_recv()
            self._far(0).wait_send()
            self._far(1).wait_send()


class Swap:
    peers = ("far",)
    copies = 1
    owns = 1

    @staticmethod
    def shape(value):
        return value.shape

    @staticmethod
    def scratch(value):
        return []

    def __init__(self, place, wires, src, dst, spare):
        self.p, self.w, self.src, self.dst = place, wires, src, dst
        self.at = wires.take(self.copies)
        self.own = wires.take_own()

    def _copy(self):
        p, at = self.p, self.at
        return self.w.copy(self.src, self.dst, p.far(1 - p.core), at, at)

    def start(self):
        @pl.when(self.p.native)
        def _():
            self.w.local(self.src, self.dst, self.own).start()

        @pl.when(jnp.logical_not(self.p.native))
        def _():
            self._copy().start()

    def relay(self):
        pass

    def relay_more(self):
        pass

    def finish(self):
        @pl.when(self.p.native)
        def _():
            self.w.local(self.src, self.dst, self.own).wait()

        @pl.when(jnp.logical_not(self.p.native))
        def _():
            self._copy().wait()


class Small:
    peers = ("beside", "above", "line")
    copies = 20
    owns = 1

    @staticmethod
    def shape(value):
        return (8,) + value.shape[2:]

    @staticmethod
    def scratch(value):
        return Total.scratch(value) + [pltpu.VMEM(value.shape[1:], value.dtype)]

    def __init__(self, place, wires, src, dst, spare):
        self.sums = spare[-1]
        self.total = Total(place, wires, src, self.sums, spare[:-1])
        self.p, self.w, self.dst = place, wires, dst
        self.at = wires.take(14)
        self.own = wires.take_own()

    def _ends(self, offset):
        p, at = self.p, self.at
        me = 2 * p.z + p.core
        to = lax.rem(me + offset, 8)
        return self.w.copy(
            self.sums.at[lax.rem(to, 2)], self.dst.at[me], p.in_line(to), at + offset - 1, at + 6 + offset
        )

    def _mine(self):
        p = self.p
        return self.w.local(self.sums.at[p.core], self.dst.at[2 * p.z + p.core], self.own)

    def start(self):
        self.total.start()

    def relay(self):
        pass

    def relay_more(self):
        self.total.relay_more()
        self.total.finish()
        for offset in range(1, 8):
            self._ends(offset).start()
        self._mine().start()

    def finish(self):
        self._mine().wait()
        for offset in range(1, 8):
            self._ends(offset).wait()


def greet(place, kinds):
    p = place
    devices = []
    if "sibling" in kinds or "line" in kinds:
        devices.append(p.sibling())
    if "cross" in kinds or "line" in kinds:
        devices += [p.cross(jnp.int32(0)), p.cross(jnp.int32(1))]
    if "far" in kinds or "line" in kinds:
        devices += [p.far(jnp.int32(0)), p.far(jnp.int32(1))]
    if "line" in kinds:
        last = 3 - p.z
        devices += [{"dp": p.base, "tensor": last}, {"dp": p.base + 1, "tensor": last}]
    if "beside" in kinds:
        devices.append(p.beside())
    if "above" in kinds:
        devices.append(p.above())
    barrier = pltpu.get_barrier_semaphore()
    for device in devices:
        pl.semaphore_signal(barrier, inc=1, device_id=device, device_id_type=MESH)
    pl.semaphore_wait(barrier, len(devices))


def round_kernel(kinds, *refs):
    count = len(kinds)
    ins, outs = refs[:count], refs[count : 2 * count]
    wires = Wires(*refs[2 * count : 2 * count + 3])
    spare = list(refs[2 * count + 3 :])
    place = Place()
    greet(place, {peer for kind, _ in kinds for peer in kind.peers})
    jobs = []
    for (kind, held), src, dst in zip(kinds, ins, outs):
        jobs.append(kind(place, wires, src, dst, spare[:held]))
        del spare[:held]
    for job in jobs:
        job.start()
    for job in jobs:
        job.relay()
    for job in jobs:
        job.relay_more()
    for job in jobs:
        job.finish()


def make_rounds():
    calls = [0]

    def rounds(*items):
        kinds, shapes, scratch = [], [], []
        copies = owns = sent = 0
        for kind, value in items:
            held = kind.scratch(value)
            kinds.append((kind, len(held)))
            scratch += held
            shapes.append(jax.ShapeDtypeStruct(kind.shape(value), value.dtype))
            copies += kind.copies
            owns += kind.owns
            sent += math.prod(kind.shape(value)) * value.dtype.itemsize
        collective_id = calls[0]
        calls[0] += 1
        return pl.pallas_call(
            lambda *refs: round_kernel(tuple(kinds), *refs),
            out_shape=tuple(shapes),
            in_specs=[pl.BlockSpec(memory_space=pltpu.VMEM)] * len(kinds),
            out_specs=tuple([pl.BlockSpec(memory_space=pltpu.VMEM)] * len(kinds)),
            scratch_shapes=[
                pltpu.SemaphoreType.DMA((copies,)),
                pltpu.SemaphoreType.DMA((copies,)),
                pltpu.SemaphoreType.DMA((max(owns, 1),)),
                *scratch,
            ],
            compiler_params=pltpu.CompilerParams(
                collective_id=collective_id,
                has_side_effects=True,
                vmem_limit_bytes=48 * 1024 * 1024,
            ),
            cost_estimate=pl.CostEstimate(flops=0, bytes_accessed=sent, transcendentals=0),
            name=f"round_{collective_id}",
        )(*[value for _, value in items])

    return rounds


def masked_scores(queries, key_vecs, segments, score_scale):
    positions = jnp.arange(key_vecs.shape[0], dtype=jnp.int32)
    allowed = (segments[:, None] == segments[None, :]) & (
        positions[None, :] <= positions[:, None]
    )
    scores = (
        jnp.einsum("qhd,khd->hqk", queries, key_vecs, preferred_element_type=jnp.float32)
        * score_scale
    )
    return jnp.where(allowed[None], scores, -jnp.inf)


def attend(queries, key_vecs, val_vecs, segments, score_scale):
    scores = masked_scores(queries, key_vecs, segments, score_scale)
    row_max = jnp.max(scores, axis=-1, keepdims=True)
    log_total = row_max + jnp.log(jnp.sum(jnp.exp(scores - row_max), axis=-1, keepdims=True))
    probs_half = jnp.exp(scores - log_total).astype(jnp.bfloat16)
    attended = jnp.einsum("hqk,khd->qhd", probs_half, val_vecs, preferred_element_type=jnp.float32)
    return (attended.astype(jnp.bfloat16).reshape(queries.shape[0], -1), log_total)


def attend_back(queries, key_vecs, val_vecs, grad_attended, log_total, segments, score_scale):
    scores = masked_scores(queries, key_vecs, segments, score_scale)
    soft_probs = jnp.exp(scores - log_total)
    probs_half = soft_probs.astype(jnp.bfloat16)
    grad_probs = jnp.einsum(
        "qhd,khd->hqk", grad_attended, val_vecs, preferred_element_type=jnp.float32
    )
    val_grad = jnp.einsum(
        "hqk,qhd->khd", probs_half, grad_attended, preferred_element_type=jnp.float32
    )
    row_dot = jnp.sum(grad_probs * soft_probs, axis=-1, keepdims=True)
    score_grad = (soft_probs * (grad_probs - row_dot) * score_scale).astype(jnp.bfloat16)
    query_grad = jnp.einsum(
        "hqk,khd->qhd", score_grad, key_vecs, preferred_element_type=jnp.float32
    )
    key_grad = jnp.einsum("hqk,qhd->khd", score_grad, queries, preferred_element_type=jnp.float32)
    return (query_grad, key_grad, val_grad)


def pack(pieces, width, tile):
    flat = jnp.concatenate([piece.reshape(-1) for piece in pieces])
    unit = width * tile
    return jnp.pad(flat, (0, -flat.shape[0] % unit)).reshape(-1, width)


def unpack(packed, shapes):
    flat = packed.reshape(packed.shape[0], -1)
    pieces = []
    at = 0
    for shape in shapes:
        length = math.prod(shape)
        pieces.append(flat[:, at : at + length].reshape((packed.shape[0],) + shape))
        at += length
    return pieces


def shards(x_in, d_out, seq_lengths, w_qkv, b_qv, w_o, w_1, b_ffn, w_2, norm_gains, vec_biases):
    exchange = make_exchange()
    own_rows, width = x_in.shape
    tensor_size = lax.axis_size("tensor")
    dp_size = lax.axis_size("dp")
    group_rows = own_rows * tensor_size
    layer_count = w_qkv.shape[0]
    local_width = w_qkv.shape[3]
    local_heads = local_width // HEAD_DIM
    qkv_width = 3 * local_width
    score_scale = 1.0 / math.sqrt(HEAD_DIM)
    segments = segment_ids(seq_lengths[0], group_rows)
    half = jnp.bfloat16

    def shard_of(name, layer_index):
        if name == "qkv":
            return w_qkv[layer_index].reshape(w_qkv.shape[1], qkv_width)
        if name == "out":
            return w_o[layer_index].T
        if name == "up":
            return w_1[layer_index]
        return w_2[layer_index].T

    weights = {}

    def step(tensor_items, fetched=(), sums=()):
        items = [("tensor", kind, value) for kind, value in tensor_items]
        items += [("dp", "paired", shard_of(*key)) for key in fetched]
        items += [("dp", "swap", value) for value in sums]
        results = list(exchange(*items))
        for position, key in enumerate(fetched):
            piece = results[len(tensor_items) + position]
            weights[key] = piece.reshape(dp_size * piece.shape[1], piece.shape[2])
        gathered = [
            piece.reshape(group_rows, width) if kind == "gather" else piece.astype(jnp.float32).sum(0)
            for (kind, _), piece in zip(tensor_items, results)
        ]
        totals = [
            piece.astype(jnp.float32).sum(0) for piece in results[len(items) - len(sums) :]
        ]
        return gathered, totals

    def to_owners(partial):
        return ("swap", partial.astype(half).reshape(tensor_size, own_rows, width))

    def by_owner(gradient):
        return gradient.astype(half).reshape(dp_size, -1, gradient.shape[-1])

    small_shapes = [b_qv.shape, b_ffn.shape, norm_gains.shape, vec_biases.shape]
    small = pack([b_qv, b_ffn, norm_gains, vec_biases], 128, 16)
    first = exchange(
        ("tensor", "gather", d_out.astype(half)),
        ("dp", "paired", small),
        ("dp", "paired", shard_of("qkv", 0)),
    )
    last_grad_half = first[0].reshape(group_rows, width)
    weights["qkv", 0] = first[2].reshape(width, qkv_width)
    qv_all, ffn_all, gain_all, bias_all = [
        jnp.moveaxis(piece, 0, -2).reshape(piece.shape[1:-1] + (-1,)).astype(jnp.float32)
        for piece in unpack(first[1], small_shapes)
    ]

    caches = []
    hidden_in = x_in
    for layer_index in range(layer_count):
        last = layer_index == layer_count - 1
        following = layer_index + 1
        gain_rows = gain_all[layer_index]
        bias_rows = bias_all[layer_index]
        normed_own, unit_one, inv_one = layer_norm(hidden_in, gain_rows[0], bias_rows[0])
        fetched = [("out", 0), ("up", 0)] if layer_index == 0 else [("down", layer_index)]
        (normed_one,), _ = step([("gather", normed_own.astype(half))], fetched)
        projected = jnp.dot(
            normed_one, weights["qkv", layer_index], preferred_element_type=jnp.float32
        ).reshape(group_rows, 3, local_width)
        qv_bias = qv_all[layer_index]
        heads = (group_rows, local_heads, HEAD_DIM)
        queries = (projected[:, 0] + qv_bias[0]).astype(half).reshape(heads)
        key_vecs = projected[:, 1].astype(half).reshape(heads)
        val_vecs = (projected[:, 2] + qv_bias[1]).astype(half).reshape(heads)
        attended, log_total = attend(queries, key_vecs, val_vecs, segments, score_scale)
        fetched = [("down", 0)] if layer_index == 0 else []
        (summed,), _ = step(
            [to_owners(contract_last(attended, weights["out", layer_index]))], fetched
        )
        residual_mid = hidden_in + summed + bias_rows[2]
        normed_own_two, unit_two, inv_two = layer_norm(residual_mid, gain_rows[1], bias_rows[1])
        fetched = [] if last else [("qkv", following), ("out", following)]
        (normed_two,), _ = step([("gather", normed_own_two.astype(half))], fetched)
        pre_act = (
            jnp.dot(normed_two, weights["up", layer_index], preferred_element_type=jnp.float32)
            + ffn_all[layer_index]
        )
        gelu_value, gelu_slope = gelu_pair(pre_act)
        activated = gelu_value.astype(half)
        ffn_partial = to_owners(contract_last(activated, weights["down", layer_index]))
        if not last:
            (summed,), _ = step([ffn_partial], [("up", following)])
            hidden_in = residual_mid + summed + bias_rows[3]
        caches.append(
            (
                unit_one,
                inv_one,
                normed_one,
                queries,
                key_vecs,
                val_vecs,
                attended,
                log_total,
                unit_two,
                inv_two,
                normed_two,
                activated,
                gelu_slope,
            )
        )
    back = d_out
    grads = {}
    small_terms = [None] * layer_count
    output = None
    for layer_index in reversed(range(layer_count)):
        last = layer_index == layer_count - 1
        gain_rows = gain_all[layer_index]
        (
            unit_one,
            inv_one,
            normed_one,
            queries,
            key_vecs,
            val_vecs,
            attended,
            log_total,
            unit_two,
            inv_two,
            normed_two,
            activated,
            gelu_slope,
        ) = caches[layer_index]
        if last:
            grad_half = last_grad_half
        else:
            (grad_half,), (grads["qkv", layer_index + 1],) = step(
                [("gather", back.astype(half))], sums=[waiting]
            )
        grad_down = by_owner(contract_first(grad_half, activated))
        grad_pre = (
            jnp.dot(grad_half, weights["down", layer_index], preferred_element_type=jnp.float32)
            * gelu_slope
        )
        grad_pre_half = grad_pre.astype(half)
        grad_up = by_owner(contract_first(normed_two, grad_pre_half))
        partial = to_owners(contract_last(grad_pre_half, weights["up", layer_index]))
        if last:
            cut = grad_up.shape[2] // 2
            (grad_normed_two, summed), (grads["down", layer_index], up_left) = step(
                [partial, ffn_partial], sums=[grad_down, grad_up[:, :, :cut]]
            )
            output = residual_mid + summed + bias_all[layer_index][3]
        else:
            (grad_normed_two,), (grads["down", layer_index],) = step([partial], sums=[grad_down])
        grad_mid = back + norm_back(grad_normed_two, unit_two, inv_two, gain_rows[1])
        (grad_mid_half,), (up_part,) = step(
            [("gather", grad_mid.astype(half))], sums=[grad_up[:, :, cut:] if last else grad_up]
        )
        grads["up", layer_index] = (
            jnp.concatenate([up_left, up_part], axis=1) if last else up_part
        )
        grad_out = by_owner(contract_first(grad_mid_half, attended))
        grad_attended = jnp.dot(
            grad_mid_half, weights["out", layer_index], preferred_element_type=jnp.float32
        )
        grad_attended = grad_attended.astype(half).reshape(group_rows, local_heads, HEAD_DIM)
        query_grad, key_grad, val_grad = attend_back(
            queries, key_vecs, val_vecs, grad_attended, log_total, segments, score_scale
        )
        flat = (group_rows, local_width)
        grad_qkv = jnp.concatenate(
            [part.astype(half).reshape(flat) for part in (query_grad, key_grad, val_grad)], axis=1
        )
        grad_qkv_weight = by_owner(contract_first(normed_one, grad_qkv))
        (grad_normed_one,), sent_now = step(
            [to_owners(contract_last(grad_qkv, weights["qkv", layer_index]))],
            sums=[grad_out] if layer_index else [grad_out, grad_qkv_weight],
        )
        grads["out", layer_index] = sent_now[0]
        if layer_index:
            waiting = grad_qkv_weight
        else:
            grads["qkv", layer_index] = sent_now[1]
        small_terms[layer_index] = (
            jnp.stack(
                [
                    jnp.sum(query_grad, axis=0).reshape(local_width),
                    jnp.sum(val_grad, axis=0).reshape(local_width),
                ]
            ),
            jnp.sum(grad_pre, axis=0),
            jnp.stack(
                [
                    jnp.sum(grad_normed_one * unit_one, axis=0),
                    jnp.sum(grad_normed_two * unit_two, axis=0),
                ]
            ),
            jnp.stack(
                [
                    jnp.sum(grad_normed_one, axis=0),
                    jnp.sum(grad_normed_two, axis=0),
                    jnp.sum(grad_mid, axis=0),
                    jnp.sum(back, axis=0),
                ]
            ),
        )
        back = grad_mid + norm_back(grad_normed_one, unit_one, inv_one, gain_rows[0])

    def split_owner(piece):
        return jnp.moveaxis(
            piece.reshape(piece.shape[:-1] + (dp_size, -1)), -2, 0
        ).reshape(dp_size, -1)

    stacked = [
        split_owner(jnp.stack([small_terms[index][member] for index in range(layer_count)]))
        for member in (2, 3, 0, 1)
    ]
    flat = jnp.concatenate(stacked, axis=1)
    flat = jnp.pad(flat, ((0, 0), (0, -flat.shape[1] % 1024)))
    (parts,) = exchange(("dp", "swap", flat.reshape(dp_size, -1, 128)))
    total = parts.sum(0)
    (shared,) = exchange(("tensor", "gather", total))
    everyone = shared.sum(0).reshape(-1)
    gain_size, bias_size = norm_gains.size, vec_biases.size
    mine = total.reshape(-1)[gain_size + bias_size :]

    def stack_layers(name, shape, transposed):
        parts = [grads[name, index] for index in range(layer_count)]
        return jnp.stack([part.T if transposed else part for part in parts]).reshape(shape)

    return (
        output,
        back,
        stack_layers("qkv", w_qkv.shape, False),
        mine[: b_qv.size].reshape(b_qv.shape),
        stack_layers("out", w_o.shape, True),
        stack_layers("up", w_1.shape, False),
        mine[b_qv.size : b_qv.size + b_ffn.size].reshape(b_ffn.shape),
        stack_layers("down", w_2.shape, True),
        everyone[:gain_size].reshape(norm_gains.shape),
        everyone[gain_size : gain_size + bias_size].reshape(vec_biases.shape),
    )


def paired_shards(
    x_in, d_out, seq_lengths, w_qkv, b_qv, w_o, w_1, b_ffn, w_2, norm_gains, vec_biases
):
    rounds = make_rounds()
    own_rows, width = x_in.shape
    group_rows = own_rows * 4
    layer_count = w_qkv.shape[0]
    local_width = w_qkv.shape[3]
    local_heads = local_width // HEAD_DIM
    qkv_width = 3 * local_width
    score_scale = 1.0 / math.sqrt(HEAD_DIM)
    half = jnp.bfloat16
    z = lax.axis_index("tensor")
    native = lax.axis_index("dp") % 2 == z // 2

    def shard_of(name, layer_index):
        if name == "qkv":
            return w_qkv[layer_index].reshape(w_qkv.shape[1], qkv_width)
        if name == "out":
            return w_o[layer_index].T
        if name == "up":
            return w_1[layer_index]
        return w_2[layer_index].T

    def spread_rows(piece):
        return piece.reshape((-1,) + piece.shape[3:])

    def halves(rows):
        return rows.astype(half).reshape(2, own_rows // 2, width)

    def to_owners(partial):
        return partial.astype(half).reshape(4, 2 * own_rows // 2, width)

    def by_owner(gradient):
        return gradient.astype(half).reshape(4, 2, -1, gradient.shape[-1])

    def added(parts):
        return parts.astype(jnp.float32).sum(0)

    small_shapes = [b_qv.shape, b_ffn.shape, norm_gains.shape, vec_biases.shape]
    small = pack([b_qv, b_ffn, norm_gains, vec_biases], 128, 16)
    lengths = jnp.pad(seq_lengths.astype(jnp.float32), ((0, 7), (0, 126)))
    small_all, x_sent, lengths, qkv_first, pair_out, pair_up = rounds(
        (Fetch, small),
        (Swap, x_in.astype(half)),
        (Swap, lengths),
        (Fetch, shard_of("qkv", 0)),
        (Pairing, shard_of("out", 0)),
        (Pairing, shard_of("up", 0)),
    )
    weights = {("qkv", 0): spread_rows(qkv_first)}
    pairs = {("out", 0): pair_out, ("up", 0): pair_up}
    sums = {}
    grads = {}

    def step(tensor_items, fetched=(), paired=(), totalled=(), delivered=(), swapped=()):
        items = list(tensor_items)
        items += [(Spread, pairs[key]) for key in fetched]
        items += [(Pairing, shard_of(*key)) for key in paired]
        items += [(Total, value) for _, value in totalled]
        items += [(Deliver, sums[key]) for key in delivered]
        items += [(Swap, value) for value in swapped]
        results = list(rounds(*items))
        given = []
        for kind, _ in tensor_items:
            piece = results.pop(0)
            given.append(piece.reshape(group_rows, width) if kind is Gather else added(piece))
        for key in fetched:
            weights[key] = spread_rows(results.pop(0))
        for key in paired:
            pairs[key] = results.pop(0)
        for key, _ in totalled:
            sums[key] = results.pop(0)
        for key in delivered:
            grads[key] = added(results.pop(0))
        given += results
        return given

    qv_all, ffn_all, gain_all, bias_all = [
        jnp.moveaxis(piece, 0, -2).reshape(piece.shape[1:-1] + (-1,)).astype(jnp.float32)
        for piece in unpack(small_all.reshape((8,) + small.shape), small_shapes)
    ]
    first_end = lengths[0, 0]
    segments = (jnp.arange(group_rows, dtype=jnp.int32) >= first_end.astype(jnp.int32)).astype(
        jnp.int32
    )

    hidden_in = jnp.where(native, x_in, x_sent.astype(jnp.float32))
    plans = [
        dict(fetched=[("out", 0), ("up", 0)], paired=[("down", 0)]),
        dict(fetched=[("down", 0)], paired=[("qkv", 1), ("out", 1)]),
        dict(fetched=[("qkv", 1), ("out", 1)], paired=[("up", 1)]),
        dict(fetched=[("up", 1)], paired=[("down", 1)]),
        dict(fetched=[("down", 1)], swapped=[d_out.astype(half)]),
        dict(),
        dict(),
    ]
    caches = []
    for layer_index in range(layer_count):
        last = layer_index == layer_count - 1
        gain_rows = gain_all[layer_index]
        bias_rows = bias_all[layer_index]
        normed_own, unit_one, inv_one = layer_norm(hidden_in, gain_rows[0], bias_rows[0])
        normed_one, *swapped = step([(Gather, halves(normed_own))], **plans.pop(0))
        if last:
            back = jnp.where(native, d_out, swapped[0].astype(jnp.float32))
        projected = jnp.dot(
            normed_one, weights["qkv", layer_index], preferred_element_type=jnp.float32
        ).reshape(group_rows, 3, local_width)
        qv_bias = qv_all[layer_index]
        heads = (group_rows, local_heads, HEAD_DIM)
        queries = (projected[:, 0] + qv_bias[0]).astype(half).reshape(heads)
        key_vecs = projected[:, 1].astype(half).reshape(heads)
        val_vecs = (projected[:, 2] + qv_bias[1]).astype(half).reshape(heads)
        attended, log_total = attend(queries, key_vecs, val_vecs, segments, score_scale)
        early = [(Gather, halves(back))] if last else []
        summed, *gathered = step(
            [(Reduce, to_owners(contract_last(attended, weights["out", layer_index])))] + early,
            **plans.pop(0),
        )
        if last:
            grad_half = gathered[0]
        residual_mid = hidden_in + summed + bias_rows[2]
        normed_own_two, unit_two, inv_two = layer_norm(residual_mid, gain_rows[1], bias_rows[1])
        (normed_two,) = step([(Gather, halves(normed_own_two))], **plans.pop(0))
        pre_act = (
            jnp.dot(normed_two, weights["up", layer_index], preferred_element_type=jnp.float32)
            + ffn_all[layer_index]
        )
        gelu_value, gelu_slope = gelu_pair(pre_act)
        activated = gelu_value.astype(half)
        ffn_partial = (Reduce, to_owners(contract_last(activated, weights["down", layer_index])))
        if not last:
            (summed,) = step([ffn_partial], **plans.pop(0))
            hidden_in = residual_mid + summed + bias_rows[3]
        caches.append(
            (
                unit_one,
                inv_one,
                normed_one,
                queries,
                key_vecs,
                val_vecs,
                attended,
                log_total,
                unit_two,
                inv_two,
                normed_two,
                activated,
                gelu_slope,
            )
        )
    small_terms = [None] * layer_count
    sent_back = []
    for layer_index in reversed(range(layer_count)):
        last = layer_index == layer_count - 1
        gain_rows = gain_all[layer_index]
        (
            unit_one,
            inv_one,
            normed_one,
            queries,
            key_vecs,
            val_vecs,
            attended,
            log_total,
            unit_two,
            inv_two,
            normed_two,
            activated,
            gelu_slope,
        ) = caches[layer_index]
        if not last:
            (grad_half,) = step(
                [(Gather, halves(back))],
                totalled=[(("qkv", layer_index + 1), waiting)],
                delivered=[("out", layer_index + 1)],
            )
        grad_down = by_owner(contract_first(grad_half, activated))
        grad_pre = (
            jnp.dot(grad_half, weights["down", layer_index], preferred_element_type=jnp.float32)
            * gelu_slope
        )
        grad_pre_half = grad_pre.astype(half)
        grad_up = by_owner(contract_first(normed_two, grad_pre_half))
        partial = (Reduce, to_owners(contract_last(grad_pre_half, weights["up", layer_index])))
        totalled = [(("down", layer_index), grad_down)]
        if last:
            grad_normed_two, summed = step([partial, ffn_partial], totalled=totalled)
            output = residual_mid + summed + bias_all[layer_index][3]
        else:
            grad_normed_two, out_swapped = step(
                [partial],
                totalled=totalled,
                delivered=[("qkv", layer_index + 1)],
                swapped=[output.astype(half)],
            )
        grad_mid = back + norm_back(grad_normed_two, unit_two, inv_two, gain_rows[1])
        (grad_mid_half,) = step(
            [(Gather, halves(grad_mid))],
            totalled=[(("up", layer_index), grad_up)],
            delivered=[("down", layer_index)],
        )
        grad_out = by_owner(contract_first(grad_mid_half, attended))
        grad_attended = jnp.dot(
            grad_mid_half, weights["out", layer_index], preferred_element_type=jnp.float32
        )
        grad_attended = grad_attended.astype(half).reshape(group_rows, local_heads, HEAD_DIM)
        query_grad, key_grad, val_grad = attend_back(
            queries, key_vecs, val_vecs, grad_attended, log_total, segments, score_scale
        )
        flat = (group_rows, local_width)
        grad_qkv = jnp.concatenate(
            [part.astype(half).reshape(flat) for part in (query_grad, key_grad, val_grad)], axis=1
        )
        waiting = by_owner(contract_first(normed_one, grad_qkv))
        totalled = [(("out", layer_index), grad_out)]
        if not last:
            totalled.append((("qkv", layer_index), waiting))
        (grad_normed_one,) = step(
            [(Reduce, to_owners(contract_last(grad_qkv, weights["qkv", layer_index])))],
            totalled=totalled,
            delivered=[("up", layer_index)],
        )
        small_terms[layer_index] = (
            jnp.stack(
                [
                    jnp.sum(query_grad, axis=0).reshape(local_width),
                    jnp.sum(val_grad, axis=0).reshape(local_width),
                ]
            ),
            jnp.sum(grad_pre, axis=0),
            jnp.stack(
                [
                    jnp.sum(grad_normed_one * unit_one, axis=0),
                    jnp.sum(grad_normed_two * unit_two, axis=0),
                ]
            ),
            jnp.stack(
                [
                    jnp.sum(grad_normed_one, axis=0),
                    jnp.sum(grad_normed_two, axis=0),
                    jnp.sum(grad_mid, axis=0),
                    jnp.sum(back, axis=0),
                ]
            ),
        )
        back = grad_mid + norm_back(grad_normed_one, unit_one, inv_one, gain_rows[0])

    def split_owner(piece):
        return jnp.moveaxis(piece.reshape(piece.shape[:-1] + (8, -1)), -2, 0).reshape(8, -1)

    stacked = [
        split_owner(jnp.stack([small_terms[index][member] for index in range(layer_count)]))
        for member in (2, 3, 0, 1)
    ]
    flat = jnp.concatenate(stacked, axis=1)
    flat = jnp.pad(flat, ((0, 0), (0, -flat.shape[1] % 2048))).reshape(4, 2, -1, 128)
    small_parts, back_swapped, out_first, qkv_first = rounds(
        (Small, flat),
        (Swap, back.astype(half)),
        (Deliver, sums["out", 0]),
        (Deliver, sums["qkv", 0]),
    )
    grads["out", 0] = added(out_first)
    grads["qkv", 0] = added(qkv_first)
    small_parts = small_parts.reshape(8, -1)
    gain_size, bias_size = norm_gains.size, vec_biases.size
    everyone = small_parts.sum(0)
    sources = jnp.arange(8, dtype=jnp.int32)
    pair = z // 2
    mine_from = (sources == 2 * z + pair) | (sources == 2 * (z + 2 - 4 * pair) + pair)
    mine = jnp.where(mine_from[:, None], small_parts, 0.0).sum(0)[gain_size + bias_size :]

    def stack_layers(name, shape, transposed):
        parts = [grads[name, index] for index in range(layer_count)]
        parts = [part.reshape(-1, part.shape[-1]) for part in parts]
        return jnp.stack([part.T if transposed else part for part in parts]).reshape(shape)

    return (
        jnp.where(native, output, out_swapped.astype(jnp.float32)),
        jnp.where(native, back, back_swapped.astype(jnp.float32)),
        stack_layers("qkv", w_qkv.shape, False),
        mine[: b_qv.size].reshape(b_qv.shape),
        stack_layers("out", w_o.shape, True),
        stack_layers("up", w_1.shape, False),
        mine[b_qv.size : b_qv.size + b_ffn.size].reshape(b_ffn.shape),
        stack_layers("down", w_2.shape, True),
        everyone[:gain_size].reshape(norm_gains.shape),
        everyone[gain_size : gain_size + bias_size].reshape(vec_biases.shape),
    )


def solution(mesh):
    in_specs = (
        P(("dp", "tensor"), None),
        P(("dp", "tensor"), None),
        P("dp", None),
        P(None, "dp", None, "tensor"),
        P(None, None, ("tensor", "dp")),
        P(None, "tensor", "dp"),
        P(None, "dp", "tensor"),
        P(None, ("tensor", "dp")),
        P(None, "tensor", "dp"),
        P(None, None, "dp"),
        P(None, None, "dp"),
    )
    out_specs = (
        P(("dp", "tensor"), None),
        P(("dp", "tensor"), None),
        P(None, "dp", None, "tensor"),
        P(None, None, ("tensor", "dp")),
        P(None, "tensor", "dp"),
        P(None, "dp", "tensor"),
        P(None, ("tensor", "dp")),
        P(None, "tensor", "dp"),
        P(None, None, "dp"),
        P(None, None, "dp"),
    )
    paired = mesh.shape["dp"] == 8 and mesh.shape["tensor"] == 4
    body = paired_shards if paired else shards
    return jax.shard_map(body, mesh=mesh, in_specs=in_specs, out_specs=out_specs, check_vma=False)
```

```python
import math

import jax
import jax.numpy as jnp
from jax import lax
from jax.experimental import pallas as pl
from jax.experimental.pallas import tpu as pltpu
from jax.sharding import PartitionSpec as P

HEAD_DIM = 64


NORM_EPS = 1e-05
GELU_COEFF = 0.7978845608028654
GELU_CUBIC = 0.044715


def layer_norm(inputs, gain_row, bias_row):
    row_mean = jnp.mean(inputs, axis=-1, keepdims=True)
    centered = inputs - row_mean
    inv_std = lax.rsqrt(jnp.mean(centered * centered, axis=-1, keepdims=True) + NORM_EPS)
    normed = centered * inv_std
    return (normed * gain_row + bias_row, normed, inv_std)


def norm_back(grad_in, normed, inv_std, gain_row):
    scaled = grad_in * gain_row
    return inv_std * (
        scaled
        - jnp.mean(scaled, axis=-1, keepdims=True)
        - normed * jnp.mean(scaled * normed, axis=-1, keepdims=True)
    )


def gelu_pair(pre_act):
    squared = pre_act * pre_act
    tangent = jnp.tanh(GELU_COEFF * (pre_act + GELU_CUBIC * squared * pre_act))
    gelu_value = 0.5 * pre_act * (1.0 + tangent)
    gelu_slope = 0.5 * (1.0 + tangent) + 0.5 * pre_act * (1.0 - tangent * tangent) * GELU_COEFF * (
        1.0 + 3.0 * GELU_CUBIC * squared
    )
    return (gelu_value, gelu_slope)


def segment_ids(lengths, total_rows):
    positions = jnp.arange(total_rows, dtype=jnp.int32)
    found = jnp.zeros_like(positions)
    end = jnp.int32(0)
    for index in range(lengths.shape[0]):
        end = end + lengths[index]
        found = found + (positions >= end).astype(jnp.int32)
    return found


def contract_first(left, right):
    return lax.dot_general(
        left, right, (((0,), (0,)), ((), ())), preferred_element_type=jnp.float32
    )


def contract_last(left, right):
    return lax.dot_general(
        left, right, (((1,), (1,)), ((), ())), preferred_element_type=jnp.float32
    )

def exchange_kernel(plan, *refs):
    count = len(plan)
    ins = refs[:count]
    outs = refs[count : 2 * count]
    send_sem, recv_sem, own_sem = refs[2 * count : 2 * count + 3]
    spare = list(refs[2 * count + 3 :])

    greeted = []
    for axis in sorted({axis for axis, _, _ in plan}):
        kinds = {kind for name, kind, _ in plan if name == axis}
        size = [n for name, _, n in plan if name == axis][0]
        me = lax.axis_index(axis)
        if kinds == {"paired"}:
            greeted.append({axis: me + 1 - 2 * (me % 2)})
            greeted += [{axis: (me + k) % size} for k in range(2, size, 2)]
        else:
            greeted += [{axis: (me + k) % size} for k in range(1, size)]
    barrier = pltpu.get_barrier_semaphore()
    for device in greeted:
        pl.semaphore_signal(
            barrier, inc=1, device_id=device, device_id_type=pl.DeviceIdType.MESH
        )
    pl.semaphore_wait(barrier, len(greeted))

    used = [0]

    def remote(src, dst, device):
        slot = used[0]
        used[0] += 1
        copy = pltpu.make_async_remote_copy(
            src_ref=src,
            dst_ref=dst,
            send_sem=send_sem.at[slot],
            recv_sem=recv_sem.at[slot],
            device_id=device,
            device_id_type=pl.DeviceIdType.MESH,
        )
        copy.start()
        return copy

    def in_line(axis, src, dst, base, place, target, arrival):
        return pltpu.make_async_remote_copy(
            src_ref=src,
            dst_ref=dst,
            send_sem=send_sem.at[base + place],
            recv_sem=recv_sem.at[base + arrival],
            device_id={axis: jnp.int32(target)},
            device_id_type=pl.DeviceIdType.MESH,
        )

    def line_start(axis, kind, src, dst, base, held):
        me = lax.axis_index(axis)
        for m in range(4):

            @pl.when(me == m)
            def _(m=m):
                if kind == "sum" and m in (0, 3):
                    far = 3 - m
                    near = 1 if m == 0 else 2
                    in_line(axis, src.at[far], held, base, far, near, 4).start()
                for target in ((2, 1), (3, 2, 0), (0, 1, 3), (1, 2))[m]:
                    if kind == "sum" and (m, target) in ((1, 3), (2, 0)):
                        continue
                    block = src.at[target] if kind == "sum" else src
                    in_line(axis, block, dst.at[m], base, target, target, m).start()

    def line_relay(axis, kind, src, dst, base, held, mixed):
        me = lax.axis_index(axis)
        for m in (1, 2):

            @pl.when(me == m)
            def _(m=m):
                far = 3 if m == 1 else 0
                near = 3 - far
                if kind == "line":
                    in_line(axis, src, dst.at[far], base, far, far, far).wait_recv()
                    in_line(axis, dst.at[far], dst.at[far], base, 4, near, far).start()
                else:
                    in_line(axis, held, held, base, far, far, 4).wait_recv()

                    def add(row, carry):
                        rows = pl.ds(row * 16, 16)
                        mixed[rows] = (
                            held[rows].astype(jnp.float32)
                            + src[far, rows].astype(jnp.float32)
                        ).astype(mixed.dtype)
                        return carry

                    lax.fori_loop(0, mixed.shape[0] // 16, add, 0)
                    in_line(axis, mixed, dst.at[m], base, far, far, m).start()

        if kind == "sum":
            for m in (0, 3):

                @pl.when(me == m)
                def _(m=m):
                    dst[3 - m] = jnp.zeros(dst.shape[1:], dst.dtype)

    def line_finish(axis, kind, src, dst, base, held, mixed):
        me = lax.axis_index(axis)
        for m in range(4):

            @pl.when(me == m)
            def _(m=m):
                block = src.at[0] if kind == "sum" else src
                for other in range(4):
                    if other == m:
                        continue
                    ends = (m, other) in ((0, 3), (3, 0))
                    relayed = (m, other) in ((1, 3), (2, 0))
                    copy = in_line(axis, block, dst.at[other], base, other, other, other)
                    if not (kind == "sum" and ends) and not (kind == "line" and relayed):
                        copy.wait_recv()
                    if not (kind == "line" and ends):
                        copy.wait_send()
                if kind == "line" and m in (1, 2):
                    in_line(axis, block, dst.at[0], base, 4, 0, 0).wait_send()

    started = []
    relays = []
    own = []
    lines = []
    for index, (axis, kind, size) in enumerate(plan):
        me = lax.axis_index(axis)
        src, dst = ins[index], outs[index]
        if kind in ("line", "sum"):
            held = spare.pop(0) if kind == "sum" else None
            mixed = spare.pop(0) if kind == "sum" else None
            line_start(axis, kind, src, dst, used[0], held)
            lines.append((axis, kind, src, dst, used[0], held, mixed))
            used[0] += 5
        elif kind == "paired":
            for k in range(2, size, 2):
                copy = remote(src, dst.at[me], {axis: (me + k) % size})
                relays.append((copy, dst, axis, (me + size - k) % size))
            started.append(remote(src, dst.at[me], {axis: me + 1 - 2 * (me % 2)}))
        else:
            for k in range(1, size):
                peer = (me + k) % size
                block = src if kind == "gather" else src.at[peer]
                started.append(remote(block, dst.at[me], {axis: peer}))
    for index, (axis, kind, size) in enumerate(plan):
        me = lax.axis_index(axis)
        block = ins[index].at[me] if kind in ("swap", "sum") else ins[index]
        copy = pltpu.make_async_copy(block, outs[index].at[me], own_sem.at[index])
        copy.start()
        own.append(copy)
    for line in lines:
        line_relay(*line)
    for copy, dst, axis, slot in relays:
        copy.wait_recv()
        me = lax.axis_index(axis)
        started.append(
            remote(dst.at[slot], dst.at[slot], {axis: me + 1 - 2 * (me % 2)})
        )
    for copy, _, _, _ in relays:
        copy.wait_send()
    for copy in own:
        copy.wait()
    for copy in started:
        copy.wait()
    for line in lines:
        line_finish(*line)


def make_exchange():
    calls = [0]

    def exchange(*items):
        plan = []
        shapes = []
        copies = 0
        sent = 0
        spare = []
        for axis, kind, value in items:
            size = lax.axis_size(axis)
            if kind == "paired" and size % 2:
                kind = "gather"
            block = value.shape[1:] if kind == "swap" else value.shape
            if axis == "tensor" and size == 4 and value.dtype == jnp.bfloat16:
                kind = {"swap": "sum", "gather": "line"}[kind]
                if kind == "sum":
                    spare += [pltpu.VMEM(block, value.dtype)] * 2
            plan.append((axis, kind, size))
            copies += 5 if kind in ("line", "sum") else size - 1
            shapes.append(jax.ShapeDtypeStruct((size,) + block, value.dtype))
            sent += (size - 1) * math.prod(block) * value.dtype.itemsize
        collective_id = calls[0]
        calls[0] += 1
        return pl.pallas_call(
            lambda *refs: exchange_kernel(tuple(plan), *refs),
            out_shape=tuple(shapes),
            in_specs=[pl.BlockSpec(memory_space=pltpu.VMEM)] * len(plan),
            out_specs=tuple([pl.BlockSpec(memory_space=pltpu.VMEM)] * len(plan)),
            scratch_shapes=[
                pltpu.SemaphoreType.DMA((copies,)),
                pltpu.SemaphoreType.DMA((copies,)),
                pltpu.SemaphoreType.DMA((len(plan),)),
                *spare,
            ],
            compiler_params=pltpu.CompilerParams(
                collective_id=collective_id,
                has_side_effects=True,
                vmem_limit_bytes=48 * 1024 * 1024,
            ),
            cost_estimate=pl.CostEstimate(flops=0, bytes_accessed=sent, transcendentals=0),
            name=f"exchange_{collective_id}",
        )(*[value for _, _, value in items])

    return exchange


SIBLING, CROSS, FAR, BESIDE, ABOVE, LINE = range(6)
EVERY_PEER = (SIBLING, CROSS, FAR, BESIDE, ABOVE)
AT_UP, AT_OUT, AT_ATTENDED, AT_QKV = range(4)
QKV, OUT, UP, DOWN = "qkv", "out", "up", "down"
MESH = pl.DeviceIdType.MESH


class Place:
    def __init__(self):
        self.dp = lax.axis_index("dp")
        self.z = lax.axis_index("tensor")
        self.core = lax.rem(self.dp, 2)
        self.pair = lax.div(self.z, 2)
        self.low = lax.rem(self.z, 2)
        self.rank = 2 * self.core + self.low
        self.native = self.core == self.pair
        self.block = lax.div(self.dp, 2)
        self.x = lax.rem(self.block, 2)
        self.y = lax.div(self.block, 2)
        self.base = self.dp - self.core

    def sibling(self):
        return {"dp": self.base + 1 - self.core, "tensor": self.z}

    def cross(self, core):
        return {"dp": self.base + core, "tensor": self.z + 1 - 2 * self.low}

    def far(self, core):
        return {"dp": self.base + core, "tensor": self.z + 2 - 4 * self.pair}

    def beside(self):
        return {"dp": self.dp + 2 - 4 * self.x, "tensor": self.z}

    def above(self):
        return {"dp": self.dp + 4 - 8 * self.y, "tensor": self.z}

    def in_line(self, index):
        return {"dp": self.base + lax.rem(index, 2), "tensor": lax.div(index, 2)}

    def rank_at(self, core, low):
        return 2 * core + low

    def block_at(self, dy, dx):
        y = 1 - self.y if dy else self.y
        x = 1 - self.x if dx else self.x
        return 2 * y + x


class Wires:
    def __init__(self, send_sem, recv_sem, own_sem):
        self.send_sem, self.recv_sem, self.own_sem = send_sem, recv_sem, own_sem
        self.used = 0
        self.own_used = 0

    def take(self, count):
        at = self.used
        self.used += count
        return at

    def take_own(self, count=1):
        at = self.own_used
        self.own_used += count
        return at

    def copy(self, src, dst, device, send, recv):
        return pltpu.make_async_remote_copy(
            src_ref=src,
            dst_ref=dst,
            send_sem=self.send_sem.at[send],
            recv_sem=self.recv_sem.at[recv],
            device_id=device,
            device_id_type=MESH,
        )

    def local(self, src, dst, slot):
        return pltpu.make_async_copy(src, dst, self.own_sem.at[slot])


def add_rows(dst, *parts):
    rows = dst.shape[0]
    step = 16 if rows % 16 == 0 else 8

    def body(index, carry):
        at = pl.ds(index * step, step)
        total = parts[0][at].astype(jnp.float32)
        for part in parts[1:]:
            total = total + part[at].astype(jnp.float32)
        dst[at] = total.astype(dst.dtype)
        return carry

    lax.fori_loop(0, rows // step, body, 0)


class Gather:
    peers = (SIBLING, CROSS)
    copies = 5
    owns = 1

    @staticmethod
    def shape(value):
        return (4,) + value.shape

    @staticmethod
    def scratch(value):
        return []

    def __init__(self, place, wires, src, dst, spare):
        self.p, self.w, self.src, self.dst = place, wires, src, dst
        self.at = wires.take(self.copies)
        self.own = wires.take_own()

    def _copies(self):
        p, w, src, dst, at = self.p, self.w, self.src, self.dst, self.at
        other = 1 - p.core
        near = p.rank_at(p.core, 1 - p.low)
        skew = p.rank_at(other, 1 - p.low)
        sib = p.sibling()
        return [
            lambda: w.copy(src, dst.at[p.rank], sib, at, at),
            lambda: w.copy(src.at[p.core], dst.at[p.rank, p.core], p.cross(p.core), at + 1, at + 1),
            lambda: w.copy(src.at[other], dst.at[p.rank, other], p.cross(other), at + 2, at + 2),
            lambda: w.copy(dst.at[near, p.core], dst.at[near, p.core], sib, at + 3, at + 4),
            lambda: w.copy(dst.at[skew, p.core], dst.at[skew, p.core], sib, at + 4, at + 3),
        ]

    def start(self):
        made = self._copies()
        for copy in (made[1], made[2], made[0]):
            copy().start()
        self.w.local(self.src, self.dst.at[self.p.rank], self.own).start()

    def relay(self):
        made = self._copies()
        made[1]().wait_recv()
        made[3]().start()
        made[2]().wait_recv()
        made[4]().start()

    def relay_more(self):
        pass

    def finish(self):
        made = self._copies()
        for index in (0, 3, 4):
            made[index]().wait_recv()
        for copy in made:
            copy().wait_send()
        self.w.local(self.src, self.dst.at[self.p.rank], self.own).wait()


class Reduce:
    peers = (SIBLING, CROSS)
    copies = 3
    owns = 1

    @staticmethod
    def shape(value):
        return (3,) + value.shape[1:]

    @staticmethod
    def scratch(value):
        return [pltpu.VMEM(value.shape[1:], value.dtype)] * 2

    def __init__(self, place, wires, src, dst, spare):
        self.p, self.w, self.src, self.dst = place, wires, src, dst
        self.held, self.mixed = spare
        self.at = wires.take(self.copies)
        self.own = wires.take_own()

    def _copies(self):
        p, w, src, dst, at = self.p, self.w, self.src, self.dst, self.at
        other = 1 - p.core
        sib = p.sibling()
        return [
            lambda: w.copy(src.at[p.rank_at(other, p.low)], dst.at[1], sib, at, at),
            lambda: w.copy(src.at[p.rank_at(other, 1 - p.low)], self.held, sib, at + 1, at + 1),
            lambda: w.copy(self.mixed, dst.at[2], p.cross(p.core), at + 2, at + 2),
        ]

    def start(self):
        made = self._copies()
        made[1]().start()
        made[0]().start()
        self.w.local(self.src.at[self.p.rank], self.dst.at[0], self.own).start()

    def relay(self):
        made = self._copies()
        made[1]().wait_recv()
        add_rows(self.mixed, self.held, self.src.at[self.p.rank_at(self.p.core, 1 - self.p.low)])
        made[2]().start()

    def relay_more(self):
        pass

    def finish(self):
        made = self._copies()
        made[0]().wait_recv()
        made[2]().wait_recv()
        for copy in made:
            copy().wait_send()
        self.w.local(self.src.at[self.p.rank], self.dst.at[0], self.own).wait()


class Pairing:
    peers = (SIBLING, FAR)
    copies = 3
    owns = 1

    @staticmethod
    def shape(value):
        return (2,) + value.shape

    @staticmethod
    def scratch(value):
        return []

    def __init__(self, place, wires, src, dst, spare):
        self.p, self.w, self.src, self.dst = place, wires, src, dst
        self.at = wires.take(self.copies)
        self.own = wires.take_own()

    def _near(self):
        p, at = self.p, self.at
        return self.w.copy(self.src, self.dst.at[p.core], p.sibling(), at, at)

    def _far(self, recv):
        p, at = self.p, self.at
        return self.w.copy(self.src, self.dst.at[p.core], p.far(p.pair), at + 1, recv)

    def start(self):
        p = self.p
        self._far(self.at + 1 + p.core).start()

        @pl.when(p.native)
        def _():
            self.w.local(self.src, self.dst.at[p.core], self.own).start()

        @pl.when(jnp.logical_not(p.native))
        def _():
            self._near().start()

    def settle(self):
        p = self.p

        @pl.when(p.native)
        def _():
            self._near().wait_recv()
            self.w.local(self.src, self.dst.at[p.core], self.own).wait()

        @pl.when(jnp.logical_not(p.native))
        def _():
            self._far(self.at + 1).wait_recv()
            self._far(self.at + 2).wait_recv()

    def sent(self):
        p = self.p
        self._far(self.at + 1).wait_send()

        @pl.when(jnp.logical_not(p.native))
        def _():
            self._near().wait_send()

    def relay(self):
        pass

    def relay_more(self):
        pass

    def finish(self):
        self.settle()
        self.sent()


class Spread:
    peers = (BESIDE, ABOVE)
    copies = 4
    owns = 1

    @staticmethod
    def shape(value):
        return (4,) + value.shape

    @staticmethod
    def scratch(value):
        return []

    def __init__(self, place, wires, src, dst, spare):
        self.p, self.w, self.src, self.dst = place, wires, src, dst
        self.at = wires.take(self.copies)
        self.own = wires.take_own()

    def _copies(self):
        p, w, src, dst, at = self.p, self.w, self.src, self.dst, self.at
        row, column = p.block_at(0, 1), p.block_at(1, 0)
        return [
            lambda: w.copy(src, dst.at[p.block], p.beside(), at, at),
            lambda: w.copy(src, dst.at[p.block], p.above(), at + 1, at + 1),
            lambda: w.copy(dst.at[row, 0], dst.at[row, 0], p.above(), at + 2, at + 2),
            lambda: w.copy(dst.at[column, 1], dst.at[column, 1], p.beside(), at + 3, at + 3),
        ]

    def start(self):
        made = self._copies()
        made[0]().start()
        made[1]().start()
        self.w.local(self.src, self.dst.at[self.p.block], self.own).start()

    def relay(self):
        pass

    def relay_more(self):
        made = self._copies()
        made[0]().wait_recv()
        made[2]().start()
        made[1]().wait_recv()
        made[3]().start()

    def finish(self):
        made = self._copies()
        made[2]().wait_recv()
        made[3]().wait_recv()
        for copy in made:
            copy().wait_send()
        self.w.local(self.src, self.dst.at[self.p.block], self.own).wait()


class Fetch:
    peers = (SIBLING, FAR, BESIDE, ABOVE)
    copies = 7
    owns = 2

    @staticmethod
    def shape(value):
        return (4, 2) + value.shape

    @staticmethod
    def scratch(value):
        return [pltpu.VMEM((2,) + value.shape, value.dtype)]

    def __init__(self, place, wires, src, dst, spare):
        self.one = Pairing(place, wires, src, spare[0], [])
        self.two = Spread(place, wires, spare[0], dst, [])

    def start(self):
        self.one.start()

    def relay(self):
        self.one.settle()
        self.two.start()

    def relay_more(self):
        self.two.relay_more()

    def finish(self):
        self.one.sent()
        self.two.finish()


class Total:
    peers = (BESIDE, ABOVE)
    copies = 6
    owns = 0

    @staticmethod
    def shape(value):
        return value.shape[1:]

    @staticmethod
    def scratch(value):
        one = pltpu.VMEM(value.shape[2:], value.dtype)
        two = pltpu.VMEM(value.shape[1:], value.dtype)
        return [two, two, two, one, one]

    def __init__(self, place, wires, src, dst, spare):
        self.p, self.w, self.src, self.dst = place, wires, src, dst
        self.from_x, self.from_y, self.last, self.to_y, self.to_x = spare
        self.at = wires.take(self.copies)

    def _copies(self):
        p, w, src, at = self.p, self.w, self.src, self.at
        here_x, here_y, skew = p.block_at(0, 1), p.block_at(1, 0), p.block_at(1, 1)
        return [
            lambda: w.copy(src.at[here_x, 0], self.from_x.at[0], p.beside(), at, at),
            lambda: w.copy(src.at[skew, 0], self.from_x.at[1], p.beside(), at + 1, at + 1),
            lambda: w.copy(src.at[here_y, 1], self.from_y.at[0], p.above(), at + 2, at + 2),
            lambda: w.copy(src.at[skew, 1], self.from_y.at[1], p.above(), at + 3, at + 3),
            lambda: w.copy(self.to_y, self.last.at[0], p.above(), at + 4, at + 4),
            lambda: w.copy(self.to_x, self.last.at[1], p.beside(), at + 5, at + 5),
        ]

    def start(self):
        made = self._copies()
        for index in (1, 3, 0, 2):
            made[index]().start()

    def relay(self):
        pass

    def relay_more(self):
        made = self._copies()
        p = self.p
        made[1]().wait_recv()
        add_rows(self.to_y, self.src.at[p.block_at(1, 0), 0], self.from_x.at[1])
        made[4]().start()
        made[3]().wait_recv()
        add_rows(self.to_x, self.src.at[p.block_at(0, 1), 1], self.from_y.at[1])
        made[5]().start()

    def finish(self):
        made = self._copies()
        p = self.p
        for index in (0, 2, 4, 5):
            made[index]().wait_recv()
        add_rows(self.dst.at[0], self.src.at[p.block, 0], self.from_x.at[0], self.last.at[0])
        add_rows(self.dst.at[1], self.src.at[p.block, 1], self.from_y.at[0], self.last.at[1])
        for copy in made:
            copy().wait_send()


class Deliver:
    peers = (SIBLING, FAR)
    copies = 4
    owns = 1

    @staticmethod
    def shape(value):
        return value.shape

    @staticmethod
    def scratch(value):
        return []

    def __init__(self, place, wires, src, dst, spare):
        self.p, self.w, self.src, self.dst = place, wires, src, dst
        self.at = wires.take(self.copies)
        self.own = wires.take_own()

    def _near(self):
        p, at = self.p, self.at
        return self.w.copy(self.src.at[1 - p.core], self.dst.at[0], p.sibling(), at, at)

    def _far(self, core):
        p, at = self.p, self.at
        return self.w.copy(
            self.src.at[core], self.dst.at[1], p.far(jnp.int32(core)), at + 1 + core, at + 1
        )

    def start(self):
        p = self.p

        @pl.when(p.native)
        def _():
            self._near().start()
            self.w.local(self.src.at[p.core], self.dst.at[0], self.own).start()

        @pl.when(jnp.logical_not(p.native))
        def _():
            self._far(0).start()
            self._far(1).start()

    def relay(self):
        pass

    def relay_more(self):
        pass

    def finish(self):
        p = self.p
        self._far(0).wait_recv()

        @pl.when(p.native)
        def _():
            self._near().wait_send()
            self.w.local(self.src.at[p.core], self.dst.at[0], self.own).wait()

        @pl.when(jnp.logical_not(p.native))
        def _():
            self._near().wait_recv()
            self._far(0).wait_send()
            self._far(1).wait_send()


class Swap:
    peers = (FAR,)
    copies = 1
    owns = 1

    @staticmethod
    def shape(value):
        return value.shape

    @staticmethod
    def scratch(value):
        return []

    def __init__(self, place, wires, src, dst, spare):
        self.p, self.w, self.src, self.dst = place, wires, src, dst
        self.at = wires.take(self.copies)
        self.own = wires.take_own()

    def _copy(self):
        p, at = self.p, self.at
        return self.w.copy(self.src, self.dst, p.far(1 - p.core), at, at)

    def start(self):
        @pl.when(self.p.native)
        def _():
            self.w.local(self.src, self.dst, self.own).start()

        @pl.when(jnp.logical_not(self.p.native))
        def _():
            self._copy().start()

    def relay(self):
        pass

    def relay_more(self):
        pass

    def finish(self):
        @pl.when(self.p.native)
        def _():
            self.w.local(self.src, self.dst, self.own).wait()

        @pl.when(jnp.logical_not(self.p.native))
        def _():
            self._copy().wait()


class Small:
    peers = (BESIDE, ABOVE, LINE)
    copies = 20
    owns = 1

    @staticmethod
    def shape(value):
        return (8,) + value.shape[2:]

    @staticmethod
    def scratch(value):
        return Total.scratch(value) + [pltpu.VMEM(value.shape[1:], value.dtype)]

    def __init__(self, place, wires, src, dst, spare):
        self.sums = spare[-1]
        self.total = Total(place, wires, src, self.sums, spare[:-1])
        self.p, self.w, self.dst = place, wires, dst
        self.at = wires.take(14)
        self.own = wires.take_own()

    def _ends(self, offset):
        p, at = self.p, self.at
        me = 2 * p.z + p.core
        to = lax.rem(me + offset, 8)
        return self.w.copy(
            self.sums.at[lax.rem(to, 2)], self.dst.at[me], p.in_line(to), at + offset - 1, at + 6 + offset
        )

    def _mine(self):
        p = self.p
        return self.w.local(self.sums.at[p.core], self.dst.at[2 * p.z + p.core], self.own)

    def start(self):
        self.total.start()

    def relay(self):
        pass

    def relay_more(self):
        self.total.relay_more()
        self.total.finish()
        for offset in range(1, 8):
            self._ends(offset).start()
        self._mine().start()

    def finish(self):
        self._mine().wait()
        for offset in range(1, 8):
            self._ends(offset).wait()


def greet(place, kinds):
    p = place
    devices = []
    if SIBLING in kinds or LINE in kinds:
        devices.append(p.sibling())
    if CROSS in kinds or LINE in kinds:
        devices += [p.cross(jnp.int32(0)), p.cross(jnp.int32(1))]
    if FAR in kinds or LINE in kinds:
        devices += [p.far(jnp.int32(0)), p.far(jnp.int32(1))]
    if LINE in kinds:
        last = 3 - p.z
        devices += [{"dp": p.base, "tensor": last}, {"dp": p.base + 1, "tensor": last}]
    if BESIDE in kinds:
        devices.append(p.beside())
    if ABOVE in kinds:
        devices.append(p.above())
    barrier = pltpu.get_barrier_semaphore()
    for device in devices:
        pl.semaphore_signal(barrier, inc=1, device_id=device, device_id_type=MESH)
    pl.semaphore_wait(barrier, len(devices))


def round_kernel(kinds, *refs):
    count = len(kinds)
    ins, outs = refs[:count], refs[count : 2 * count]
    wires = Wires(*refs[2 * count : 2 * count + 3])
    spare = list(refs[2 * count + 3 :])
    place = Place()
    greet(place, {peer for kind, _ in kinds for peer in kind.peers})
    jobs = []
    for (kind, held), src, dst in zip(kinds, ins, outs):
        jobs.append(kind(place, wires, src, dst, spare[:held]))
        del spare[:held]
    for job in jobs:
        job.start()
    for job in jobs:
        job.relay()
    for job in jobs:
        job.relay_more()
    for job in jobs:
        job.finish()


def make_rounds():
    calls = [0]

    def rounds(*items):
        kinds, shapes, scratch = [], [], []
        copies = owns = sent = 0
        for kind, value in items:
            held = kind.scratch(value)
            kinds.append((kind, len(held)))
            scratch += held
            shapes.append(jax.ShapeDtypeStruct(kind.shape(value), value.dtype))
            copies += kind.copies
            owns += kind.owns
            sent += math.prod(kind.shape(value)) * value.dtype.itemsize
        collective_id = calls[0]
        calls[0] += 1
        return pl.pallas_call(
            lambda *refs: round_kernel(tuple(kinds), *refs),
            out_shape=tuple(shapes),
            in_specs=[pl.BlockSpec(memory_space=pltpu.VMEM)] * len(kinds),
            out_specs=tuple([pl.BlockSpec(memory_space=pltpu.VMEM)] * len(kinds)),
            scratch_shapes=[
                pltpu.SemaphoreType.DMA((copies,)),
                pltpu.SemaphoreType.DMA((copies,)),
                pltpu.SemaphoreType.DMA((max(owns, 1),)),
                *scratch,
            ],
            compiler_params=pltpu.CompilerParams(
                collective_id=collective_id,
                has_side_effects=True,
                vmem_limit_bytes=48 * 1024 * 1024,
            ),
            cost_estimate=pl.CostEstimate(flops=0, bytes_accessed=sent, transcendentals=0),
            name=f"round_{collective_id}",
        )(*[value for _, value in items])

    return rounds


def masked_scores(queries, key_vecs, segments, score_scale):
    positions = jnp.arange(key_vecs.shape[0], dtype=jnp.int32)
    allowed = (segments[:, None] == segments[None, :]) & (
        positions[None, :] <= positions[:, None]
    )
    scores = (
        jnp.einsum("qhd,khd->hqk", queries, key_vecs, preferred_element_type=jnp.float32)
        * score_scale
    )
    return jnp.where(allowed[None], scores, -jnp.inf)


def attend(queries, key_vecs, val_vecs, segments, score_scale):
    scores = masked_scores(queries, key_vecs, segments, score_scale)
    row_max = jnp.max(scores, axis=-1, keepdims=True)
    log_total = row_max + jnp.log(jnp.sum(jnp.exp(scores - row_max), axis=-1, keepdims=True))
    probs_half = jnp.exp(scores - log_total).astype(jnp.bfloat16)
    attended = jnp.einsum("hqk,khd->qhd", probs_half, val_vecs, preferred_element_type=jnp.float32)
    return (attended.astype(jnp.bfloat16).reshape(queries.shape[0], -1), log_total)


def attend_back(queries, key_vecs, val_vecs, grad_attended, log_total, segments, score_scale):
    scores = masked_scores(queries, key_vecs, segments, score_scale)
    soft_probs = jnp.exp(scores - log_total)
    probs_half = soft_probs.astype(jnp.bfloat16)
    grad_probs = jnp.einsum(
        "qhd,khd->hqk", grad_attended, val_vecs, preferred_element_type=jnp.float32
    )
    val_grad = jnp.einsum(
        "hqk,qhd->khd", probs_half, grad_attended, preferred_element_type=jnp.float32
    )
    row_dot = jnp.sum(grad_probs * soft_probs, axis=-1, keepdims=True)
    score_grad = (soft_probs * (grad_probs - row_dot) * score_scale).astype(jnp.bfloat16)
    query_grad = jnp.einsum(
        "hqk,khd->qhd", score_grad, key_vecs, preferred_element_type=jnp.float32
    )
    key_grad = jnp.einsum("hqk,qhd->khd", score_grad, queries, preferred_element_type=jnp.float32)
    return (query_grad, key_grad, val_grad)


def pack(pieces, width, tile):
    flat = jnp.concatenate([piece.reshape(-1) for piece in pieces])
    unit = width * tile
    return jnp.pad(flat, (0, -flat.shape[0] % unit)).reshape(-1, width)


def unpack(packed, shapes):
    flat = packed.reshape(packed.shape[0], -1)
    pieces = []
    at = 0
    for shape in shapes:
        length = math.prod(shape)
        pieces.append(flat[:, at : at + length].reshape((packed.shape[0],) + shape))
        at += length
    return pieces


def shards(x_in, d_out, seq_lengths, w_qkv, b_qv, w_o, w_1, b_ffn, w_2, norm_gains, vec_biases):
    exchange = make_exchange()
    own_rows, width = x_in.shape
    tensor_size = lax.axis_size("tensor")
    dp_size = lax.axis_size("dp")
    group_rows = own_rows * tensor_size
    layer_count = w_qkv.shape[0]
    local_width = w_qkv.shape[3]
    local_heads = local_width // HEAD_DIM
    qkv_width = 3 * local_width
    score_scale = 1.0 / math.sqrt(HEAD_DIM)
    segments = segment_ids(seq_lengths[0], group_rows)
    half = jnp.bfloat16

    def shard_of(name, layer_index):
        if name == "qkv":
            return w_qkv[layer_index].reshape(w_qkv.shape[1], qkv_width)
        if name == "out":
            return w_o[layer_index].T
        if name == "up":
            return w_1[layer_index]
        return w_2[layer_index].T

    weights = {}

    def step(tensor_items, fetched=(), sums=()):
        items = [("tensor", kind, value) for kind, value in tensor_items]
        items += [("dp", "paired", shard_of(*key)) for key in fetched]
        items += [("dp", "swap", value) for value in sums]
        results = list(exchange(*items))
        for position, key in enumerate(fetched):
            piece = results[len(tensor_items) + position]
            weights[key] = piece.reshape(dp_size * piece.shape[1], piece.shape[2])
        gathered = [
            piece.reshape(group_rows, width) if kind == "gather" else piece.astype(jnp.float32).sum(0)
            for (kind, _), piece in zip(tensor_items, results)
        ]
        totals = [
            piece.astype(jnp.float32).sum(0) for piece in results[len(items) - len(sums) :]
        ]
        return gathered, totals

    def to_owners(partial):
        return ("swap", partial.astype(half).reshape(tensor_size, own_rows, width))

    def by_owner(gradient):
        return gradient.astype(half).reshape(dp_size, -1, gradient.shape[-1])

    small_shapes = [b_qv.shape, b_ffn.shape, norm_gains.shape, vec_biases.shape]
    small = pack([b_qv, b_ffn, norm_gains, vec_biases], 128, 16)
    first = exchange(
        ("tensor", "gather", d_out.astype(half)),
        ("dp", "paired", small),
        ("dp", "paired", shard_of("qkv", 0)),
    )
    last_grad_half = first[0].reshape(group_rows, width)
    weights["qkv", 0] = first[2].reshape(width, qkv_width)
    qv_all, ffn_all, gain_all, bias_all = [
        jnp.moveaxis(piece, 0, -2).reshape(piece.shape[1:-1] + (-1,)).astype(jnp.float32)
        for piece in unpack(first[1], small_shapes)
    ]

    caches = []
    hidden_in = x_in
    for layer_index in range(layer_count):
        last = layer_index == layer_count - 1
        following = layer_index + 1
        gain_rows = gain_all[layer_index]
        bias_rows = bias_all[layer_index]
        normed_own, unit_one, inv_one = layer_norm(hidden_in, gain_rows[0], bias_rows[0])
        fetched = [("out", 0), ("up", 0)] if layer_index == 0 else [("down", layer_index)]
        (normed_one,), _ = step([("gather", normed_own.astype(half))], fetched)
        projected = jnp.dot(
            normed_one, weights["qkv", layer_index], preferred_element_type=jnp.float32
        ).reshape(group_rows, 3, local_width)
        qv_bias = qv_all[layer_index]
        heads = (group_rows, local_heads, HEAD_DIM)
        queries = (projected[:, 0] + qv_bias[0]).astype(half).reshape(heads)
        key_vecs = projected[:, 1].astype(half).reshape(heads)
        val_vecs = (projected[:, 2] + qv_bias[1]).astype(half).reshape(heads)
        attended, log_total = attend(queries, key_vecs, val_vecs, segments, score_scale)
        fetched = [("down", 0)] if layer_index == 0 else []
        (summed,), _ = step(
            [to_owners(contract_last(attended, weights["out", layer_index]))], fetched
        )
        residual_mid = hidden_in + summed + bias_rows[2]
        normed_own_two, unit_two, inv_two = layer_norm(residual_mid, gain_rows[1], bias_rows[1])
        fetched = [] if last else [("qkv", following), ("out", following)]
        (normed_two,), _ = step([("gather", normed_own_two.astype(half))], fetched)
        pre_act = (
            jnp.dot(normed_two, weights["up", layer_index], preferred_element_type=jnp.float32)
            + ffn_all[layer_index]
        )
        gelu_value, gelu_slope = gelu_pair(pre_act)
        activated = gelu_value.astype(half)
        ffn_partial = to_owners(contract_last(activated, weights["down", layer_index]))
        if not last:
            (summed,), _ = step([ffn_partial], [("up", following)])
            hidden_in = residual_mid + summed + bias_rows[3]
        caches.append(
            (
                unit_one,
                inv_one,
                normed_one,
                queries,
                key_vecs,
                val_vecs,
                attended,
                log_total,
                unit_two,
                inv_two,
                normed_two,
                activated,
                gelu_slope,
            )
        )
    back = d_out
    grads = {}
    small_terms = [None] * layer_count
    output = None
    for layer_index in reversed(range(layer_count)):
        last = layer_index == layer_count - 1
        gain_rows = gain_all[layer_index]
        (
            unit_one,
            inv_one,
            normed_one,
            queries,
            key_vecs,
            val_vecs,
            attended,
            log_total,
            unit_two,
            inv_two,
            normed_two,
            activated,
            gelu_slope,
        ) = caches[layer_index]
        if last:
            grad_half = last_grad_half
        else:
            (grad_half,), (grads["qkv", layer_index + 1],) = step(
                [("gather", back.astype(half))], sums=[waiting]
            )
        grad_down = by_owner(contract_first(grad_half, activated))
        grad_pre = (
            jnp.dot(grad_half, weights["down", layer_index], preferred_element_type=jnp.float32)
            * gelu_slope
        )
        grad_pre_half = grad_pre.astype(half)
        grad_up = by_owner(contract_first(normed_two, grad_pre_half))
        partial = to_owners(contract_last(grad_pre_half, weights["up", layer_index]))
        if last:
            cut = grad_up.shape[2] // 2
            (grad_normed_two, summed), (grads["down", layer_index], up_left) = step(
                [partial, ffn_partial], sums=[grad_down, grad_up[:, :, :cut]]
            )
            output = residual_mid + summed + bias_all[layer_index][3]
        else:
            (grad_normed_two,), (grads["down", layer_index],) = step([partial], sums=[grad_down])
        grad_mid = back + norm_back(grad_normed_two, unit_two, inv_two, gain_rows[1])
        (grad_mid_half,), (up_part,) = step(
            [("gather", grad_mid.astype(half))], sums=[grad_up[:, :, cut:] if last else grad_up]
        )
        grads["up", layer_index] = (
            jnp.concatenate([up_left, up_part], axis=1) if last else up_part
        )
        grad_out = by_owner(contract_first(grad_mid_half, attended))
        grad_attended = jnp.dot(
            grad_mid_half, weights["out", layer_index], preferred_element_type=jnp.float32
        )
        grad_attended = grad_attended.astype(half).reshape(group_rows, local_heads, HEAD_DIM)
        query_grad, key_grad, val_grad = attend_back(
            queries, key_vecs, val_vecs, grad_attended, log_total, segments, score_scale
        )
        flat = (group_rows, local_width)
        grad_qkv = jnp.concatenate(
            [part.astype(half).reshape(flat) for part in (query_grad, key_grad, val_grad)], axis=1
        )
        grad_qkv_weight = by_owner(contract_first(normed_one, grad_qkv))
        (grad_normed_one,), sent_now = step(
            [to_owners(contract_last(grad_qkv, weights["qkv", layer_index]))],
            sums=[grad_out] if layer_index else [grad_out, grad_qkv_weight],
        )
        grads["out", layer_index] = sent_now[0]
        if layer_index:
            waiting = grad_qkv_weight
        else:
            grads["qkv", layer_index] = sent_now[1]
        small_terms[layer_index] = (
            jnp.stack(
                [
                    jnp.sum(query_grad, axis=0).reshape(local_width),
                    jnp.sum(val_grad, axis=0).reshape(local_width),
                ]
            ),
            jnp.sum(grad_pre, axis=0),
            jnp.stack(
                [
                    jnp.sum(grad_normed_one * unit_one, axis=0),
                    jnp.sum(grad_normed_two * unit_two, axis=0),
                ]
            ),
            jnp.stack(
                [
                    jnp.sum(grad_normed_one, axis=0),
                    jnp.sum(grad_normed_two, axis=0),
                    jnp.sum(grad_mid, axis=0),
                    jnp.sum(back, axis=0),
                ]
            ),
        )
        back = grad_mid + norm_back(grad_normed_one, unit_one, inv_one, gain_rows[0])

    def split_owner(piece):
        return jnp.moveaxis(
            piece.reshape(piece.shape[:-1] + (dp_size, -1)), -2, 0
        ).reshape(dp_size, -1)

    stacked = [
        split_owner(jnp.stack([small_terms[index][member] for index in range(layer_count)]))
        for member in (2, 3, 0, 1)
    ]
    flat = jnp.concatenate(stacked, axis=1)
    flat = jnp.pad(flat, ((0, 0), (0, -flat.shape[1] % 1024)))
    (parts,) = exchange(("dp", "swap", flat.reshape(dp_size, -1, 128)))
    total = parts.sum(0)
    (shared,) = exchange(("tensor", "gather", total))
    everyone = shared.sum(0).reshape(-1)
    gain_size, bias_size = norm_gains.size, vec_biases.size
    mine = total.reshape(-1)[gain_size + bias_size :]

    def stack_layers(name, shape, transposed):
        parts = [grads[name, index] for index in range(layer_count)]
        return jnp.stack([part.T if transposed else part for part in parts]).reshape(shape)

    return (
        output,
        back,
        stack_layers("qkv", w_qkv.shape, False),
        mine[: b_qv.size].reshape(b_qv.shape),
        stack_layers("out", w_o.shape, True),
        stack_layers("up", w_1.shape, False),
        mine[b_qv.size : b_qv.size + b_ffn.size].reshape(b_ffn.shape),
        stack_layers("down", w_2.shape, True),
        everyone[:gain_size].reshape(norm_gains.shape),
        everyone[gain_size : gain_size + bias_size].reshape(vec_biases.shape),
    )


def dot_nn(left, right):
    return jnp.dot(left, right, preferred_element_type=jnp.float32)


class GatherHere(Gather):
    def __init__(self, place, wires, dst):
        super().__init__(place, wires, dst.at[place.rank], dst, [])

    def start(self):
        made = self._copies()
        for index in (1, 2, 0):
            made[index]().start()

    def wait_sibling(self):
        self._copies()[0]().wait_recv()

    def finish(self):
        made = self._copies()
        for index in (3, 4):
            made[index]().wait_recv()
        for copy in made:
            copy().wait_send()


class ReduceHere(Reduce):
    def __init__(self, place, wires, src, dst, spare):
        super().__init__(place, wires, src, dst, spare)

    def _copies(self):
        p, w, src, dst, at = self.p, self.w, self.src, self.dst, self.at
        other = 1 - p.core
        sib = p.sibling()
        return [
            lambda: w.copy(src.at[p.rank_at(other, p.low)], dst.at[0], sib, at, at),
            lambda: w.copy(src.at[p.rank_at(other, 1 - p.low)], self.held, sib, at + 1, at + 1),
            lambda: w.copy(self.mixed, dst.at[1], p.cross(p.core), at + 2, at + 2),
        ]

    def start_cross(self):
        self._copies()[1]().start()

    def start_near(self):
        self._copies()[0]().start()

    def finish(self):
        made = self._copies()
        made[0]().wait_recv()
        made[2]().wait_recv()
        for copy in made:
            copy().wait_send()

    def total(self, rows):
        first = self.src[self.p.rank, rows].astype(jnp.float32)
        return first + self.dst[0, rows].astype(jnp.float32) + self.dst[1, rows].astype(jnp.float32)


class Env:
    pass


def make_fused():
    calls = [32]

    def fused(body, ins, outs, scratch, kinds, hbm=(), flops=0):
        names_in, names_out, names_spare = list(ins), list(outs), list(scratch)

        def kernel(*refs):
            k = Env()
            refs = list(refs)
            for name in names_in + names_out:
                setattr(k, name, refs.pop(0))
            k.wires = Wires(*refs[:3])
            for name, ref in zip(names_spare, refs[3:]):
                setattr(k, name, ref)
            k.place = Place()
            greet(k.place, kinds)
            body(k)
            assert k.wires.used <= 144 and k.wires.own_used <= 64

        collective_id = calls[0]
        calls[0] += 1
        results = pl.pallas_call(
            kernel,
            out_shape=tuple(jax.ShapeDtypeStruct(*outs[name]) for name in names_out),
            in_specs=[
                pl.BlockSpec(memory_space=pltpu.HBM if name in hbm else pltpu.VMEM)
                for name in names_in
            ],
            out_specs=tuple([pl.BlockSpec(memory_space=pltpu.VMEM)] * len(names_out)),
            scratch_shapes=[
                pltpu.SemaphoreType.DMA((144,)),
                pltpu.SemaphoreType.DMA((144,)),
                pltpu.SemaphoreType.DMA((64,)),
                *[pltpu.VMEM(*scratch[name]) for name in names_spare],
            ],
            compiler_params=pltpu.CompilerParams(
                collective_id=collective_id,
                has_side_effects=True,
                vmem_limit_bytes=56 * 1024 * 1024,
            ),
            cost_estimate=pl.CostEstimate(
                flops=flops, bytes_accessed=16 * 1024 * 1024, transcendentals=0
            ),
            name=f"fused_{collective_id}",
        )(*[ins[name] for name in names_in])
        made = Env()
        made.__dict__.update(zip(names_out, results))
        return made

    return fused


def chips(place):
    other = 1 - place.core
    return (
        (place.rank, place.rank_at(other, place.low)),
        (place.rank_at(place.core, 1 - place.low), place.rank_at(other, 1 - place.low)),
    )


def two(ref, ranks, lanes=slice(None)):
    parts = [ref[rank, ..., lanes] for rank in ranks]
    return jnp.concatenate([part.reshape(-1, part.shape[-1]) for part in parts], axis=0)


def whole(ref, lanes=slice(None)):
    part = ref[..., lanes]
    return part.reshape(-1, part.shape[-1])


def put_two(ref, ranks, value, lanes=slice(None)):
    rows = value.shape[0] // 2
    ref[ranks[0], :, lanes] = value[:rows].astype(ref.dtype)
    ref[ranks[1], :, lanes] = value[rows:].astype(ref.dtype)


def lanes_at(index, size=256):
    return pl.ds(pl.multiple_of(index * size, size), size)


def loop(count, body):
    def step(index, carry):
        body(index)
        return carry

    lax.fori_loop(0, count, step, 0)


def columns_of(ref, block):
    return jnp.concatenate([ref[block, 0], ref[block, 1]], axis=1)


def all_columns(ref, rows):
    return jnp.concatenate([ref[block, core, rows] for block in range(4) for core in range(2)], axis=1)


ROWS = 32


def visible(k, block):
    shape = (128, (block + 1) * 128)
    end = k.lengths[0:1, 0:1].astype(jnp.int32)
    at_query = lax.broadcasted_iota(jnp.int32, shape, 0) + block * 128
    at_key = lax.broadcasted_iota(jnp.int32, shape, 1)
    late_query = jnp.where(at_query >= end, 1, 0)
    late_key = jnp.where(at_key >= end, 1, 0)
    return (late_query == late_key) & (at_key <= at_query)


def attention_forward(k, on_sent, on_gathered, on_attended):
    p = k.place
    here, there = chips(p)
    for at in range(4):
        rows = pl.ds(at * ROWS, ROWS)
        normed, _, _ = layer_norm(k.hidden[rows], k.vecs[0:1], k.vecs[2:3])
        k.n1[p.rank, at // 2, pl.ds(at % 2 * ROWS, ROWS)] = normed.astype(jnp.bfloat16)
    gather = GatherHere(p, k.wires, k.n1)
    gather.start()
    on_sent()

    def project(ranks):
        rows = two(k.n1, ranks)
        for index, (dst, bias) in enumerate(((k.q, 0), (k.key, None), (k.val, 1))):
            weight = k.w_qkv[:, :, index * 128 : index * 128 + 128].reshape(1024, 256)
            made = dot_nn(rows, weight)
            if bias is not None:
                made = made + k.qv_bias[bias : bias + 1]
            put_two(dst, ranks, made)

    gather.wait_sibling()
    gather.relay()
    on_gathered()
    project(here)
    gather.finish()
    project(there)
    scale = 1.0 / math.sqrt(HEAD_DIM)
    for block in range(4):
        seen = visible(k, block)
        count = (block + 1) * 128
        for head in range(4):
            lanes = slice(head * HEAD_DIM, head * HEAD_DIM + HEAD_DIM)
            keys = k.key[: block + 1, :, lanes].reshape(count, HEAD_DIM)
            vals = k.val[: block + 1, :, lanes].reshape(count, HEAD_DIM)
            scores = contract_last(k.q[block, :, lanes], keys) * scale
            scores = jnp.where(seen, scores, -jnp.inf)
            raised = jnp.exp(scores - jnp.max(scores, axis=-1, keepdims=True))
            probs = raised * (1.0 / jnp.sum(raised, axis=-1, keepdims=True))
            probs = probs.astype(jnp.bfloat16)
            k.probs[head, pl.ds(block * 128, 128), :count] = probs
            k.att[block, :, lanes] = dot_nn(probs, vals).astype(jnp.bfloat16)
    on_attended()

    def out(ranks):
        rows = two(k.att, ranks)

        def column(block):
            put_two(k.part_a, ranks, dot_nn(rows, columns_of(k.w_out, block)), lanes_at(block))

        loop(4, column)

    reduce = ReduceHere(p, k.wires, k.part_a, k.got_a, (k.held_a, k.mixed_a))
    out(there)
    reduce.start_cross()
    out(here)
    reduce.start_near()
    reduce.relay()
    return reduce


def feed_forward(k, reduce, on_sent, on_gathered, on_raised, part):
    p = k.place
    here, there = chips(p)
    reduce.finish()
    for at in range(4):
        rows = pl.ds(at * ROWS, ROWS)
        mid = k.hidden[rows] + reduce.total(rows) + k.vecs[4:5]
        k.mid[rows] = mid
        normed, _, _ = layer_norm(mid, k.vecs[1:2], k.vecs[3:4])
        k.n2[p.rank, at // 2, pl.ds(at % 2 * ROWS, ROWS)] = normed.astype(jnp.bfloat16)
    gather = GatherHere(p, k.wires, k.n2)
    gather.start()
    on_sent()

    def up(ranks):
        def column(index):
            lanes = lanes_at(index)
            rows = two(k.n2, ranks)
            weight = k.w_up[:, :, :, lanes].reshape(1024, 256)
            pre_act = dot_nn(rows, weight) + k.ffn_bias[0:1, lanes]
            value, slope = gelu_pair(pre_act)
            put_two(k.act, ranks, value, lanes)
            put_two(k.slope, ranks, slope, lanes)

        loop(4, column)

    gather.wait_sibling()
    gather.relay()
    on_gathered()
    up(here)
    gather.finish()
    up(there)
    on_raised()

    def down(ranks):
        def column(block):
            rows = two(k.act, ranks)
            put_two(part, ranks, dot_nn(rows, columns_of(k.w_down, block)), lanes_at(block))

        loop(4, column)

    return down, here, there


def unpack_small(small_all, views):
    parts = [small_all[block, core].astype(jnp.float32) for block in range(4) for core in range(2)]

    def row(index):
        return jnp.concatenate([part[index : index + 1] for part in parts], axis=1)

    for layer, k in enumerate(views):
        for index in range(2):
            k.vecs[index : index + 1] = row(3 + 2 * layer + index)
            at = 64 * layer + 32 * index
            k.qv_bias[index : index + 1] = jnp.concatenate(
                [part[0:1, at : at + 32] for part in parts], axis=1
            )
        for index in range(4):
            k.vecs[2 + index : 3 + index] = row(7 + 4 * layer + index)
        k.ffn_bias[0:1] = row(1 + layer)


def pack_small(flat, layers):
    flat[...] = jnp.zeros(flat.shape, flat.dtype)
    for shard in range(8):
        block, core = shard // 2, shard % 2
        lanes = slice(shard * 128, shard * 128 + 128)
        quarter = slice(shard * 32, shard * 32 + 32)
        pieces = []
        for layer, (col, col_qv, col_ffn) in enumerate(layers):
            flat[block, core, 2 * layer : 2 * layer + 2] = col[0:2, lanes]
            flat[block, core, 4 + 4 * layer : 8 + 4 * layer] = col[2:6, lanes]
            flat[block, core, 13 + layer : 14 + layer] = col_ffn[0:1, lanes]
            pieces += [col_qv[0:1, quarter], col_qv[1:2, quarter]]
        flat[block, core, 12:13] = jnp.concatenate(pieces, axis=1)


def feed_forward_back(k, gather):
    p = k.place
    here, there = chips(p)

    def pre(ranks, first):
        def rows_of(index):
            lanes = lanes_at(index)
            weight = all_columns(k.w_down, lanes)
            grad = contract_last(two(k.gh, ranks), weight) * two(k.slope, ranks, lanes).astype(
                jnp.float32
            )
            put_two(k.gp, ranks, grad, lanes)
            summed = jnp.sum(grad, axis=0, keepdims=True)
            k.col_ffn[0:1, lanes] = summed if first else k.col_ffn[0:1, lanes] + summed

        loop(4, rows_of)

    if gather is not None:
        gather.wait_sibling()
    pre(here, True)
    if gather is not None:
        gather.relay()
        gather.finish()
    pre(there, False)

    def term(ranks):
        def column(block):
            rows = two(k.gp, ranks)
            weight = k.w_up[block].reshape(256, 1024)
            put_two(k.part_a, ranks, contract_last(rows, weight), lanes_at(block))

        loop(4, column)

    reduce = ReduceHere(p, k.wires, k.part_a, k.got_a, (k.held_a, k.mixed_a))
    term(there)
    reduce.start_cross()
    term(here)
    reduce.start_near()
    reduce.relay()

    def turn(index):
        lanes = lanes_at(index)
        k.turned[lanes] = whole(k.act, lanes).T

    loop(4, turn)

    def grad_down(block):
        made = dot_nn(k.turned[...], whole(k.gh, lanes_at(block)))
        k.g_down[block, 0] = made[:, :128].astype(jnp.bfloat16)
        k.g_down[block, 1] = made[:, 128:].astype(jnp.bfloat16)

    loop(4, grad_down)
    return reduce


def grad_up(k):
    def rows_of(block):
        turned = whole(k.n2, lanes_at(block)).T
        made = dot_nn(turned, whole(k.gp))
        k.g_up[block] = made.astype(jnp.bfloat16).reshape(2, 128, 1024)

    loop(4, rows_of)


def through_norm(k, reduce, hidden, back, sums, gain, dst, put):
    totals = None
    for at in range(4):
        rows = pl.ds(at * ROWS, ROWS)
        grad = reduce.total(rows)
        _, unit, inv = layer_norm(hidden[rows], 1.0, 0.0)
        was = back[rows]
        now = was + norm_back(grad, unit, inv, k.vecs[gain : gain + 1])
        dst[rows] = now
        put(at, now)
        terms = [grad * unit, grad, now, was]
        terms = [jnp.sum(term, axis=0, keepdims=True) for term in terms]
        totals = terms if totals is None else [a + b for a, b in zip(totals, terms)]
    for row, total in zip(sums, totals):
        if row is not None:
            k.col[row : row + 1] = total


def attention_back(k, reduce, background, third):
    p = k.place
    here, there = chips(p)
    reduce.finish()

    def put(at, now):
        k.gm[p.rank, at // 2, pl.ds(at % 2 * ROWS, ROWS)] = now.astype(jnp.bfloat16)

    through_norm(k, reduce, k.mid, k.back, (1, 3, 4, 5), 1, k.grad_mid, put)
    gather = GatherHere(p, k.wires, k.gm)
    gather.start()
    grad_up(k)
    background(AT_UP)

    def attended(ranks):
        weight = all_columns(k.w_out, slice(None))
        put_two(k.ga, ranks, contract_last(two(k.gm, ranks), weight))

    gather.wait_sibling()
    attended(here)
    gather.relay()
    gather.finish()
    attended(there)

    def grad_out(block):
        made = dot_nn(whole(k.att).T, whole(k.gm, lanes_at(block)))
        k.g_out[block, 0] = made[:, :128].astype(jnp.bfloat16)
        k.g_out[block, 1] = made[:, 128:].astype(jnp.bfloat16)

    loop(4, grad_out)
    background(AT_OUT)
    scale = 1.0 / math.sqrt(HEAD_DIM)
    for head in range(4):
        lanes = slice(head * HEAD_DIM, head * HEAD_DIM + HEAD_DIM)
        for block in range(4):
            rows = pl.ds(block * 128, 128)
            count = (block + 1) * 128
            keys = k.key[: block + 1, :, lanes].reshape(count, HEAD_DIM)
            vals = k.val[: block + 1, :, lanes].reshape(count, HEAD_DIM)
            probs = k.probs[head, rows, :count].astype(jnp.float32)
            grad_probs = contract_last(k.ga[block, :, lanes], vals)
            row_dot = jnp.sum(grad_probs * probs, axis=-1, keepdims=True)
            score_grad = (probs * (grad_probs - row_dot) * scale).astype(jnp.bfloat16)
            k.ds[head % 2, rows, :count] = score_grad
            query_grad = dot_nn(score_grad, keys)
            k.gq[0, block, :, lanes] = query_grad.astype(jnp.bfloat16)
            summed = jnp.sum(query_grad, axis=0, keepdims=True)
            k.col_qv[0:1, lanes] = summed if block == 0 else k.col_qv[0:1, lanes] + summed
        for block in range(4):
            below = pl.ds(block * 128, 512 - block * 128)
            cols = slice(block * 128, block * 128 + 128)
            count = 512 - block * 128
            queries = k.q[block:, :, lanes].reshape(count, HEAD_DIM)
            grads = k.ga[block:, :, lanes].reshape(count, HEAD_DIM)
            key_grad = contract_first(k.ds[head % 2, below, cols], queries)
            val_grad = contract_first(k.probs[head, below, cols], grads)
            k.gq[1, block, :, lanes] = key_grad.astype(jnp.bfloat16)
            k.gq[2, block, :, lanes] = val_grad.astype(jnp.bfloat16)
            summed = jnp.sum(val_grad, axis=0, keepdims=True)
            k.col_qv[1:2, lanes] = summed if block == 0 else k.col_qv[1:2, lanes] + summed
    background(AT_ATTENDED)

    def term(ranks):
        rows = [two(k.gq.at[index], ranks) for index in range(3)]

        def column(block):
            made = None
            for index in range(3):
                weight = k.w_qkv[block, :, index * 128 : index * 128 + 128].reshape(256, 256)
                one = contract_last(rows[index], weight)
                made = one if made is None else made + one
            put_two(k.part_b, ranks, made, lanes_at(block))

        loop(4, column)

    reduce = ReduceHere(p, k.wires, k.part_b, k.got_b, (k.held_b, k.mixed_b))
    term(there)
    reduce.start_cross()
    term(here)
    reduce.start_near()
    reduce.relay()

    def turn(index):
        lanes = lanes_at(index)
        k.turned[lanes] = whole(k.n1, lanes).T

    loop(4, turn)
    for index in range(3):
        rows = pl.ds(index * 128, 128)

        def grad_qkv(block):
            made = dot_nn(k.turned[lanes_at(block)], whole(k.gq.at[index]))
            k.g_qkv[block, :, rows] = made.astype(jnp.bfloat16).reshape(2, 128, 256)

        loop(4, grad_qkv)
        third(index)
    background(AT_QKV)
    reduce.finish()
    through_norm(
        k, reduce, k.hidden, k.grad_mid, (0, 2, None, None), 0, k.back_out, lambda at, now: None
    )


def total_scratch(name, rows, cols, half=jnp.bfloat16):
    one, two = ((rows, cols), half), ((2, rows, cols), half)
    return {f"{name}_t{index}": value for index, value in enumerate((two, two, two, one, one))}


def paired_shards(
    x_in, d_out, seq_lengths, w_qkv, b_qv, w_o, w_1, b_ffn, w_2, norm_gains, vec_biases
):
    fused = make_fused()
    own_rows, width = x_in.shape
    layer_count = w_qkv.shape[0]
    half, full = jnp.bfloat16, jnp.float32
    z = lax.axis_index("tensor")
    native = lax.axis_index("dp") % 2 == z // 2
    qkv_turned = jnp.transpose(w_qkv, (0, 2, 1, 3)).reshape(layer_count, 384, 256)
    shapes = {QKV: (384, 256), OUT: (256, 128), UP: (128, 1024), DOWN: (1024, 128)}
    def pair_spec(name):
        return ((2,) + shapes[name], half)

    def full_spec(name):
        return ((4, 2) + shapes[name], half)

    def added(parts):
        return parts[0].astype(full) + parts[1].astype(full)

    small_shapes = [b_qv.shape, b_ffn.shape, norm_gains.shape, vec_biases.shape]
    small = pack([b_qv, b_ffn, norm_gains, vec_biases], 128, 16)
    lengths = jnp.pad(seq_lengths.astype(full), ((0, 7), (0, 126)))

    rows_spec = ((4, 2, own_rows // 2, width), half)
    heads_spec = ((4, own_rows, 256), half)
    wide_spec = ((4, own_rows, width), half)
    own_half = ((own_rows, width), half)
    own_full = ((own_rows, width), full)
    two_half = ((2, own_rows, width), half)
    reduce_a = dict(part_a=wide_spec, got_a=two_half, held_a=own_half, mixed_a=own_half)
    reduce_b = dict(part_b=wide_spec, got_b=two_half, held_b=own_half, mixed_b=own_half)
    saved_specs = dict(
        hidden=own_full,
        vecs=((8, width), full),
        n1=rows_spec,
        q=heads_spec,
        key=heads_spec,
        val=heads_spec,
        probs=((4, 512, 512), half),
        att=heads_spec,
        mid=own_full,
        n2=rows_spec,
        act=wide_spec,
        slope=wide_spec,
        w_qkv=full_spec(QKV),
        w_out=full_spec(OUT),
        w_up=full_spec(UP),
        w_down=full_spec(DOWN),
    )
    own_specs = dict(
        reduce_a,
        qv_bias=((8, 256), full),
        ffn_bias=((8, width), full),
        pair_qkv=pair_spec(QKV),
        pair_out=pair_spec(OUT),
        pair_up=pair_spec(UP),
        pair_down=pair_spec(DOWN),
    )

    def of_layers(specs):
        return {f"{name}_{layer}": spec for name, spec in specs.items() for layer in range(2)}

    def view(k, layer):
        made = Env()
        for name, ref in k.__dict__.items():
            if name.endswith(f"_{layer}"):
                setattr(made, name[:-2], ref)
        made.place, made.wires = k.place, k.wires
        return made

    def forward(k):
        p, w = k.place, k.wires
        k0, k1 = view(k, 0), view(k, 1)
        small_job = Fetch(p, w, k.small, k.small_all, [k.small_pair])
        length_job = Swap(p, w, k.lengths_in, k.lengths, [])
        swap_x = Swap(p, w, k.x_half, k.x_got, [])
        swap_d = Swap(p, w, k.d_half, k.d_got, [])
        k0.lengths = k1.lengths = k.lengths

        def fetch_qkv(layer, v):
            jobs = []
            for index in range(3):
                rows = pl.ds(index * 128, 128)
                dst, pair = v.w_qkv.at[:, :, rows], v.pair_qkv.at[:, rows]
                jobs.append(Fetch(p, w, k.s_qkv.at[layer, rows], dst, [pair]))
            return jobs

        def fetch_rest(layer, v):
            return (
                Fetch(p, w, k.s_out.at[layer], v.w_out, [v.pair_out]),
                Fetch(p, w, k.s_up.at[layer], v.w_up, [v.pair_up]),
                Fetch(p, w, k.s_down.at[layer], v.w_down, [v.pair_down]),
            )

        qkv_0, qkv_1 = fetch_qkv(0, k0), fetch_qkv(1, k1)
        out_0, up_0, down_0 = fetch_rest(0, k0)
        out_1, up_1, down_1 = fetch_rest(1, k1)
        for at in range(4):
            rows = pl.ds(at * ROWS, ROWS)
            k.x_half[rows] = k.x_in[rows].astype(half)
        small_job.start()
        length_job.start()
        swap_x.start()
        for job in qkv_0:
            job.start()
        out_0.start()
        small_job.relay()
        small_job.relay_more()
        small_job.finish()
        unpack_small(k.small_all, (k0, k1))
        length_job.finish()
        swap_x.finish()
        for at in range(4):
            rows = pl.ds(at * ROWS, ROWS)
            k0.hidden[rows] = jnp.where(p.native, k.x_in[rows], k.x_got[rows].astype(full))
            k.d_half[rows] = k.d_in[rows].astype(half)

        def first_sent():
            qkv_0[0].relay()
            qkv_0[1].relay()
            up_0.start()

        def first_gathered():
            qkv_0[2].relay()
            out_0.relay()
            for job in qkv_0:
                job.relay_more()
            up_0.relay()
            down_0.start()
            for job in qkv_0:
                job.finish()

        def first_attended():
            out_0.relay_more()
            out_0.finish()
            up_0.relay_more()
            down_0.relay()
            for job in qkv_1:
                job.start()
            out_1.start()

        reduce = attention_forward(k0, first_sent, first_gathered, first_attended)

        def first_raised():
            down_0.relay_more()
            for job in qkv_1:
                job.relay()
            out_1.relay()
            up_1.start()
            down_0.finish()

        column, here, there = feed_forward(
            k0, reduce, lambda: None, up_0.finish, first_raised, k.part_b
        )
        second = ReduceHere(p, w, k.part_b, k.got_b, (k.held_b, k.mixed_b))
        column(there)
        second.start_cross()
        column(here)
        second.start_near()
        second.relay()
        for job in qkv_1:
            job.relay_more()
        up_1.relay()
        swap_d.start()
        down_1.start()
        second.finish()
        for at in range(4):
            rows = pl.ds(at * ROWS, ROWS)
            k1.hidden[rows] = k0.mid[rows] + second.total(rows) + k0.vecs[5:6]
        grads = GatherHere(p, w, k.gh)

        def last_gathered():
            for job in qkv_1:
                job.finish()
            out_1.relay_more()
            swap_d.finish()

        def last_attended():
            out_1.finish()
            up_1.relay_more()
            down_1.relay()
            for at in range(4):
                rows = pl.ds(at * ROWS, ROWS)
                k.back[rows] = jnp.where(p.native, k.d_in[rows], k.d_got[rows].astype(full))
                k.gh[p.rank, at // 2, pl.ds(at % 2 * ROWS, ROWS)] = k.back[rows].astype(half)

        reduce = attention_forward(k1, lambda: None, last_gathered, last_attended)
        grads.start()

        def raised():
            down_1.relay_more()
            grads.wait_sibling()
            grads.relay()
            down_1.finish()

        column, here, there = feed_forward(k1, reduce, lambda: None, up_1.finish, raised, k.ffn_part)
        column(there)
        column(here)
        grads.finish()

    ahead = fused(
        forward,
        dict(
            x_in=x_in,
            d_in=d_out,
            lengths_in=lengths,
            small=small,
            s_qkv=qkv_turned,
            s_out=w_o,
            s_up=w_1,
            s_down=w_2,
        ),
        dict(of_layers(saved_specs), back=own_full, gh=rows_spec, ffn_part=wide_spec),
        dict(
            of_layers(own_specs),
            **reduce_b,
            lengths=((8, 128), full),
            small_pair=((2, 16, 128), half),
            small_all=((4, 2, 16, 128), half),
            x_half=own_half,
            x_got=own_half,
            d_half=own_half,
            d_got=own_half,
        ),
        EVERY_PEER,
        hbm=("s_qkv", "s_out", "s_up", "s_down"),
    )

    back_spare = dict(
        reduce_a,
        **reduce_b,
        gp=wide_spec,
        turned=((1024, 512), half),
        gm=rows_spec,
        ga=heads_spec,
        ds=((2, 512, 512), half),
        gq=((3, 4, own_rows, 256), half),
        grad_mid=own_full,
        g_down=full_spec(DOWN),
        g_up=full_spec(UP),
        g_out=full_spec(OUT),
        **total_scratch(DOWN, 1024, 128),
        **total_scratch(UP, 128, 1024),
        **total_scratch(OUT, 256, 128),
    )
    back_outs = dict(
        back_out=own_full,
        col=((8, width), full),
        col_qv=((8, 256), full),
        col_ffn=((8, width), full),
        sum_down=pair_spec(DOWN),
        sum_up=pair_spec(UP),
        sum_out=pair_spec(OUT),
    )

    def job_total(k, name, src, dst):
        spare = [getattr(k, f"{name}_t{index}") for index in range(5)]
        return Total(k.place, k.wires, src, dst, spare)

    def backward_last(k):
        p, w = k.place, k.wires
        ffn = ReduceHere(p, w, k.ffn_part, k.got_f, (k.held_f, k.mixed_f))
        down = job_total(k, DOWN, k.g_down, k.sum_down)
        up = job_total(k, UP, k.g_up, k.sum_up)
        out = job_total(k, OUT, k.g_out, k.sum_out)
        to_down = Deliver(p, w, k.sum_down, k.done_down, [])
        ffn.start_cross()
        ffn.start_near()

        def background(point):
            if point == AT_UP:
                down.relay_more()
                up.start()
            if point == AT_OUT:
                out.start()
                down.finish()
                to_down.start()
            if point == AT_ATTENDED:
                up.relay_more()
                out.relay_more()
            if point == AT_QKV:
                up.finish()
                out.finish()

        reduce = feed_forward_back(k, None)
        ffn.relay()
        down.start()
        attention_back(k, reduce, background, lambda index: None)
        ffn.finish()
        for at in range(4):
            rows = pl.ds(at * ROWS, ROWS)
            made = k.mid[rows] + ffn.total(rows) + k.vecs[5:6]
            k.output[rows] = made
            k.out_half[rows] = made.astype(half)
        to_down.finish()

    def backward_first(k):
        p, w = k.place, k.wires
        for at in range(4):
            rows = pl.ds(at * ROWS, ROWS)
            k.gh[p.rank, at // 2, pl.ds(at % 2 * ROWS, ROWS)] = k.back[rows].astype(half)
        gather = GatherHere(p, w, k.gh)
        last_qkv = job_total(k, "last", k.last_qkv, k.last_sum)
        to_last = Deliver(p, w, k.last_sum, k.done_last_qkv, [])
        to_last_up = Deliver(p, w, k.last_up, k.done_last_up, [])
        to_last_out = Deliver(p, w, k.last_out, k.done_last_out, [])
        down = job_total(k, DOWN, k.g_down, k.sum_down)
        up = job_total(k, UP, k.g_up, k.sum_up)
        out = job_total(k, OUT, k.g_out, k.sum_out)
        qkv, to_qkv = [], []
        for index in range(3):
            rows = pl.ds(index * 128, 128)
            spare = [getattr(k, f"qkv_t{at}") for at in range(5)]
            spare = [ref.at[:, rows] for ref in spare[:3]] + [ref.at[rows] for ref in spare[3:]]
            src, dst = k.g_qkv.at[:, :, rows], k.sum_qkv.at[:, rows]
            qkv.append(Total(p, w, src, dst, spare))
            to_qkv.append(Deliver(p, w, dst, k.done_qkv.at[:, rows], []))
        to_down = Deliver(p, w, k.sum_down, k.done_down, [])
        to_up = Deliver(p, w, k.sum_up, k.done_up, [])
        to_out = Deliver(p, w, k.sum_out, k.done_out, [])
        swap = Swap(p, w, k.out_half, k.out_sent, [])
        swap_back = Swap(p, w, k.back_half, k.back_sent, [])
        small_job = Small(
            p, w, k.flat, k.small_parts, [getattr(k, f"small_t{at}") for at in range(5)] + [k.small_sums]
        )
        gather.start()
        last_qkv.start()
        to_last_up.start()
        to_last_out.start()

        def background(point):
            if point == AT_UP:
                down.relay_more()
                up.start()
            if point == AT_OUT:
                out.start()
                down.finish()
                to_down.start()
                swap.start()
            if point == AT_ATTENDED:
                up.relay_more()
                out.relay_more()
            if point == AT_QKV:
                out.finish()
                to_out.start()
                up.finish()
                to_up.start()

        reduce = feed_forward_back(k, gather)
        last_qkv.relay_more()
        down.start()
        last_qkv.finish()
        to_last.start()
        attention_back(k, reduce, background, lambda index: qkv[index].start())
        for at in range(4):
            rows = pl.ds(at * ROWS, ROWS)
            k.back_half[rows] = k.back_out[rows].astype(half)
        swap_back.start()
        pack_small(k.flat, ((k.col, k.col_qv, k.col_ffn), (k.last_col, k.last_col_qv, k.last_col_ffn)))
        small_job.start()
        for job in qkv:
            job.relay_more()
        small_job.relay_more()
        for job, then in zip(qkv, to_qkv):
            job.finish()
            then.start()
        small_job.finish()
        for job in (to_last, to_last_up, to_last_out, to_down, to_out, to_up, swap, swap_back):
            job.finish()
        for job in to_qkv:
            job.finish()

    def saved(layer):
        return {name: getattr(ahead, f"{name}_{layer}") for name in saved_specs}

    last = fused(
        backward_last,
        dict(saved(1), back=ahead.back, gh=ahead.gh, ffn_part=ahead.ffn_part),
        dict(
            back_outs,
            output=own_full,
            out_half=own_half,
            g_qkv=full_spec(QKV),
            done_down=pair_spec(DOWN),
        ),
        dict(back_spare, got_f=two_half, held_f=own_half, mixed_f=own_half),
        EVERY_PEER,
    )
    first = fused(
        backward_first,
        dict(
            saved(0),
            back=last.back_out,
            last_qkv=last.g_qkv,
            last_up=last.sum_up,
            last_out=last.sum_out,
            last_col=last.col,
            last_col_qv=last.col_qv,
            last_col_ffn=last.col_ffn,
            out_half=last.out_half,
        ),
        dict(
            back_outs,
            done_last_qkv=pair_spec(QKV),
            done_last_up=pair_spec(UP),
            done_last_out=pair_spec(OUT),
            done_qkv=pair_spec(QKV),
            done_down=pair_spec(DOWN),
            done_up=pair_spec(UP),
            done_out=pair_spec(OUT),
            out_sent=own_half,
            back_sent=own_half,
            small_parts=((8, 16, 128), full),
        ),
        dict(
            back_spare,
            gh=rows_spec,
            g_qkv=full_spec(QKV),
            sum_qkv=pair_spec(QKV),
            last_sum=pair_spec(QKV),
            back_half=own_half,
            flat=((4, 2, 16, 128), full),
            small_sums=((2, 16, 128), full),
            **total_scratch("last", 384, 256),
            **total_scratch(QKV, 384, 256),
            **total_scratch("small", 16, 128, full),
        ),
        (SIBLING, CROSS, FAR, BESIDE, ABOVE, LINE),
    )
    output, back = last.output, first.back_out
    small_parts = first.small_parts
    small_parts = small_parts.reshape(8, -1)
    gain_size, bias_size = norm_gains.size, vec_biases.size
    everyone = small_parts.sum(0)
    sources = jnp.arange(8, dtype=jnp.int32)
    pair = z // 2
    mine_from = (sources == 2 * z + pair) | (sources == 2 * (z + 2 - 4 * pair) + pair)
    mine = jnp.where(mine_from[:, None], small_parts, 0.0).sum(0)[gain_size + bias_size :]

    def stacked_layers(first_part, last_part):
        return jnp.stack([added(first_part), added(last_part)])

    grad_qkv = stacked_layers(first.done_qkv, first.done_last_qkv)
    grad_qkv = jnp.transpose(grad_qkv.reshape(layer_count, 3, 128, 256), (0, 2, 1, 3))
    return (
        jnp.where(native, output, first.out_sent.astype(full)),
        jnp.where(native, back, first.back_sent.astype(full)),
        grad_qkv,
        mine[: b_qv.size].reshape(b_qv.shape),
        stacked_layers(first.done_out, first.done_last_out),
        stacked_layers(first.done_up, first.done_last_up),
        mine[b_qv.size : b_qv.size + b_ffn.size].reshape(b_ffn.shape),
        stacked_layers(first.done_down, last.done_down),
        everyone[:gain_size].reshape(norm_gains.shape),
        everyone[gain_size : gain_size + bias_size].reshape(vec_biases.shape),
    )


def solution(mesh):
    in_specs = (
        P(("dp", "tensor"), None),
        P(("dp", "tensor"), None),
        P("dp", None),
        P(None, "dp", None, "tensor"),
        P(None, None, ("tensor", "dp")),
        P(None, "tensor", "dp"),
        P(None, "dp", "tensor"),
        P(None, ("tensor", "dp")),
        P(None, "tensor", "dp"),
        P(None, None, "dp"),
        P(None, None, "dp"),
    )
    out_specs = (
        P(("dp", "tensor"), None),
        P(("dp", "tensor"), None),
        P(None, "dp", None, "tensor"),
        P(None, None, ("tensor", "dp")),
        P(None, "tensor", "dp"),
        P(None, "dp", "tensor"),
        P(None, ("tensor", "dp")),
        P(None, "tensor", "dp"),
        P(None, None, "dp"),
        P(None, None, "dp"),
    )
    paired = mesh.shape["dp"] == 8 and mesh.shape["tensor"] == 4
    body = paired_shards if paired else shards
    return jax.shard_map(body, mesh=mesh, in_specs=in_specs, out_specs=out_specs, check_vma=False)
```

```python
import math

import jax
import jax.numpy as jnp
from jax import lax
from jax.experimental import pallas as pl
from jax.experimental.pallas import tpu as pltpu
from jax.sharding import PartitionSpec as P

HEAD_DIM = 64


NORM_EPS = 1e-05
GELU_COEFF = 0.7978845608028654
GELU_CUBIC = 0.044715


def layer_norm(inputs, gain_row, bias_row):
    row_mean = jnp.mean(inputs, axis=-1, keepdims=True)
    centered = inputs - row_mean
    inv_std = lax.rsqrt(jnp.mean(centered * centered, axis=-1, keepdims=True) + NORM_EPS)
    normed = centered * inv_std
    return (normed * gain_row + bias_row, normed, inv_std)


def norm_back(grad_in, normed, inv_std, gain_row):
    scaled = grad_in * gain_row
    return inv_std * (
        scaled
        - jnp.mean(scaled, axis=-1, keepdims=True)
        - normed * jnp.mean(scaled * normed, axis=-1, keepdims=True)
    )


def gelu_pair(pre_act):
    squared = pre_act * pre_act
    tangent = jnp.tanh(GELU_COEFF * (pre_act + GELU_CUBIC * squared * pre_act))
    gelu_value = 0.5 * pre_act * (1.0 + tangent)
    gelu_slope = 0.5 * (1.0 + tangent) + 0.5 * pre_act * (1.0 - tangent * tangent) * GELU_COEFF * (
        1.0 + 3.0 * GELU_CUBIC * squared
    )
    return (gelu_value, gelu_slope)


def segment_ids(lengths, total_rows):
    positions = jnp.arange(total_rows, dtype=jnp.int32)
    found = jnp.zeros_like(positions)
    end = jnp.int32(0)
    for index in range(lengths.shape[0]):
        end = end + lengths[index]
        found = found + (positions >= end).astype(jnp.int32)
    return found


def contract_first(left, right):
    return lax.dot_general(
        left, right, (((0,), (0,)), ((), ())), preferred_element_type=jnp.float32
    )


def contract_last(left, right):
    return lax.dot_general(
        left, right, (((1,), (1,)), ((), ())), preferred_element_type=jnp.float32
    )

def exchange_kernel(plan, *refs):
    count = len(plan)
    ins = refs[:count]
    outs = refs[count : 2 * count]
    send_sem, recv_sem, own_sem = refs[2 * count : 2 * count + 3]
    spare = list(refs[2 * count + 3 :])

    greeted = []
    for axis in sorted({axis for axis, _, _ in plan}):
        kinds = {kind for name, kind, _ in plan if name == axis}
        size = [n for name, _, n in plan if name == axis][0]
        me = lax.axis_index(axis)
        if kinds == {"paired"}:
            greeted.append({axis: me + 1 - 2 * (me % 2)})
            greeted += [{axis: (me + k) % size} for k in range(2, size, 2)]
        else:
            greeted += [{axis: (me + k) % size} for k in range(1, size)]
    barrier = pltpu.get_barrier_semaphore()
    for device in greeted:
        pl.semaphore_signal(
            barrier, inc=1, device_id=device, device_id_type=pl.DeviceIdType.MESH
        )
    pl.semaphore_wait(barrier, len(greeted))

    used = [0]

    def remote(src, dst, device):
        slot = used[0]
        used[0] += 1
        copy = pltpu.make_async_remote_copy(
            src_ref=src,
            dst_ref=dst,
            send_sem=send_sem.at[slot],
            recv_sem=recv_sem.at[slot],
            device_id=device,
            device_id_type=pl.DeviceIdType.MESH,
        )
        copy.start()
        return copy

    def in_line(axis, src, dst, base, place, target, arrival):
        return pltpu.make_async_remote_copy(
            src_ref=src,
            dst_ref=dst,
            send_sem=send_sem.at[base + place],
            recv_sem=recv_sem.at[base + arrival],
            device_id={axis: jnp.int32(target)},
            device_id_type=pl.DeviceIdType.MESH,
        )

    def line_start(axis, kind, src, dst, base, held):
        me = lax.axis_index(axis)
        for m in range(4):

            @pl.when(me == m)
            def _(m=m):
                if kind == "sum" and m in (0, 3):
                    far = 3 - m
                    near = 1 if m == 0 else 2
                    in_line(axis, src.at[far], held, base, far, near, 4).start()
                for target in ((2, 1), (3, 2, 0), (0, 1, 3), (1, 2))[m]:
                    if kind == "sum" and (m, target) in ((1, 3), (2, 0)):
                        continue
                    block = src.at[target] if kind == "sum" else src
                    in_line(axis, block, dst.at[m], base, target, target, m).start()

    def line_relay(axis, kind, src, dst, base, held, mixed):
        me = lax.axis_index(axis)
        for m in (1, 2):

            @pl.when(me == m)
            def _(m=m):
                far = 3 if m == 1 else 0
                near = 3 - far
                if kind == "line":
                    in_line(axis, src, dst.at[far], base, far, far, far).wait_recv()
                    in_line(axis, dst.at[far], dst.at[far], base, 4, near, far).start()
                else:
                    in_line(axis, held, held, base, far, far, 4).wait_recv()

                    def add(row, carry):
                        rows = pl.ds(row * 16, 16)
                        mixed[rows] = (
                            held[rows].astype(jnp.float32)
                            + src[far, rows].astype(jnp.float32)
                        ).astype(mixed.dtype)
                        return carry

                    lax.fori_loop(0, mixed.shape[0] // 16, add, 0)
                    in_line(axis, mixed, dst.at[m], base, far, far, m).start()

        if kind == "sum":
            for m in (0, 3):

                @pl.when(me == m)
                def _(m=m):
                    dst[3 - m] = jnp.zeros(dst.shape[1:], dst.dtype)

    def line_finish(axis, kind, src, dst, base, held, mixed):
        me = lax.axis_index(axis)
        for m in range(4):

            @pl.when(me == m)
            def _(m=m):
                block = src.at[0] if kind == "sum" else src
                for other in range(4):
                    if other == m:
                        continue
                    ends = (m, other) in ((0, 3), (3, 0))
                    relayed = (m, other) in ((1, 3), (2, 0))
                    copy = in_line(axis, block, dst.at[other], base, other, other, other)
                    if not (kind == "sum" and ends) and not (kind == "line" and relayed):
                        copy.wait_recv()
                    if not (kind == "line" and ends):
                        copy.wait_send()
                if kind == "line" and m in (1, 2):
                    in_line(axis, block, dst.at[0], base, 4, 0, 0).wait_send()

    started = []
    relays = []
    own = []
    lines = []
    for index, (axis, kind, size) in enumerate(plan):
        me = lax.axis_index(axis)
        src, dst = ins[index], outs[index]
        if kind in ("line", "sum"):
            held = spare.pop(0) if kind == "sum" else None
            mixed = spare.pop(0) if kind == "sum" else None
            line_start(axis, kind, src, dst, used[0], held)
            lines.append((axis, kind, src, dst, used[0], held, mixed))
            used[0] += 5
        elif kind == "paired":
            for k in range(2, size, 2):
                copy = remote(src, dst.at[me], {axis: (me + k) % size})
                relays.append((copy, dst, axis, (me + size - k) % size))
            started.append(remote(src, dst.at[me], {axis: me + 1 - 2 * (me % 2)}))
        else:
            for k in range(1, size):
                peer = (me + k) % size
                block = src if kind == "gather" else src.at[peer]
                started.append(remote(block, dst.at[me], {axis: peer}))
    for index, (axis, kind, size) in enumerate(plan):
        me = lax.axis_index(axis)
        block = ins[index].at[me] if kind in ("swap", "sum") else ins[index]
        copy = pltpu.make_async_copy(block, outs[index].at[me], own_sem.at[index])
        copy.start()
        own.append(copy)
    for line in lines:
        line_relay(*line)
    for copy, dst, axis, slot in relays:
        copy.wait_recv()
        me = lax.axis_index(axis)
        started.append(
            remote(dst.at[slot], dst.at[slot], {axis: me + 1 - 2 * (me % 2)})
        )
    for copy, _, _, _ in relays:
        copy.wait_send()
    for copy in own:
        copy.wait()
    for copy in started:
        copy.wait()
    for line in lines:
        line_finish(*line)


def make_exchange():
    calls = [0]

    def exchange(*items):
        plan = []
        shapes = []
        copies = 0
        sent = 0
        spare = []
        for axis, kind, value in items:
            size = lax.axis_size(axis)
            if kind == "paired" and size % 2:
                kind = "gather"
            block = value.shape[1:] if kind == "swap" else value.shape
            if axis == "tensor" and size == 4 and value.dtype == jnp.bfloat16:
                kind = {"swap": "sum", "gather": "line"}[kind]
                if kind == "sum":
                    spare += [pltpu.VMEM(block, value.dtype)] * 2
            plan.append((axis, kind, size))
            copies += 5 if kind in ("line", "sum") else size - 1
            shapes.append(jax.ShapeDtypeStruct((size,) + block, value.dtype))
            sent += (size - 1) * math.prod(block) * value.dtype.itemsize
        collective_id = calls[0]
        calls[0] += 1
        return pl.pallas_call(
            lambda *refs: exchange_kernel(tuple(plan), *refs),
            out_shape=tuple(shapes),
            in_specs=[pl.BlockSpec(memory_space=pltpu.VMEM)] * len(plan),
            out_specs=tuple([pl.BlockSpec(memory_space=pltpu.VMEM)] * len(plan)),
            scratch_shapes=[
                pltpu.SemaphoreType.DMA((copies,)),
                pltpu.SemaphoreType.DMA((copies,)),
                pltpu.SemaphoreType.DMA((len(plan),)),
                *spare,
            ],
            compiler_params=pltpu.CompilerParams(
                collective_id=collective_id,
                has_side_effects=True,
                vmem_limit_bytes=48 * 1024 * 1024,
            ),
            cost_estimate=pl.CostEstimate(flops=0, bytes_accessed=sent, transcendentals=0),
            name=f"exchange_{collective_id}",
        )(*[value for _, _, value in items])

    return exchange


SIBLING, CROSS, FAR, BESIDE, ABOVE, LINE = range(6)
EVERY_PEER = (SIBLING, CROSS, FAR, BESIDE, ABOVE)
AT_UP, AT_OUT, AT_HEADS, AT_ATTENDED, AT_QKV = range(5)
QKV, OUT, UP, DOWN = "qkv", "out", "up", "down"
MESH = pl.DeviceIdType.MESH


class Place:
    def __init__(self):
        self.dp = lax.axis_index("dp")
        self.z = lax.axis_index("tensor")
        self.core = lax.rem(self.dp, 2)
        self.pair = lax.div(self.z, 2)
        self.low = lax.rem(self.z, 2)
        self.rank = 2 * self.core + self.low
        self.native = self.core == self.pair
        self.block = lax.div(self.dp, 2)
        self.x = lax.rem(self.block, 2)
        self.y = lax.div(self.block, 2)
        self.base = self.dp - self.core

    def sibling(self):
        return {"dp": self.base + 1 - self.core, "tensor": self.z}

    def cross(self, core):
        return {"dp": self.base + core, "tensor": self.z + 1 - 2 * self.low}

    def far(self, core):
        return {"dp": self.base + core, "tensor": self.z + 2 - 4 * self.pair}

    def beside(self):
        return {"dp": self.dp + 2 - 4 * self.x, "tensor": self.z}

    def above(self):
        return {"dp": self.dp + 4 - 8 * self.y, "tensor": self.z}

    def in_line(self, index):
        return {"dp": self.base + lax.rem(index, 2), "tensor": lax.div(index, 2)}

    def rank_at(self, core, low):
        return 2 * core + low

    def block_at(self, dy, dx):
        y = 1 - self.y if dy else self.y
        x = 1 - self.x if dx else self.x
        return 2 * y + x


class Wires:
    def __init__(self, send_sem, recv_sem, own_sem):
        self.send_sem, self.recv_sem, self.own_sem = send_sem, recv_sem, own_sem
        self.used = 0
        self.own_used = 0

    def take(self, count):
        at = self.used
        self.used += count
        return at

    def take_own(self, count=1):
        at = self.own_used
        self.own_used += count
        return at

    def copy(self, src, dst, device, send, recv):
        return pltpu.make_async_remote_copy(
            src_ref=src,
            dst_ref=dst,
            send_sem=self.send_sem.at[send],
            recv_sem=self.recv_sem.at[recv],
            device_id=device,
            device_id_type=MESH,
        )

    def local(self, src, dst, slot):
        return pltpu.make_async_copy(src, dst, self.own_sem.at[slot])


def add_rows(dst, *parts):
    rows = dst.shape[0]
    step = 16 if rows % 16 == 0 else 8

    def body(index, carry):
        at = pl.ds(index * step, step)
        total = parts[0][at].astype(jnp.float32)
        for part in parts[1:]:
            total = total + part[at].astype(jnp.float32)
        dst[at] = total.astype(dst.dtype)
        return carry

    lax.fori_loop(0, rows // step, body, 0)


class Gather:
    peers = (SIBLING, CROSS)
    copies = 5
    owns = 1

    @staticmethod
    def shape(value):
        return (4,) + value.shape

    @staticmethod
    def scratch(value):
        return []

    def __init__(self, place, wires, src, dst, spare):
        self.p, self.w, self.src, self.dst = place, wires, src, dst
        self.at = wires.take(self.copies)
        self.own = wires.take_own()

    def _copies(self):
        p, w, src, dst, at = self.p, self.w, self.src, self.dst, self.at
        other = 1 - p.core
        near = p.rank_at(p.core, 1 - p.low)
        skew = p.rank_at(other, 1 - p.low)
        sib = p.sibling()
        return [
            lambda: w.copy(src, dst.at[p.rank], sib, at, at),
            lambda: w.copy(src.at[p.core], dst.at[p.rank, p.core], p.cross(p.core), at + 1, at + 1),
            lambda: w.copy(src.at[other], dst.at[p.rank, other], p.cross(other), at + 2, at + 2),
            lambda: w.copy(dst.at[near, p.core], dst.at[near, p.core], sib, at + 3, at + 4),
            lambda: w.copy(dst.at[skew, p.core], dst.at[skew, p.core], sib, at + 4, at + 3),
        ]

    def start(self):
        made = self._copies()
        for copy in (made[1], made[2], made[0]):
            copy().start()
        self.w.local(self.src, self.dst.at[self.p.rank], self.own).start()

    def relay(self):
        made = self._copies()
        made[1]().wait_recv()
        made[3]().start()
        made[2]().wait_recv()
        made[4]().start()

    def relay_more(self):
        pass

    def finish(self):
        made = self._copies()
        for index in (0, 3, 4):
            made[index]().wait_recv()
        for copy in made:
            copy().wait_send()
        self.w.local(self.src, self.dst.at[self.p.rank], self.own).wait()


class Reduce:
    peers = (SIBLING, CROSS)
    copies = 3
    owns = 1

    @staticmethod
    def shape(value):
        return (3,) + value.shape[1:]

    @staticmethod
    def scratch(value):
        return [pltpu.VMEM(value.shape[1:], value.dtype)] * 2

    def __init__(self, place, wires, src, dst, spare):
        self.p, self.w, self.src, self.dst = place, wires, src, dst
        self.held, self.mixed = spare
        self.at = wires.take(self.copies)
        self.own = wires.take_own()

    def _copies(self):
        p, w, src, dst, at = self.p, self.w, self.src, self.dst, self.at
        other = 1 - p.core
        sib = p.sibling()
        return [
            lambda: w.copy(src.at[p.rank_at(other, p.low)], dst.at[1], sib, at, at),
            lambda: w.copy(src.at[p.rank_at(other, 1 - p.low)], self.held, sib, at + 1, at + 1),
            lambda: w.copy(self.mixed, dst.at[2], p.cross(p.core), at + 2, at + 2),
        ]

    def start(self):
        made = self._copies()
        made[1]().start()
        made[0]().start()
        self.w.local(self.src.at[self.p.rank], self.dst.at[0], self.own).start()

    def relay(self):
        made = self._copies()
        made[1]().wait_recv()
        add_rows(self.mixed, self.held, self.src.at[self.p.rank_at(self.p.core, 1 - self.p.low)])
        made[2]().start()

    def relay_more(self):
        pass

    def finish(self):
        made = self._copies()
        made[0]().wait_recv()
        made[2]().wait_recv()
        for copy in made:
            copy().wait_send()
        self.w.local(self.src.at[self.p.rank], self.dst.at[0], self.own).wait()


class Pairing:
    peers = (SIBLING, FAR)
    copies = 3
    owns = 1

    @staticmethod
    def shape(value):
        return (2,) + value.shape

    @staticmethod
    def scratch(value):
        return []

    def __init__(self, place, wires, src, dst, spare):
        self.p, self.w, self.src, self.dst = place, wires, src, dst
        self.at = wires.take(self.copies)
        self.own = wires.take_own()

    def _near(self):
        p, at = self.p, self.at
        return self.w.copy(self.src, self.dst.at[p.core], p.sibling(), at, at)

    def _far(self, recv):
        p, at = self.p, self.at
        return self.w.copy(self.src, self.dst.at[p.core], p.far(p.pair), at + 1, recv)

    def start(self):
        p = self.p
        self._far(self.at + 1 + p.core).start()

        @pl.when(p.native)
        def _():
            self.w.local(self.src, self.dst.at[p.core], self.own).start()

        @pl.when(jnp.logical_not(p.native))
        def _():
            self._near().start()

    def settle(self):
        p = self.p

        @pl.when(p.native)
        def _():
            self._near().wait_recv()
            self.w.local(self.src, self.dst.at[p.core], self.own).wait()

        @pl.when(jnp.logical_not(p.native))
        def _():
            self._far(self.at + 1).wait_recv()
            self._far(self.at + 2).wait_recv()

    def sent(self):
        p = self.p
        self._far(self.at + 1).wait_send()

        @pl.when(jnp.logical_not(p.native))
        def _():
            self._near().wait_send()

    def relay(self):
        pass

    def relay_more(self):
        pass

    def finish(self):
        self.settle()
        self.sent()


class Spread:
    peers = (BESIDE, ABOVE)
    copies = 4
    owns = 1

    @staticmethod
    def shape(value):
        return (4,) + value.shape

    @staticmethod
    def scratch(value):
        return []

    def __init__(self, place, wires, src, dst, spare):
        self.p, self.w, self.src, self.dst = place, wires, src, dst
        self.at = wires.take(self.copies)
        self.own = wires.take_own()

    def _copies(self):
        p, w, src, dst, at = self.p, self.w, self.src, self.dst, self.at
        row, column = p.block_at(0, 1), p.block_at(1, 0)
        return [
            lambda: w.copy(src, dst.at[p.block], p.beside(), at, at),
            lambda: w.copy(src, dst.at[p.block], p.above(), at + 1, at + 1),
            lambda: w.copy(dst.at[row, 0], dst.at[row, 0], p.above(), at + 2, at + 2),
            lambda: w.copy(dst.at[column, 1], dst.at[column, 1], p.beside(), at + 3, at + 3),
        ]

    def start(self):
        made = self._copies()
        made[0]().start()
        made[1]().start()
        self.w.local(self.src, self.dst.at[self.p.block], self.own).start()

    def relay(self):
        pass

    def relay_more(self):
        made = self._copies()
        made[0]().wait_recv()
        made[2]().start()
        made[1]().wait_recv()
        made[3]().start()

    def finish(self):
        made = self._copies()
        made[2]().wait_recv()
        made[3]().wait_recv()
        for copy in made:
            copy().wait_send()
        self.w.local(self.src, self.dst.at[self.p.block], self.own).wait()


class Fetch:
    peers = (SIBLING, FAR, BESIDE, ABOVE)
    copies = 7
    owns = 2

    @staticmethod
    def shape(value):
        return (4, 2) + value.shape

    @staticmethod
    def scratch(value):
        return [pltpu.VMEM((2,) + value.shape, value.dtype)]

    def __init__(self, place, wires, src, dst, spare):
        self.one = Pairing(place, wires, src, spare[0], [])
        self.two = Spread(place, wires, spare[0], dst, [])

    def start(self):
        self.one.start()

    def relay(self):
        self.one.settle()
        self.two.start()

    def relay_more(self):
        self.two.relay_more()

    def finish(self):
        self.one.sent()
        self.two.finish()


class Total:
    peers = (BESIDE, ABOVE)
    copies = 6
    owns = 0

    @staticmethod
    def shape(value):
        return value.shape[1:]

    @staticmethod
    def scratch(value):
        one = pltpu.VMEM(value.shape[2:], value.dtype)
        two = pltpu.VMEM(value.shape[1:], value.dtype)
        return [two, two, two, one, one]

    def __init__(self, place, wires, src, dst, spare):
        self.p, self.w, self.src, self.dst = place, wires, src, dst
        self.from_x, self.from_y, self.last, self.to_y, self.to_x = spare
        self.at = wires.take(self.copies)

    def _copies(self):
        p, w, src, at = self.p, self.w, self.src, self.at
        here_x, here_y, skew = p.block_at(0, 1), p.block_at(1, 0), p.block_at(1, 1)
        return [
            lambda: w.copy(src.at[here_x, 0], self.from_x.at[0], p.beside(), at, at),
            lambda: w.copy(src.at[skew, 0], self.from_x.at[1], p.beside(), at + 1, at + 1),
            lambda: w.copy(src.at[here_y, 1], self.from_y.at[0], p.above(), at + 2, at + 2),
            lambda: w.copy(src.at[skew, 1], self.from_y.at[1], p.above(), at + 3, at + 3),
            lambda: w.copy(self.to_y, self.last.at[0], p.above(), at + 4, at + 4),
            lambda: w.copy(self.to_x, self.last.at[1], p.beside(), at + 5, at + 5),
        ]

    def start(self):
        made = self._copies()
        for index in (1, 3, 0, 2):
            made[index]().start()

    def relay(self):
        pass

    def relay_more(self):
        made = self._copies()
        p = self.p
        made[1]().wait_recv()
        add_rows(self.to_y, self.src.at[p.block_at(1, 0), 0], self.from_x.at[1])
        made[4]().start()
        made[3]().wait_recv()
        add_rows(self.to_x, self.src.at[p.block_at(0, 1), 1], self.from_y.at[1])
        made[5]().start()

    def finish(self):
        made = self._copies()
        p = self.p
        for index in (0, 2, 4, 5):
            made[index]().wait_recv()
        add_rows(self.dst.at[0], self.src.at[p.block, 0], self.from_x.at[0], self.last.at[0])
        add_rows(self.dst.at[1], self.src.at[p.block, 1], self.from_y.at[0], self.last.at[1])
        for copy in made:
            copy().wait_send()


class Deliver:
    peers = (SIBLING, FAR)
    copies = 4
    owns = 1

    @staticmethod
    def shape(value):
        return value.shape

    @staticmethod
    def scratch(value):
        return []

    def __init__(self, place, wires, src, dst, spare):
        self.p, self.w, self.src, self.dst = place, wires, src, dst
        self.at = wires.take(self.copies)
        self.own = wires.take_own()

    def _near(self):
        p, at = self.p, self.at
        return self.w.copy(self.src.at[1 - p.core], self.dst.at[0], p.sibling(), at, at)

    def _far(self, core):
        p, at = self.p, self.at
        return self.w.copy(
            self.src.at[core], self.dst.at[1], p.far(jnp.int32(core)), at + 1 + core, at + 1
        )

    def start(self):
        p = self.p

        @pl.when(p.native)
        def _():
            self._near().start()
            self.w.local(self.src.at[p.core], self.dst.at[0], self.own).start()

        @pl.when(jnp.logical_not(p.native))
        def _():
            self._far(0).start()
            self._far(1).start()

    def relay(self):
        pass

    def relay_more(self):
        pass

    def finish(self):
        p = self.p
        self._far(0).wait_recv()

        @pl.when(p.native)
        def _():
            self._near().wait_send()
            self.w.local(self.src.at[p.core], self.dst.at[0], self.own).wait()

        @pl.when(jnp.logical_not(p.native))
        def _():
            self._near().wait_recv()
            self._far(0).wait_send()
            self._far(1).wait_send()


class Swap:
    peers = (FAR,)
    copies = 1
    owns = 1

    @staticmethod
    def shape(value):
        return value.shape

    @staticmethod
    def scratch(value):
        return []

    def __init__(self, place, wires, src, dst, spare):
        self.p, self.w, self.src, self.dst = place, wires, src, dst
        self.at = wires.take(self.copies)
        self.own = wires.take_own()

    def _copy(self):
        p, at = self.p, self.at
        return self.w.copy(self.src, self.dst, p.far(1 - p.core), at, at)

    def start(self):
        @pl.when(self.p.native)
        def _():
            self.w.local(self.src, self.dst, self.own).start()

        @pl.when(jnp.logical_not(self.p.native))
        def _():
            self._copy().start()

    def relay(self):
        pass

    def relay_more(self):
        pass

    def finish(self):
        @pl.when(self.p.native)
        def _():
            self.w.local(self.src, self.dst, self.own).wait()

        @pl.when(jnp.logical_not(self.p.native))
        def _():
            self._copy().wait()


class Small:
    peers = (BESIDE, ABOVE, LINE)
    copies = 20
    owns = 1

    @staticmethod
    def shape(value):
        return (8,) + value.shape[2:]

    @staticmethod
    def scratch(value):
        return Total.scratch(value) + [pltpu.VMEM(value.shape[1:], value.dtype)]

    def __init__(self, place, wires, src, dst, spare):
        self.sums = spare[-1]
        self.total = Total(place, wires, src, self.sums, spare[:-1])
        self.p, self.w, self.dst = place, wires, dst
        self.at = wires.take(14)
        self.own = wires.take_own()

    def _ends(self, offset):
        p, at = self.p, self.at
        me = 2 * p.z + p.core
        to = lax.rem(me + offset, 8)
        return self.w.copy(
            self.sums.at[lax.rem(to, 2)], self.dst.at[me], p.in_line(to), at + offset - 1, at + 6 + offset
        )

    def _mine(self):
        p = self.p
        return self.w.local(self.sums.at[p.core], self.dst.at[2 * p.z + p.core], self.own)

    def start(self):
        self.total.start()

    def relay(self):
        pass

    def relay_more(self):
        self.total.relay_more()
        self.total.finish()
        for offset in range(1, 8):
            self._ends(offset).start()
        self._mine().start()

    def finish(self):
        self._mine().wait()
        for offset in range(1, 8):
            self._ends(offset).wait()


def greet(place, kinds):
    p = place
    devices = []
    if SIBLING in kinds or LINE in kinds:
        devices.append(p.sibling())
    if CROSS in kinds or LINE in kinds:
        devices += [p.cross(jnp.int32(0)), p.cross(jnp.int32(1))]
    if FAR in kinds or LINE in kinds:
        devices += [p.far(jnp.int32(0)), p.far(jnp.int32(1))]
    if LINE in kinds:
        last = 3 - p.z
        devices += [{"dp": p.base, "tensor": last}, {"dp": p.base + 1, "tensor": last}]
    if BESIDE in kinds:
        devices.append(p.beside())
    if ABOVE in kinds:
        devices.append(p.above())
    barrier = pltpu.get_barrier_semaphore()
    for device in devices:
        pl.semaphore_signal(barrier, inc=1, device_id=device, device_id_type=MESH)
    pl.semaphore_wait(barrier, len(devices))


def round_kernel(kinds, *refs):
    count = len(kinds)
    ins, outs = refs[:count], refs[count : 2 * count]
    wires = Wires(*refs[2 * count : 2 * count + 3])
    spare = list(refs[2 * count + 3 :])
    place = Place()
    greet(place, {peer for kind, _ in kinds for peer in kind.peers})
    jobs = []
    for (kind, held), src, dst in zip(kinds, ins, outs):
        jobs.append(kind(place, wires, src, dst, spare[:held]))
        del spare[:held]
    for job in jobs:
        job.start()
    for job in jobs:
        job.relay()
    for job in jobs:
        job.relay_more()
    for job in jobs:
        job.finish()


def make_rounds():
    calls = [0]

    def rounds(*items):
        kinds, shapes, scratch = [], [], []
        copies = owns = sent = 0
        for kind, value in items:
            held = kind.scratch(value)
            kinds.append((kind, len(held)))
            scratch += held
            shapes.append(jax.ShapeDtypeStruct(kind.shape(value), value.dtype))
            copies += kind.copies
            owns += kind.owns
            sent += math.prod(kind.shape(value)) * value.dtype.itemsize
        collective_id = calls[0]
        calls[0] += 1
        return pl.pallas_call(
            lambda *refs: round_kernel(tuple(kinds), *refs),
            out_shape=tuple(shapes),
            in_specs=[pl.BlockSpec(memory_space=pltpu.VMEM)] * len(kinds),
            out_specs=tuple([pl.BlockSpec(memory_space=pltpu.VMEM)] * len(kinds)),
            scratch_shapes=[
                pltpu.SemaphoreType.DMA((copies,)),
                pltpu.SemaphoreType.DMA((copies,)),
                pltpu.SemaphoreType.DMA((max(owns, 1),)),
                *scratch,
            ],
            compiler_params=pltpu.CompilerParams(
                collective_id=collective_id,
                has_side_effects=True,
                vmem_limit_bytes=48 * 1024 * 1024,
            ),
            cost_estimate=pl.CostEstimate(flops=0, bytes_accessed=sent, transcendentals=0),
            name=f"round_{collective_id}",
        )(*[value for _, value in items])

    return rounds


def masked_scores(queries, key_vecs, segments, score_scale):
    positions = jnp.arange(key_vecs.shape[0], dtype=jnp.int32)
    allowed = (segments[:, None] == segments[None, :]) & (
        positions[None, :] <= positions[:, None]
    )
    scores = (
        jnp.einsum("qhd,khd->hqk", queries, key_vecs, preferred_element_type=jnp.float32)
        * score_scale
    )
    return jnp.where(allowed[None], scores, -jnp.inf)


def attend(queries, key_vecs, val_vecs, segments, score_scale):
    scores = masked_scores(queries, key_vecs, segments, score_scale)
    row_max = jnp.max(scores, axis=-1, keepdims=True)
    log_total = row_max + jnp.log(jnp.sum(jnp.exp(scores - row_max), axis=-1, keepdims=True))
    probs_half = jnp.exp(scores - log_total).astype(jnp.bfloat16)
    attended = jnp.einsum("hqk,khd->qhd", probs_half, val_vecs, preferred_element_type=jnp.float32)
    return (attended.astype(jnp.bfloat16).reshape(queries.shape[0], -1), log_total)


def attend_back(queries, key_vecs, val_vecs, grad_attended, log_total, segments, score_scale):
    scores = masked_scores(queries, key_vecs, segments, score_scale)
    soft_probs = jnp.exp(scores - log_total)
    probs_half = soft_probs.astype(jnp.bfloat16)
    grad_probs = jnp.einsum(
        "qhd,khd->hqk", grad_attended, val_vecs, preferred_element_type=jnp.float32
    )
    val_grad = jnp.einsum(
        "hqk,qhd->khd", probs_half, grad_attended, preferred_element_type=jnp.float32
    )
    row_dot = jnp.sum(grad_probs * soft_probs, axis=-1, keepdims=True)
    score_grad = (soft_probs * (grad_probs - row_dot) * score_scale).astype(jnp.bfloat16)
    query_grad = jnp.einsum(
        "hqk,khd->qhd", score_grad, key_vecs, preferred_element_type=jnp.float32
    )
    key_grad = jnp.einsum("hqk,qhd->khd", score_grad, queries, preferred_element_type=jnp.float32)
    return (query_grad, key_grad, val_grad)


def pack(pieces, width, tile):
    flat = jnp.concatenate([piece.reshape(-1) for piece in pieces])
    unit = width * tile
    return jnp.pad(flat, (0, -flat.shape[0] % unit)).reshape(-1, width)


def unpack(packed, shapes):
    flat = packed.reshape(packed.shape[0], -1)
    pieces = []
    at = 0
    for shape in shapes:
        length = math.prod(shape)
        pieces.append(flat[:, at : at + length].reshape((packed.shape[0],) + shape))
        at += length
    return pieces


def shards(x_in, d_out, seq_lengths, w_qkv, b_qv, w_o, w_1, b_ffn, w_2, norm_gains, vec_biases):
    exchange = make_exchange()
    own_rows, width = x_in.shape
    tensor_size = lax.axis_size("tensor")
    dp_size = lax.axis_size("dp")
    group_rows = own_rows * tensor_size
    layer_count = w_qkv.shape[0]
    local_width = w_qkv.shape[3]
    local_heads = local_width // HEAD_DIM
    qkv_width = 3 * local_width
    score_scale = 1.0 / math.sqrt(HEAD_DIM)
    segments = segment_ids(seq_lengths[0], group_rows)
    half = jnp.bfloat16

    def shard_of(name, layer_index):
        if name == "qkv":
            return w_qkv[layer_index].reshape(w_qkv.shape[1], qkv_width)
        if name == "out":
            return w_o[layer_index].T
        if name == "up":
            return w_1[layer_index]
        return w_2[layer_index].T

    weights = {}

    def step(tensor_items, fetched=(), sums=()):
        items = [("tensor", kind, value) for kind, value in tensor_items]
        items += [("dp", "paired", shard_of(*key)) for key in fetched]
        items += [("dp", "swap", value) for value in sums]
        results = list(exchange(*items))
        for position, key in enumerate(fetched):
            piece = results[len(tensor_items) + position]
            weights[key] = piece.reshape(dp_size * piece.shape[1], piece.shape[2])
        gathered = [
            piece.reshape(group_rows, width) if kind == "gather" else piece.astype(jnp.float32).sum(0)
            for (kind, _), piece in zip(tensor_items, results)
        ]
        totals = [
            piece.astype(jnp.float32).sum(0) for piece in results[len(items) - len(sums) :]
        ]
        return gathered, totals

    def to_owners(partial):
        return ("swap", partial.astype(half).reshape(tensor_size, own_rows, width))

    def by_owner(gradient):
        return gradient.astype(half).reshape(dp_size, -1, gradient.shape[-1])

    small_shapes = [b_qv.shape, b_ffn.shape, norm_gains.shape, vec_biases.shape]
    small = pack([b_qv, b_ffn, norm_gains, vec_biases], 128, 16)
    first = exchange(
        ("tensor", "gather", d_out.astype(half)),
        ("dp", "paired", small),
        ("dp", "paired", shard_of("qkv", 0)),
    )
    last_grad_half = first[0].reshape(group_rows, width)
    weights["qkv", 0] = first[2].reshape(width, qkv_width)
    qv_all, ffn_all, gain_all, bias_all = [
        jnp.moveaxis(piece, 0, -2).reshape(piece.shape[1:-1] + (-1,)).astype(jnp.float32)
        for piece in unpack(first[1], small_shapes)
    ]

    caches = []
    hidden_in = x_in
    for layer_index in range(layer_count):
        last = layer_index == layer_count - 1
        following = layer_index + 1
        gain_rows = gain_all[layer_index]
        bias_rows = bias_all[layer_index]
        normed_own, unit_one, inv_one = layer_norm(hidden_in, gain_rows[0], bias_rows[0])
        fetched = [("out", 0), ("up", 0)] if layer_index == 0 else [("down", layer_index)]
        (normed_one,), _ = step([("gather", normed_own.astype(half))], fetched)
        projected = jnp.dot(
            normed_one, weights["qkv", layer_index], preferred_element_type=jnp.float32
        ).reshape(group_rows, 3, local_width)
        qv_bias = qv_all[layer_index]
        heads = (group_rows, local_heads, HEAD_DIM)
        queries = (projected[:, 0] + qv_bias[0]).astype(half).reshape(heads)
        key_vecs = projected[:, 1].astype(half).reshape(heads)
        val_vecs = (projected[:, 2] + qv_bias[1]).astype(half).reshape(heads)
        attended, log_total = attend(queries, key_vecs, val_vecs, segments, score_scale)
        fetched = [("down", 0)] if layer_index == 0 else []
        (summed,), _ = step(
            [to_owners(contract_last(attended, weights["out", layer_index]))], fetched
        )
        residual_mid = hidden_in + summed + bias_rows[2]
        normed_own_two, unit_two, inv_two = layer_norm(residual_mid, gain_rows[1], bias_rows[1])
        fetched = [] if last else [("qkv", following), ("out", following)]
        (normed_two,), _ = step([("gather", normed_own_two.astype(half))], fetched)
        pre_act = (
            jnp.dot(normed_two, weights["up", layer_index], preferred_element_type=jnp.float32)
            + ffn_all[layer_index]
        )
        gelu_value, gelu_slope = gelu_pair(pre_act)
        activated = gelu_value.astype(half)
        ffn_partial = to_owners(contract_last(activated, weights["down", layer_index]))
        if not last:
            (summed,), _ = step([ffn_partial], [("up", following)])
            hidden_in = residual_mid + summed + bias_rows[3]
        caches.append(
            (
                unit_one,
                inv_one,
                normed_one,
                queries,
                key_vecs,
                val_vecs,
                attended,
                log_total,
                unit_two,
                inv_two,
                normed_two,
                activated,
                gelu_slope,
            )
        )
    back = d_out
    grads = {}
    small_terms = [None] * layer_count
    output = None
    for layer_index in reversed(range(layer_count)):
        last = layer_index == layer_count - 1
        gain_rows = gain_all[layer_index]
        (
            unit_one,
            inv_one,
            normed_one,
            queries,
            key_vecs,
            val_vecs,
            attended,
            log_total,
            unit_two,
            inv_two,
            normed_two,
            activated,
            gelu_slope,
        ) = caches[layer_index]
        if last:
            grad_half = last_grad_half
        else:
            (grad_half,), (grads["qkv", layer_index + 1],) = step(
                [("gather", back.astype(half))], sums=[waiting]
            )
        grad_down = by_owner(contract_first(grad_half, activated))
        grad_pre = (
            jnp.dot(grad_half, weights["down", layer_index], preferred_element_type=jnp.float32)
            * gelu_slope
        )
        grad_pre_half = grad_pre.astype(half)
        grad_up = by_owner(contract_first(normed_two, grad_pre_half))
        partial = to_owners(contract_last(grad_pre_half, weights["up", layer_index]))
        if last:
            cut = grad_up.shape[2] // 2
            (grad_normed_two, summed), (grads["down", layer_index], up_left) = step(
                [partial, ffn_partial], sums=[grad_down, grad_up[:, :, :cut]]
            )
            output = residual_mid + summed + bias_all[layer_index][3]
        else:
            (grad_normed_two,), (grads["down", layer_index],) = step([partial], sums=[grad_down])
        grad_mid = back + norm_back(grad_normed_two, unit_two, inv_two, gain_rows[1])
        (grad_mid_half,), (up_part,) = step(
            [("gather", grad_mid.astype(half))], sums=[grad_up[:, :, cut:] if last else grad_up]
        )
        grads["up", layer_index] = (
            jnp.concatenate([up_left, up_part], axis=1) if last else up_part
        )
        grad_out = by_owner(contract_first(grad_mid_half, attended))
        grad_attended = jnp.dot(
            grad_mid_half, weights["out", layer_index], preferred_element_type=jnp.float32
        )
        grad_attended = grad_attended.astype(half).reshape(group_rows, local_heads, HEAD_DIM)
        query_grad, key_grad, val_grad = attend_back(
            queries, key_vecs, val_vecs, grad_attended, log_total, segments, score_scale
        )
        flat = (group_rows, local_width)
        grad_qkv = jnp.concatenate(
            [part.astype(half).reshape(flat) for part in (query_grad, key_grad, val_grad)], axis=1
        )
        grad_qkv_weight = by_owner(contract_first(normed_one, grad_qkv))
        (grad_normed_one,), sent_now = step(
            [to_owners(contract_last(grad_qkv, weights["qkv", layer_index]))],
            sums=[grad_out] if layer_index else [grad_out, grad_qkv_weight],
        )
        grads["out", layer_index] = sent_now[0]
        if layer_index:
            waiting = grad_qkv_weight
        else:
            grads["qkv", layer_index] = sent_now[1]
        small_terms[layer_index] = (
            jnp.stack(
                [
                    jnp.sum(query_grad, axis=0).reshape(local_width),
                    jnp.sum(val_grad, axis=0).reshape(local_width),
                ]
            ),
            jnp.sum(grad_pre, axis=0),
            jnp.stack(
                [
                    jnp.sum(grad_normed_one * unit_one, axis=0),
                    jnp.sum(grad_normed_two * unit_two, axis=0),
                ]
            ),
            jnp.stack(
                [
                    jnp.sum(grad_normed_one, axis=0),
                    jnp.sum(grad_normed_two, axis=0),
                    jnp.sum(grad_mid, axis=0),
                    jnp.sum(back, axis=0),
                ]
            ),
        )
        back = grad_mid + norm_back(grad_normed_one, unit_one, inv_one, gain_rows[0])

    def split_owner(piece):
        return jnp.moveaxis(
            piece.reshape(piece.shape[:-1] + (dp_size, -1)), -2, 0
        ).reshape(dp_size, -1)

    stacked = [
        split_owner(jnp.stack([small_terms[index][member] for index in range(layer_count)]))
        for member in (2, 3, 0, 1)
    ]
    flat = jnp.concatenate(stacked, axis=1)
    flat = jnp.pad(flat, ((0, 0), (0, -flat.shape[1] % 1024)))
    (parts,) = exchange(("dp", "swap", flat.reshape(dp_size, -1, 128)))
    total = parts.sum(0)
    (shared,) = exchange(("tensor", "gather", total))
    everyone = shared.sum(0).reshape(-1)
    gain_size, bias_size = norm_gains.size, vec_biases.size
    mine = total.reshape(-1)[gain_size + bias_size :]

    def stack_layers(name, shape, transposed):
        parts = [grads[name, index] for index in range(layer_count)]
        return jnp.stack([part.T if transposed else part for part in parts]).reshape(shape)

    return (
        output,
        back,
        stack_layers("qkv", w_qkv.shape, False),
        mine[: b_qv.size].reshape(b_qv.shape),
        stack_layers("out", w_o.shape, True),
        stack_layers("up", w_1.shape, False),
        mine[b_qv.size : b_qv.size + b_ffn.size].reshape(b_ffn.shape),
        stack_layers("down", w_2.shape, True),
        everyone[:gain_size].reshape(norm_gains.shape),
        everyone[gain_size : gain_size + bias_size].reshape(vec_biases.shape),
    )


def dot_nn(left, right):
    return jnp.dot(left, right, preferred_element_type=jnp.float32)


class GatherHere(Gather):
    def __init__(self, place, wires, dst):
        super().__init__(place, wires, dst.at[place.rank], dst, [])

    def start(self):
        made = self._copies()
        for index in (1, 2, 0):
            made[index]().start()

    def wait_sibling(self):
        self._copies()[0]().wait_recv()

    def finish(self):
        made = self._copies()
        for index in (3, 4):
            made[index]().wait_recv()
        for copy in made:
            copy().wait_send()


class ReduceHere(Reduce):
    def __init__(self, place, wires, src, dst, spare):
        super().__init__(place, wires, src, dst, spare)

    def _copies(self):
        p, w, src, dst, at = self.p, self.w, self.src, self.dst, self.at
        other = 1 - p.core
        sib = p.sibling()
        return [
            lambda: w.copy(src.at[p.rank_at(other, p.low)], dst.at[0], sib, at, at),
            lambda: w.copy(src.at[p.rank_at(other, 1 - p.low)], self.held, sib, at + 1, at + 1),
            lambda: w.copy(self.mixed, dst.at[1], p.cross(p.core), at + 2, at + 2),
        ]

    def start_cross(self):
        self._copies()[1]().start()

    def start_near(self):
        self._copies()[0]().start()

    def finish(self):
        made = self._copies()
        made[0]().wait_recv()
        made[2]().wait_recv()
        for copy in made:
            copy().wait_send()

    def total(self, rows):
        first = self.src[self.p.rank, rows].astype(jnp.float32)
        return first + self.dst[0, rows].astype(jnp.float32) + self.dst[1, rows].astype(jnp.float32)


class Env:
    pass


class Mover:
    def __init__(self, wires):
        self.wires = wires
        self.open = {}

    def start(self, src, dst, name):
        slot = self.wires.take_own()
        self.open[name] = (src, dst, slot)
        self.wires.local(src, dst, slot).start()

    def wait(self, *names):
        for name in names or list(self.open):
            self.wires.local(*self.open.pop(name)).wait()


def make_fused():
    calls = [32]

    def fused(body, ins, outs, scratch, kinds, hbm=()):
        names_in, names_out, names_spare = list(ins), list(outs), list(scratch)

        def kernel(*refs):
            k = Env()
            refs = list(refs)
            for name in names_in + names_out:
                setattr(k, name, refs.pop(0))
            k.wires = Wires(*refs[:3])
            for name, ref in zip(names_spare, refs[3:]):
                setattr(k, name, ref)
            k.place = Place()
            greet(k.place, kinds)
            body(k)
            assert k.wires.used <= 320 and k.wires.own_used <= 192

        collective_id = calls[0]
        calls[0] += 1
        results = pl.pallas_call(
            kernel,
            out_shape=tuple(jax.ShapeDtypeStruct(*outs[name]) for name in names_out),
            in_specs=[
                pl.BlockSpec(memory_space=pltpu.HBM if name in hbm else pltpu.VMEM)
                for name in names_in
            ],
            out_specs=tuple(
                pl.BlockSpec(memory_space=pltpu.HBM if name in hbm else pltpu.VMEM)
                for name in names_out
            ),
            scratch_shapes=[
                pltpu.SemaphoreType.DMA((320,)),
                pltpu.SemaphoreType.DMA((320,)),
                pltpu.SemaphoreType.DMA((192,)),
                *[pltpu.VMEM(*scratch[name]) for name in names_spare],
            ],
            compiler_params=pltpu.CompilerParams(
                collective_id=collective_id,
                has_side_effects=True,
                vmem_limit_bytes=60 * 1024 * 1024,
            ),
            cost_estimate=pl.CostEstimate(
                flops=0, bytes_accessed=16 * 1024 * 1024, transcendentals=0
            ),
            name=f"fused_{collective_id}",
        )(*[ins[name] for name in names_in])
        made = Env()
        made.__dict__.update(zip(names_out, results))
        return made

    return fused


def chips(place):
    other = 1 - place.core
    return (
        (place.rank, place.rank_at(other, place.low)),
        (place.rank_at(place.core, 1 - place.low), place.rank_at(other, 1 - place.low)),
    )


def two(ref, ranks, lanes=slice(None)):
    parts = [ref[rank, ..., lanes] for rank in ranks]
    return jnp.concatenate([part.reshape(-1, part.shape[-1]) for part in parts], axis=0)


def whole(ref, lanes=slice(None)):
    part = ref[..., lanes]
    return part.reshape(-1, part.shape[-1])


def put_two(ref, ranks, value, lanes=slice(None)):
    rows = value.shape[0] // 2
    ref[ranks[0], :, lanes] = value[:rows].astype(ref.dtype)
    ref[ranks[1], :, lanes] = value[rows:].astype(ref.dtype)


def lanes_at(index, size=256):
    return pl.ds(pl.multiple_of(index * size, size), size)


def loop(count, body):
    def step(index, carry):
        body(index)
        return carry

    lax.fori_loop(0, count, step, 0)


def columns_of(ref, block):
    return jnp.concatenate([ref[block, 0], ref[block, 1]], axis=1)


def all_columns(ref, rows):
    return jnp.concatenate([ref[block, core, rows] for block in range(4) for core in range(2)], axis=1)


ROWS = 32


def visible(k, block):
    shape = (128, (block + 1) * 128)
    end = k.lengths[0:1, 0:1].astype(jnp.int32)
    at_query = lax.broadcasted_iota(jnp.int32, shape, 0) + block * 128
    at_key = lax.broadcasted_iota(jnp.int32, shape, 1)
    late_query = jnp.where(at_query >= end, 1, 0)
    late_key = jnp.where(at_key >= end, 1, 0)
    return (late_query == late_key) & (at_key <= at_query)


def attention_forward(k, on_sent, on_gathered, on_middle, on_attended):
    p = k.place
    here, there = chips(p)
    for at in range(4):
        rows = pl.ds(at * ROWS, ROWS)
        normed, _, _ = layer_norm(k.hidden[rows], k.vecs[0:1], k.vecs[2:3])
        k.n1[p.rank, at // 2, pl.ds(at % 2 * ROWS, ROWS)] = normed.astype(jnp.bfloat16)
    gather = GatherHere(p, k.wires, k.n1)
    gather.start()
    on_sent()

    def project(ranks):
        rows = two(k.n1, ranks)
        for index, (dst, bias) in enumerate(((k.q, 0), (k.key, None), (k.val, 1))):
            weight = k.w_qkv[:, :, index * 128 : index * 128 + 128].reshape(1024, 256)
            made = dot_nn(rows, weight)
            if bias is not None:
                made = made + k.qv_bias[bias : bias + 1]
            put_two(dst, ranks, made)

    gather.wait_sibling()
    gather.relay()
    on_gathered()
    project(here)
    gather.finish()
    project(there)
    scale = 1.0 / math.sqrt(HEAD_DIM)
    for block in range(4):
        if block == 3:
            on_middle()
        seen = visible(k, block)
        count = (block + 1) * 128
        for head in range(4):
            lanes = slice(head * HEAD_DIM, head * HEAD_DIM + HEAD_DIM)
            keys = k.key[: block + 1, :, lanes].reshape(count, HEAD_DIM)
            vals = k.val[: block + 1, :, lanes].reshape(count, HEAD_DIM)
            scores = contract_last(k.q[block, :, lanes], keys) * scale
            scores = jnp.where(seen, scores, -jnp.inf)
            raised = jnp.exp(scores - jnp.max(scores, axis=-1, keepdims=True))
            probs = raised * (1.0 / jnp.sum(raised, axis=-1, keepdims=True))
            probs = probs.astype(jnp.bfloat16)
            k.probs[head, pl.ds(block * 128, 128), :count] = probs
            k.att[block, :, lanes] = dot_nn(probs, vals).astype(jnp.bfloat16)
    on_attended()

    def out(ranks):
        rows = two(k.att, ranks)

        def column(block):
            put_two(k.part_a, ranks, dot_nn(rows, columns_of(k.w_out, block)), lanes_at(block))

        loop(4, column)

    reduce = ReduceHere(p, k.wires, k.part_a, k.got_a, (k.held_a, k.mixed_a))
    out(there)
    reduce.start_cross()
    out(here)
    reduce.start_near()
    reduce.relay()
    return reduce


def feed_forward(k, reduce, on_sent, on_gathered, on_raised, part):
    p = k.place
    here, there = chips(p)
    reduce.finish()
    for at in range(4):
        rows = pl.ds(at * ROWS, ROWS)
        mid = k.hidden[rows] + reduce.total(rows) + k.vecs[4:5]
        k.mid[rows] = mid
        normed, _, _ = layer_norm(mid, k.vecs[1:2], k.vecs[3:4])
        k.n2[p.rank, at // 2, pl.ds(at % 2 * ROWS, ROWS)] = normed.astype(jnp.bfloat16)
    gather = GatherHere(p, k.wires, k.n2)
    gather.start()
    on_sent()

    def up(ranks):
        def column(index):
            lanes = lanes_at(index)
            rows = two(k.n2, ranks)
            weight = k.w_up[:, :, :, lanes].reshape(1024, 256)
            pre_act = dot_nn(rows, weight) + k.ffn_bias[0:1, lanes]
            value, slope = gelu_pair(pre_act)
            put_two(k.act, ranks, value, lanes)
            put_two(k.slope, ranks, slope, lanes)

        loop(4, column)

    gather.wait_sibling()
    gather.relay()
    on_gathered()
    up(here)
    gather.finish()
    up(there)
    on_raised()

    def down(ranks):
        def column(block):
            rows = two(k.act, ranks)
            put_two(part, ranks, dot_nn(rows, columns_of(k.w_down, block)), lanes_at(block))

        loop(4, column)

    return down, here, there


def unpack_small(small_all, views):
    parts = [small_all[block, core].astype(jnp.float32) for block in range(4) for core in range(2)]

    def row(index):
        return jnp.concatenate([part[index : index + 1] for part in parts], axis=1)

    for layer, k in enumerate(views):
        for index in range(2):
            k.vecs[index : index + 1] = row(3 + 2 * layer + index)
            at = 64 * layer + 32 * index
            k.qv_bias[index : index + 1] = jnp.concatenate(
                [part[0:1, at : at + 32] for part in parts], axis=1
            )
        for index in range(4):
            k.vecs[2 + index : 3 + index] = row(7 + 4 * layer + index)
        k.ffn_bias[0:1] = row(1 + layer)


def pack_small(flat, layers):
    flat[...] = jnp.zeros(flat.shape, flat.dtype)
    for shard in range(8):
        block, core = shard // 2, shard % 2
        lanes = slice(shard * 128, shard * 128 + 128)
        quarter = slice(shard * 32, shard * 32 + 32)
        pieces = []
        for layer, (col, col_qv, col_ffn) in enumerate(layers):
            flat[block, core, 2 * layer : 2 * layer + 2] = col[0:2, lanes]
            flat[block, core, 4 + 4 * layer : 8 + 4 * layer] = col[2:6, lanes]
            flat[block, core, 13 + layer : 14 + layer] = col_ffn[0:1, lanes]
            pieces += [col_qv[0:1, quarter], col_qv[1:2, quarter]]
        flat[block, core, 12:13] = jnp.concatenate(pieces, axis=1)


def feed_forward_back(k, gather, on_gathered, on_grad_down):
    p = k.place
    here, there = chips(p)

    def pre(ranks, first):
        def rows_of(index):
            lanes = lanes_at(index)
            weight = all_columns(k.w_down, lanes)
            grad = contract_last(two(k.gh, ranks), weight) * two(k.slope, ranks, lanes).astype(
                jnp.float32
            )
            put_two(k.gp, ranks, grad, lanes)
            summed = jnp.sum(grad, axis=0, keepdims=True)
            k.col_ffn[0:1, lanes] = summed if first else k.col_ffn[0:1, lanes] + summed

        loop(4, rows_of)

    if gather is not None:
        gather.wait_sibling()
        gather.relay()
    on_gathered()
    pre(here, True)
    if gather is not None:
        gather.finish()

    def turn(index):
        lanes = lanes_at(index)
        k.turned[lanes] = whole(k.act, lanes).T

    loop(4, turn)

    def grad_down(block):
        made = dot_nn(k.turned[...], whole(k.gh, lanes_at(block)))
        k.g_down[block, 0] = made[:, :128].astype(jnp.bfloat16)
        k.g_down[block, 1] = made[:, 128:].astype(jnp.bfloat16)

    loop(4, grad_down)
    on_grad_down()
    pre(there, False)

    def term(ranks):
        def column(block):
            rows = two(k.gp, ranks)
            weight = k.w_up[block].reshape(256, 1024)
            put_two(k.part_a, ranks, contract_last(rows, weight), lanes_at(block))

        loop(4, column)

    reduce = ReduceHere(p, k.wires, k.part_a, k.got_a, (k.held_a, k.mixed_a))
    term(there)
    reduce.start_cross()
    term(here)
    reduce.start_near()
    reduce.relay()
    return reduce


def grad_up(k):
    def rows_of(block):
        turned = whole(k.n2, lanes_at(block)).T
        made = dot_nn(turned, whole(k.gp))
        k.g_up[block] = made.astype(jnp.bfloat16).reshape(2, 128, 1024)

    loop(4, rows_of)


def through_norm(k, reduce, hidden, back, sums, gain, dst, put):
    totals = None
    for at in range(4):
        rows = pl.ds(at * ROWS, ROWS)
        grad = reduce.total(rows)
        _, unit, inv = layer_norm(hidden[rows], 1.0, 0.0)
        was = back[rows]
        now = was + norm_back(grad, unit, inv, k.vecs[gain : gain + 1])
        dst[rows] = now
        put(at, now)
        terms = [grad * unit, grad, now, was]
        terms = [jnp.sum(term, axis=0, keepdims=True) for term in terms]
        totals = terms if totals is None else [a + b for a, b in zip(totals, terms)]
    for row, total in zip(sums, totals):
        if row is not None:
            k.col[row : row + 1] = total


def grad_qkv_thirds(k, third):
    def turn(index):
        lanes = lanes_at(index)
        k.turned[lanes] = whole(k.n1, lanes).T

    loop(4, turn)
    for index in range(3):
        rows = pl.ds(index * 128, 128)

        def grad_qkv(block):
            made = dot_nn(k.turned[lanes_at(block)], whole(k.gq.at[index]))
            k.g_qkv[block, :, rows] = made.astype(jnp.bfloat16).reshape(2, 128, 256)

        loop(4, grad_qkv)
        third(index)

def attention_back(k, reduce, background, third, weights_first):
    p = k.place
    here, there = chips(p)
    reduce.finish()

    def put(at, now):
        k.gm[p.rank, at // 2, pl.ds(at % 2 * ROWS, ROWS)] = now.astype(jnp.bfloat16)

    through_norm(k, reduce, k.mid, k.back, (1, 3, 4, 5), 1, k.grad_mid, put)
    gather = GatherHere(p, k.wires, k.gm)
    gather.start()
    grad_up(k)
    background(AT_UP)

    def attended(ranks):
        weight = all_columns(k.w_out, slice(None))
        put_two(k.ga, ranks, contract_last(two(k.gm, ranks), weight))

    gather.wait_sibling()
    gather.relay()
    attended(here)
    gather.finish()
    attended(there)

    def grad_out(block):
        made = dot_nn(whole(k.att).T, whole(k.gm, lanes_at(block)))
        k.g_out[block, 0] = made[:, :128].astype(jnp.bfloat16)
        k.g_out[block, 1] = made[:, 128:].astype(jnp.bfloat16)

    loop(4, grad_out)
    background(AT_OUT)
    scale = 1.0 / math.sqrt(HEAD_DIM)
    for head in range(4):
        lanes = slice(head * HEAD_DIM, head * HEAD_DIM + HEAD_DIM)
        for block in range(4):
            rows = pl.ds(block * 128, 128)
            count = (block + 1) * 128
            keys = k.key[: block + 1, :, lanes].reshape(count, HEAD_DIM)
            vals = k.val[: block + 1, :, lanes].reshape(count, HEAD_DIM)
            probs = k.probs[head, rows, :count].astype(jnp.float32)
            grad_probs = contract_last(k.ga[block, :, lanes], vals)
            row_dot = jnp.sum(grad_probs * probs, axis=-1, keepdims=True)
            score_grad = (probs * (grad_probs - row_dot) * scale).astype(jnp.bfloat16)
            k.ds[head % 2, rows, :count] = score_grad
            query_grad = dot_nn(score_grad, keys)
            k.gq[0, block, :, lanes] = query_grad.astype(jnp.bfloat16)
            summed = jnp.sum(query_grad, axis=0, keepdims=True)
            k.col_qv[0:1, lanes] = summed if block == 0 else k.col_qv[0:1, lanes] + summed
        if head == 1:
            background(AT_HEADS)
        for block in range(4):
            below = pl.ds(block * 128, 512 - block * 128)
            cols = slice(block * 128, block * 128 + 128)
            count = 512 - block * 128
            queries = k.q[block:, :, lanes].reshape(count, HEAD_DIM)
            grads = k.ga[block:, :, lanes].reshape(count, HEAD_DIM)
            key_grad = contract_first(k.ds[head % 2, below, cols], queries)
            val_grad = contract_first(k.probs[head, below, cols], grads)
            k.gq[1, block, :, lanes] = key_grad.astype(jnp.bfloat16)
            k.gq[2, block, :, lanes] = val_grad.astype(jnp.bfloat16)
            summed = jnp.sum(val_grad, axis=0, keepdims=True)
            k.col_qv[1:2, lanes] = summed if block == 0 else k.col_qv[1:2, lanes] + summed
    background(AT_ATTENDED)

    if weights_first:
        grad_qkv_thirds(k, third)

    def term(ranks):
        rows = [two(k.gq.at[index], ranks) for index in range(3)]

        def column(block):
            made = None
            for index in range(3):
                weight = k.w_qkv[block, :, index * 128 : index * 128 + 128].reshape(256, 256)
                one = contract_last(rows[index], weight)
                made = one if made is None else made + one
            put_two(k.part_b, ranks, made, lanes_at(block))

        loop(4, column)

    reduce = ReduceHere(p, k.wires, k.part_b, k.got_b, (k.held_b, k.mixed_b))
    term(there)
    reduce.start_cross()
    term(here)
    reduce.start_near()
    reduce.relay()

    if not weights_first:
        grad_qkv_thirds(k, third)
    background(AT_QKV)
    reduce.finish()
    through_norm(
        k, reduce, k.hidden, k.grad_mid, (0, 2, None, None), 0, k.back_out, lambda at, now: None
    )


def total_scratch(name, rows, cols, half=jnp.bfloat16):
    one, two = ((rows, cols), half), ((2, rows, cols), half)
    return {f"{name}_t{index}": value for index, value in enumerate((two, two, two, one, one))}


def paired_shards(
    x_in, d_out, seq_lengths, w_qkv, b_qv, w_o, w_1, b_ffn, w_2, norm_gains, vec_biases
):
    fused = make_fused()
    own_rows, width = x_in.shape
    layer_count = w_qkv.shape[0]
    half, full = jnp.bfloat16, jnp.float32
    z = lax.axis_index("tensor")
    native = lax.axis_index("dp") % 2 == z // 2
    qkv_turned = jnp.transpose(w_qkv, (0, 2, 1, 3)).reshape(layer_count, 384, 256)
    shapes = {QKV: (384, 256), OUT: (256, 128), UP: (128, 1024), DOWN: (1024, 128)}
    def pair_spec(name):
        return ((2,) + shapes[name], half)

    def full_spec(name):
        return ((4, 2) + shapes[name], half)

    def added(parts):
        return parts[0].astype(full) + parts[1].astype(full)

    small_shapes = [b_qv.shape, b_ffn.shape, norm_gains.shape, vec_biases.shape]
    small = pack([b_qv, b_ffn, norm_gains, vec_biases], 128, 16)
    lengths = jnp.pad(seq_lengths.astype(full), ((0, 7), (0, 126)))

    rows_spec = ((4, 2, own_rows // 2, width), half)
    heads_spec = ((4, own_rows, 256), half)
    wide_spec = ((4, own_rows, width), half)
    own_half = ((own_rows, width), half)
    own_full = ((own_rows, width), full)
    two_half = ((2, own_rows, width), half)
    reduce_a = dict(part_a=wide_spec, got_a=two_half, held_a=own_half, mixed_a=own_half)
    reduce_b = dict(part_b=wide_spec, got_b=two_half, held_b=own_half, mixed_b=own_half)
    saved_specs = dict(
        hidden=own_full,
        vecs=((8, width), full),
        n1=rows_spec,
        q=heads_spec,
        key=heads_spec,
        val=heads_spec,
        probs=((4, 512, 512), half),
        att=heads_spec,
        mid=own_full,
        n2=rows_spec,
        act=wide_spec,
        slope=wide_spec,
        w_qkv=full_spec(QKV),
        w_out=full_spec(OUT),
        w_up=full_spec(UP),
        w_down=full_spec(DOWN),
    )
    own_specs = dict(
        reduce_a,
        qv_bias=((8, 256), full),
        ffn_bias=((8, width), full),
        pair_qkv=pair_spec(QKV),
        pair_out=pair_spec(OUT),
        pair_up=pair_spec(UP),
        pair_down=pair_spec(DOWN),
    )

    group_a, group_b, group_c = ("w_down", "slope"), ("w_up", "act", "n2"), ("mid", "att", "w_out")
    group_d, group_e = ("probs", "key", "val", "q", "w_qkv", "n1"), ("hidden",)

    def of_layers(specs):
        return {f"{name}_{layer}": spec for name, spec in specs.items() for layer in range(2)}

    def view(k, layer):
        made = Env()
        for name, ref in k.__dict__.items():
            if name.endswith(f"_{layer}"):
                setattr(made, name[:-2], ref)
        made.place, made.wires = k.place, k.wires
        return made

    def forward(k):
        p, w = k.place, k.wires
        k0, k1 = view(k, 0), view(k, 1)
        small_job = Fetch(p, w, k.small, k.small_all, [k.small_pair])
        length_job = Swap(p, w, k.lengths_in, k.lengths, [])
        swap_x = Swap(p, w, k.x_half, k.x_got, [])
        swap_d = Swap(p, w, k.d_half, k.d_got, [])
        k0.lengths = k1.lengths = k.lengths

        def fetch_qkv(layer, v):
            jobs = []
            for index in range(3):
                rows = pl.ds(index * 128, 128)
                dst, pair = v.w_qkv.at[:, :, rows], v.pair_qkv.at[:, rows]
                jobs.append(Fetch(p, w, k.s_qkv.at[layer, rows], dst, [pair]))
            return jobs

        def fetch_rest(layer, v):
            return (
                Fetch(p, w, k.s_out.at[layer], v.w_out, [v.pair_out]),
                Fetch(p, w, k.s_up.at[layer], v.w_up, [v.pair_up]),
                Fetch(p, w, k.s_down.at[layer], v.w_down, [v.pair_down]),
            )

        qkv_0, qkv_1 = fetch_qkv(0, k0), fetch_qkv(1, k1)
        out_0, up_0, down_0 = fetch_rest(0, k0)
        out_1, up_1, down_1 = fetch_rest(1, k1)
        for at in range(4):
            rows = pl.ds(at * ROWS, ROWS)
            k.x_half[rows] = k.x_in[rows].astype(half)
        mover = Mover(w)

        small_job.start()
        length_job.start()
        swap_x.start()
        small_job.relay()
        small_job.relay_more()
        for job in qkv_0:
            job.start()

        @pl.when(p.native)
        def _():
            for job in qkv_0:
                job.relay()

        small_job.finish()
        unpack_small(k.small_all, (k0, k1))
        length_job.finish()
        swap_x.finish()
        for at in range(4):
            rows = pl.ds(at * ROWS, ROWS)
            k0.hidden[rows] = jnp.where(p.native, k.x_in[rows], k.x_got[rows].astype(full))
            k.d_half[rows] = k.d_in[rows].astype(half)

        def first_sent():
            @pl.when(jnp.logical_not(p.native))
            def _():
                for job in qkv_0:
                    job.relay()

            out_0.start()
            up_0.start()

        def first_gathered():
            for job in qkv_0:
                job.relay_more()
            out_0.relay()
            for job in qkv_0:
                job.finish()

        def first_middle():
            out_0.relay_more()
            up_0.relay()
            down_0.start()

        reduce = attention_forward(k0, first_sent, first_gathered, first_middle, out_0.finish)
        up_0.relay_more()

        def first_sent_two():
            down_0.relay()
            for job in qkv_1:
                job.start()
            out_1.start()

        def first_raised():
            down_0.relay_more()
            for job in qkv_1:
                job.relay()
            out_1.relay()
            up_1.start()
            down_0.finish()

        column, here, there = feed_forward(
            k0, reduce, first_sent_two, up_0.finish, first_raised, k.part_b
        )
        second = ReduceHere(p, w, k.part_b, k.got_b, (k.held_b, k.mixed_b))
        column(there)
        second.start_cross()
        column(here)
        second.start_near()
        second.relay()
        for job in qkv_1:
            job.relay_more()
        out_1.relay_more()
        for name in group_a + group_b + group_c + group_d + group_e:
            mover.start(getattr(k0, name), getattr(k, f"h_{name}"), name)
        second.finish()
        for at in range(4):
            rows = pl.ds(at * ROWS, ROWS)
            k1.hidden[rows] = k0.mid[rows] + second.total(rows) + k0.vecs[5:6]
        grads = GatherHere(p, w, k.gh)

        def last_sent():
            up_1.relay()
            down_1.start()
            swap_d.start()

        def last_gathered():
            for job in qkv_1:
                job.finish()
            out_1.finish()

        def last_attended():
            down_1.relay()
            swap_d.finish()
            for at in range(4):
                rows = pl.ds(at * ROWS, ROWS)
                k.back[rows] = jnp.where(p.native, k.d_in[rows], k.d_got[rows].astype(full))
                k.gh[p.rank, at // 2, pl.ds(at % 2 * ROWS, ROWS)] = k.back[rows].astype(half)

        reduce = attention_forward(k1, last_sent, last_gathered, up_1.relay_more, last_attended)

        def last_gathered_two():
            up_1.finish()
            down_1.relay_more()
            grads.start()

        def raised():
            grads.wait_sibling()
            grads.relay()
            down_1.finish()

        column, here, there = feed_forward(
            k1, reduce, lambda: None, last_gathered_two, raised, k.ffn_part
        )
        column(there)
        column(here)
        grads.finish()
        mover.wait()

    totals = dict(shapes)
    spare = dict(
        of_layers(own_specs),
        **of_layers(saved_specs),
        **reduce_b,
        back=own_full,
        gh=rows_spec,
        ffn_part=wide_spec,
        lengths=((8, 128), full),
        small_pair=((2, 16, 128), half),
        small_all=((4, 2, 16, 128), half),
        x_half=own_half,
        x_got=own_half,
        d_half=own_half,
        d_got=own_half,
        turned=((1024, 512), half),
        ds=((2, 512, 512), half),
        gq=((3, 4, own_rows, 256), half),
        out_half=own_half,
        back_half=own_half,
        flat=((4, 2, 16, 128), full),
        small_sums=((2, 16, 128), full),
        g_last=full_spec(QKV),
        **total_scratch("small", 16, 128, full),
        **total_scratch("last", *shapes[QKV]),
    )
    for name, shape in shapes.items():
        spare.update(total_scratch(name, *shape))
    spare.update(
        of_layers(dict(col=((8, width), full), col_qv=((8, 256), full), col_ffn=((8, width), full)))
    )

    def backward(k):
        p, w = k.place, k.wires
        mover = Mover(w)
        first, last = view(k, 0), view(k, 1)
        for name in saved_specs:
            setattr(k, name, getattr(last, name))
        for name in shapes:
            setattr(k, f"g_{name}", getattr(first, f"w_{name}"))
        k.gm, k.gp, k.ga, k.grad_mid = first.n1, first.act, first.att, first.mid
        k.part_a, k.got_a, k.held_a, k.mixed_a = first.part_a, first.got_a, first.held_a, first.mixed_a
        k0, k1 = Env(), Env()
        for v, layer in ((k0, first), (k1, last)):
            v.__dict__.update(k.__dict__)
            v.vecs, v.col, v.col_qv, v.col_ffn = layer.vecs, layer.col, layer.col_qv, layer.col_ffn
        k1.back_out = k0.back = first.hidden
        k1.g_qkv = k.g_last

        def load(names):
            for name in names:
                mover.start(getattr(k, f"h_{name}"), getattr(k, name), name)

        def job_total(name, layer):
            spare = [getattr(k, f"{name}_t{at}") for at in range(5)]
            return Total(p, w, getattr(k, f"g_{name}"), getattr(k, f"pair_{name}_{layer}"), spare)

        def job_deliver(name, layer):
            src, dst = getattr(k, f"pair_{name}_{layer}"), getattr(k, f"done_{name}_{layer}")
            return Deliver(p, w, src, dst, [])

        def thirds(layer, v, name):
            made = []
            for index in range(3):
                rows = pl.ds(index * 128, 128)
                spare = [getattr(k, f"{name}_t{at}") for at in range(5)]
                spare = [ref.at[:, rows] for ref in spare[:3]] + [ref.at[rows] for ref in spare[3:]]
                dst = getattr(k, f"pair_{QKV}_{layer}").at[:, rows]
                done = getattr(k, f"done_{QKV}_{layer}").at[:, rows]
                made.append(
                    (
                        Total(p, w, v.g_qkv.at[:, :, rows], dst, spare),
                        Deliver(p, w, dst, done, []),
                    )
                )
            return made

        ffn = ReduceHere(p, w, k.ffn_part, last.got_a, (last.held_a, last.mixed_a))
        swap = Swap(p, w, k.out_half, k.out_sent, [])
        swap_back = Swap(p, w, k.back_half, k.back_sent, [])
        qkv_1, qkv_0 = thirds(1, k1, "last"), thirds(0, k0, QKV)
        down_1, up_1, out_1 = [job_total(name, 1) for name in (DOWN, UP, OUT)]
        down_0, up_0, out_0 = [job_total(name, 0) for name in (DOWN, UP, OUT)]
        to_down_1, to_up_1, to_out_1 = [job_deliver(name, 1) for name in (DOWN, UP, OUT)]
        to_down_0, to_up_0, to_out_0 = [job_deliver(name, 0) for name in (DOWN, UP, OUT)]
        small_job = Small(
            p, w, k.flat, k.small_parts, [getattr(k, f"small_t{at}") for at in range(5)] + [k.small_sums]
        )
        reduce = feed_forward_back(k1, None, lambda: None, down_1.start)
        ffn.start_cross()
        ffn.start_near()
        ffn.relay()

        def last_background(point):
            if point == AT_UP:
                load(group_a + group_b)
                down_1.relay_more()
                up_1.start()
            if point == AT_OUT:
                ffn.finish()
                for at in range(4):
                    rows = pl.ds(at * ROWS, ROWS)
                    made = k.mid[rows] + ffn.total(rows) + k1.vecs[5:6]
                    k.output[rows] = made
                    k.out_half[rows] = made.astype(half)
                out_1.start()
                load(group_c)
                down_1.finish()
            if point == AT_HEADS:
                up_1.relay_more()
                out_1.relay_more()
                to_down_1.start()
            if point == AT_QKV:
                load(group_d)
                up_1.finish()
                out_1.finish()

        attention_back(k1, reduce, last_background, lambda index: qkv_1[index][0].start(), False)
        load(group_e)
        for at in range(4):
            rows = pl.ds(at * ROWS, ROWS)
            k.gh[p.rank, at // 2, pl.ds(at % 2 * ROWS, ROWS)] = k0.back[rows].astype(half)
        gather = GatherHere(p, w, k.gh)
        gather.start()
        mover.wait(*group_a, *group_b)

        def first_started():
            for job, _ in qkv_1:
                job.relay_more()
            to_up_1.start()
            to_out_1.start()

        def first_grad_down():
            for job, _ in qkv_1:
                job.finish()
            down_0.start()

        reduce = feed_forward_back(k0, gather, first_started, first_grad_down)
        mover.wait(*group_c, *group_d, *group_e)

        def first_background(point):
            if point == AT_UP:
                down_0.relay_more()
                up_0.start()
            if point == AT_OUT:
                for _, job in qkv_1:
                    job.start()
                out_0.start()
                down_0.finish()
                swap.start()
            if point == AT_HEADS:
                up_0.relay_more()
                out_0.relay_more()
                to_down_0.start()
            if point == AT_ATTENDED:
                up_0.finish()
                to_up_0.start()
                out_0.finish()
                to_out_0.start()

        attention_back(k0, reduce, first_background, lambda index: qkv_0[index][0].start(), True)
        pack_small(k.flat, [(v.col, v.col_qv, v.col_ffn) for v in (k0, k1)])
        small_job.start()
        for at in range(4):
            rows = pl.ds(at * ROWS, ROWS)
            k.back_half[rows] = k.back_out[rows].astype(half)
        swap_back.start()
        qkv_0[0][0].relay_more()
        qkv_0[1][0].relay_more()
        qkv_0[0][0].finish()
        qkv_0[0][1].start()
        qkv_0[2][0].relay_more()
        small_job.relay_more()
        for job, then in qkv_0[1:]:
            job.finish()
            then.start()
        small_job.finish()
        for job in (to_down_1, to_up_1, to_out_1, to_down_0, to_up_0, to_out_0, swap, swap_back):
            job.finish()
        for _, job in qkv_1 + qkv_0:
            job.finish()
        mover.wait()

    done_specs = {
        f"done_{name}_{layer}": pair_spec(name) for name in totals for layer in range(2)
    }
    def both(k):
        forward(k)
        backward(k)

    spilled = {f"h_{name}": spec for name, spec in saved_specs.items()}
    last = fused(
        both,
        dict(
            x_in=x_in,
            d_in=d_out,
            lengths_in=lengths,
            small=small,
            s_qkv=qkv_turned,
            s_out=w_o,
            s_up=w_1,
            s_down=w_2,
        ),
        dict(
            done_specs,
            **spilled,
            output=own_full,
            back_out=own_full,
            out_sent=own_half,
            back_sent=own_half,
            small_parts=((8, 16, 128), full),
        ),
        spare,
        (SIBLING, CROSS, FAR, BESIDE, ABOVE, LINE),
        hbm=[f"s_{name}" for name in shapes] + list(spilled) + list(done_specs),
    )
    output, back = last.output, last.back_out
    small_parts = last.small_parts
    small_parts = small_parts.reshape(8, -1)
    gain_size, bias_size = norm_gains.size, vec_biases.size
    everyone = small_parts.sum(0)
    sources = jnp.arange(8, dtype=jnp.int32)
    pair = z // 2
    mine_from = (sources == 2 * z + pair) | (sources == 2 * (z + 2 - 4 * pair) + pair)
    mine = jnp.where(mine_from[:, None], small_parts, 0.0).sum(0)[gain_size + bias_size :]

    def stacked_layers(name):
        return jnp.stack([added(getattr(last, f"done_{name}_{layer}")) for layer in range(2)])

    grad_qkv = stacked_layers(QKV)
    grad_qkv = jnp.transpose(grad_qkv.reshape(layer_count, 3, 128, 256), (0, 2, 1, 3))
    return (
        jnp.where(native, output, last.out_sent.astype(full)),
        jnp.where(native, back, last.back_sent.astype(full)),
        grad_qkv,
        mine[: b_qv.size].reshape(b_qv.shape),
        stacked_layers(OUT),
        stacked_layers(UP),
        mine[b_qv.size : b_qv.size + b_ffn.size].reshape(b_ffn.shape),
        stacked_layers(DOWN),
        everyone[:gain_size].reshape(norm_gains.shape),
        everyone[gain_size : gain_size + bias_size].reshape(vec_biases.shape),
    )


def solution(mesh):
    in_specs = (
        P(("dp", "tensor"), None),
        P(("dp", "tensor"), None),
        P("dp", None),
        P(None, "dp", None, "tensor"),
        P(None, None, ("tensor", "dp")),
        P(None, "tensor", "dp"),
        P(None, "dp", "tensor"),
        P(None, ("tensor", "dp")),
        P(None, "tensor", "dp"),
        P(None, None, "dp"),
        P(None, None, "dp"),
    )
    out_specs = (
        P(("dp", "tensor"), None),
        P(("dp", "tensor"), None),
        P(None, "dp", None, "tensor"),
        P(None, None, ("tensor", "dp")),
        P(None, "tensor", "dp"),
        P(None, "dp", "tensor"),
        P(None, ("tensor", "dp")),
        P(None, "tensor", "dp"),
        P(None, None, "dp"),
        P(None, None, "dp"),
    )
    paired = mesh.shape["dp"] == 8 and mesh.shape["tensor"] == 4
    body = paired_shards if paired else shards
    return jax.shard_map(body, mesh=mesh, in_specs=in_specs, out_specs=out_specs, check_vma=False)
```

```python
import math

import jax
import jax.numpy as jnp
from jax import lax
from jax.experimental import pallas as pl
from jax.experimental.pallas import tpu as pltpu
from jax.sharding import PartitionSpec as P

HEAD_DIM = 64


NORM_EPS = 1e-05
GELU_COEFF = 0.7978845608028654
GELU_CUBIC = 0.044715


def layer_norm(inputs, gain_row, bias_row):
    row_mean = jnp.mean(inputs, axis=-1, keepdims=True)
    centered = inputs - row_mean
    inv_std = lax.rsqrt(jnp.mean(centered * centered, axis=-1, keepdims=True) + NORM_EPS)
    normed = centered * inv_std
    return (normed * gain_row + bias_row, normed, inv_std)


def norm_back(grad_in, normed, inv_std, gain_row):
    scaled = grad_in * gain_row
    return inv_std * (
        scaled
        - jnp.mean(scaled, axis=-1, keepdims=True)
        - normed * jnp.mean(scaled * normed, axis=-1, keepdims=True)
    )


def gelu_pair(pre_act):
    squared = pre_act * pre_act
    tangent = jnp.tanh(GELU_COEFF * (pre_act + GELU_CUBIC * squared * pre_act))
    gelu_value = 0.5 * pre_act * (1.0 + tangent)
    gelu_slope = 0.5 * (1.0 + tangent) + 0.5 * pre_act * (1.0 - tangent * tangent) * GELU_COEFF * (
        1.0 + 3.0 * GELU_CUBIC * squared
    )
    return (gelu_value, gelu_slope)


def segment_ids(lengths, total_rows):
    positions = jnp.arange(total_rows, dtype=jnp.int32)
    found = jnp.zeros_like(positions)
    end = jnp.int32(0)
    for index in range(lengths.shape[0]):
        end = end + lengths[index]
        found = found + (positions >= end).astype(jnp.int32)
    return found


def contract_first(left, right):
    return lax.dot_general(
        left, right, (((0,), (0,)), ((), ())), preferred_element_type=jnp.float32
    )


def contract_last(left, right):
    return lax.dot_general(
        left, right, (((1,), (1,)), ((), ())), preferred_element_type=jnp.float32
    )

def exchange_kernel(plan, *refs):
    count = len(plan)
    ins = refs[:count]
    outs = refs[count : 2 * count]
    send_sem, recv_sem, own_sem = refs[2 * count : 2 * count + 3]
    spare = list(refs[2 * count + 3 :])

    greeted = []
    for axis in sorted({axis for axis, _, _ in plan}):
        kinds = {kind for name, kind, _ in plan if name == axis}
        size = [n for name, _, n in plan if name == axis][0]
        me = lax.axis_index(axis)
        if kinds == {"paired"}:
            greeted.append({axis: me + 1 - 2 * (me % 2)})
            greeted += [{axis: (me + k) % size} for k in range(2, size, 2)]
        else:
            greeted += [{axis: (me + k) % size} for k in range(1, size)]
    barrier = pltpu.get_barrier_semaphore()
    for device in greeted:
        pl.semaphore_signal(
            barrier, inc=1, device_id=device, device_id_type=pl.DeviceIdType.MESH
        )
    pl.semaphore_wait(barrier, len(greeted))

    used = [0]

    def remote(src, dst, device):
        slot = used[0]
        used[0] += 1
        copy = pltpu.make_async_remote_copy(
            src_ref=src,
            dst_ref=dst,
            send_sem=send_sem.at[slot],
            recv_sem=recv_sem.at[slot],
            device_id=device,
            device_id_type=pl.DeviceIdType.MESH,
        )
        copy.start()
        return copy

    def in_line(axis, src, dst, base, place, target, arrival):
        return pltpu.make_async_remote_copy(
            src_ref=src,
            dst_ref=dst,
            send_sem=send_sem.at[base + place],
            recv_sem=recv_sem.at[base + arrival],
            device_id={axis: jnp.int32(target)},
            device_id_type=pl.DeviceIdType.MESH,
        )

    def line_start(axis, kind, src, dst, base, held):
        me = lax.axis_index(axis)
        for m in range(4):

            @pl.when(me == m)
            def _(m=m):
                if kind == "sum" and m in (0, 3):
                    far = 3 - m
                    near = 1 if m == 0 else 2
                    in_line(axis, src.at[far], held, base, far, near, 4).start()
                for target in ((2, 1), (3, 2, 0), (0, 1, 3), (1, 2))[m]:
                    if kind == "sum" and (m, target) in ((1, 3), (2, 0)):
                        continue
                    block = src.at[target] if kind == "sum" else src
                    in_line(axis, block, dst.at[m], base, target, target, m).start()

    def line_relay(axis, kind, src, dst, base, held, mixed):
        me = lax.axis_index(axis)
        for m in (1, 2):

            @pl.when(me == m)
            def _(m=m):
                far = 3 if m == 1 else 0
                near = 3 - far
                if kind == "line":
                    in_line(axis, src, dst.at[far], base, far, far, far).wait_recv()
                    in_line(axis, dst.at[far], dst.at[far], base, 4, near, far).start()
                else:
                    in_line(axis, held, held, base, far, far, 4).wait_recv()

                    def add(row, carry):
                        rows = pl.ds(row * 16, 16)
                        mixed[rows] = (
                            held[rows].astype(jnp.float32)
                            + src[far, rows].astype(jnp.float32)
                        ).astype(mixed.dtype)
                        return carry

                    lax.fori_loop(0, mixed.shape[0] // 16, add, 0)
                    in_line(axis, mixed, dst.at[m], base, far, far, m).start()

        if kind == "sum":
            for m in (0, 3):

                @pl.when(me == m)
                def _(m=m):
                    dst[3 - m] = jnp.zeros(dst.shape[1:], dst.dtype)

    def line_finish(axis, kind, src, dst, base, held, mixed):
        me = lax.axis_index(axis)
        for m in range(4):

            @pl.when(me == m)
            def _(m=m):
                block = src.at[0] if kind == "sum" else src
                for other in range(4):
                    if other == m:
                        continue
                    ends = (m, other) in ((0, 3), (3, 0))
                    relayed = (m, other) in ((1, 3), (2, 0))
                    copy = in_line(axis, block, dst.at[other], base, other, other, other)
                    if not (kind == "sum" and ends) and not (kind == "line" and relayed):
                        copy.wait_recv()
                    if not (kind == "line" and ends):
                        copy.wait_send()
                if kind == "line" and m in (1, 2):
                    in_line(axis, block, dst.at[0], base, 4, 0, 0).wait_send()

    started = []
    relays = []
    own = []
    lines = []
    for index, (axis, kind, size) in enumerate(plan):
        me = lax.axis_index(axis)
        src, dst = ins[index], outs[index]
        if kind in ("line", "sum"):
            held = spare.pop(0) if kind == "sum" else None
            mixed = spare.pop(0) if kind == "sum" else None
            line_start(axis, kind, src, dst, used[0], held)
            lines.append((axis, kind, src, dst, used[0], held, mixed))
            used[0] += 5
        elif kind == "paired":
            for k in range(2, size, 2):
                copy = remote(src, dst.at[me], {axis: (me + k) % size})
                relays.append((copy, dst, axis, (me + size - k) % size))
            started.append(remote(src, dst.at[me], {axis: me + 1 - 2 * (me % 2)}))
        else:
            for k in range(1, size):
                peer = (me + k) % size
                block = src if kind == "gather" else src.at[peer]
                started.append(remote(block, dst.at[me], {axis: peer}))
    for index, (axis, kind, size) in enumerate(plan):
        me = lax.axis_index(axis)
        block = ins[index].at[me] if kind in ("swap", "sum") else ins[index]
        copy = pltpu.make_async_copy(block, outs[index].at[me], own_sem.at[index])
        copy.start()
        own.append(copy)
    for line in lines:
        line_relay(*line)
    for copy, dst, axis, slot in relays:
        copy.wait_recv()
        me = lax.axis_index(axis)
        started.append(
            remote(dst.at[slot], dst.at[slot], {axis: me + 1 - 2 * (me % 2)})
        )
    for copy, _, _, _ in relays:
        copy.wait_send()
    for copy in own:
        copy.wait()
    for copy in started:
        copy.wait()
    for line in lines:
        line_finish(*line)


def make_exchange():
    calls = [0]

    def exchange(*items):
        plan = []
        shapes = []
        copies = 0
        sent = 0
        spare = []
        for axis, kind, value in items:
            size = lax.axis_size(axis)
            if kind == "paired" and size % 2:
                kind = "gather"
            block = value.shape[1:] if kind == "swap" else value.shape
            if axis == "tensor" and size == 4 and value.dtype == jnp.bfloat16:
                kind = {"swap": "sum", "gather": "line"}[kind]
                if kind == "sum":
                    spare += [pltpu.VMEM(block, value.dtype)] * 2
            plan.append((axis, kind, size))
            copies += 5 if kind in ("line", "sum") else size - 1
            shapes.append(jax.ShapeDtypeStruct((size,) + block, value.dtype))
            sent += (size - 1) * math.prod(block) * value.dtype.itemsize
        collective_id = calls[0]
        calls[0] += 1
        return pl.pallas_call(
            lambda *refs: exchange_kernel(tuple(plan), *refs),
            out_shape=tuple(shapes),
            in_specs=[pl.BlockSpec(memory_space=pltpu.VMEM)] * len(plan),
            out_specs=tuple([pl.BlockSpec(memory_space=pltpu.VMEM)] * len(plan)),
            scratch_shapes=[
                pltpu.SemaphoreType.DMA((copies,)),
                pltpu.SemaphoreType.DMA((copies,)),
                pltpu.SemaphoreType.DMA((len(plan),)),
                *spare,
            ],
            compiler_params=pltpu.CompilerParams(
                collective_id=collective_id,
                has_side_effects=True,
                vmem_limit_bytes=48 * 1024 * 1024,
            ),
            cost_estimate=pl.CostEstimate(flops=0, bytes_accessed=sent, transcendentals=0),
            name=f"exchange_{collective_id}",
        )(*[value for _, _, value in items])

    return exchange


SIBLING, CROSS, FAR, BESIDE, ABOVE, LINE = range(6)
EVERY_PEER = (SIBLING, CROSS, FAR, BESIDE, ABOVE)
AT_UP, AT_SUMMED, AT_OUT, AT_HEADS, AT_LATE, AT_ATTENDED, AT_QKV = range(7)
QKV, OUT, UP, DOWN = "qkv", "out", "up", "down"
MESH = pl.DeviceIdType.MESH


class Place:
    def __init__(self):
        self.dp = lax.axis_index("dp")
        self.z = lax.axis_index("tensor")
        self.core = lax.rem(self.dp, 2)
        self.pair = lax.div(self.z, 2)
        self.low = lax.rem(self.z, 2)
        self.rank = 2 * self.core + self.low
        self.native = self.core == self.pair
        self.block = lax.div(self.dp, 2)
        self.x = lax.rem(self.block, 2)
        self.y = lax.div(self.block, 2)
        self.base = self.dp - self.core

    def sibling(self):
        return {"dp": self.base + 1 - self.core, "tensor": self.z}

    def cross(self, core):
        return {"dp": self.base + core, "tensor": self.z + 1 - 2 * self.low}

    def far(self, core):
        return {"dp": self.base + core, "tensor": self.z + 2 - 4 * self.pair}

    def beside(self):
        return {"dp": self.dp + 2 - 4 * self.x, "tensor": self.z}

    def above(self):
        return {"dp": self.dp + 4 - 8 * self.y, "tensor": self.z}

    def in_line(self, index):
        return {"dp": self.base + lax.rem(index, 2), "tensor": lax.div(index, 2)}

    def rank_at(self, core, low):
        return 2 * core + low

    def block_at(self, dy, dx):
        y = 1 - self.y if dy else self.y
        x = 1 - self.x if dx else self.x
        return 2 * y + x


class Wires:
    def __init__(self, send_sem, recv_sem, own_sem):
        self.send_sem, self.recv_sem, self.own_sem = send_sem, recv_sem, own_sem
        self.used = 0
        self.own_used = 0

    def take(self, count):
        at = self.used
        self.used += count
        return at

    def take_own(self, count=1):
        at = self.own_used
        self.own_used += count
        return at

    def copy(self, src, dst, device, send, recv):
        return pltpu.make_async_remote_copy(
            src_ref=src,
            dst_ref=dst,
            send_sem=self.send_sem.at[send],
            recv_sem=self.recv_sem.at[recv],
            device_id=device,
            device_id_type=MESH,
        )

    def local(self, src, dst, slot):
        return pltpu.make_async_copy(src, dst, self.own_sem.at[slot])


def add_rows(dst, *parts):
    rows = dst.shape[0]
    step = 16 if rows % 16 == 0 else 8

    def body(index, carry):
        at = pl.ds(index * step, step)
        total = parts[0][at].astype(jnp.float32)
        for part in parts[1:]:
            total = total + part[at].astype(jnp.float32)
        dst[at] = total.astype(dst.dtype)
        return carry

    lax.fori_loop(0, rows // step, body, 0)


class Gather:
    peers = (SIBLING, CROSS)
    copies = 5
    owns = 1

    @staticmethod
    def shape(value):
        return (4,) + value.shape

    @staticmethod
    def scratch(value):
        return []

    def __init__(self, place, wires, src, dst, spare):
        self.p, self.w, self.src, self.dst = place, wires, src, dst
        self.at = wires.take(self.copies)
        self.own = wires.take_own()

    def _copies(self):
        p, w, src, dst, at = self.p, self.w, self.src, self.dst, self.at
        other = 1 - p.core
        near = p.rank_at(p.core, 1 - p.low)
        skew = p.rank_at(other, 1 - p.low)
        sib = p.sibling()
        return [
            lambda: w.copy(src, dst.at[p.rank], sib, at, at),
            lambda: w.copy(src.at[p.core], dst.at[p.rank, p.core], p.cross(p.core), at + 1, at + 1),
            lambda: w.copy(src.at[other], dst.at[p.rank, other], p.cross(other), at + 2, at + 2),
            lambda: w.copy(dst.at[near, p.core], dst.at[near, p.core], sib, at + 3, at + 4),
            lambda: w.copy(dst.at[skew, p.core], dst.at[skew, p.core], sib, at + 4, at + 3),
        ]

    def start(self):
        made = self._copies()
        for copy in (made[1], made[2], made[0]):
            copy().start()
        self.w.local(self.src, self.dst.at[self.p.rank], self.own).start()

    def relay(self):
        made = self._copies()
        made[1]().wait_recv()
        made[3]().start()
        made[2]().wait_recv()
        made[4]().start()

    def relay_more(self):
        pass

    def finish(self):
        made = self._copies()
        for index in (0, 3, 4):
            made[index]().wait_recv()
        for copy in made:
            copy().wait_send()
        self.w.local(self.src, self.dst.at[self.p.rank], self.own).wait()


class Reduce:
    peers = (SIBLING, CROSS)
    copies = 3
    owns = 1

    @staticmethod
    def shape(value):
        return (3,) + value.shape[1:]

    @staticmethod
    def scratch(value):
        return [pltpu.VMEM(value.shape[1:], value.dtype)] * 2

    def __init__(self, place, wires, src, dst, spare):
        self.p, self.w, self.src, self.dst = place, wires, src, dst
        self.held, self.mixed = spare
        self.at = wires.take(self.copies)
        self.own = wires.take_own()

    def _copies(self):
        p, w, src, dst, at = self.p, self.w, self.src, self.dst, self.at
        other = 1 - p.core
        sib = p.sibling()
        return [
            lambda: w.copy(src.at[p.rank_at(other, p.low)], dst.at[1], sib, at, at),
            lambda: w.copy(src.at[p.rank_at(other, 1 - p.low)], self.held, sib, at + 1, at + 1),
            lambda: w.copy(self.mixed, dst.at[2], p.cross(p.core), at + 2, at + 2),
        ]

    def start(self):
        made = self._copies()
        made[1]().start()
        made[0]().start()
        self.w.local(self.src.at[self.p.rank], self.dst.at[0], self.own).start()

    def relay(self):
        made = self._copies()
        made[1]().wait_recv()
        add_rows(self.mixed, self.held, self.src.at[self.p.rank_at(self.p.core, 1 - self.p.low)])
        made[2]().start()

    def relay_more(self):
        pass

    def finish(self):
        made = self._copies()
        made[0]().wait_recv()
        made[2]().wait_recv()
        for copy in made:
            copy().wait_send()
        self.w.local(self.src.at[self.p.rank], self.dst.at[0], self.own).wait()


class Pairing:
    peers = (SIBLING, FAR)
    copies = 3
    owns = 1

    @staticmethod
    def shape(value):
        return (2,) + value.shape

    @staticmethod
    def scratch(value):
        return []

    def __init__(self, place, wires, src, dst, spare):
        self.p, self.w, self.src, self.dst = place, wires, src, dst
        self.at = wires.take(self.copies)
        self.own = wires.take_own()

    def _near(self):
        p, at = self.p, self.at
        return self.w.copy(self.src, self.dst.at[p.core], p.sibling(), at, at)

    def _far(self, recv):
        p, at = self.p, self.at
        return self.w.copy(self.src, self.dst.at[p.core], p.far(p.pair), at + 1, recv)

    def start(self):
        p = self.p
        self._far(self.at + 1 + p.core).start()

        @pl.when(p.native)
        def _():
            self.w.local(self.src, self.dst.at[p.core], self.own).start()

        @pl.when(jnp.logical_not(p.native))
        def _():
            self._near().start()

    def settle(self):
        p = self.p

        @pl.when(p.native)
        def _():
            self._near().wait_recv()
            self.w.local(self.src, self.dst.at[p.core], self.own).wait()

        @pl.when(jnp.logical_not(p.native))
        def _():
            self._far(self.at + 1).wait_recv()
            self._far(self.at + 2).wait_recv()

    def sent(self):
        p = self.p
        self._far(self.at + 1).wait_send()

        @pl.when(jnp.logical_not(p.native))
        def _():
            self._near().wait_send()

    def relay(self):
        pass

    def relay_more(self):
        pass

    def finish(self):
        self.settle()
        self.sent()


class Spread:
    peers = (BESIDE, ABOVE)
    copies = 4
    owns = 1

    @staticmethod
    def shape(value):
        return (4,) + value.shape

    @staticmethod
    def scratch(value):
        return []

    def __init__(self, place, wires, src, dst, spare):
        self.p, self.w, self.src, self.dst = place, wires, src, dst
        self.at = wires.take(self.copies)
        self.own = wires.take_own()

    def _copies(self):
        p, w, src, dst, at = self.p, self.w, self.src, self.dst, self.at
        row, column = p.block_at(0, 1), p.block_at(1, 0)
        return [
            lambda: w.copy(src, dst.at[p.block], p.beside(), at, at),
            lambda: w.copy(src, dst.at[p.block], p.above(), at + 1, at + 1),
            lambda: w.copy(dst.at[row, 0], dst.at[row, 0], p.above(), at + 2, at + 2),
            lambda: w.copy(dst.at[column, 1], dst.at[column, 1], p.beside(), at + 3, at + 3),
        ]

    def start(self):
        made = self._copies()
        made[0]().start()
        made[1]().start()
        self.w.local(self.src, self.dst.at[self.p.block], self.own).start()

    def relay(self):
        pass

    def relay_more(self):
        made = self._copies()
        made[0]().wait_recv()
        made[2]().start()
        made[1]().wait_recv()
        made[3]().start()

    def finish(self):
        made = self._copies()
        made[2]().wait_recv()
        made[3]().wait_recv()
        for copy in made:
            copy().wait_send()
        self.w.local(self.src, self.dst.at[self.p.block], self.own).wait()


class Fetch:
    peers = (SIBLING, FAR, BESIDE, ABOVE)
    copies = 7
    owns = 2

    @staticmethod
    def shape(value):
        return (4, 2) + value.shape

    @staticmethod
    def scratch(value):
        return [pltpu.VMEM((2,) + value.shape, value.dtype)]

    def __init__(self, place, wires, src, dst, spare):
        self.one = Pairing(place, wires, src, spare[0], [])
        self.two = Spread(place, wires, spare[0], dst, [])

    def start(self):
        self.one.start()

    def relay(self):
        self.one.settle()
        self.two.start()

    def relay_more(self):
        self.two.relay_more()

    def finish(self):
        self.one.sent()
        self.two.finish()


class Total:
    peers = (BESIDE, ABOVE)
    copies = 6
    owns = 0

    @staticmethod
    def shape(value):
        return value.shape[1:]

    @staticmethod
    def scratch(value):
        one = pltpu.VMEM(value.shape[2:], value.dtype)
        two = pltpu.VMEM(value.shape[1:], value.dtype)
        return [two, two, two, one, one]

    def __init__(self, place, wires, src, dst, spare):
        self.p, self.w, self.src, self.dst = place, wires, src, dst
        self.from_x, self.from_y, self.last, self.to_y, self.to_x = spare
        self.at = wires.take(self.copies)

    def _copies(self):
        p, w, src, at = self.p, self.w, self.src, self.at
        here_x, here_y, skew = p.block_at(0, 1), p.block_at(1, 0), p.block_at(1, 1)
        return [
            lambda: w.copy(src.at[here_x, 0], self.from_x.at[0], p.beside(), at, at),
            lambda: w.copy(src.at[skew, 0], self.from_x.at[1], p.beside(), at + 1, at + 1),
            lambda: w.copy(src.at[here_y, 1], self.from_y.at[0], p.above(), at + 2, at + 2),
            lambda: w.copy(src.at[skew, 1], self.from_y.at[1], p.above(), at + 3, at + 3),
            lambda: w.copy(self.to_y, self.last.at[0], p.above(), at + 4, at + 4),
            lambda: w.copy(self.to_x, self.last.at[1], p.beside(), at + 5, at + 5),
        ]

    def start(self):
        made = self._copies()
        for index in (1, 3, 0, 2):
            made[index]().start()

    def relay(self):
        pass

    def relay_more(self):
        made = self._copies()
        p = self.p
        made[1]().wait_recv()
        add_rows(self.to_y, self.src.at[p.block_at(1, 0), 0], self.from_x.at[1])
        made[4]().start()
        made[3]().wait_recv()
        add_rows(self.to_x, self.src.at[p.block_at(0, 1), 1], self.from_y.at[1])
        made[5]().start()

    def finish(self):
        made = self._copies()
        p = self.p
        for index in (0, 2, 4, 5):
            made[index]().wait_recv()
        add_rows(self.dst.at[0], self.src.at[p.block, 0], self.from_x.at[0], self.last.at[0])
        add_rows(self.dst.at[1], self.src.at[p.block, 1], self.from_y.at[0], self.last.at[1])
        for copy in made:
            copy().wait_send()


class Deliver:
    peers = (SIBLING, FAR)
    copies = 4
    owns = 1

    @staticmethod
    def shape(value):
        return value.shape

    @staticmethod
    def scratch(value):
        return []

    def __init__(self, place, wires, src, dst, spare):
        self.p, self.w, self.src, self.dst = place, wires, src, dst
        self.at = wires.take(self.copies)
        self.own = wires.take_own()

    def _near(self):
        p, at = self.p, self.at
        return self.w.copy(self.src.at[1 - p.core], self.dst.at[0], p.sibling(), at, at)

    def _far(self, core):
        p, at = self.p, self.at
        return self.w.copy(
            self.src.at[core], self.dst.at[1], p.far(jnp.int32(core)), at + 1 + core, at + 1
        )

    def start(self):
        p = self.p

        @pl.when(p.native)
        def _():
            self._near().start()
            self.w.local(self.src.at[p.core], self.dst.at[0], self.own).start()

        @pl.when(jnp.logical_not(p.native))
        def _():
            self._far(0).start()
            self._far(1).start()

    def relay(self):
        pass

    def relay_more(self):
        pass

    def finish(self):
        p = self.p
        self._far(0).wait_recv()

        @pl.when(p.native)
        def _():
            self._near().wait_send()
            self.w.local(self.src.at[p.core], self.dst.at[0], self.own).wait()

        @pl.when(jnp.logical_not(p.native))
        def _():
            self._near().wait_recv()
            self._far(0).wait_send()
            self._far(1).wait_send()


class Swap:
    peers = (FAR,)
    copies = 1
    owns = 1

    @staticmethod
    def shape(value):
        return value.shape

    @staticmethod
    def scratch(value):
        return []

    def __init__(self, place, wires, src, dst, spare):
        self.p, self.w, self.src, self.dst = place, wires, src, dst
        self.at = wires.take(self.copies)
        self.own = wires.take_own()

    def _copy(self):
        p, at = self.p, self.at
        return self.w.copy(self.src, self.dst, p.far(1 - p.core), at, at)

    def start(self):
        @pl.when(self.p.native)
        def _():
            self.w.local(self.src, self.dst, self.own).start()

        @pl.when(jnp.logical_not(self.p.native))
        def _():
            self._copy().start()

    def relay(self):
        pass

    def relay_more(self):
        pass

    def finish(self):
        @pl.when(self.p.native)
        def _():
            self.w.local(self.src, self.dst, self.own).wait()

        @pl.when(jnp.logical_not(self.p.native))
        def _():
            self._copy().wait()


class Small:
    peers = (BESIDE, ABOVE, LINE)
    copies = 20
    owns = 1

    @staticmethod
    def shape(value):
        return (8,) + value.shape[2:]

    @staticmethod
    def scratch(value):
        return Total.scratch(value) + [pltpu.VMEM(value.shape[1:], value.dtype)]

    def __init__(self, place, wires, src, dst, spare):
        self.sums = spare[-1]
        self.total = Total(place, wires, src, self.sums, spare[:-1])
        self.p, self.w, self.dst = place, wires, dst
        self.at = wires.take(14)
        self.own = wires.take_own()

    def _ends(self, offset):
        p, at = self.p, self.at
        me = 2 * p.z + p.core
        to = lax.rem(me + offset, 8)
        return self.w.copy(
            self.sums.at[lax.rem(to, 2)], self.dst.at[me], p.in_line(to), at + offset - 1, at + 6 + offset
        )

    def _mine(self):
        p = self.p
        return self.w.local(self.sums.at[p.core], self.dst.at[2 * p.z + p.core], self.own)

    def start(self):
        self.total.start()

    def relay(self):
        pass

    def relay_more(self):
        self.total.relay_more()
        self.total.finish()
        for offset in range(1, 8):
            self._ends(offset).start()
        self._mine().start()

    def finish(self):
        self._mine().wait()
        for offset in range(1, 8):
            self._ends(offset).wait()


def greet(place, kinds):
    p = place
    devices = []
    if SIBLING in kinds or LINE in kinds:
        devices.append(p.sibling())
    if CROSS in kinds or LINE in kinds:
        devices += [p.cross(jnp.int32(0)), p.cross(jnp.int32(1))]
    if FAR in kinds or LINE in kinds:
        devices += [p.far(jnp.int32(0)), p.far(jnp.int32(1))]
    if LINE in kinds:
        last = 3 - p.z
        devices += [{"dp": p.base, "tensor": last}, {"dp": p.base + 1, "tensor": last}]
    if BESIDE in kinds:
        devices.append(p.beside())
    if ABOVE in kinds:
        devices.append(p.above())
    barrier = pltpu.get_barrier_semaphore()
    for device in devices:
        pl.semaphore_signal(barrier, inc=1, device_id=device, device_id_type=MESH)
    pl.semaphore_wait(barrier, len(devices))


def round_kernel(kinds, *refs):
    count = len(kinds)
    ins, outs = refs[:count], refs[count : 2 * count]
    wires = Wires(*refs[2 * count : 2 * count + 3])
    spare = list(refs[2 * count + 3 :])
    place = Place()
    greet(place, {peer for kind, _ in kinds for peer in kind.peers})
    jobs = []
    for (kind, held), src, dst in zip(kinds, ins, outs):
        jobs.append(kind(place, wires, src, dst, spare[:held]))
        del spare[:held]
    for job in jobs:
        job.start()
    for job in jobs:
        job.relay()
    for job in jobs:
        job.relay_more()
    for job in jobs:
        job.finish()


def make_rounds():
    calls = [0]

    def rounds(*items):
        kinds, shapes, scratch = [], [], []
        copies = owns = sent = 0
        for kind, value in items:
            held = kind.scratch(value)
            kinds.append((kind, len(held)))
            scratch += held
            shapes.append(jax.ShapeDtypeStruct(kind.shape(value), value.dtype))
            copies += kind.copies
            owns += kind.owns
            sent += math.prod(kind.shape(value)) * value.dtype.itemsize
        collective_id = calls[0]
        calls[0] += 1
        return pl.pallas_call(
            lambda *refs: round_kernel(tuple(kinds), *refs),
            out_shape=tuple(shapes),
            in_specs=[pl.BlockSpec(memory_space=pltpu.VMEM)] * len(kinds),
            out_specs=tuple([pl.BlockSpec(memory_space=pltpu.VMEM)] * len(kinds)),
            scratch_shapes=[
                pltpu.SemaphoreType.DMA((copies,)),
                pltpu.SemaphoreType.DMA((copies,)),
                pltpu.SemaphoreType.DMA((max(owns, 1),)),
                *scratch,
            ],
            compiler_params=pltpu.CompilerParams(
                collective_id=collective_id,
                has_side_effects=True,
                vmem_limit_bytes=48 * 1024 * 1024,
            ),
            cost_estimate=pl.CostEstimate(flops=0, bytes_accessed=sent, transcendentals=0),
            name=f"round_{collective_id}",
        )(*[value for _, value in items])

    return rounds


def masked_scores(queries, key_vecs, segments, score_scale):
    positions = jnp.arange(key_vecs.shape[0], dtype=jnp.int32)
    allowed = (segments[:, None] == segments[None, :]) & (
        positions[None, :] <= positions[:, None]
    )
    scores = (
        jnp.einsum("qhd,khd->hqk", queries, key_vecs, preferred_element_type=jnp.float32)
        * score_scale
    )
    return jnp.where(allowed[None], scores, -jnp.inf)


def attend(queries, key_vecs, val_vecs, segments, score_scale):
    scores = masked_scores(queries, key_vecs, segments, score_scale)
    row_max = jnp.max(scores, axis=-1, keepdims=True)
    log_total = row_max + jnp.log(jnp.sum(jnp.exp(scores - row_max), axis=-1, keepdims=True))
    probs_half = jnp.exp(scores - log_total).astype(jnp.bfloat16)
    attended = jnp.einsum("hqk,khd->qhd", probs_half, val_vecs, preferred_element_type=jnp.float32)
    return (attended.astype(jnp.bfloat16).reshape(queries.shape[0], -1), log_total)


def attend_back(queries, key_vecs, val_vecs, grad_attended, log_total, segments, score_scale):
    scores = masked_scores(queries, key_vecs, segments, score_scale)
    soft_probs = jnp.exp(scores - log_total)
    probs_half = soft_probs.astype(jnp.bfloat16)
    grad_probs = jnp.einsum(
        "qhd,khd->hqk", grad_attended, val_vecs, preferred_element_type=jnp.float32
    )
    val_grad = jnp.einsum(
        "hqk,qhd->khd", probs_half, grad_attended, preferred_element_type=jnp.float32
    )
    row_dot = jnp.sum(grad_probs * soft_probs, axis=-1, keepdims=True)
    score_grad = (soft_probs * (grad_probs - row_dot) * score_scale).astype(jnp.bfloat16)
    query_grad = jnp.einsum(
        "hqk,khd->qhd", score_grad, key_vecs, preferred_element_type=jnp.float32
    )
    key_grad = jnp.einsum("hqk,qhd->khd", score_grad, queries, preferred_element_type=jnp.float32)
    return (query_grad, key_grad, val_grad)


def pack(pieces, width, tile):
    flat = jnp.concatenate([piece.reshape(-1) for piece in pieces])
    unit = width * tile
    return jnp.pad(flat, (0, -flat.shape[0] % unit)).reshape(-1, width)


def unpack(packed, shapes):
    flat = packed.reshape(packed.shape[0], -1)
    pieces = []
    at = 0
    for shape in shapes:
        length = math.prod(shape)
        pieces.append(flat[:, at : at + length].reshape((packed.shape[0],) + shape))
        at += length
    return pieces


def shards(x_in, d_out, seq_lengths, w_qkv, b_qv, w_o, w_1, b_ffn, w_2, norm_gains, vec_biases):
    exchange = make_exchange()
    own_rows, width = x_in.shape
    tensor_size = lax.axis_size("tensor")
    dp_size = lax.axis_size("dp")
    group_rows = own_rows * tensor_size
    layer_count = w_qkv.shape[0]
    local_width = w_qkv.shape[3]
    local_heads = local_width // HEAD_DIM
    qkv_width = 3 * local_width
    score_scale = 1.0 / math.sqrt(HEAD_DIM)
    segments = segment_ids(seq_lengths[0], group_rows)
    half = jnp.bfloat16

    def shard_of(name, layer_index):
        if name == "qkv":
            return w_qkv[layer_index].reshape(w_qkv.shape[1], qkv_width)
        if name == "out":
            return w_o[layer_index].T
        if name == "up":
            return w_1[layer_index]
        return w_2[layer_index].T

    weights = {}

    def step(tensor_items, fetched=(), sums=()):
        items = [("tensor", kind, value) for kind, value in tensor_items]
        items += [("dp", "paired", shard_of(*key)) for key in fetched]
        items += [("dp", "swap", value) for value in sums]
        results = list(exchange(*items))
        for position, key in enumerate(fetched):
            piece = results[len(tensor_items) + position]
            weights[key] = piece.reshape(dp_size * piece.shape[1], piece.shape[2])
        gathered = [
            piece.reshape(group_rows, width) if kind == "gather" else piece.astype(jnp.float32).sum(0)
            for (kind, _), piece in zip(tensor_items, results)
        ]
        totals = [
            piece.astype(jnp.float32).sum(0) for piece in results[len(items) - len(sums) :]
        ]
        return gathered, totals

    def to_owners(partial):
        return ("swap", partial.astype(half).reshape(tensor_size, own_rows, width))

    def by_owner(gradient):
        return gradient.astype(half).reshape(dp_size, -1, gradient.shape[-1])

    small_shapes = [b_qv.shape, b_ffn.shape, norm_gains.shape, vec_biases.shape]
    small = pack([b_qv, b_ffn, norm_gains, vec_biases], 128, 16)
    first = exchange(
        ("tensor", "gather", d_out.astype(half)),
        ("dp", "paired", small),
        ("dp", "paired", shard_of("qkv", 0)),
    )
    last_grad_half = first[0].reshape(group_rows, width)
    weights["qkv", 0] = first[2].reshape(width, qkv_width)
    qv_all, ffn_all, gain_all, bias_all = [
        jnp.moveaxis(piece, 0, -2).reshape(piece.shape[1:-1] + (-1,)).astype(jnp.float32)
        for piece in unpack(first[1], small_shapes)
    ]

    caches = []
    hidden_in = x_in
    for layer_index in range(layer_count):
        last = layer_index == layer_count - 1
        following = layer_index + 1
        gain_rows = gain_all[layer_index]
        bias_rows = bias_all[layer_index]
        normed_own, unit_one, inv_one = layer_norm(hidden_in, gain_rows[0], bias_rows[0])
        fetched = [("out", 0), ("up", 0)] if layer_index == 0 else [("down", layer_index)]
        (normed_one,), _ = step([("gather", normed_own.astype(half))], fetched)
        projected = jnp.dot(
            normed_one, weights["qkv", layer_index], preferred_element_type=jnp.float32
        ).reshape(group_rows, 3, local_width)
        qv_bias = qv_all[layer_index]
        heads = (group_rows, local_heads, HEAD_DIM)
        queries = (projected[:, 0] + qv_bias[0]).astype(half).reshape(heads)
        key_vecs = projected[:, 1].astype(half).reshape(heads)
        val_vecs = (projected[:, 2] + qv_bias[1]).astype(half).reshape(heads)
        attended, log_total = attend(queries, key_vecs, val_vecs, segments, score_scale)
        fetched = [("down", 0)] if layer_index == 0 else []
        (summed,), _ = step(
            [to_owners(contract_last(attended, weights["out", layer_index]))], fetched
        )
        residual_mid = hidden_in + summed + bias_rows[2]
        normed_own_two, unit_two, inv_two = layer_norm(residual_mid, gain_rows[1], bias_rows[1])
        fetched = [] if last else [("qkv", following), ("out", following)]
        (normed_two,), _ = step([("gather", normed_own_two.astype(half))], fetched)
        pre_act = (
            jnp.dot(normed_two, weights["up", layer_index], preferred_element_type=jnp.float32)
            + ffn_all[layer_index]
        )
        gelu_value, gelu_slope = gelu_pair(pre_act)
        activated = gelu_value.astype(half)
        ffn_partial = to_owners(contract_last(activated, weights["down", layer_index]))
        if not last:
            (summed,), _ = step([ffn_partial], [("up", following)])
            hidden_in = residual_mid + summed + bias_rows[3]
        caches.append(
            (
                unit_one,
                inv_one,
                normed_one,
                queries,
                key_vecs,
                val_vecs,
                attended,
                log_total,
                unit_two,
                inv_two,
                normed_two,
                activated,
                gelu_slope,
            )
        )
    back = d_out
    grads = {}
    small_terms = [None] * layer_count
    output = None
    for layer_index in reversed(range(layer_count)):
        last = layer_index == layer_count - 1
        gain_rows = gain_all[layer_index]
        (
            unit_one,
            inv_one,
            normed_one,
            queries,
            key_vecs,
            val_vecs,
            attended,
            log_total,
            unit_two,
            inv_two,
            normed_two,
            activated,
            gelu_slope,
        ) = caches[layer_index]
        if last:
            grad_half = last_grad_half
        else:
            (grad_half,), (grads["qkv", layer_index + 1],) = step(
                [("gather", back.astype(half))], sums=[waiting]
            )
        grad_down = by_owner(contract_first(grad_half, activated))
        grad_pre = (
            jnp.dot(grad_half, weights["down", layer_index], preferred_element_type=jnp.float32)
            * gelu_slope
        )
        grad_pre_half = grad_pre.astype(half)
        grad_up = by_owner(contract_first(normed_two, grad_pre_half))
        partial = to_owners(contract_last(grad_pre_half, weights["up", layer_index]))
        if last:
            cut = grad_up.shape[2] // 2
            (grad_normed_two, summed), (grads["down", layer_index], up_left) = step(
                [partial, ffn_partial], sums=[grad_down, grad_up[:, :, :cut]]
            )
            output = residual_mid + summed + bias_all[layer_index][3]
        else:
            (grad_normed_two,), (grads["down", layer_index],) = step([partial], sums=[grad_down])
        grad_mid = back + norm_back(grad_normed_two, unit_two, inv_two, gain_rows[1])
        (grad_mid_half,), (up_part,) = step(
            [("gather", grad_mid.astype(half))], sums=[grad_up[:, :, cut:] if last else grad_up]
        )
        grads["up", layer_index] = (
            jnp.concatenate([up_left, up_part], axis=1) if last else up_part
        )
        grad_out = by_owner(contract_first(grad_mid_half, attended))
        grad_attended = jnp.dot(
            grad_mid_half, weights["out", layer_index], preferred_element_type=jnp.float32
        )
        grad_attended = grad_attended.astype(half).reshape(group_rows, local_heads, HEAD_DIM)
        query_grad, key_grad, val_grad = attend_back(
            queries, key_vecs, val_vecs, grad_attended, log_total, segments, score_scale
        )
        flat = (group_rows, local_width)
        grad_qkv = jnp.concatenate(
            [part.astype(half).reshape(flat) for part in (query_grad, key_grad, val_grad)], axis=1
        )
        grad_qkv_weight = by_owner(contract_first(normed_one, grad_qkv))
        (grad_normed_one,), sent_now = step(
            [to_owners(contract_last(grad_qkv, weights["qkv", layer_index]))],
            sums=[grad_out] if layer_index else [grad_out, grad_qkv_weight],
        )
        grads["out", layer_index] = sent_now[0]
        if layer_index:
            waiting = grad_qkv_weight
        else:
            grads["qkv", layer_index] = sent_now[1]
        small_terms[layer_index] = (
            jnp.stack(
                [
                    jnp.sum(query_grad, axis=0).reshape(local_width),
                    jnp.sum(val_grad, axis=0).reshape(local_width),
                ]
            ),
            jnp.sum(grad_pre, axis=0),
            jnp.stack(
                [
                    jnp.sum(grad_normed_one * unit_one, axis=0),
                    jnp.sum(grad_normed_two * unit_two, axis=0),
                ]
            ),
            jnp.stack(
                [
                    jnp.sum(grad_normed_one, axis=0),
                    jnp.sum(grad_normed_two, axis=0),
                    jnp.sum(grad_mid, axis=0),
                    jnp.sum(back, axis=0),
                ]
            ),
        )
        back = grad_mid + norm_back(grad_normed_one, unit_one, inv_one, gain_rows[0])

    def split_owner(piece):
        return jnp.moveaxis(
            piece.reshape(piece.shape[:-1] + (dp_size, -1)), -2, 0
        ).reshape(dp_size, -1)

    stacked = [
        split_owner(jnp.stack([small_terms[index][member] for index in range(layer_count)]))
        for member in (2, 3, 0, 1)
    ]
    flat = jnp.concatenate(stacked, axis=1)
    flat = jnp.pad(flat, ((0, 0), (0, -flat.shape[1] % 1024)))
    (parts,) = exchange(("dp", "swap", flat.reshape(dp_size, -1, 128)))
    total = parts.sum(0)
    (shared,) = exchange(("tensor", "gather", total))
    everyone = shared.sum(0).reshape(-1)
    gain_size, bias_size = norm_gains.size, vec_biases.size
    mine = total.reshape(-1)[gain_size + bias_size :]

    def stack_layers(name, shape, transposed):
        parts = [grads[name, index] for index in range(layer_count)]
        return jnp.stack([part.T if transposed else part for part in parts]).reshape(shape)

    return (
        output,
        back,
        stack_layers("qkv", w_qkv.shape, False),
        mine[: b_qv.size].reshape(b_qv.shape),
        stack_layers("out", w_o.shape, True),
        stack_layers("up", w_1.shape, False),
        mine[b_qv.size : b_qv.size + b_ffn.size].reshape(b_ffn.shape),
        stack_layers("down", w_2.shape, True),
        everyone[:gain_size].reshape(norm_gains.shape),
        everyone[gain_size : gain_size + bias_size].reshape(vec_biases.shape),
    )


def dot_nn(left, right):
    return jnp.dot(left, right, preferred_element_type=jnp.float32)


class GatherHere(Gather):
    def __init__(self, place, wires, dst):
        super().__init__(place, wires, dst.at[place.rank], dst, [])

    def start(self):
        made = self._copies()
        for index in (1, 2, 0):
            made[index]().start()

    def wait_sibling(self):
        self._copies()[0]().wait_recv()

    def finish(self):
        made = self._copies()
        for index in (3, 4):
            made[index]().wait_recv()
        for copy in made:
            copy().wait_send()


class ReduceHere(Reduce):
    def __init__(self, place, wires, src, dst, spare):
        super().__init__(place, wires, src, dst, spare)

    def _copies(self):
        p, w, src, dst, at = self.p, self.w, self.src, self.dst, self.at
        other = 1 - p.core
        sib = p.sibling()
        return [
            lambda: w.copy(src.at[p.rank_at(other, p.low)], dst.at[0], sib, at, at),
            lambda: w.copy(src.at[p.rank_at(other, 1 - p.low)], self.held, sib, at + 1, at + 1),
            lambda: w.copy(self.mixed, dst.at[1], p.cross(p.core), at + 2, at + 2),
        ]

    def start_cross(self):
        self._copies()[1]().start()

    def start_near(self):
        self._copies()[0]().start()

    def finish(self):
        made = self._copies()
        made[0]().wait_recv()
        made[2]().wait_recv()
        for copy in made:
            copy().wait_send()

    def total(self, rows):
        first = self.src[self.p.rank, rows].astype(jnp.float32)
        return first + self.dst[0, rows].astype(jnp.float32) + self.dst[1, rows].astype(jnp.float32)


class Env:
    pass


class Mover:
    def __init__(self, wires):
        self.wires = wires
        self.open = {}

    def start(self, src, dst, name):
        slot = self.wires.take_own()
        self.open[name] = (src, dst, slot)
        self.wires.local(src, dst, slot).start()

    def wait(self, *names):
        for name in names or list(self.open):
            self.wires.local(*self.open.pop(name)).wait()


def make_fused():
    calls = [32]

    def fused(body, ins, outs, scratch, kinds, hbm=()):
        names_in, names_out, names_spare = list(ins), list(outs), list(scratch)

        def kernel(*refs):
            k = Env()
            refs = list(refs)
            for name in names_in + names_out:
                setattr(k, name, refs.pop(0))
            k.wires = Wires(*refs[:3])
            for name, ref in zip(names_spare, refs[3:]):
                setattr(k, name, ref)
            k.place = Place()
            greet(k.place, kinds)
            body(k)
            assert k.wires.used <= 320 and k.wires.own_used <= 192

        collective_id = calls[0]
        calls[0] += 1
        results = pl.pallas_call(
            kernel,
            out_shape=tuple(jax.ShapeDtypeStruct(*outs[name]) for name in names_out),
            in_specs=[
                pl.BlockSpec(memory_space=pltpu.HBM if name in hbm else pltpu.VMEM)
                for name in names_in
            ],
            out_specs=tuple(
                pl.BlockSpec(memory_space=pltpu.HBM if name in hbm else pltpu.VMEM)
                for name in names_out
            ),
            scratch_shapes=[
                pltpu.SemaphoreType.DMA((320,)),
                pltpu.SemaphoreType.DMA((320,)),
                pltpu.SemaphoreType.DMA((192,)),
                *[pltpu.VMEM(*scratch[name]) for name in names_spare],
            ],
            compiler_params=pltpu.CompilerParams(
                collective_id=collective_id,
                has_side_effects=True,
                vmem_limit_bytes=60 * 1024 * 1024,
            ),
            cost_estimate=pl.CostEstimate(
                flops=0, bytes_accessed=16 * 1024 * 1024, transcendentals=0
            ),
            name=f"fused_{collective_id}",
        )(*[ins[name] for name in names_in])
        made = Env()
        made.__dict__.update(zip(names_out, results))
        return made

    return fused


def chips(place):
    other = 1 - place.core
    return (
        (place.rank, place.rank_at(other, place.low)),
        (place.rank_at(place.core, 1 - place.low), place.rank_at(other, 1 - place.low)),
    )


def two(ref, ranks, lanes=slice(None)):
    parts = [ref[rank, ..., lanes] for rank in ranks]
    return jnp.concatenate([part.reshape(-1, part.shape[-1]) for part in parts], axis=0)


def whole(ref, lanes=slice(None)):
    part = ref[..., lanes]
    return part.reshape(-1, part.shape[-1])


def put_two(ref, ranks, value, lanes=slice(None)):
    rows = value.shape[0] // 2
    ref[ranks[0], :, lanes] = value[:rows].astype(ref.dtype)
    ref[ranks[1], :, lanes] = value[rows:].astype(ref.dtype)


def lanes_at(index, size=256):
    return pl.ds(pl.multiple_of(index * size, size), size)


def loop(count, body):
    def step(index, carry):
        body(index)
        return carry

    lax.fori_loop(0, count, step, 0)


def columns_of(ref, block):
    return jnp.concatenate([ref[block, 0], ref[block, 1]], axis=1)


def all_columns(ref, rows):
    return jnp.concatenate([ref[block, core, rows] for block in range(4) for core in range(2)], axis=1)


ROWS = 32


def visible(k, block):
    shape = (128, (block + 1) * 128)
    end = k.lengths[0:1, 0:1].astype(jnp.int32)
    at_query = lax.broadcasted_iota(jnp.int32, shape, 0) + block * 128
    at_key = lax.broadcasted_iota(jnp.int32, shape, 1)
    late_query = jnp.where(at_query >= end, 1, 0)
    late_key = jnp.where(at_key >= end, 1, 0)
    return (late_query == late_key) & (at_key <= at_query)


def attention_forward(k, on_sent, on_gathered, on_middle, on_attended):
    p = k.place
    here, there = chips(p)
    for at in range(4):
        rows = pl.ds(at * ROWS, ROWS)
        normed, _, _ = layer_norm(k.hidden[rows], k.vecs[0:1], k.vecs[2:3])
        k.n1[p.rank, at // 2, pl.ds(at % 2 * ROWS, ROWS)] = normed.astype(jnp.bfloat16)
    gather = GatherHere(p, k.wires, k.n1)
    gather.start()
    on_sent()

    def project(ranks):
        rows = two(k.n1, ranks)
        for index, (dst, bias) in enumerate(((k.q, 0), (k.key, None), (k.val, 1))):
            weight = k.w_qkv[:, :, index * 128 : index * 128 + 128].reshape(1024, 256)
            made = dot_nn(rows, weight)
            if bias is not None:
                made = made + k.qv_bias[bias : bias + 1]
            put_two(dst, ranks, made)

    gather.wait_sibling()
    gather.relay()
    on_gathered()
    project(here)
    gather.finish()
    project(there)
    scale = 1.0 / math.sqrt(HEAD_DIM)
    for block in range(4):
        if block == 3:
            on_middle()
        seen = visible(k, block)
        count = (block + 1) * 128
        for head in range(4):
            lanes = slice(head * HEAD_DIM, head * HEAD_DIM + HEAD_DIM)
            keys = k.key[: block + 1, :, lanes].reshape(count, HEAD_DIM)
            vals = k.val[: block + 1, :, lanes].reshape(count, HEAD_DIM)
            scores = contract_last(k.q[block, :, lanes], keys) * scale
            scores = jnp.where(seen, scores, -jnp.inf)
            raised = jnp.exp(scores - jnp.max(scores, axis=-1, keepdims=True))
            probs = raised * (1.0 / jnp.sum(raised, axis=-1, keepdims=True))
            probs = probs.astype(jnp.bfloat16)
            k.probs[head, pl.ds(block * 128, 128), :count] = probs
            k.att[block, :, lanes] = dot_nn(probs, vals).astype(jnp.bfloat16)
    on_attended()

    def out(ranks):
        rows = two(k.att, ranks)

        def column(block):
            put_two(k.part_a, ranks, dot_nn(rows, columns_of(k.w_out, block)), lanes_at(block))

        loop(4, column)

    reduce = ReduceHere(p, k.wires, k.part_a, k.got_a, (k.held_a, k.mixed_a))
    out(there)
    reduce.start_cross()
    out(here)
    reduce.start_near()
    reduce.relay()
    return reduce


def feed_forward(k, reduce, on_sent, on_gathered, on_raised, part):
    p = k.place
    here, there = chips(p)
    reduce.finish()
    for at in range(4):
        rows = pl.ds(at * ROWS, ROWS)
        mid = k.hidden[rows] + reduce.total(rows) + k.vecs[4:5]
        k.mid[rows] = mid
        normed, _, _ = layer_norm(mid, k.vecs[1:2], k.vecs[3:4])
        k.n2[p.rank, at // 2, pl.ds(at % 2 * ROWS, ROWS)] = normed.astype(jnp.bfloat16)
    gather = GatherHere(p, k.wires, k.n2)
    gather.start()
    on_sent()

    def up(ranks):
        def column(index):
            lanes = lanes_at(index)
            rows = two(k.n2, ranks)
            weight = k.w_up[:, :, :, lanes].reshape(1024, 256)
            pre_act = dot_nn(rows, weight) + k.ffn_bias[0:1, lanes]
            value, slope = gelu_pair(pre_act)
            put_two(k.act, ranks, value, lanes)
            put_two(k.slope, ranks, slope, lanes)

        loop(4, column)

    gather.wait_sibling()
    gather.relay()
    on_gathered()
    up(here)
    gather.finish()
    up(there)
    on_raised()

    def down(ranks):
        def column(block):
            rows = two(k.act, ranks)
            put_two(part, ranks, dot_nn(rows, columns_of(k.w_down, block)), lanes_at(block))

        loop(4, column)

    return down, here, there


def unpack_small(small_all, views):
    parts = [small_all[block, core].astype(jnp.float32) for block in range(4) for core in range(2)]

    def row(index):
        return jnp.concatenate([part[index : index + 1] for part in parts], axis=1)

    for layer, k in enumerate(views):
        for index in range(2):
            k.vecs[index : index + 1] = row(3 + 2 * layer + index)
            at = 64 * layer + 32 * index
            k.qv_bias[index : index + 1] = jnp.concatenate(
                [part[0:1, at : at + 32] for part in parts], axis=1
            )
        for index in range(4):
            k.vecs[2 + index : 3 + index] = row(7 + 4 * layer + index)
        k.ffn_bias[0:1] = row(1 + layer)


def pack_small(flat, layers):
    flat[...] = jnp.zeros(flat.shape, flat.dtype)
    for shard in range(8):
        block, core = shard // 2, shard % 2
        lanes = slice(shard * 128, shard * 128 + 128)
        quarter = slice(shard * 32, shard * 32 + 32)
        pieces = []
        for layer, (col, col_qv, col_ffn) in enumerate(layers):
            flat[block, core, 2 * layer : 2 * layer + 2] = col[0:2, lanes]
            flat[block, core, 4 + 4 * layer : 8 + 4 * layer] = col[2:6, lanes]
            flat[block, core, 13 + layer : 14 + layer] = col_ffn[0:1, lanes]
            pieces += [col_qv[0:1, quarter], col_qv[1:2, quarter]]
        flat[block, core, 12:13] = jnp.concatenate(pieces, axis=1)


def feed_forward_back(k, gather, on_gathered, on_grad_down):
    p = k.place
    here, there = chips(p)

    def pre(ranks, first):
        def rows_of(index):
            lanes = lanes_at(index)
            weight = all_columns(k.w_down, lanes)
            grad = contract_last(two(k.gh, ranks), weight) * two(k.slope, ranks, lanes).astype(
                jnp.float32
            )
            put_two(k.gp, ranks, grad, lanes)
            summed = jnp.sum(grad, axis=0, keepdims=True)
            k.col_ffn[0:1, lanes] = summed if first else k.col_ffn[0:1, lanes] + summed

        loop(4, rows_of)

    if gather is not None:
        gather.wait_sibling()
        gather.relay()
    on_gathered()
    pre(here, True)
    if gather is not None:
        gather.finish()

    def turn(index):
        lanes = lanes_at(index)
        k.turned[lanes] = whole(k.act, lanes).T

    loop(4, turn)

    def grad_down(block):
        made = dot_nn(k.turned[...], whole(k.gh, lanes_at(block)))
        k.g_down[block, 0] = made[:, :128].astype(jnp.bfloat16)
        k.g_down[block, 1] = made[:, 128:].astype(jnp.bfloat16)

    loop(4, grad_down)
    on_grad_down()
    pre(there, False)

    def term(ranks):
        def column(block):
            rows = two(k.gp, ranks)
            weight = k.w_up[block].reshape(256, 1024)
            put_two(k.part_a, ranks, contract_last(rows, weight), lanes_at(block))

        loop(4, column)

    reduce = ReduceHere(p, k.wires, k.part_a, k.got_a, (k.held_a, k.mixed_a))
    term(there)
    reduce.start_cross()
    term(here)
    reduce.start_near()
    reduce.relay()
    return reduce


def grad_up(k):
    def rows_of(block):
        turned = whole(k.n2, lanes_at(block)).T
        made = dot_nn(turned, whole(k.gp))
        k.g_up[block] = made.astype(jnp.bfloat16).reshape(2, 128, 1024)

    loop(4, rows_of)


def through_norm(k, reduce, hidden, back, sums, gain, dst, put):
    totals = None
    for at in range(4):
        rows = pl.ds(at * ROWS, ROWS)
        grad = reduce.total(rows)
        _, unit, inv = layer_norm(hidden[rows], 1.0, 0.0)
        was = back[rows]
        now = was + norm_back(grad, unit, inv, k.vecs[gain : gain + 1])
        dst[rows] = now
        put(at, now)
        terms = [grad * unit, grad, now, was]
        terms = [jnp.sum(term, axis=0, keepdims=True) for term in terms]
        totals = terms if totals is None else [a + b for a, b in zip(totals, terms)]
    for row, total in zip(sums, totals):
        if row is not None:
            k.col[row : row + 1] = total


def grad_qkv_thirds(k, third):
    def turn(index):
        lanes = lanes_at(index)
        k.turned[lanes] = whole(k.n1, lanes).T

    loop(4, turn)
    for index in range(3):
        rows = pl.ds(index * 128, 128)

        def grad_qkv(block):
            made = dot_nn(k.turned[lanes_at(block)], whole(k.gq.at[index]))
            k.g_qkv[block, :, rows] = made.astype(jnp.bfloat16).reshape(2, 128, 256)

        loop(4, grad_qkv)
        third(index)

def attention_back(k, reduce, background, third, weights_first):
    p = k.place
    here, there = chips(p)
    grad_up(k)
    background(AT_UP)
    reduce.finish()
    background(AT_SUMMED)

    def put(at, now):
        k.gm[p.rank, at // 2, pl.ds(at % 2 * ROWS, ROWS)] = now.astype(jnp.bfloat16)

    through_norm(k, reduce, k.mid, k.back, (1, 3, 4, 5), 1, k.grad_mid, put)
    gather = GatherHere(p, k.wires, k.gm)
    gather.start()

    def attended(ranks):
        weight = all_columns(k.w_out, slice(None))
        put_two(k.ga, ranks, contract_last(two(k.gm, ranks), weight))

    gather.wait_sibling()
    gather.relay()
    attended(here)
    gather.finish()
    attended(there)

    def grad_out(block):
        made = dot_nn(whole(k.att).T, whole(k.gm, lanes_at(block)))
        k.g_out[block, 0] = made[:, :128].astype(jnp.bfloat16)
        k.g_out[block, 1] = made[:, 128:].astype(jnp.bfloat16)

    loop(4, grad_out)
    background(AT_OUT)
    scale = 1.0 / math.sqrt(HEAD_DIM)
    for head in range(4):
        lanes = slice(head * HEAD_DIM, head * HEAD_DIM + HEAD_DIM)
        for block in range(4):
            rows = pl.ds(block * 128, 128)
            count = (block + 1) * 128
            keys = k.key[: block + 1, :, lanes].reshape(count, HEAD_DIM)
            vals = k.val[: block + 1, :, lanes].reshape(count, HEAD_DIM)
            probs = k.probs[head, rows, :count].astype(jnp.float32)
            grad_probs = contract_last(k.ga[block, :, lanes], vals)
            row_dot = jnp.sum(grad_probs * probs, axis=-1, keepdims=True)
            score_grad = (probs * (grad_probs - row_dot) * scale).astype(jnp.bfloat16)
            k.ds[head % 2, rows, :count] = score_grad
            query_grad = dot_nn(score_grad, keys)
            k.gq[0, block, :, lanes] = query_grad.astype(jnp.bfloat16)
            summed = jnp.sum(query_grad, axis=0, keepdims=True)
            k.col_qv[0:1, lanes] = summed if block == 0 else k.col_qv[0:1, lanes] + summed
        if head in (0, 2):
            background(AT_LATE if head else AT_HEADS)
        for block in range(4):
            below = pl.ds(block * 128, 512 - block * 128)
            cols = slice(block * 128, block * 128 + 128)
            count = 512 - block * 128
            queries = k.q[block:, :, lanes].reshape(count, HEAD_DIM)
            grads = k.ga[block:, :, lanes].reshape(count, HEAD_DIM)
            key_grad = contract_first(k.ds[head % 2, below, cols], queries)
            val_grad = contract_first(k.probs[head, below, cols], grads)
            k.gq[1, block, :, lanes] = key_grad.astype(jnp.bfloat16)
            k.gq[2, block, :, lanes] = val_grad.astype(jnp.bfloat16)
            summed = jnp.sum(val_grad, axis=0, keepdims=True)
            k.col_qv[1:2, lanes] = summed if block == 0 else k.col_qv[1:2, lanes] + summed
    background(AT_ATTENDED)

    if weights_first:
        grad_qkv_thirds(k, third)

    def term(ranks):
        rows = [two(k.gq.at[index], ranks) for index in range(3)]

        def column(block):
            made = None
            for index in range(3):
                weight = k.w_qkv[block, :, index * 128 : index * 128 + 128].reshape(256, 256)
                one = contract_last(rows[index], weight)
                made = one if made is None else made + one
            put_two(k.part_b, ranks, made, lanes_at(block))

        loop(4, column)

    reduce = ReduceHere(p, k.wires, k.part_b, k.got_b, (k.held_b, k.mixed_b))
    term(there)
    reduce.start_cross()
    term(here)
    reduce.start_near()
    reduce.relay()

    if not weights_first:
        grad_qkv_thirds(k, third)
    background(AT_QKV)
    reduce.finish()
    through_norm(
        k, reduce, k.hidden, k.grad_mid, (0, 2, None, None), 0, k.back_out, lambda at, now: None
    )


def total_scratch(name, rows, cols, half=jnp.bfloat16):
    one, two = ((rows, cols), half), ((2, rows, cols), half)
    return {f"{name}_t{index}": value for index, value in enumerate((two, two, two, one, one))}


def paired_shards(
    x_in, d_out, seq_lengths, w_qkv, b_qv, w_o, w_1, b_ffn, w_2, norm_gains, vec_biases
):
    fused = make_fused()
    own_rows, width = x_in.shape
    layer_count = w_qkv.shape[0]
    half, full = jnp.bfloat16, jnp.float32
    z = lax.axis_index("tensor")
    qkv_turned = jnp.transpose(w_qkv, (0, 2, 1, 3)).reshape(layer_count, 384, 256)
    shapes = {QKV: (384, 256), OUT: (256, 128), UP: (128, 1024), DOWN: (1024, 128)}
    def pair_spec(name):
        return ((2,) + shapes[name], half)

    def full_spec(name):
        return ((4, 2) + shapes[name], half)

    def added(parts):
        return parts[0].astype(full) + parts[1].astype(full)

    small_shapes = [b_qv.shape, b_ffn.shape, norm_gains.shape, vec_biases.shape]
    small = pack([b_qv, b_ffn, norm_gains, vec_biases], 128, 16)
    lengths = jnp.pad(seq_lengths.astype(full), ((0, 7), (0, 126)))

    rows_spec = ((4, 2, own_rows // 2, width), half)
    heads_spec = ((4, own_rows, 256), half)
    wide_spec = ((4, own_rows, width), half)
    own_half = ((own_rows, width), half)
    own_full = ((own_rows, width), full)
    two_half = ((2, own_rows, width), half)
    reduce_a = dict(part_a=wide_spec, got_a=two_half, held_a=own_half, mixed_a=own_half)
    reduce_b = dict(part_b=wide_spec, got_b=two_half, held_b=own_half, mixed_b=own_half)
    saved_specs = dict(
        hidden=own_full,
        vecs=((8, width), full),
        n1=rows_spec,
        q=heads_spec,
        key=heads_spec,
        val=heads_spec,
        probs=((4, 512, 512), half),
        att=heads_spec,
        mid=own_full,
        n2=rows_spec,
        act=wide_spec,
        slope=wide_spec,
        w_qkv=full_spec(QKV),
        w_out=full_spec(OUT),
        w_up=full_spec(UP),
        w_down=full_spec(DOWN),
    )
    own_specs = dict(
        reduce_a,
        qv_bias=((8, 256), full),
        ffn_bias=((8, width), full),
        pair_qkv=pair_spec(QKV),
        pair_out=pair_spec(OUT),
        pair_up=pair_spec(UP),
        pair_down=pair_spec(DOWN),
    )

    group_a, group_b, group_c = ("w_down", "slope"), ("w_up", "act", "n2"), ("mid", "att", "w_out")
    group_d, group_e = ("probs", "key", "val", "q", "w_qkv", "n1"), ("hidden",)

    def of_layers(specs):
        return {f"{name}_{layer}": spec for name, spec in specs.items() for layer in range(2)}

    def view(k, layer):
        made = Env()
        for name, ref in k.__dict__.items():
            if name.endswith(f"_{layer}"):
                setattr(made, name[:-2], ref)
        made.place, made.wires = k.place, k.wires
        return made

    def forward(k):
        p, w = k.place, k.wires
        k0, k1 = view(k, 0), view(k, 1)
        small_job = Fetch(p, w, k.small, k.small_all, [k.small_pair])
        length_job = Swap(p, w, k.lengths_in, k.lengths, [])
        swap_x = Swap(p, w, k.x_half, k.x_got, [])
        swap_d = Swap(p, w, k.d_half, k.d_got, [])
        k0.lengths = k1.lengths = k.lengths

        def fetch_qkv(layer, v):
            jobs = []
            for index in range(3):
                rows = pl.ds(index * 128, 128)
                dst, pair = v.w_qkv.at[:, :, rows], v.pair_qkv.at[:, rows]
                jobs.append(Fetch(p, w, k.s_qkv.at[layer, rows], dst, [pair]))
            return jobs

        def fetch_rest(layer, v):
            return (
                Fetch(p, w, k.s_out.at[layer], v.w_out, [v.pair_out]),
                Fetch(p, w, k.s_up.at[layer], v.w_up, [v.pair_up]),
                Fetch(p, w, k.s_down.at[layer], v.w_down, [v.pair_down]),
            )

        qkv_0, qkv_1 = fetch_qkv(0, k0), fetch_qkv(1, k1)
        out_0, up_0, down_0 = fetch_rest(0, k0)
        out_1, up_1, down_1 = fetch_rest(1, k1)
        for at in range(4):
            rows = pl.ds(at * ROWS, ROWS)
            k.x_half[rows] = k.x_in[rows].astype(half)
        mover = Mover(w)

        small_job.start()
        length_job.start()
        swap_x.start()
        small_job.relay()
        small_job.relay_more()
        for job in qkv_0:
            job.start()

        @pl.when(p.native)
        def _():
            for job in qkv_0:
                job.relay()

        small_job.finish()
        unpack_small(k.small_all, (k0, k1))
        length_job.finish()
        swap_x.finish()
        for at in range(4):
            rows = pl.ds(at * ROWS, ROWS)
            k0.hidden[rows] = jnp.where(p.native, k.x_in[rows], k.x_got[rows].astype(full))
            k.d_half[rows] = k.d_in[rows].astype(half)

        def first_sent():
            @pl.when(jnp.logical_not(p.native))
            def _():
                for job in qkv_0:
                    job.relay()

        def first_gathered():
            out_0.start()
            up_0.start()
            for job in qkv_0:
                job.relay_more()
            out_0.relay()
            for job in qkv_0:
                job.finish()

        def first_attended():
            out_0.relay_more()
            up_0.relay()
            down_0.start()
            out_0.finish()

        reduce = attention_forward(k0, first_sent, first_gathered, lambda: None, first_attended)

        def first_sent_two():
            up_0.relay_more()
            down_0.relay()

        def first_gathered_two():
            for job in qkv_1:
                job.start()
            out_1.start()
            up_0.finish()

        def first_raised():
            down_0.relay_more()
            for job in qkv_1:
                job.relay()
            out_1.relay()
            up_1.start()
            down_0.finish()

        column, here, there = feed_forward(
            k0, reduce, first_sent_two, first_gathered_two, first_raised, k.part_b
        )
        second = ReduceHere(p, w, k.part_b, k.got_b, (k.held_b, k.mixed_b))
        column(there)
        second.start_cross()
        column(here)
        second.start_near()
        second.relay()
        for job in qkv_1:
            job.relay_more()
        out_1.relay_more()
        for name in group_a + group_b + group_c + group_d + group_e:
            mover.start(getattr(k0, name), getattr(k, f"h_{name}"), name)
        second.finish()
        for at in range(4):
            rows = pl.ds(at * ROWS, ROWS)
            k1.hidden[rows] = k0.mid[rows] + second.total(rows) + k0.vecs[5:6]
        grads = GatherHere(p, w, k.gh)

        def last_sent():
            up_1.relay()

        def last_gathered():
            down_1.start()
            swap_d.start()
            for job in qkv_1:
                job.finish()
            out_1.finish()

        def last_attended():
            down_1.relay()

        reduce = attention_forward(k1, last_sent, last_gathered, up_1.relay_more, last_attended)

        def last_gathered_two():
            up_1.finish()
            down_1.relay_more()
            swap_d.finish()
            for at in range(4):
                rows = pl.ds(at * ROWS, ROWS)
                k.back[rows] = jnp.where(p.native, k.d_in[rows], k.d_got[rows].astype(full))
                k.gh[p.rank, at // 2, pl.ds(at % 2 * ROWS, ROWS)] = k.back[rows].astype(half)
            grads.start()

        def raised():
            grads.wait_sibling()
            grads.relay()
            down_1.finish()

        column, here, there = feed_forward(
            k1, reduce, lambda: None, last_gathered_two, raised, k.ffn_part
        )
        column(there)
        column(here)
        grads.finish()
        mover.wait()

    totals = dict(shapes)
    spare = dict(
        of_layers(own_specs),
        **of_layers(saved_specs),
        **reduce_b,
        back=own_full,
        gh=rows_spec,
        ffn_part=wide_spec,
        lengths=((8, 128), full),
        small_pair=((2, 16, 128), half),
        small_all=((4, 2, 16, 128), half),
        x_half=own_half,
        x_got=own_half,
        d_half=own_half,
        d_got=own_half,
        turned=((1024, 512), half),
        ds=((2, 512, 512), half),
        gq=((3, 4, own_rows, 256), half),
        out_half=own_half,
        back_half=own_half,
        made=own_full,
        back_out=own_full,
        out_sent=own_half,
        back_sent=own_half,
        flat=((4, 2, 16, 128), full),
        small_sums=((2, 16, 128), full),
        g_last=full_spec(QKV),
        **total_scratch("small", 16, 128, full),
        **total_scratch("last", *shapes[QKV]),
    )
    for name, shape in shapes.items():
        spare.update(total_scratch(name, *shape))
    spare.update(
        of_layers(dict(col=((8, width), full), col_qv=((8, 256), full), col_ffn=((8, width), full)))
    )

    def backward(k):
        p, w = k.place, k.wires
        mover = Mover(w)
        first, last = view(k, 0), view(k, 1)
        for name in saved_specs:
            setattr(k, name, getattr(last, name))
        for name in shapes:
            setattr(k, f"g_{name}", getattr(first, f"w_{name}"))
        k.gm, k.gp, k.ga, k.grad_mid = first.n1, first.act, first.att, first.mid
        k.part_a, k.got_a, k.held_a, k.mixed_a = first.part_a, first.got_a, first.held_a, first.mixed_a
        k0, k1 = Env(), Env()
        for v, layer in ((k0, first), (k1, last)):
            v.__dict__.update(k.__dict__)
            v.vecs, v.col, v.col_qv, v.col_ffn = layer.vecs, layer.col, layer.col_qv, layer.col_ffn
        k1.back_out = k0.back = first.hidden
        k1.g_qkv = k.g_last

        def load(names):
            for name in names:
                mover.start(getattr(k, f"h_{name}"), getattr(k, name), name)

        def job_total(name, layer):
            spare = [getattr(k, f"{name}_t{at}") for at in range(5)]
            return Total(p, w, getattr(k, f"g_{name}"), getattr(k, f"pair_{name}_{layer}"), spare)

        def job_deliver(name, layer):
            src, dst = getattr(k, f"pair_{name}_{layer}"), getattr(k, f"done_{name}_{layer}")
            return Deliver(p, w, src, dst, [])

        def thirds(layer, v, name):
            made = []
            for index in range(3):
                rows = pl.ds(index * 128, 128)
                spare = [getattr(k, f"{name}_t{at}") for at in range(5)]
                spare = [ref.at[:, rows] for ref in spare[:3]] + [ref.at[rows] for ref in spare[3:]]
                dst = getattr(k, f"pair_{QKV}_{layer}").at[:, rows]
                done = getattr(k, f"done_{QKV}_{layer}").at[:, rows]
                made.append(
                    (
                        Total(p, w, v.g_qkv.at[:, :, rows], dst, spare),
                        Deliver(p, w, dst, done, []),
                    )
                )
            return made

        ffn = ReduceHere(p, w, k.ffn_part, last.got_a, (last.held_a, last.mixed_a))
        swap = Swap(p, w, k.out_half, k.out_sent, [])
        swap_back = Swap(p, w, k.back_half, k.back_sent, [])
        qkv_1, qkv_0 = thirds(1, k1, "last"), thirds(0, k0, QKV)
        down_1, up_1, out_1 = [job_total(name, 1) for name in (DOWN, UP, OUT)]
        down_0, up_0, out_0 = [job_total(name, 0) for name in (DOWN, UP, OUT)]
        to_down_1, to_up_1, to_out_1 = [job_deliver(name, 1) for name in (DOWN, UP, OUT)]
        to_down_0, to_up_0, to_out_0 = [job_deliver(name, 0) for name in (DOWN, UP, OUT)]
        small_job = Small(
            p, w, k.flat, k.small_parts, [getattr(k, f"small_t{at}") for at in range(5)] + [k.small_sums]
        )
        reduce = feed_forward_back(k1, None, lambda: None, down_1.start)
        ffn.start_cross()
        ffn.start_near()
        ffn.relay()

        def last_background(point):
            if point == AT_UP:
                load(group_a + group_b)
                up_1.start()
            if point == AT_SUMMED:
                down_1.relay_more()
            if point == AT_OUT:
                ffn.finish()
                for at in range(4):
                    rows = pl.ds(at * ROWS, ROWS)
                    made = k.mid[rows] + ffn.total(rows) + k1.vecs[5:6]
                    k.made[rows] = made
                    k.out_half[rows] = made.astype(half)
                swap.start()
                load(group_c)
                out_1.start()
            if point == AT_HEADS:
                down_1.finish()
                to_down_1.start()
            if point == AT_LATE:
                up_1.relay_more()
                out_1.relay_more()
            if point == AT_QKV:
                load(group_d)
                up_1.finish()
                to_up_1.start()
                out_1.finish()
                to_out_1.start()

        attention_back(k1, reduce, last_background, lambda index: qkv_1[index][0].start(), False)
        load(group_e)
        for at in range(4):
            rows = pl.ds(at * ROWS, ROWS)
            k.gh[p.rank, at // 2, pl.ds(at % 2 * ROWS, ROWS)] = k0.back[rows].astype(half)
        gather = GatherHere(p, w, k.gh)
        gather.start()
        mover.wait(*group_a, *group_b)

        def first_started():
            for job, _ in qkv_1:
                job.relay_more()

        def first_grad_down():
            for job, _ in qkv_1:
                job.finish()
            down_0.start()

        reduce = feed_forward_back(k0, gather, first_started, first_grad_down)
        mover.wait(*group_c, *group_d, *group_e)

        for _, job in qkv_1:
            job.start()

        def first_background(point):
            if point == AT_UP:
                up_0.start()
            if point == AT_SUMMED:
                down_0.relay_more()
            if point == AT_OUT:
                out_0.start()
            if point == AT_HEADS:
                down_0.finish()
                to_down_0.start()
            if point == AT_LATE:
                up_0.relay_more()
                out_0.relay_more()
            if point == AT_QKV:
                up_0.finish()
                to_up_0.start()
                out_0.finish()
                to_out_0.start()
                qkv_0[0][0].relay_more()
                qkv_0[1][0].relay_more()

        attention_back(k0, reduce, first_background, lambda index: qkv_0[index][0].start(), True)
        pack_small(k.flat, [(v.col, v.col_qv, v.col_ffn) for v in (k0, k1)])
        small_job.start()
        for at in range(4):
            rows = pl.ds(at * ROWS, ROWS)
            k.back_half[rows] = k.back_out[rows].astype(half)
        qkv_0[0][0].finish()
        qkv_0[2][0].relay_more()
        small_job.relay_more()
        swap_back.start()
        qkv_0[0][1].start()
        for job, then in qkv_0[1:]:
            job.finish()
            then.start()
        small_job.finish()
        swap.finish()
        swap_back.finish()
        for at in range(4):
            rows = pl.ds(at * ROWS, ROWS)
            k.output[rows] = jnp.where(p.native, k.made[rows], k.out_sent[rows].astype(full))
            k.grad_x[rows] = jnp.where(p.native, k.back_out[rows], k.back_sent[rows].astype(full))
        for job in (to_down_1, to_up_1, to_out_1, to_down_0, to_up_0, to_out_0):
            job.finish()
        for _, job in qkv_1 + qkv_0:
            job.finish()
        mover.wait()

    done_specs = {
        f"done_{name}_{layer}": pair_spec(name) for name in totals for layer in range(2)
    }
    def both(k):
        forward(k)
        backward(k)

    spilled = {f"h_{name}": spec for name, spec in saved_specs.items()}
    last = fused(
        both,
        dict(
            x_in=x_in,
            d_in=d_out,
            lengths_in=lengths,
            small=small,
            s_qkv=qkv_turned,
            s_out=w_o,
            s_up=w_1,
            s_down=w_2,
        ),
        dict(
            done_specs,
            **spilled,
            output=own_full,
            grad_x=own_full,
            small_parts=((8, 16, 128), full),
        ),
        spare,
        (SIBLING, CROSS, FAR, BESIDE, ABOVE, LINE),
        hbm=[f"s_{name}" for name in shapes] + list(spilled) + list(done_specs),
    )
    small_parts = last.small_parts
    small_parts = small_parts.reshape(8, -1)
    gain_size, bias_size = norm_gains.size, vec_biases.size
    everyone = small_parts.sum(0)
    sources = jnp.arange(8, dtype=jnp.int32)
    pair = z // 2
    mine_from = (sources == 2 * z + pair) | (sources == 2 * (z + 2 - 4 * pair) + pair)
    mine = jnp.where(mine_from[:, None], small_parts, 0.0).sum(0)[gain_size + bias_size :]

    def stacked_layers(name):
        return jnp.stack([added(getattr(last, f"done_{name}_{layer}")) for layer in range(2)])

    grad_qkv = stacked_layers(QKV)
    grad_qkv = jnp.transpose(grad_qkv.reshape(layer_count, 3, 128, 256), (0, 2, 1, 3))
    return (
        last.output,
        last.grad_x,
        grad_qkv,
        mine[: b_qv.size].reshape(b_qv.shape),
        stacked_layers(OUT),
        stacked_layers(UP),
        mine[b_qv.size : b_qv.size + b_ffn.size].reshape(b_ffn.shape),
        stacked_layers(DOWN),
        everyone[:gain_size].reshape(norm_gains.shape),
        everyone[gain_size : gain_size + bias_size].reshape(vec_biases.shape),
    )


def solution(mesh):
    in_specs = (
        P(("dp", "tensor"), None),
        P(("dp", "tensor"), None),
        P("dp", None),
        P(None, "dp", None, "tensor"),
        P(None, None, ("tensor", "dp")),
        P(None, "tensor", "dp"),
        P(None, "dp", "tensor"),
        P(None, ("tensor", "dp")),
        P(None, "tensor", "dp"),
        P(None, None, "dp"),
        P(None, None, "dp"),
    )
    out_specs = (
        P(("dp", "tensor"), None),
        P(("dp", "tensor"), None),
        P(None, "dp", None, "tensor"),
        P(None, None, ("tensor", "dp")),
        P(None, "tensor", "dp"),
        P(None, "dp", "tensor"),
        P(None, ("tensor", "dp")),
        P(None, "tensor", "dp"),
        P(None, None, "dp"),
        P(None, None, "dp"),
    )
    paired = mesh.shape["dp"] == 8 and mesh.shape["tensor"] == 4
    body = paired_shards if paired else shards
    return jax.shard_map(body, mesh=mesh, in_specs=in_specs, out_specs=out_specs, check_vma=False)
```

```python
import math

import jax
import jax.numpy as jnp
from jax import lax
from jax.experimental import pallas as pl
from jax.experimental.pallas import tpu as pltpu
from jax.sharding import PartitionSpec as P

HEAD_DIM = 64


NORM_EPS = 1e-05
GELU_COEFF = 0.7978845608028654
GELU_CUBIC = 0.044715


def layer_norm(inputs, gain_row, bias_row):
    row_mean = jnp.mean(inputs, axis=-1, keepdims=True)
    centered = inputs - row_mean
    inv_std = lax.rsqrt(jnp.mean(centered * centered, axis=-1, keepdims=True) + NORM_EPS)
    normed = centered * inv_std
    return (normed * gain_row + bias_row, normed, inv_std)


def norm_back(grad_in, normed, inv_std, gain_row):
    scaled = grad_in * gain_row
    return inv_std * (
        scaled
        - jnp.mean(scaled, axis=-1, keepdims=True)
        - normed * jnp.mean(scaled * normed, axis=-1, keepdims=True)
    )


def gelu_pair(pre_act):
    squared = pre_act * pre_act
    tangent = jnp.tanh(GELU_COEFF * (pre_act + GELU_CUBIC * squared * pre_act))
    gelu_value = 0.5 * pre_act * (1.0 + tangent)
    gelu_slope = 0.5 * (1.0 + tangent) + 0.5 * pre_act * (1.0 - tangent * tangent) * GELU_COEFF * (
        1.0 + 3.0 * GELU_CUBIC * squared
    )
    return (gelu_value, gelu_slope)


def segment_ids(lengths, total_rows):
    positions = jnp.arange(total_rows, dtype=jnp.int32)
    found = jnp.zeros_like(positions)
    end = jnp.int32(0)
    for index in range(lengths.shape[0]):
        end = end + lengths[index]
        found = found + (positions >= end).astype(jnp.int32)
    return found


def contract_first(left, right):
    return lax.dot_general(
        left, right, (((0,), (0,)), ((), ())), preferred_element_type=jnp.float32
    )


def contract_last(left, right):
    return lax.dot_general(
        left, right, (((1,), (1,)), ((), ())), preferred_element_type=jnp.float32
    )

def exchange_kernel(plan, *refs):
    count = len(plan)
    ins = refs[:count]
    outs = refs[count : 2 * count]
    send_sem, recv_sem, own_sem = refs[2 * count : 2 * count + 3]
    spare = list(refs[2 * count + 3 :])

    greeted = []
    for axis in sorted({axis for axis, _, _ in plan}):
        kinds = {kind for name, kind, _ in plan if name == axis}
        size = [n for name, _, n in plan if name == axis][0]
        me = lax.axis_index(axis)
        if kinds == {"paired"}:
            greeted.append({axis: me + 1 - 2 * (me % 2)})
            greeted += [{axis: (me + k) % size} for k in range(2, size, 2)]
        else:
            greeted += [{axis: (me + k) % size} for k in range(1, size)]
    barrier = pltpu.get_barrier_semaphore()
    for device in greeted:
        pl.semaphore_signal(
            barrier, inc=1, device_id=device, device_id_type=pl.DeviceIdType.MESH
        )
    pl.semaphore_wait(barrier, len(greeted))

    used = [0]

    def remote(src, dst, device):
        slot = used[0]
        used[0] += 1
        copy = pltpu.make_async_remote_copy(
            src_ref=src,
            dst_ref=dst,
            send_sem=send_sem.at[slot],
            recv_sem=recv_sem.at[slot],
            device_id=device,
            device_id_type=pl.DeviceIdType.MESH,
        )
        copy.start()
        return copy

    def in_line(axis, src, dst, base, place, target, arrival):
        return pltpu.make_async_remote_copy(
            src_ref=src,
            dst_ref=dst,
            send_sem=send_sem.at[base + place],
            recv_sem=recv_sem.at[base + arrival],
            device_id={axis: jnp.int32(target)},
            device_id_type=pl.DeviceIdType.MESH,
        )

    def line_start(axis, kind, src, dst, base, held):
        me = lax.axis_index(axis)
        for m in range(4):

            @pl.when(me == m)
            def _(m=m):
                if kind == "sum" and m in (0, 3):
                    far = 3 - m
                    near = 1 if m == 0 else 2
                    in_line(axis, src.at[far], held, base, far, near, 4).start()
                for target in ((2, 1), (3, 2, 0), (0, 1, 3), (1, 2))[m]:
                    if kind == "sum" and (m, target) in ((1, 3), (2, 0)):
                        continue
                    block = src.at[target] if kind == "sum" else src
                    in_line(axis, block, dst.at[m], base, target, target, m).start()

    def line_relay(axis, kind, src, dst, base, held, mixed):
        me = lax.axis_index(axis)
        for m in (1, 2):

            @pl.when(me == m)
            def _(m=m):
                far = 3 if m == 1 else 0
                near = 3 - far
                if kind == "line":
                    in_line(axis, src, dst.at[far], base, far, far, far).wait_recv()
                    in_line(axis, dst.at[far], dst.at[far], base, 4, near, far).start()
                else:
                    in_line(axis, held, held, base, far, far, 4).wait_recv()

                    def add(row, carry):
                        rows = pl.ds(row * 16, 16)
                        mixed[rows] = (
                            held[rows].astype(jnp.float32)
                            + src[far, rows].astype(jnp.float32)
                        ).astype(mixed.dtype)
                        return carry

                    lax.fori_loop(0, mixed.shape[0] // 16, add, 0)
                    in_line(axis, mixed, dst.at[m], base, far, far, m).start()

        if kind == "sum":
            for m in (0, 3):

                @pl.when(me == m)
                def _(m=m):
                    dst[3 - m] = jnp.zeros(dst.shape[1:], dst.dtype)

    def line_finish(axis, kind, src, dst, base, held, mixed):
        me = lax.axis_index(axis)
        for m in range(4):

            @pl.when(me == m)
            def _(m=m):
                block = src.at[0] if kind == "sum" else src
                for other in range(4):
                    if other == m:
                        continue
                    ends = (m, other) in ((0, 3), (3, 0))
                    relayed = (m, other) in ((1, 3), (2, 0))
                    copy = in_line(axis, block, dst.at[other], base, other, other, other)
                    if not (kind == "sum" and ends) and not (kind == "line" and relayed):
                        copy.wait_recv()
                    if not (kind == "line" and ends):
                        copy.wait_send()
                if kind == "line" and m in (1, 2):
                    in_line(axis, block, dst.at[0], base, 4, 0, 0).wait_send()

    started = []
    relays = []
    own = []
    lines = []
    for index, (axis, kind, size) in enumerate(plan):
        me = lax.axis_index(axis)
        src, dst = ins[index], outs[index]
        if kind in ("line", "sum"):
            held = spare.pop(0) if kind == "sum" else None
            mixed = spare.pop(0) if kind == "sum" else None
            line_start(axis, kind, src, dst, used[0], held)
            lines.append((axis, kind, src, dst, used[0], held, mixed))
            used[0] += 5
        elif kind == "paired":
            for k in range(2, size, 2):
                copy = remote(src, dst.at[me], {axis: (me + k) % size})
                relays.append((copy, dst, axis, (me + size - k) % size))
            started.append(remote(src, dst.at[me], {axis: me + 1 - 2 * (me % 2)}))
        else:
            for k in range(1, size):
                peer = (me + k) % size
                block = src if kind == "gather" else src.at[peer]
                started.append(remote(block, dst.at[me], {axis: peer}))
    for index, (axis, kind, size) in enumerate(plan):
        me = lax.axis_index(axis)
        block = ins[index].at[me] if kind in ("swap", "sum") else ins[index]
        copy = pltpu.make_async_copy(block, outs[index].at[me], own_sem.at[index])
        copy.start()
        own.append(copy)
    for line in lines:
        line_relay(*line)
    for copy, dst, axis, slot in relays:
        copy.wait_recv()
        me = lax.axis_index(axis)
        started.append(
            remote(dst.at[slot], dst.at[slot], {axis: me + 1 - 2 * (me % 2)})
        )
    for copy, _, _, _ in relays:
        copy.wait_send()
    for copy in own:
        copy.wait()
    for copy in started:
        copy.wait()
    for line in lines:
        line_finish(*line)


def make_exchange():
    calls = [0]

    def exchange(*items):
        plan = []
        shapes = []
        copies = 0
        sent = 0
        spare = []
        for axis, kind, value in items:
            size = lax.axis_size(axis)
            if kind == "paired" and size % 2:
                kind = "gather"
            block = value.shape[1:] if kind == "swap" else value.shape
            if axis == "tensor" and size == 4 and value.dtype == jnp.bfloat16:
                kind = {"swap": "sum", "gather": "line"}[kind]
                if kind == "sum":
                    spare += [pltpu.VMEM(block, value.dtype)] * 2
            plan.append((axis, kind, size))
            copies += 5 if kind in ("line", "sum") else size - 1
            shapes.append(jax.ShapeDtypeStruct((size,) + block, value.dtype))
            sent += (size - 1) * math.prod(block) * value.dtype.itemsize
        collective_id = calls[0]
        calls[0] += 1
        return pl.pallas_call(
            lambda *refs: exchange_kernel(tuple(plan), *refs),
            out_shape=tuple(shapes),
            in_specs=[pl.BlockSpec(memory_space=pltpu.VMEM)] * len(plan),
            out_specs=tuple([pl.BlockSpec(memory_space=pltpu.VMEM)] * len(plan)),
            scratch_shapes=[
                pltpu.SemaphoreType.DMA((copies,)),
                pltpu.SemaphoreType.DMA((copies,)),
                pltpu.SemaphoreType.DMA((len(plan),)),
                *spare,
            ],
            compiler_params=pltpu.CompilerParams(
                collective_id=collective_id,
                has_side_effects=True,
                vmem_limit_bytes=48 * 1024 * 1024,
            ),
            cost_estimate=pl.CostEstimate(flops=0, bytes_accessed=sent, transcendentals=0),
            name=f"exchange_{collective_id}",
        )(*[value for _, _, value in items])

    return exchange


SIBLING, CROSS, FAR, BESIDE, ABOVE, LINE = range(6)
EVERY_PEER = (SIBLING, CROSS, FAR, BESIDE, ABOVE)
AT_UP, AT_SUMMED, AT_OUT, AT_HEADS, AT_LATE, AT_ATTENDED, AT_QKV = range(7)
QKV, OUT, UP, DOWN = "qkv", "out", "up", "down"
MESH = pl.DeviceIdType.MESH


class Place:
    def __init__(self):
        self.dp = lax.axis_index("dp")
        self.z = lax.axis_index("tensor")
        self.core = lax.rem(self.dp, 2)
        self.pair = lax.div(self.z, 2)
        self.low = lax.rem(self.z, 2)
        self.rank = 2 * self.core + self.low
        self.native = self.core == self.pair
        self.block = lax.div(self.dp, 2)
        self.x = lax.rem(self.block, 2)
        self.y = lax.div(self.block, 2)
        self.base = self.dp - self.core

    def sibling(self):
        return {"dp": self.base + 1 - self.core, "tensor": self.z}

    def cross(self, core):
        return {"dp": self.base + core, "tensor": self.z + 1 - 2 * self.low}

    def far(self, core):
        return {"dp": self.base + core, "tensor": self.z + 2 - 4 * self.pair}

    def beside(self):
        return {"dp": self.dp + 2 - 4 * self.x, "tensor": self.z}

    def above(self):
        return {"dp": self.dp + 4 - 8 * self.y, "tensor": self.z}

    def in_line(self, index):
        return {"dp": self.base + lax.rem(index, 2), "tensor": lax.div(index, 2)}

    def rank_at(self, core, low):
        return 2 * core + low

    def block_at(self, dy, dx):
        y = 1 - self.y if dy else self.y
        x = 1 - self.x if dx else self.x
        return 2 * y + x


class Wires:
    def __init__(self, send_sem, recv_sem, own_sem):
        self.send_sem, self.recv_sem, self.own_sem = send_sem, recv_sem, own_sem
        self.used = 0
        self.own_used = 0

    def take(self, count):
        at = self.used
        self.used += count
        return at

    def take_own(self, count=1):
        at = self.own_used
        self.own_used += count
        return at

    def copy(self, src, dst, device, send, recv):
        return pltpu.make_async_remote_copy(
            src_ref=src,
            dst_ref=dst,
            send_sem=self.send_sem.at[send],
            recv_sem=self.recv_sem.at[recv],
            device_id=device,
            device_id_type=MESH,
        )

    def local(self, src, dst, slot):
        return pltpu.make_async_copy(src, dst, self.own_sem.at[slot])


def add_rows(dst, *parts):
    rows = dst.shape[0]
    step = 16 if rows % 16 == 0 else 8

    def body(index, carry):
        at = pl.ds(index * step, step)
        total = parts[0][at].astype(jnp.float32)
        for part in parts[1:]:
            total = total + part[at].astype(jnp.float32)
        dst[at] = total.astype(dst.dtype)
        return carry

    lax.fori_loop(0, rows // step, body, 0)


class Gather:
    peers = (SIBLING, CROSS)
    copies = 5
    owns = 1

    @staticmethod
    def shape(value):
        return (4,) + value.shape

    @staticmethod
    def scratch(value):
        return []

    def __init__(self, place, wires, src, dst, spare):
        self.p, self.w, self.src, self.dst = place, wires, src, dst
        self.at = wires.take(self.copies)
        self.own = wires.take_own()

    def _copies(self):
        p, w, src, dst, at = self.p, self.w, self.src, self.dst, self.at
        other = 1 - p.core
        near = p.rank_at(p.core, 1 - p.low)
        skew = p.rank_at(other, 1 - p.low)
        sib = p.sibling()
        return [
            lambda: w.copy(src, dst.at[p.rank], sib, at, at),
            lambda: w.copy(src.at[p.core], dst.at[p.rank, p.core], p.cross(p.core), at + 1, at + 1),
            lambda: w.copy(src.at[other], dst.at[p.rank, other], p.cross(other), at + 2, at + 2),
            lambda: w.copy(dst.at[near, p.core], dst.at[near, p.core], sib, at + 3, at + 4),
            lambda: w.copy(dst.at[skew, p.core], dst.at[skew, p.core], sib, at + 4, at + 3),
        ]

    def start(self):
        made = self._copies()
        for copy in (made[1], made[2], made[0]):
            copy().start()
        self.w.local(self.src, self.dst.at[self.p.rank], self.own).start()

    def relay(self):
        made = self._copies()
        made[1]().wait_recv()
        made[3]().start()
        made[2]().wait_recv()
        made[4]().start()

    def relay_more(self):
        pass

    def finish(self):
        made = self._copies()
        for index in (0, 3, 4):
            made[index]().wait_recv()
        for copy in made:
            copy().wait_send()
        self.w.local(self.src, self.dst.at[self.p.rank], self.own).wait()


class Reduce:
    peers = (SIBLING, CROSS)
    copies = 3
    owns = 1

    @staticmethod
    def shape(value):
        return (3,) + value.shape[1:]

    @staticmethod
    def scratch(value):
        return [pltpu.VMEM(value.shape[1:], value.dtype)] * 2

    def __init__(self, place, wires, src, dst, spare):
        self.p, self.w, self.src, self.dst = place, wires, src, dst
        self.held, self.mixed = spare
        self.at = wires.take(self.copies)
        self.own = wires.take_own()

    def _copies(self):
        p, w, src, dst, at = self.p, self.w, self.src, self.dst, self.at
        other = 1 - p.core
        sib = p.sibling()
        return [
            lambda: w.copy(src.at[p.rank_at(other, p.low)], dst.at[1], sib, at, at),
            lambda: w.copy(src.at[p.rank_at(other, 1 - p.low)], self.held, sib, at + 1, at + 1),
            lambda: w.copy(self.mixed, dst.at[2], p.cross(p.core), at + 2, at + 2),
        ]

    def start(self):
        made = self._copies()
        made[1]().start()
        made[0]().start()
        self.w.local(self.src.at[self.p.rank], self.dst.at[0], self.own).start()

    def relay(self):
        made = self._copies()
        made[1]().wait_recv()
        add_rows(self.mixed, self.held, self.src.at[self.p.rank_at(self.p.core, 1 - self.p.low)])
        made[2]().start()

    def relay_more(self):
        pass

    def finish(self):
        made = self._copies()
        made[0]().wait_recv()
        made[2]().wait_recv()
        for copy in made:
            copy().wait_send()
        self.w.local(self.src.at[self.p.rank], self.dst.at[0], self.own).wait()


class Pairing:
    peers = (SIBLING, FAR)
    copies = 3
    owns = 1

    @staticmethod
    def shape(value):
        return (2,) + value.shape

    @staticmethod
    def scratch(value):
        return []

    def __init__(self, place, wires, src, dst, spare):
        self.p, self.w, self.src, self.dst = place, wires, src, dst
        self.at = wires.take(self.copies)
        self.own = wires.take_own()

    def _near(self):
        p, at = self.p, self.at
        return self.w.copy(self.src, self.dst.at[p.core], p.sibling(), at, at)

    def _far(self, recv):
        p, at = self.p, self.at
        return self.w.copy(self.src, self.dst.at[p.core], p.far(p.pair), at + 1, recv)

    def start(self):
        p = self.p
        self._far(self.at + 1 + p.core).start()

        @pl.when(p.native)
        def _():
            self.w.local(self.src, self.dst.at[p.core], self.own).start()

        @pl.when(jnp.logical_not(p.native))
        def _():
            self._near().start()

    def settle(self):
        p = self.p

        @pl.when(p.native)
        def _():
            self._near().wait_recv()
            self.w.local(self.src, self.dst.at[p.core], self.own).wait()

        @pl.when(jnp.logical_not(p.native))
        def _():
            self._far(self.at + 1).wait_recv()
            self._far(self.at + 2).wait_recv()

    def sent(self):
        p = self.p
        self._far(self.at + 1).wait_send()

        @pl.when(jnp.logical_not(p.native))
        def _():
            self._near().wait_send()

    def relay(self):
        pass

    def relay_more(self):
        pass

    def finish(self):
        self.settle()
        self.sent()


class Spread:
    peers = (BESIDE, ABOVE)
    copies = 4
    owns = 1

    @staticmethod
    def shape(value):
        return (4,) + value.shape

    @staticmethod
    def scratch(value):
        return []

    def __init__(self, place, wires, src, dst, spare):
        self.p, self.w, self.src, self.dst = place, wires, src, dst
        self.at = wires.take(self.copies)
        self.own = wires.take_own()

    def _copies(self):
        p, w, src, dst, at = self.p, self.w, self.src, self.dst, self.at
        row, column = p.block_at(0, 1), p.block_at(1, 0)
        return [
            lambda: w.copy(src, dst.at[p.block], p.beside(), at, at),
            lambda: w.copy(src, dst.at[p.block], p.above(), at + 1, at + 1),
            lambda: w.copy(dst.at[row, 0], dst.at[row, 0], p.above(), at + 2, at + 2),
            lambda: w.copy(dst.at[column, 1], dst.at[column, 1], p.beside(), at + 3, at + 3),
        ]

    def start(self):
        made = self._copies()
        made[0]().start()
        made[1]().start()
        self.w.local(self.src, self.dst.at[self.p.block], self.own).start()

    def relay(self):
        pass

    def relay_more(self):
        made = self._copies()
        made[0]().wait_recv()
        made[2]().start()
        made[1]().wait_recv()
        made[3]().start()

    def finish(self):
        made = self._copies()
        made[2]().wait_recv()
        made[3]().wait_recv()
        for copy in made:
            copy().wait_send()
        self.w.local(self.src, self.dst.at[self.p.block], self.own).wait()


class Fetch:
    peers = (SIBLING, FAR, BESIDE, ABOVE)
    copies = 7
    owns = 2

    @staticmethod
    def shape(value):
        return (4, 2) + value.shape

    @staticmethod
    def scratch(value):
        return [pltpu.VMEM((2,) + value.shape, value.dtype)]

    def __init__(self, place, wires, src, dst, spare):
        self.one = Pairing(place, wires, src, spare[0], [])
        self.two = Spread(place, wires, spare[0], dst, [])

    def start(self):
        self.one.start()

    def relay(self):
        self.one.settle()
        self.two.start()

    def relay_more(self):
        self.two.relay_more()

    def finish(self):
        self.one.sent()
        self.two.finish()


class Total:
    peers = (BESIDE, ABOVE)
    copies = 6
    owns = 0

    @staticmethod
    def shape(value):
        return value.shape[1:]

    @staticmethod
    def scratch(value):
        one = pltpu.VMEM(value.shape[2:], value.dtype)
        two = pltpu.VMEM(value.shape[1:], value.dtype)
        return [two, two, two, one, one]

    def __init__(self, place, wires, src, dst, spare):
        self.p, self.w, self.src, self.dst = place, wires, src, dst
        self.from_x, self.from_y, self.last, self.to_y, self.to_x = spare
        self.at = wires.take(self.copies)

    def _copies(self):
        p, w, src, at = self.p, self.w, self.src, self.at
        here_x, here_y, skew = p.block_at(0, 1), p.block_at(1, 0), p.block_at(1, 1)
        return [
            lambda: w.copy(src.at[here_x, 0], self.from_x.at[0], p.beside(), at, at),
            lambda: w.copy(src.at[skew, 0], self.from_x.at[1], p.beside(), at + 1, at + 1),
            lambda: w.copy(src.at[here_y, 1], self.from_y.at[0], p.above(), at + 2, at + 2),
            lambda: w.copy(src.at[skew, 1], self.from_y.at[1], p.above(), at + 3, at + 3),
            lambda: w.copy(self.to_y, self.last.at[0], p.above(), at + 4, at + 4),
            lambda: w.copy(self.to_x, self.last.at[1], p.beside(), at + 5, at + 5),
        ]

    def start(self):
        made = self._copies()
        for index in (1, 3, 0, 2):
            made[index]().start()

    def relay(self):
        pass

    def relay_more(self):
        made = self._copies()
        p = self.p
        made[1]().wait_recv()
        add_rows(self.to_y, self.src.at[p.block_at(1, 0), 0], self.from_x.at[1])
        made[4]().start()
        made[3]().wait_recv()
        add_rows(self.to_x, self.src.at[p.block_at(0, 1), 1], self.from_y.at[1])
        made[5]().start()

    def finish(self):
        made = self._copies()
        p = self.p
        for index in (0, 2, 4, 5):
            made[index]().wait_recv()
        add_rows(self.dst.at[0], self.src.at[p.block, 0], self.from_x.at[0], self.last.at[0])
        add_rows(self.dst.at[1], self.src.at[p.block, 1], self.from_y.at[0], self.last.at[1])
        for copy in made:
            copy().wait_send()


class Deliver:
    peers = (SIBLING, FAR)
    copies = 4
    owns = 1

    @staticmethod
    def shape(value):
        return value.shape

    @staticmethod
    def scratch(value):
        return []

    def __init__(self, place, wires, src, dst, spare):
        self.p, self.w, self.src, self.dst = place, wires, src, dst
        self.at = wires.take(self.copies)
        self.own = wires.take_own()

    def _near(self):
        p, at = self.p, self.at
        return self.w.copy(self.src.at[1 - p.core], self.dst.at[0], p.sibling(), at, at)

    def _far(self, core):
        p, at = self.p, self.at
        return self.w.copy(
            self.src.at[core], self.dst.at[1], p.far(jnp.int32(core)), at + 1 + core, at + 1
        )

    def start(self):
        p = self.p

        @pl.when(p.native)
        def _():
            self._near().start()
            self.w.local(self.src.at[p.core], self.dst.at[0], self.own).start()

        @pl.when(jnp.logical_not(p.native))
        def _():
            self._far(0).start()
            self._far(1).start()

    def relay(self):
        pass

    def relay_more(self):
        pass

    def finish(self):
        p = self.p
        self._far(0).wait_recv()

        @pl.when(p.native)
        def _():
            self._near().wait_send()
            self.w.local(self.src.at[p.core], self.dst.at[0], self.own).wait()

        @pl.when(jnp.logical_not(p.native))
        def _():
            self._near().wait_recv()
            self._far(0).wait_send()
            self._far(1).wait_send()


class Swap:
    peers = (FAR,)
    copies = 1
    owns = 1

    @staticmethod
    def shape(value):
        return value.shape

    @staticmethod
    def scratch(value):
        return []

    def __init__(self, place, wires, src, dst, spare):
        self.p, self.w, self.src, self.dst = place, wires, src, dst
        self.at = wires.take(self.copies)
        self.own = wires.take_own()

    def _copy(self):
        p, at = self.p, self.at
        return self.w.copy(self.src, self.dst, p.far(1 - p.core), at, at)

    def start(self):
        @pl.when(self.p.native)
        def _():
            self.w.local(self.src, self.dst, self.own).start()

        @pl.when(jnp.logical_not(self.p.native))
        def _():
            self._copy().start()

    def relay(self):
        pass

    def relay_more(self):
        pass

    def finish(self):
        @pl.when(self.p.native)
        def _():
            self.w.local(self.src, self.dst, self.own).wait()

        @pl.when(jnp.logical_not(self.p.native))
        def _():
            self._copy().wait()


class Small:
    peers = (BESIDE, ABOVE, LINE)
    copies = 20
    owns = 1

    @staticmethod
    def shape(value):
        return (8,) + value.shape[2:]

    @staticmethod
    def scratch(value):
        return Total.scratch(value) + [pltpu.VMEM(value.shape[1:], value.dtype)]

    def __init__(self, place, wires, src, dst, spare):
        self.sums = spare[-1]
        self.total = Total(place, wires, src, self.sums, spare[:-1])
        self.p, self.w, self.dst = place, wires, dst
        self.at = wires.take(14)
        self.own = wires.take_own()

    def _ends(self, offset):
        p, at = self.p, self.at
        me = 2 * p.z + p.core
        to = lax.rem(me + offset, 8)
        return self.w.copy(
            self.sums.at[lax.rem(to, 2)], self.dst.at[me], p.in_line(to), at + offset - 1, at + 6 + offset
        )

    def _mine(self):
        p = self.p
        return self.w.local(self.sums.at[p.core], self.dst.at[2 * p.z + p.core], self.own)

    def start(self):
        self.total.start()

    def relay(self):
        pass

    def relay_more(self):
        self.total.relay_more()
        self.total.finish()
        for offset in range(1, 8):
            self._ends(offset).start()
        self._mine().start()

    def finish(self):
        self._mine().wait()
        for offset in range(1, 8):
            self._ends(offset).wait()


def greet(place, kinds):
    p = place
    devices = []
    if SIBLING in kinds or LINE in kinds:
        devices.append(p.sibling())
    if CROSS in kinds or LINE in kinds:
        devices += [p.cross(jnp.int32(0)), p.cross(jnp.int32(1))]
    if FAR in kinds or LINE in kinds:
        devices += [p.far(jnp.int32(0)), p.far(jnp.int32(1))]
    if LINE in kinds:
        last = 3 - p.z
        devices += [{"dp": p.base, "tensor": last}, {"dp": p.base + 1, "tensor": last}]
    if BESIDE in kinds:
        devices.append(p.beside())
    if ABOVE in kinds:
        devices.append(p.above())
    barrier = pltpu.get_barrier_semaphore()
    for device in devices:
        pl.semaphore_signal(barrier, inc=1, device_id=device, device_id_type=MESH)
    pl.semaphore_wait(barrier, len(devices))


def round_kernel(kinds, *refs):
    count = len(kinds)
    ins, outs = refs[:count], refs[count : 2 * count]
    wires = Wires(*refs[2 * count : 2 * count + 3])
    spare = list(refs[2 * count + 3 :])
    place = Place()
    greet(place, {peer for kind, _ in kinds for peer in kind.peers})
    jobs = []
    for (kind, held), src, dst in zip(kinds, ins, outs):
        jobs.append(kind(place, wires, src, dst, spare[:held]))
        del spare[:held]
    for job in jobs:
        job.start()
    for job in jobs:
        job.relay()
    for job in jobs:
        job.relay_more()
    for job in jobs:
        job.finish()


def make_rounds():
    calls = [0]

    def rounds(*items):
        kinds, shapes, scratch = [], [], []
        copies = owns = sent = 0
        for kind, value in items:
            held = kind.scratch(value)
            kinds.append((kind, len(held)))
            scratch += held
            shapes.append(jax.ShapeDtypeStruct(kind.shape(value), value.dtype))
            copies += kind.copies
            owns += kind.owns
            sent += math.prod(kind.shape(value)) * value.dtype.itemsize
        collective_id = calls[0]
        calls[0] += 1
        return pl.pallas_call(
            lambda *refs: round_kernel(tuple(kinds), *refs),
            out_shape=tuple(shapes),
            in_specs=[pl.BlockSpec(memory_space=pltpu.VMEM)] * len(kinds),
            out_specs=tuple([pl.BlockSpec(memory_space=pltpu.VMEM)] * len(kinds)),
            scratch_shapes=[
                pltpu.SemaphoreType.DMA((copies,)),
                pltpu.SemaphoreType.DMA((copies,)),
                pltpu.SemaphoreType.DMA((max(owns, 1),)),
                *scratch,
            ],
            compiler_params=pltpu.CompilerParams(
                collective_id=collective_id,
                has_side_effects=True,
                vmem_limit_bytes=48 * 1024 * 1024,
            ),
            cost_estimate=pl.CostEstimate(flops=0, bytes_accessed=sent, transcendentals=0),
            name=f"round_{collective_id}",
        )(*[value for _, value in items])

    return rounds


def masked_scores(queries, key_vecs, segments, score_scale):
    positions = jnp.arange(key_vecs.shape[0], dtype=jnp.int32)
    allowed = (segments[:, None] == segments[None, :]) & (
        positions[None, :] <= positions[:, None]
    )
    scores = (
        jnp.einsum("qhd,khd->hqk", queries, key_vecs, preferred_element_type=jnp.float32)
        * score_scale
    )
    return jnp.where(allowed[None], scores, -jnp.inf)


def attend(queries, key_vecs, val_vecs, segments, score_scale):
    scores = masked_scores(queries, key_vecs, segments, score_scale)
    row_max = jnp.max(scores, axis=-1, keepdims=True)
    log_total = row_max + jnp.log(jnp.sum(jnp.exp(scores - row_max), axis=-1, keepdims=True))
    probs_half = jnp.exp(scores - log_total).astype(jnp.bfloat16)
    attended = jnp.einsum("hqk,khd->qhd", probs_half, val_vecs, preferred_element_type=jnp.float32)
    return (attended.astype(jnp.bfloat16).reshape(queries.shape[0], -1), log_total)


def attend_back(queries, key_vecs, val_vecs, grad_attended, log_total, segments, score_scale):
    scores = masked_scores(queries, key_vecs, segments, score_scale)
    soft_probs = jnp.exp(scores - log_total)
    probs_half = soft_probs.astype(jnp.bfloat16)
    grad_probs = jnp.einsum(
        "qhd,khd->hqk", grad_attended, val_vecs, preferred_element_type=jnp.float32
    )
    val_grad = jnp.einsum(
        "hqk,qhd->khd", probs_half, grad_attended, preferred_element_type=jnp.float32
    )
    row_dot = jnp.sum(grad_probs * soft_probs, axis=-1, keepdims=True)
    score_grad = (soft_probs * (grad_probs - row_dot) * score_scale).astype(jnp.bfloat16)
    query_grad = jnp.einsum(
        "hqk,khd->qhd", score_grad, key_vecs, preferred_element_type=jnp.float32
    )
    key_grad = jnp.einsum("hqk,qhd->khd", score_grad, queries, preferred_element_type=jnp.float32)
    return (query_grad, key_grad, val_grad)


def pack(pieces, width, tile):
    flat = jnp.concatenate([piece.reshape(-1) for piece in pieces])
    unit = width * tile
    return jnp.pad(flat, (0, -flat.shape[0] % unit)).reshape(-1, width)


def unpack(packed, shapes):
    flat = packed.reshape(packed.shape[0], -1)
    pieces = []
    at = 0
    for shape in shapes:
        length = math.prod(shape)
        pieces.append(flat[:, at : at + length].reshape((packed.shape[0],) + shape))
        at += length
    return pieces


def shards(x_in, d_out, seq_lengths, w_qkv, b_qv, w_o, w_1, b_ffn, w_2, norm_gains, vec_biases):
    exchange = make_exchange()
    own_rows, width = x_in.shape
    tensor_size = lax.axis_size("tensor")
    dp_size = lax.axis_size("dp")
    group_rows = own_rows * tensor_size
    layer_count = w_qkv.shape[0]
    local_width = w_qkv.shape[3]
    local_heads = local_width // HEAD_DIM
    qkv_width = 3 * local_width
    score_scale = 1.0 / math.sqrt(HEAD_DIM)
    segments = segment_ids(seq_lengths[0], group_rows)
    half = jnp.bfloat16

    def shard_of(name, layer_index):
        if name == "qkv":
            return w_qkv[layer_index].reshape(w_qkv.shape[1], qkv_width)
        if name == "out":
            return w_o[layer_index].T
        if name == "up":
            return w_1[layer_index]
        return w_2[layer_index].T

    weights = {}

    def step(tensor_items, fetched=(), sums=()):
        items = [("tensor", kind, value) for kind, value in tensor_items]
        items += [("dp", "paired", shard_of(*key)) for key in fetched]
        items += [("dp", "swap", value) for value in sums]
        results = list(exchange(*items))
        for position, key in enumerate(fetched):
            piece = results[len(tensor_items) + position]
            weights[key] = piece.reshape(dp_size * piece.shape[1], piece.shape[2])
        gathered = [
            piece.reshape(group_rows, width) if kind == "gather" else piece.astype(jnp.float32).sum(0)
            for (kind, _), piece in zip(tensor_items, results)
        ]
        totals = [
            piece.astype(jnp.float32).sum(0) for piece in results[len(items) - len(sums) :]
        ]
        return gathered, totals

    def to_owners(partial):
        return ("swap", partial.astype(half).reshape(tensor_size, own_rows, width))

    def by_owner(gradient):
        return gradient.astype(half).reshape(dp_size, -1, gradient.shape[-1])

    small_shapes = [b_qv.shape, b_ffn.shape, norm_gains.shape, vec_biases.shape]
    small = pack([b_qv, b_ffn, norm_gains, vec_biases], 128, 16)
    first = exchange(
        ("tensor", "gather", d_out.astype(half)),
        ("dp", "paired", small),
        ("dp", "paired", shard_of("qkv", 0)),
    )
    last_grad_half = first[0].reshape(group_rows, width)
    weights["qkv", 0] = first[2].reshape(width, qkv_width)
    qv_all, ffn_all, gain_all, bias_all = [
        jnp.moveaxis(piece, 0, -2).reshape(piece.shape[1:-1] + (-1,)).astype(jnp.float32)
        for piece in unpack(first[1], small_shapes)
    ]

    caches = []
    hidden_in = x_in
    for layer_index in range(layer_count):
        last = layer_index == layer_count - 1
        following = layer_index + 1
        gain_rows = gain_all[layer_index]
        bias_rows = bias_all[layer_index]
        normed_own, unit_one, inv_one = layer_norm(hidden_in, gain_rows[0], bias_rows[0])
        fetched = [("out", 0), ("up", 0)] if layer_index == 0 else [("down", layer_index)]
        (normed_one,), _ = step([("gather", normed_own.astype(half))], fetched)
        projected = jnp.dot(
            normed_one, weights["qkv", layer_index], preferred_element_type=jnp.float32
        ).reshape(group_rows, 3, local_width)
        qv_bias = qv_all[layer_index]
        heads = (group_rows, local_heads, HEAD_DIM)
        queries = (projected[:, 0] + qv_bias[0]).astype(half).reshape(heads)
        key_vecs = projected[:, 1].astype(half).reshape(heads)
        val_vecs = (projected[:, 2] + qv_bias[1]).astype(half).reshape(heads)
        attended, log_total = attend(queries, key_vecs, val_vecs, segments, score_scale)
        fetched = [("down", 0)] if layer_index == 0 else []
        (summed,), _ = step(
            [to_owners(contract_last(attended, weights["out", layer_index]))], fetched
        )
        residual_mid = hidden_in + summed + bias_rows[2]
        normed_own_two, unit_two, inv_two = layer_norm(residual_mid, gain_rows[1], bias_rows[1])
        fetched = [] if last else [("qkv", following), ("out", following)]
        (normed_two,), _ = step([("gather", normed_own_two.astype(half))], fetched)
        pre_act = (
            jnp.dot(normed_two, weights["up", layer_index], preferred_element_type=jnp.float32)
            + ffn_all[layer_index]
        )
        gelu_value, gelu_slope = gelu_pair(pre_act)
        activated = gelu_value.astype(half)
        ffn_partial = to_owners(contract_last(activated, weights["down", layer_index]))
        if not last:
            (summed,), _ = step([ffn_partial], [("up", following)])
            hidden_in = residual_mid + summed + bias_rows[3]
        caches.append(
            (
                unit_one,
                inv_one,
                normed_one,
                queries,
                key_vecs,
                val_vecs,
                attended,
                log_total,
                unit_two,
                inv_two,
                normed_two,
                activated,
                gelu_slope,
            )
        )
    back = d_out
    grads = {}
    small_terms = [None] * layer_count
    output = None
    for layer_index in reversed(range(layer_count)):
        last = layer_index == layer_count - 1
        gain_rows = gain_all[layer_index]
        (
            unit_one,
            inv_one,
            normed_one,
            queries,
            key_vecs,
            val_vecs,
            attended,
            log_total,
            unit_two,
            inv_two,
            normed_two,
            activated,
            gelu_slope,
        ) = caches[layer_index]
        if last:
            grad_half = last_grad_half
        else:
            (grad_half,), (grads["qkv", layer_index + 1],) = step(
                [("gather", back.astype(half))], sums=[waiting]
            )
        grad_down = by_owner(contract_first(grad_half, activated))
        grad_pre = (
            jnp.dot(grad_half, weights["down", layer_index], preferred_element_type=jnp.float32)
            * gelu_slope
        )
        grad_pre_half = grad_pre.astype(half)
        grad_up = by_owner(contract_first(normed_two, grad_pre_half))
        partial = to_owners(contract_last(grad_pre_half, weights["up", layer_index]))
        if last:
            cut = grad_up.shape[2] // 2
            (grad_normed_two, summed), (grads["down", layer_index], up_left) = step(
                [partial, ffn_partial], sums=[grad_down, grad_up[:, :, :cut]]
            )
            output = residual_mid + summed + bias_all[layer_index][3]
        else:
            (grad_normed_two,), (grads["down", layer_index],) = step([partial], sums=[grad_down])
        grad_mid = back + norm_back(grad_normed_two, unit_two, inv_two, gain_rows[1])
        (grad_mid_half,), (up_part,) = step(
            [("gather", grad_mid.astype(half))], sums=[grad_up[:, :, cut:] if last else grad_up]
        )
        grads["up", layer_index] = (
            jnp.concatenate([up_left, up_part], axis=1) if last else up_part
        )
        grad_out = by_owner(contract_first(grad_mid_half, attended))
        grad_attended = jnp.dot(
            grad_mid_half, weights["out", layer_index], preferred_element_type=jnp.float32
        )
        grad_attended = grad_attended.astype(half).reshape(group_rows, local_heads, HEAD_DIM)
        query_grad, key_grad, val_grad = attend_back(
            queries, key_vecs, val_vecs, grad_attended, log_total, segments, score_scale
        )
        flat = (group_rows, local_width)
        grad_qkv = jnp.concatenate(
            [part.astype(half).reshape(flat) for part in (query_grad, key_grad, val_grad)], axis=1
        )
        grad_qkv_weight = by_owner(contract_first(normed_one, grad_qkv))
        (grad_normed_one,), sent_now = step(
            [to_owners(contract_last(grad_qkv, weights["qkv", layer_index]))],
            sums=[grad_out] if layer_index else [grad_out, grad_qkv_weight],
        )
        grads["out", layer_index] = sent_now[0]
        if layer_index:
            waiting = grad_qkv_weight
        else:
            grads["qkv", layer_index] = sent_now[1]
        small_terms[layer_index] = (
            jnp.stack(
                [
                    jnp.sum(query_grad, axis=0).reshape(local_width),
                    jnp.sum(val_grad, axis=0).reshape(local_width),
                ]
            ),
            jnp.sum(grad_pre, axis=0),
            jnp.stack(
                [
                    jnp.sum(grad_normed_one * unit_one, axis=0),
                    jnp.sum(grad_normed_two * unit_two, axis=0),
                ]
            ),
            jnp.stack(
                [
                    jnp.sum(grad_normed_one, axis=0),
                    jnp.sum(grad_normed_two, axis=0),
                    jnp.sum(grad_mid, axis=0),
                    jnp.sum(back, axis=0),
                ]
            ),
        )
        back = grad_mid + norm_back(grad_normed_one, unit_one, inv_one, gain_rows[0])

    def split_owner(piece):
        return jnp.moveaxis(
            piece.reshape(piece.shape[:-1] + (dp_size, -1)), -2, 0
        ).reshape(dp_size, -1)

    stacked = [
        split_owner(jnp.stack([small_terms[index][member] for index in range(layer_count)]))
        for member in (2, 3, 0, 1)
    ]
    flat = jnp.concatenate(stacked, axis=1)
    flat = jnp.pad(flat, ((0, 0), (0, -flat.shape[1] % 1024)))
    (parts,) = exchange(("dp", "swap", flat.reshape(dp_size, -1, 128)))
    total = parts.sum(0)
    (shared,) = exchange(("tensor", "gather", total))
    everyone = shared.sum(0).reshape(-1)
    gain_size, bias_size = norm_gains.size, vec_biases.size
    mine = total.reshape(-1)[gain_size + bias_size :]

    def stack_layers(name, shape, transposed):
        parts = [grads[name, index] for index in range(layer_count)]
        return jnp.stack([part.T if transposed else part for part in parts]).reshape(shape)

    return (
        output,
        back,
        stack_layers("qkv", w_qkv.shape, False),
        mine[: b_qv.size].reshape(b_qv.shape),
        stack_layers("out", w_o.shape, True),
        stack_layers("up", w_1.shape, False),
        mine[b_qv.size : b_qv.size + b_ffn.size].reshape(b_ffn.shape),
        stack_layers("down", w_2.shape, True),
        everyone[:gain_size].reshape(norm_gains.shape),
        everyone[gain_size : gain_size + bias_size].reshape(vec_biases.shape),
    )


def dot_nn(left, right):
    return jnp.dot(left, right, preferred_element_type=jnp.float32)


class GatherHere(Gather):
    def __init__(self, place, wires, dst):
        super().__init__(place, wires, dst.at[place.rank], dst, [])

    def start(self):
        made = self._copies()
        for index in (1, 2, 0):
            made[index]().start()

    def wait_sibling(self):
        self._copies()[0]().wait_recv()

    def finish(self):
        made = self._copies()
        for index in (3, 4):
            made[index]().wait_recv()
        for copy in made:
            copy().wait_send()


class ReduceHere(Reduce):
    def __init__(self, place, wires, src, dst, spare):
        super().__init__(place, wires, src, dst, spare)

    def _copies(self):
        p, w, src, dst, at = self.p, self.w, self.src, self.dst, self.at
        other = 1 - p.core
        sib = p.sibling()
        return [
            lambda: w.copy(src.at[p.rank_at(other, p.low)], dst.at[0], sib, at, at),
            lambda: w.copy(src.at[p.rank_at(other, 1 - p.low)], self.held, sib, at + 1, at + 1),
            lambda: w.copy(self.mixed, dst.at[1], p.cross(p.core), at + 2, at + 2),
        ]

    def start_cross(self):
        self._copies()[1]().start()

    def start_near(self):
        self._copies()[0]().start()

    def finish(self):
        made = self._copies()
        made[0]().wait_recv()
        made[2]().wait_recv()
        for copy in made:
            copy().wait_send()

    def total(self, rows):
        first = self.src[self.p.rank, rows].astype(jnp.float32)
        return first + self.dst[0, rows].astype(jnp.float32) + self.dst[1, rows].astype(jnp.float32)


class Env:
    pass


class Mover:
    def __init__(self, wires):
        self.wires = wires
        self.open = {}

    def start(self, src, dst, name):
        slot = self.wires.take_own()
        self.open[name] = (src, dst, slot)
        self.wires.local(src, dst, slot).start()

    def wait(self, *names):
        for name in names or list(self.open):
            self.wires.local(*self.open.pop(name)).wait()


def make_fused():
    calls = [32]

    def fused(body, ins, outs, scratch, kinds, hbm=()):
        names_in, names_out, names_spare = list(ins), list(outs), list(scratch)

        def kernel(*refs):
            k = Env()
            refs = list(refs)
            for name in names_in + names_out:
                setattr(k, name, refs.pop(0))
            k.wires = Wires(*refs[:3])
            for name, ref in zip(names_spare, refs[3:]):
                setattr(k, name, ref)
            k.place = Place()
            greet(k.place, kinds)
            body(k)
            assert k.wires.used <= 320 and k.wires.own_used <= 192

        collective_id = calls[0]
        calls[0] += 1
        results = pl.pallas_call(
            kernel,
            out_shape=tuple(jax.ShapeDtypeStruct(*outs[name]) for name in names_out),
            in_specs=[
                pl.BlockSpec(memory_space=pltpu.HBM if name in hbm else pltpu.VMEM)
                for name in names_in
            ],
            out_specs=tuple(
                pl.BlockSpec(memory_space=pltpu.HBM if name in hbm else pltpu.VMEM)
                for name in names_out
            ),
            scratch_shapes=[
                pltpu.SemaphoreType.DMA((320,)),
                pltpu.SemaphoreType.DMA((320,)),
                pltpu.SemaphoreType.DMA((192,)),
                *[pltpu.VMEM(*scratch[name]) for name in names_spare],
            ],
            compiler_params=pltpu.CompilerParams(
                collective_id=collective_id,
                has_side_effects=True,
                vmem_limit_bytes=60 * 1024 * 1024,
            ),
            cost_estimate=pl.CostEstimate(
                flops=0, bytes_accessed=16 * 1024 * 1024, transcendentals=0
            ),
            name=f"fused_{collective_id}",
        )(*[ins[name] for name in names_in])
        made = Env()
        made.__dict__.update(zip(names_out, results))
        return made

    return fused


def chips(place):
    other = 1 - place.core
    return (
        (place.rank, place.rank_at(other, place.low)),
        (place.rank_at(place.core, 1 - place.low), place.rank_at(other, 1 - place.low)),
    )


def two(ref, ranks, lanes=slice(None)):
    parts = [ref[rank, ..., lanes] for rank in ranks]
    return jnp.concatenate([part.reshape(-1, part.shape[-1]) for part in parts], axis=0)


def whole(ref, lanes=slice(None)):
    part = ref[..., lanes]
    return part.reshape(-1, part.shape[-1])


def put_two(ref, ranks, value, lanes=slice(None)):
    rows = value.shape[0] // 2
    ref[ranks[0], :, lanes] = value[:rows].astype(ref.dtype)
    ref[ranks[1], :, lanes] = value[rows:].astype(ref.dtype)


def lanes_at(index, size=256):
    return pl.ds(pl.multiple_of(index * size, size), size)


def loop(count, body):
    def step(index, carry):
        body(index)
        return carry

    lax.fori_loop(0, count, step, 0)


def columns_of(ref, block):
    return jnp.concatenate([ref[block, 0], ref[block, 1]], axis=1)


def all_columns(ref, rows):
    return jnp.concatenate([ref[block, core, rows] for block in range(4) for core in range(2)], axis=1)


ROWS = 32


def visible(k, block):
    shape = (128, (block + 1) * 128)
    end = k.lengths[0:1, 0:1].astype(jnp.int32)
    at_query = lax.broadcasted_iota(jnp.int32, shape, 0) + block * 128
    at_key = lax.broadcasted_iota(jnp.int32, shape, 1)
    late_query = jnp.where(at_query >= end, 1, 0)
    late_key = jnp.where(at_key >= end, 1, 0)
    return (late_query == late_key) & (at_key <= at_query)


def attention_forward(k, on_sent, on_gathered, on_middle, on_attended):
    p = k.place
    here, there = chips(p)
    for at in range(4):
        rows = pl.ds(at * ROWS, ROWS)
        normed, _, _ = layer_norm(k.hidden[rows], k.vecs[0:1], k.vecs[2:3])
        k.n1[p.rank, at // 2, pl.ds(at % 2 * ROWS, ROWS)] = normed.astype(jnp.bfloat16)
    gather = GatherHere(p, k.wires, k.n1)
    gather.start()
    on_sent()

    def project(ranks):
        rows = two(k.n1, ranks)
        for index, (dst, bias) in enumerate(((k.q, 0), (k.key, None), (k.val, 1))):
            weight = k.w_qkv[:, :, index * 128 : index * 128 + 128].reshape(1024, 256)
            made = dot_nn(rows, weight)
            if bias is not None:
                made = made + k.qv_bias[bias : bias + 1]
            put_two(dst, ranks, made)

    gather.wait_sibling()
    gather.relay()
    on_gathered()
    project(here)
    gather.finish()
    project(there)
    scale = 1.0 / math.sqrt(HEAD_DIM)
    for block in range(4):
        if block in (1, 3):
            on_middle(block)
        seen = visible(k, block)
        count = (block + 1) * 128
        for head in range(4):
            lanes = slice(head * HEAD_DIM, head * HEAD_DIM + HEAD_DIM)
            keys = k.key[: block + 1, :, lanes].reshape(count, HEAD_DIM)
            vals = k.val[: block + 1, :, lanes].reshape(count, HEAD_DIM)
            scores = contract_last(k.q[block, :, lanes], keys) * scale
            scores = jnp.where(seen, scores, -jnp.inf)
            raised = jnp.exp(scores - jnp.max(scores, axis=-1, keepdims=True))
            probs = raised * (1.0 / jnp.sum(raised, axis=-1, keepdims=True))
            probs = probs.astype(jnp.bfloat16)
            k.probs[head, pl.ds(block * 128, 128), :count] = probs
            k.att[block, :, lanes] = dot_nn(probs, vals).astype(jnp.bfloat16)
    on_attended()

    def out(ranks):
        rows = two(k.att, ranks)

        def column(block):
            put_two(k.part_a, ranks, dot_nn(rows, columns_of(k.w_out, block)), lanes_at(block))

        loop(4, column)

    reduce = ReduceHere(p, k.wires, k.part_a, k.got_a, (k.held_a, k.mixed_a))
    out(there)
    reduce.start_cross()
    out(here)
    reduce.start_near()
    reduce.relay()
    return reduce


def feed_forward(k, reduce, on_sent, on_gathered, on_raised, part):
    p = k.place
    here, there = chips(p)
    reduce.finish()
    for at in range(4):
        rows = pl.ds(at * ROWS, ROWS)
        mid = k.hidden[rows] + reduce.total(rows) + k.vecs[4:5]
        k.mid[rows] = mid
        normed, _, _ = layer_norm(mid, k.vecs[1:2], k.vecs[3:4])
        k.n2[p.rank, at // 2, pl.ds(at % 2 * ROWS, ROWS)] = normed.astype(jnp.bfloat16)
    gather = GatherHere(p, k.wires, k.n2)
    gather.start()
    on_sent()

    def up(ranks):
        def column(index):
            lanes = lanes_at(index)
            rows = two(k.n2, ranks)
            weight = k.w_up[:, :, :, lanes].reshape(1024, 256)
            pre_act = dot_nn(rows, weight) + k.ffn_bias[0:1, lanes]
            value, slope = gelu_pair(pre_act)
            put_two(k.act, ranks, value, lanes)
            put_two(k.slope, ranks, slope, lanes)

        loop(4, column)

    gather.wait_sibling()
    gather.relay()
    on_gathered()
    up(here)
    gather.finish()
    up(there)
    on_raised()

    def down(ranks):
        def column(block):
            rows = two(k.act, ranks)
            put_two(part, ranks, dot_nn(rows, columns_of(k.w_down, block)), lanes_at(block))

        loop(4, column)

    return down, here, there


def unpack_small(small_all, views):
    parts = [small_all[block, core].astype(jnp.float32) for block in range(4) for core in range(2)]

    def row(index):
        return jnp.concatenate([part[index : index + 1] for part in parts], axis=1)

    for layer, k in enumerate(views):
        for index in range(2):
            k.vecs[index : index + 1] = row(3 + 2 * layer + index)
            at = 64 * layer + 32 * index
            k.qv_bias[index : index + 1] = jnp.concatenate(
                [part[0:1, at : at + 32] for part in parts], axis=1
            )
        for index in range(4):
            k.vecs[2 + index : 3 + index] = row(7 + 4 * layer + index)
        k.ffn_bias[0:1] = row(1 + layer)


def pack_small(flat, layers):
    flat[...] = jnp.zeros(flat.shape, flat.dtype)
    for shard in range(8):
        block, core = shard // 2, shard % 2
        lanes = slice(shard * 128, shard * 128 + 128)
        quarter = slice(shard * 32, shard * 32 + 32)
        pieces = []
        for layer, (col, col_qv, col_ffn) in enumerate(layers):
            flat[block, core, 2 * layer : 2 * layer + 2] = col[0:2, lanes]
            flat[block, core, 4 + 4 * layer : 8 + 4 * layer] = col[2:6, lanes]
            flat[block, core, 13 + layer : 14 + layer] = col_ffn[0:1, lanes]
            pieces += [col_qv[0:1, quarter], col_qv[1:2, quarter]]
        flat[block, core, 12:13] = jnp.concatenate(pieces, axis=1)


def feed_forward_back(k, gather, on_gathered, on_grad_down):
    p = k.place
    here, there = chips(p)

    def pre(ranks, first):
        def rows_of(index):
            lanes = lanes_at(index)
            weight = all_columns(k.w_down, lanes)
            grad = contract_last(two(k.gh, ranks), weight) * two(k.slope, ranks, lanes).astype(
                jnp.float32
            )
            put_two(k.gp, ranks, grad, lanes)
            summed = jnp.sum(grad, axis=0, keepdims=True)
            k.col_ffn[0:1, lanes] = summed if first else k.col_ffn[0:1, lanes] + summed

        loop(4, rows_of)

    if gather is not None:
        gather.wait_sibling()
        gather.relay()
    on_gathered()
    pre(here, True)
    if gather is not None:
        gather.finish()

    def turn(index):
        lanes = lanes_at(index)
        k.turned[lanes] = whole(k.act, lanes).T

    loop(4, turn)

    def grad_down(block):
        made = dot_nn(k.turned[...], whole(k.gh, lanes_at(block)))
        k.g_down[block, 0] = made[:, :128].astype(jnp.bfloat16)
        k.g_down[block, 1] = made[:, 128:].astype(jnp.bfloat16)

    loop(4, grad_down)
    on_grad_down()
    pre(there, False)

    def term(ranks):
        def column(block):
            rows = two(k.gp, ranks)
            weight = k.w_up[block].reshape(256, 1024)
            put_two(k.part_a, ranks, contract_last(rows, weight), lanes_at(block))

        loop(4, column)

    reduce = ReduceHere(p, k.wires, k.part_a, k.got_a, (k.held_a, k.mixed_a))
    term(there)
    reduce.start_cross()
    term(here)
    reduce.start_near()
    reduce.relay()
    return reduce


def grad_up(k):
    def rows_of(block):
        turned = whole(k.n2, lanes_at(block)).T
        made = dot_nn(turned, whole(k.gp))
        k.g_up[block] = made.astype(jnp.bfloat16).reshape(2, 128, 1024)

    loop(4, rows_of)


def through_norm(k, reduce, hidden, back, sums, gain, dst, put):
    totals = None
    for at in range(4):
        rows = pl.ds(at * ROWS, ROWS)
        grad = reduce.total(rows)
        _, unit, inv = layer_norm(hidden[rows], 1.0, 0.0)
        was = back[rows]
        now = was + norm_back(grad, unit, inv, k.vecs[gain : gain + 1])
        dst[rows] = now
        put(at, now)
        terms = [grad * unit, grad, now, was]
        terms = [jnp.sum(term, axis=0, keepdims=True) for term in terms]
        totals = terms if totals is None else [a + b for a, b in zip(totals, terms)]
    for row, total in zip(sums, totals):
        if row is not None:
            k.col[row : row + 1] = total


def grad_qkv_thirds(k, third):
    def turn(index):
        lanes = lanes_at(index)
        k.turned[lanes] = whole(k.n1, lanes).T

    loop(4, turn)
    for index in range(3):
        rows = pl.ds(index * 128, 128)

        def grad_qkv(block):
            made = dot_nn(k.turned[lanes_at(block)], whole(k.gq.at[index]))
            k.g_qkv[block, :, rows] = made.astype(jnp.bfloat16).reshape(2, 128, 256)

        loop(4, grad_qkv)
        third(index)

def attention_back(k, reduce, background, third, weights_first):
    p = k.place
    here, there = chips(p)
    grad_up(k)
    background(AT_UP)
    reduce.finish()
    background(AT_SUMMED)

    def put(at, now):
        k.gm[p.rank, at // 2, pl.ds(at % 2 * ROWS, ROWS)] = now.astype(jnp.bfloat16)

    through_norm(k, reduce, k.mid, k.back, (1, 3, 4, 5), 1, k.grad_mid, put)
    gather = GatherHere(p, k.wires, k.gm)
    gather.start()

    def attended(ranks):
        weight = all_columns(k.w_out, slice(None))
        put_two(k.ga, ranks, contract_last(two(k.gm, ranks), weight))

    gather.wait_sibling()
    gather.relay()
    attended(here)
    gather.finish()
    attended(there)

    def grad_out(block):
        made = dot_nn(whole(k.att).T, whole(k.gm, lanes_at(block)))
        k.g_out[block, 0] = made[:, :128].astype(jnp.bfloat16)
        k.g_out[block, 1] = made[:, 128:].astype(jnp.bfloat16)

    loop(4, grad_out)
    background(AT_OUT)
    scale = 1.0 / math.sqrt(HEAD_DIM)
    for head in range(4):
        lanes = slice(head * HEAD_DIM, head * HEAD_DIM + HEAD_DIM)
        for block in range(4):
            rows = pl.ds(block * 128, 128)
            count = (block + 1) * 128
            keys = k.key[: block + 1, :, lanes].reshape(count, HEAD_DIM)
            vals = k.val[: block + 1, :, lanes].reshape(count, HEAD_DIM)
            probs = k.probs[head, rows, :count].astype(jnp.float32)
            grad_probs = contract_last(k.ga[block, :, lanes], vals)
            row_dot = jnp.sum(grad_probs * probs, axis=-1, keepdims=True)
            score_grad = (probs * (grad_probs - row_dot) * scale).astype(jnp.bfloat16)
            k.ds[head % 2, rows, :count] = score_grad
            query_grad = dot_nn(score_grad, keys)
            k.gq[0, block, :, lanes] = query_grad.astype(jnp.bfloat16)
            summed = jnp.sum(query_grad, axis=0, keepdims=True)
            k.col_qv[0:1, lanes] = summed if block == 0 else k.col_qv[0:1, lanes] + summed
        if head in (0, 2):
            background(AT_LATE if head else AT_HEADS)
        for block in range(4):
            below = pl.ds(block * 128, 512 - block * 128)
            cols = slice(block * 128, block * 128 + 128)
            count = 512 - block * 128
            queries = k.q[block:, :, lanes].reshape(count, HEAD_DIM)
            grads = k.ga[block:, :, lanes].reshape(count, HEAD_DIM)
            key_grad = contract_first(k.ds[head % 2, below, cols], queries)
            val_grad = contract_first(k.probs[head, below, cols], grads)
            k.gq[1, block, :, lanes] = key_grad.astype(jnp.bfloat16)
            k.gq[2, block, :, lanes] = val_grad.astype(jnp.bfloat16)
            summed = jnp.sum(val_grad, axis=0, keepdims=True)
            k.col_qv[1:2, lanes] = summed if block == 0 else k.col_qv[1:2, lanes] + summed
    background(AT_ATTENDED)

    if weights_first:
        grad_qkv_thirds(k, third)

    def term(ranks):
        rows = [two(k.gq.at[index], ranks) for index in range(3)]

        def column(block):
            made = None
            for index in range(3):
                weight = k.w_qkv[block, :, index * 128 : index * 128 + 128].reshape(256, 256)
                one = contract_last(rows[index], weight)
                made = one if made is None else made + one
            put_two(k.part_b, ranks, made, lanes_at(block))

        loop(4, column)

    reduce = ReduceHere(p, k.wires, k.part_b, k.got_b, (k.held_b, k.mixed_b))
    term(there)
    reduce.start_cross()
    term(here)
    reduce.start_near()
    reduce.relay()

    if not weights_first:
        grad_qkv_thirds(k, third)
    background(AT_QKV)
    reduce.finish()
    through_norm(
        k, reduce, k.hidden, k.grad_mid, (0, 2, None, None), 0, k.back_out, lambda at, now: None
    )


def total_scratch(name, rows, cols, half=jnp.bfloat16):
    one, two = ((rows, cols), half), ((2, rows, cols), half)
    return {f"{name}_t{index}": value for index, value in enumerate((two, two, two, one, one))}


def paired_shards(
    x_in, d_out, seq_lengths, w_qkv, b_qv, w_o, w_1, b_ffn, w_2, norm_gains, vec_biases
):
    fused = make_fused()
    own_rows, width = x_in.shape
    layer_count = w_qkv.shape[0]
    half, full = jnp.bfloat16, jnp.float32
    z = lax.axis_index("tensor")
    qkv_turned = jnp.transpose(w_qkv, (0, 2, 1, 3)).reshape(layer_count, 384, 256)
    shapes = {QKV: (384, 256), OUT: (256, 128), UP: (128, 1024), DOWN: (1024, 128)}
    def pair_spec(name):
        return ((2,) + shapes[name], half)

    def full_spec(name):
        return ((4, 2) + shapes[name], half)

    def added(parts):
        return parts[0].astype(full) + parts[1].astype(full)

    small_shapes = [b_qv.shape, b_ffn.shape, norm_gains.shape, vec_biases.shape]
    small = pack([b_qv, b_ffn, norm_gains, vec_biases], 128, 16)
    lengths = jnp.pad(seq_lengths.astype(full), ((0, 7), (0, 126)))

    rows_spec = ((4, 2, own_rows // 2, width), half)
    heads_spec = ((4, own_rows, 256), half)
    wide_spec = ((4, own_rows, width), half)
    own_half = ((own_rows, width), half)
    own_full = ((own_rows, width), full)
    two_half = ((2, own_rows, width), half)
    reduce_a = dict(part_a=wide_spec, got_a=two_half, held_a=own_half, mixed_a=own_half)
    reduce_b = dict(part_b=wide_spec, got_b=two_half, held_b=own_half, mixed_b=own_half)
    saved_specs = dict(
        hidden=own_full,
        vecs=((8, width), full),
        n1=rows_spec,
        q=heads_spec,
        key=heads_spec,
        val=heads_spec,
        probs=((4, 512, 512), half),
        att=heads_spec,
        mid=own_full,
        n2=rows_spec,
        act=wide_spec,
        slope=wide_spec,
        w_qkv=full_spec(QKV),
        w_out=full_spec(OUT),
        w_up=full_spec(UP),
        w_down=full_spec(DOWN),
    )
    own_specs = dict(
        reduce_a,
        qv_bias=((8, 256), full),
        ffn_bias=((8, width), full),
        pair_qkv=pair_spec(QKV),
        pair_out=pair_spec(OUT),
        pair_up=pair_spec(UP),
        pair_down=pair_spec(DOWN),
    )

    group_a, group_b, group_c = ("w_down", "slope"), ("w_up", "act", "n2"), ("mid", "att", "w_out")
    group_d, group_e = ("probs", "key", "val", "q", "w_qkv", "n1"), ("hidden",)

    def of_layers(specs):
        return {f"{name}_{layer}": spec for name, spec in specs.items() for layer in range(2)}

    def view(k, layer):
        made = Env()
        for name, ref in k.__dict__.items():
            if name.endswith(f"_{layer}"):
                setattr(made, name[:-2], ref)
        made.place, made.wires = k.place, k.wires
        return made

    def forward(k):
        p, w = k.place, k.wires
        k0, k1 = view(k, 0), view(k, 1)
        small_job = Fetch(p, w, k.small, k.small_all, [k.small_pair])
        length_job = Swap(p, w, k.lengths_in, k.lengths, [])
        swap_x = Swap(p, w, k.x_half, k.x_got, [])
        swap_d = Swap(p, w, k.d_half, k.d_got, [])
        k0.lengths = k1.lengths = k.lengths

        def relay_native(*jobs):
            @pl.when(p.native)
            def _():
                for job in jobs:
                    job.relay()

        def relay_foreign(*jobs):
            @pl.when(jnp.logical_not(p.native))
            def _():
                for job in jobs:
                    job.relay()

        def fetch_qkv(layer, v):
            jobs = []
            for index in range(3):
                rows = pl.ds(index * 128, 128)
                dst, pair = v.w_qkv.at[:, :, rows], v.pair_qkv.at[:, rows]
                jobs.append(Fetch(p, w, k.s_qkv.at[layer, rows], dst, [pair]))
            return jobs

        def fetch_rest(layer, v):
            return (
                Fetch(p, w, k.s_out.at[layer], v.w_out, [v.pair_out]),
                Fetch(p, w, k.s_up.at[layer], v.w_up, [v.pair_up]),
                Fetch(p, w, k.s_down.at[layer], v.w_down, [v.pair_down]),
            )

        qkv_0, qkv_1 = fetch_qkv(0, k0), fetch_qkv(1, k1)
        out_0, up_0, down_0 = fetch_rest(0, k0)
        out_1, up_1, down_1 = fetch_rest(1, k1)
        for at in range(4):
            rows = pl.ds(at * ROWS, ROWS)
            k.x_half[rows] = k.x_in[rows].astype(half)
        mover = Mover(w)

        small_job.start()
        length_job.start()
        swap_x.start()
        small_job.relay()
        small_job.relay_more()
        for job in qkv_0:
            job.start()

        @pl.when(p.native)
        def _():
            for job in qkv_0:
                job.relay()

        small_job.finish()
        unpack_small(k.small_all, (k0, k1))
        length_job.finish()
        swap_x.finish()
        for at in range(4):
            rows = pl.ds(at * ROWS, ROWS)
            k0.hidden[rows] = jnp.where(p.native, k.x_in[rows], k.x_got[rows].astype(full))
            k.d_half[rows] = k.d_in[rows].astype(half)

        def first_sent():
            @pl.when(jnp.logical_not(p.native))
            def _():
                for job in qkv_0:
                    job.relay()

        def first_gathered():
            out_0.start()
            up_0.start()
            for job in qkv_0:
                job.relay_more()
            relay_native(out_0, up_0)
            for job in qkv_0:
                job.finish()

        def first_middle(block):
            if block == 1:
                relay_foreign(out_0)
            else:
                out_0.relay_more()

        def first_attended():
            relay_foreign(up_0)
            down_0.start()
            out_0.finish()

        reduce = attention_forward(k0, first_sent, first_gathered, first_middle, first_attended)
        relay_native(down_0)

        def first_sent_two():
            up_0.relay_more()
            relay_foreign(down_0)

        def first_gathered_two():
            for job in qkv_1:
                job.start()
            out_1.start()
            up_0.finish()
            relay_native(*qkv_1, out_1)

        def first_raised():
            down_0.relay_more()
            relay_foreign(*qkv_1, out_1)
            up_1.start()
            down_0.finish()

        column, here, there = feed_forward(
            k0, reduce, first_sent_two, first_gathered_two, first_raised, k.part_b
        )
        second = ReduceHere(p, w, k.part_b, k.got_b, (k.held_b, k.mixed_b))
        column(there)
        second.start_cross()
        column(here)
        second.start_near()
        second.relay()
        for job in qkv_1:
            job.relay_more()
        out_1.relay_more()
        relay_native(up_1)
        for name in group_a + group_b + group_c + group_d + group_e:
            mover.start(getattr(k0, name), getattr(k, f"h_{name}"), name)
        second.finish()
        for at in range(4):
            rows = pl.ds(at * ROWS, ROWS)
            k1.hidden[rows] = k0.mid[rows] + second.total(rows) + k0.vecs[5:6]
        grads = GatherHere(p, w, k.gh)

        def last_sent():
            relay_foreign(up_1)

        def last_gathered():
            down_1.start()
            swap_d.start()
            for job in qkv_1:
                job.finish()
            out_1.finish()

        def last_middle(block):
            if block == 1:
                relay_native(down_1)
            else:
                up_1.relay_more()

        def last_attended():
            relay_foreign(down_1)

        reduce = attention_forward(k1, last_sent, last_gathered, last_middle, last_attended)

        def last_gathered_two():
            up_1.finish()
            down_1.relay_more()
            swap_d.finish()
            for at in range(4):
                rows = pl.ds(at * ROWS, ROWS)
                k.back[rows] = jnp.where(p.native, k.d_in[rows], k.d_got[rows].astype(full))
                k.gh[p.rank, at // 2, pl.ds(at % 2 * ROWS, ROWS)] = k.back[rows].astype(half)
            grads.start()

        def raised():
            grads.wait_sibling()
            grads.relay()
            down_1.finish()

        column, here, there = feed_forward(
            k1, reduce, lambda: None, last_gathered_two, raised, k.ffn_part
        )
        column(there)
        column(here)
        grads.finish()
        mover.wait()

    totals = dict(shapes)
    spare = dict(
        of_layers(own_specs),
        **of_layers(saved_specs),
        **reduce_b,
        back=own_full,
        gh=rows_spec,
        ffn_part=wide_spec,
        lengths=((8, 128), full),
        small_pair=((2, 16, 128), half),
        small_all=((4, 2, 16, 128), half),
        x_half=own_half,
        x_got=own_half,
        d_half=own_half,
        d_got=own_half,
        turned=((1024, 512), half),
        ds=((2, 512, 512), half),
        gq=((3, 4, own_rows, 256), half),
        out_half=own_half,
        back_half=own_half,
        made=own_full,
        back_out=own_full,
        out_sent=own_half,
        back_sent=own_half,
        flat=((4, 2, 16, 128), full),
        small_sums=((2, 16, 128), full),
        g_last=full_spec(QKV),
        **total_scratch("small", 16, 128, full),
        **total_scratch("last", *shapes[QKV]),
    )
    for name, shape in shapes.items():
        spare.update(total_scratch(name, *shape))
    spare.update(
        of_layers(dict(col=((8, width), full), col_qv=((8, 256), full), col_ffn=((8, width), full)))
    )

    def backward(k):
        p, w = k.place, k.wires
        mover = Mover(w)
        first, last = view(k, 0), view(k, 1)
        for name in saved_specs:
            setattr(k, name, getattr(last, name))
        for name in shapes:
            setattr(k, f"g_{name}", getattr(first, f"w_{name}"))
        k.gm, k.gp, k.ga, k.grad_mid = first.n1, first.act, first.att, first.mid
        k.part_a, k.got_a, k.held_a, k.mixed_a = first.part_a, first.got_a, first.held_a, first.mixed_a
        k0, k1 = Env(), Env()
        for v, layer in ((k0, first), (k1, last)):
            v.__dict__.update(k.__dict__)
            v.vecs, v.col, v.col_qv, v.col_ffn = layer.vecs, layer.col, layer.col_qv, layer.col_ffn
        k1.back_out = k0.back = first.hidden
        k1.g_qkv = k.g_last

        def load(names):
            for name in names:
                mover.start(getattr(k, f"h_{name}"), getattr(k, name), name)

        def job_total(name, layer):
            spare = [getattr(k, f"{name}_t{at}") for at in range(5)]
            return Total(p, w, getattr(k, f"g_{name}"), getattr(k, f"pair_{name}_{layer}"), spare)

        def job_deliver(name, layer):
            src, dst = getattr(k, f"pair_{name}_{layer}"), getattr(k, f"done_{name}_{layer}")
            return Deliver(p, w, src, dst, [])

        def thirds(layer, v, name):
            made = []
            for index in range(3):
                rows = pl.ds(index * 128, 128)
                spare = [getattr(k, f"{name}_t{at}") for at in range(5)]
                spare = [ref.at[:, rows] for ref in spare[:3]] + [ref.at[rows] for ref in spare[3:]]
                dst = getattr(k, f"pair_{QKV}_{layer}").at[:, rows]
                done = getattr(k, f"done_{QKV}_{layer}").at[:, rows]
                made.append(
                    (
                        Total(p, w, v.g_qkv.at[:, :, rows], dst, spare),
                        Deliver(p, w, dst, done, []),
                    )
                )
            return made

        ffn = ReduceHere(p, w, k.ffn_part, last.got_a, (last.held_a, last.mixed_a))
        swap = Swap(p, w, k.out_half, k.out_sent, [])
        swap_back = Swap(p, w, k.back_half, k.back_sent, [])
        qkv_1, qkv_0 = thirds(1, k1, "last"), thirds(0, k0, QKV)
        down_1, up_1, out_1 = [job_total(name, 1) for name in (DOWN, UP, OUT)]
        down_0, up_0, out_0 = [job_total(name, 0) for name in (DOWN, UP, OUT)]
        to_down_1, to_up_1, to_out_1 = [job_deliver(name, 1) for name in (DOWN, UP, OUT)]
        to_down_0, to_up_0, to_out_0 = [job_deliver(name, 0) for name in (DOWN, UP, OUT)]
        small_job = Small(
            p, w, k.flat, k.small_parts, [getattr(k, f"small_t{at}") for at in range(5)] + [k.small_sums]
        )
        reduce = feed_forward_back(k1, None, lambda: None, down_1.start)
        def last_background(point):
            if point == AT_UP:
                load(group_a + group_b)
                up_1.start()
            if point == AT_SUMMED:
                down_1.relay_more()
            if point == AT_OUT:
                ffn.start_cross()
                ffn.start_near()
                out_1.start()
            if point == AT_HEADS:
                ffn.relay()
                down_1.finish()
                to_down_1.start()
            if point == AT_LATE:
                up_1.relay_more()
                out_1.relay_more()
                ffn.finish()
                for at in range(4):
                    rows = pl.ds(at * ROWS, ROWS)
                    made = k.mid[rows] + ffn.total(rows) + k1.vecs[5:6]
                    k.made[rows] = made
                    k.out_half[rows] = made.astype(half)
                load(group_c)
            if point == AT_QKV:
                load(group_d)
                up_1.finish()
                out_1.finish()

        attention_back(k1, reduce, last_background, lambda index: qkv_1[index][0].start(), False)
        load(group_e)
        for at in range(4):
            rows = pl.ds(at * ROWS, ROWS)
            k.gh[p.rank, at // 2, pl.ds(at % 2 * ROWS, ROWS)] = k0.back[rows].astype(half)
        gather = GatherHere(p, w, k.gh)
        gather.start()
        mover.wait(*group_a, *group_b)

        def first_started():
            to_up_1.start()
            for job, _ in qkv_1:
                job.relay_more()

        def first_grad_down():
            for job, _ in qkv_1:
                job.finish()
            down_0.start()

        reduce = feed_forward_back(k0, gather, first_started, first_grad_down)
        mover.wait(*group_c, *group_d, *group_e)

        for _, job in qkv_1:
            job.start()
        to_out_1.start()

        def first_background(point):
            if point == AT_UP:
                up_0.start()
            if point == AT_SUMMED:
                down_0.relay_more()
            if point == AT_OUT:
                swap.start()
                out_0.start()
            if point == AT_HEADS:
                down_0.finish()
                to_down_0.start()
            if point == AT_LATE:
                up_0.relay_more()
                out_0.relay_more()
            if point == AT_QKV:
                up_0.finish()
                to_up_0.start()
                out_0.finish()
                to_out_0.start()
                qkv_0[0][0].relay_more()
                qkv_0[1][0].relay_more()

        attention_back(k0, reduce, first_background, lambda index: qkv_0[index][0].start(), True)
        pack_small(k.flat, [(v.col, v.col_qv, v.col_ffn) for v in (k0, k1)])
        small_job.start()
        for at in range(4):
            rows = pl.ds(at * ROWS, ROWS)
            k.back_half[rows] = k.back_out[rows].astype(half)
        qkv_0[0][0].finish()
        qkv_0[2][0].relay_more()
        small_job.relay_more()
        swap_back.start()
        qkv_0[0][1].start()
        for job, then in qkv_0[1:]:
            job.finish()
            then.start()
        small_job.finish()
        swap.finish()
        swap_back.finish()
        for at in range(4):
            rows = pl.ds(at * ROWS, ROWS)
            k.output[rows] = jnp.where(p.native, k.made[rows], k.out_sent[rows].astype(full))
            k.grad_x[rows] = jnp.where(p.native, k.back_out[rows], k.back_sent[rows].astype(full))
        for job in (to_down_1, to_up_1, to_out_1, to_down_0, to_up_0, to_out_0):
            job.finish()
        for _, job in qkv_1 + qkv_0:
            job.finish()
        mover.wait()

    done_specs = {
        f"done_{name}_{layer}": pair_spec(name) for name in totals for layer in range(2)
    }
    def both(k):
        forward(k)
        backward(k)

    spilled = {f"h_{name}": spec for name, spec in saved_specs.items()}
    last = fused(
        both,
        dict(
            x_in=x_in,
            d_in=d_out,
            lengths_in=lengths,
            small=small,
            s_qkv=qkv_turned,
            s_out=w_o,
            s_up=w_1,
            s_down=w_2,
        ),
        dict(
            done_specs,
            **spilled,
            output=own_full,
            grad_x=own_full,
            small_parts=((8, 16, 128), full),
        ),
        spare,
        (SIBLING, CROSS, FAR, BESIDE, ABOVE, LINE),
        hbm=[f"s_{name}" for name in shapes] + list(spilled) + list(done_specs),
    )
    small_parts = last.small_parts
    small_parts = small_parts.reshape(8, -1)
    gain_size, bias_size = norm_gains.size, vec_biases.size
    everyone = small_parts.sum(0)
    sources = jnp.arange(8, dtype=jnp.int32)
    pair = z // 2
    mine_from = (sources == 2 * z + pair) | (sources == 2 * (z + 2 - 4 * pair) + pair)
    mine = jnp.where(mine_from[:, None], small_parts, 0.0).sum(0)[gain_size + bias_size :]

    def stacked_layers(name):
        return jnp.stack([added(getattr(last, f"done_{name}_{layer}")) for layer in range(2)])

    grad_qkv = stacked_layers(QKV)
    grad_qkv = jnp.transpose(grad_qkv.reshape(layer_count, 3, 128, 256), (0, 2, 1, 3))
    return (
        last.output,
        last.grad_x,
        grad_qkv,
        mine[: b_qv.size].reshape(b_qv.shape),
        stacked_layers(OUT),
        stacked_layers(UP),
        mine[b_qv.size : b_qv.size + b_ffn.size].reshape(b_ffn.shape),
        stacked_layers(DOWN),
        everyone[:gain_size].reshape(norm_gains.shape),
        everyone[gain_size : gain_size + bias_size].reshape(vec_biases.shape),
    )


def solution(mesh):
    in_specs = (
        P(("dp", "tensor"), None),
        P(("dp", "tensor"), None),
        P("dp", None),
        P(None, "dp", None, "tensor"),
        P(None, None, ("tensor", "dp")),
        P(None, "tensor", "dp"),
        P(None, "dp", "tensor"),
        P(None, ("tensor", "dp")),
        P(None, "tensor", "dp"),
        P(None, None, "dp"),
        P(None, None, "dp"),
    )
    out_specs = (
        P(("dp", "tensor"), None),
        P(("dp", "tensor"), None),
        P(None, "dp", None, "tensor"),
        P(None, None, ("tensor", "dp")),
        P(None, "tensor", "dp"),
        P(None, "dp", "tensor"),
        P(None, ("tensor", "dp")),
        P(None, "tensor", "dp"),
        P(None, None, "dp"),
        P(None, None, "dp"),
    )
    paired = mesh.shape["dp"] == 8 and mesh.shape["tensor"] == 4
    body = paired_shards if paired else shards
    return jax.shard_map(body, mesh=mesh, in_specs=in_specs, out_specs=out_specs, check_vma=False)
```

```python
import math

import jax
import jax.numpy as jnp
from jax import lax
from jax.experimental import pallas as pl
from jax.experimental.pallas import tpu as pltpu
from jax.sharding import PartitionSpec as P

HEAD_DIM = 64


NORM_EPS = 1e-05
GELU_COEFF = 0.7978845608028654
GELU_CUBIC = 0.044715


def layer_norm(inputs, gain_row, bias_row):
    row_mean = jnp.mean(inputs, axis=-1, keepdims=True)
    centered = inputs - row_mean
    inv_std = lax.rsqrt(jnp.mean(centered * centered, axis=-1, keepdims=True) + NORM_EPS)
    normed = centered * inv_std
    return (normed * gain_row + bias_row, normed, inv_std)


def norm_back(grad_in, normed, inv_std, gain_row):
    scaled = grad_in * gain_row
    return inv_std * (
        scaled
        - jnp.mean(scaled, axis=-1, keepdims=True)
        - normed * jnp.mean(scaled * normed, axis=-1, keepdims=True)
    )


def gelu_pair(pre_act):
    squared = pre_act * pre_act
    tangent = jnp.tanh(GELU_COEFF * (pre_act + GELU_CUBIC * squared * pre_act))
    gelu_value = 0.5 * pre_act * (1.0 + tangent)
    gelu_slope = 0.5 * (1.0 + tangent) + 0.5 * pre_act * (1.0 - tangent * tangent) * GELU_COEFF * (
        1.0 + 3.0 * GELU_CUBIC * squared
    )
    return (gelu_value, gelu_slope)


def segment_ids(lengths, total_rows):
    positions = jnp.arange(total_rows, dtype=jnp.int32)
    found = jnp.zeros_like(positions)
    end = jnp.int32(0)
    for index in range(lengths.shape[0]):
        end = end + lengths[index]
        found = found + (positions >= end).astype(jnp.int32)
    return found


def contract_first(left, right):
    return lax.dot_general(
        left, right, (((0,), (0,)), ((), ())), preferred_element_type=jnp.float32
    )


def contract_last(left, right):
    return lax.dot_general(
        left, right, (((1,), (1,)), ((), ())), preferred_element_type=jnp.float32
    )

def exchange_kernel(plan, *refs):
    count = len(plan)
    ins = refs[:count]
    outs = refs[count : 2 * count]
    send_sem, recv_sem, own_sem = refs[2 * count : 2 * count + 3]
    spare = list(refs[2 * count + 3 :])

    greeted = []
    for axis in sorted({axis for axis, _, _ in plan}):
        kinds = {kind for name, kind, _ in plan if name == axis}
        size = [n for name, _, n in plan if name == axis][0]
        me = lax.axis_index(axis)
        if kinds == {"paired"}:
            greeted.append({axis: me + 1 - 2 * (me % 2)})
            greeted += [{axis: (me + k) % size} for k in range(2, size, 2)]
        else:
            greeted += [{axis: (me + k) % size} for k in range(1, size)]
    barrier = pltpu.get_barrier_semaphore()
    for device in greeted:
        pl.semaphore_signal(
            barrier, inc=1, device_id=device, device_id_type=pl.DeviceIdType.MESH
        )
    pl.semaphore_wait(barrier, len(greeted))

    used = [0]

    def remote(src, dst, device):
        slot = used[0]
        used[0] += 1
        copy = pltpu.make_async_remote_copy(
            src_ref=src,
            dst_ref=dst,
            send_sem=send_sem.at[slot],
            recv_sem=recv_sem.at[slot],
            device_id=device,
            device_id_type=pl.DeviceIdType.MESH,
        )
        copy.start()
        return copy

    def in_line(axis, src, dst, base, place, target, arrival):
        return pltpu.make_async_remote_copy(
            src_ref=src,
            dst_ref=dst,
            send_sem=send_sem.at[base + place],
            recv_sem=recv_sem.at[base + arrival],
            device_id={axis: jnp.int32(target)},
            device_id_type=pl.DeviceIdType.MESH,
        )

    def line_start(axis, kind, src, dst, base, held):
        me = lax.axis_index(axis)
        for m in range(4):

            @pl.when(me == m)
            def _(m=m):
                if kind == "sum" and m in (0, 3):
                    far = 3 - m
                    near = 1 if m == 0 else 2
                    in_line(axis, src.at[far], held, base, far, near, 4).start()
                for target in ((2, 1), (3, 2, 0), (0, 1, 3), (1, 2))[m]:
                    if kind == "sum" and (m, target) in ((1, 3), (2, 0)):
                        continue
                    block = src.at[target] if kind == "sum" else src
                    in_line(axis, block, dst.at[m], base, target, target, m).start()

    def line_relay(axis, kind, src, dst, base, held, mixed):
        me = lax.axis_index(axis)
        for m in (1, 2):

            @pl.when(me == m)
            def _(m=m):
                far = 3 if m == 1 else 0
                near = 3 - far
                if kind == "line":
                    in_line(axis, src, dst.at[far], base, far, far, far).wait_recv()
                    in_line(axis, dst.at[far], dst.at[far], base, 4, near, far).start()
                else:
                    in_line(axis, held, held, base, far, far, 4).wait_recv()

                    def add(row, carry):
                        rows = pl.ds(row * 16, 16)
                        mixed[rows] = (
                            held[rows].astype(jnp.float32)
                            + src[far, rows].astype(jnp.float32)
                        ).astype(mixed.dtype)
                        return carry

                    lax.fori_loop(0, mixed.shape[0] // 16, add, 0)
                    in_line(axis, mixed, dst.at[m], base, far, far, m).start()

        if kind == "sum":
            for m in (0, 3):

                @pl.when(me == m)
                def _(m=m):
                    dst[3 - m] = jnp.zeros(dst.shape[1:], dst.dtype)

    def line_finish(axis, kind, src, dst, base, held, mixed):
        me = lax.axis_index(axis)
        for m in range(4):

            @pl.when(me == m)
            def _(m=m):
                block = src.at[0] if kind == "sum" else src
                for other in range(4):
                    if other == m:
                        continue
                    ends = (m, other) in ((0, 3), (3, 0))
                    relayed = (m, other) in ((1, 3), (2, 0))
                    copy = in_line(axis, block, dst.at[other], base, other, other, other)
                    if not (kind == "sum" and ends) and not (kind == "line" and relayed):
                        copy.wait_recv()
                    if not (kind == "line" and ends):
                        copy.wait_send()
                if kind == "line" and m in (1, 2):
                    in_line(axis, block, dst.at[0], base, 4, 0, 0).wait_send()

    started = []
    relays = []
    own = []
    lines = []
    for index, (axis, kind, size) in enumerate(plan):
        me = lax.axis_index(axis)
        src, dst = ins[index], outs[index]
        if kind in ("line", "sum"):
            held = spare.pop(0) if kind == "sum" else None
            mixed = spare.pop(0) if kind == "sum" else None
            line_start(axis, kind, src, dst, used[0], held)
            lines.append((axis, kind, src, dst, used[0], held, mixed))
            used[0] += 5
        elif kind == "paired":
            for k in range(2, size, 2):
                copy = remote(src, dst.at[me], {axis: (me + k) % size})
                relays.append((copy, dst, axis, (me + size - k) % size))
            started.append(remote(src, dst.at[me], {axis: me + 1 - 2 * (me % 2)}))
        else:
            for k in range(1, size):
                peer = (me + k) % size
                block = src if kind == "gather" else src.at[peer]
                started.append(remote(block, dst.at[me], {axis: peer}))
    for index, (axis, kind, size) in enumerate(plan):
        me = lax.axis_index(axis)
        block = ins[index].at[me] if kind in ("swap", "sum") else ins[index]
        copy = pltpu.make_async_copy(block, outs[index].at[me], own_sem.at[index])
        copy.start()
        own.append(copy)
    for line in lines:
        line_relay(*line)
    for copy, dst, axis, slot in relays:
        copy.wait_recv()
        me = lax.axis_index(axis)
        started.append(
            remote(dst.at[slot], dst.at[slot], {axis: me + 1 - 2 * (me % 2)})
        )
    for copy, _, _, _ in relays:
        copy.wait_send()
    for copy in own:
        copy.wait()
    for copy in started:
        copy.wait()
    for line in lines:
        line_finish(*line)


def make_exchange():
    calls = [0]

    def exchange(*items):
        plan = []
        shapes = []
        copies = 0
        sent = 0
        spare = []
        for axis, kind, value in items:
            size = lax.axis_size(axis)
            if kind == "paired" and size % 2:
                kind = "gather"
            block = value.shape[1:] if kind == "swap" else value.shape
            if axis == "tensor" and size == 4 and value.dtype == jnp.bfloat16:
                kind = {"swap": "sum", "gather": "line"}[kind]
                if kind == "sum":
                    spare += [pltpu.VMEM(block, value.dtype)] * 2
            plan.append((axis, kind, size))
            copies += 5 if kind in ("line", "sum") else size - 1
            shapes.append(jax.ShapeDtypeStruct((size,) + block, value.dtype))
            sent += (size - 1) * math.prod(block) * value.dtype.itemsize
        collective_id = calls[0]
        calls[0] += 1
        return pl.pallas_call(
            lambda *refs: exchange_kernel(tuple(plan), *refs),
            out_shape=tuple(shapes),
            in_specs=[pl.BlockSpec(memory_space=pltpu.VMEM)] * len(plan),
            out_specs=tuple([pl.BlockSpec(memory_space=pltpu.VMEM)] * len(plan)),
            scratch_shapes=[
                pltpu.SemaphoreType.DMA((copies,)),
                pltpu.SemaphoreType.DMA((copies,)),
                pltpu.SemaphoreType.DMA((len(plan),)),
                *spare,
            ],
            compiler_params=pltpu.CompilerParams(
                collective_id=collective_id,
                has_side_effects=True,
                vmem_limit_bytes=48 * 1024 * 1024,
            ),
            cost_estimate=pl.CostEstimate(flops=0, bytes_accessed=sent, transcendentals=0),
            name=f"exchange_{collective_id}",
        )(*[value for _, _, value in items])

    return exchange


SIBLING, CROSS, FAR, BESIDE, ABOVE, LINE = range(6)
EVERY_PEER = (SIBLING, CROSS, FAR, BESIDE, ABOVE)
AT_UP, AT_SUMMED, AT_OUT, AT_HEADS, AT_LATE, AT_ATTENDED, AT_QKV = range(7)
QKV, OUT, UP, DOWN = "qkv", "out", "up", "down"
MESH = pl.DeviceIdType.MESH


class Place:
    def __init__(self):
        self.dp = lax.axis_index("dp")
        self.z = lax.axis_index("tensor")
        self.core = lax.rem(self.dp, 2)
        self.pair = lax.div(self.z, 2)
        self.low = lax.rem(self.z, 2)
        self.rank = 2 * self.core + self.low
        self.native = self.core == self.pair
        self.block = lax.div(self.dp, 2)
        self.x = lax.rem(self.block, 2)
        self.y = lax.div(self.block, 2)
        self.base = self.dp - self.core

    def sibling(self):
        return {"dp": self.base + 1 - self.core, "tensor": self.z}

    def cross(self, core):
        return {"dp": self.base + core, "tensor": self.z + 1 - 2 * self.low}

    def far(self, core):
        return {"dp": self.base + core, "tensor": self.z + 2 - 4 * self.pair}

    def beside(self):
        return {"dp": self.dp + 2 - 4 * self.x, "tensor": self.z}

    def above(self):
        return {"dp": self.dp + 4 - 8 * self.y, "tensor": self.z}

    def in_line(self, index):
        return {"dp": self.base + lax.rem(index, 2), "tensor": lax.div(index, 2)}

    def rank_at(self, core, low):
        return 2 * core + low

    def block_at(self, dy, dx):
        y = 1 - self.y if dy else self.y
        x = 1 - self.x if dx else self.x
        return 2 * y + x


class Wires:
    def __init__(self, send_sem, recv_sem, own_sem):
        self.send_sem, self.recv_sem, self.own_sem = send_sem, recv_sem, own_sem
        self.used = 0
        self.own_used = 0

    def take(self, count):
        at = self.used
        self.used += count
        return at

    def take_own(self, count=1):
        at = self.own_used
        self.own_used += count
        return at

    def copy(self, src, dst, device, send, recv):
        return pltpu.make_async_remote_copy(
            src_ref=src,
            dst_ref=dst,
            send_sem=self.send_sem.at[send],
            recv_sem=self.recv_sem.at[recv],
            device_id=device,
            device_id_type=MESH,
        )

    def local(self, src, dst, slot):
        return pltpu.make_async_copy(src, dst, self.own_sem.at[slot])


def add_rows(dst, *parts):
    rows = dst.shape[0]
    step = 16 if rows % 16 == 0 else 8

    def body(index, carry):
        at = pl.ds(index * step, step)
        total = parts[0][at].astype(jnp.float32)
        for part in parts[1:]:
            total = total + part[at].astype(jnp.float32)
        dst[at] = total.astype(dst.dtype)
        return carry

    lax.fori_loop(0, rows // step, body, 0)


class Gather:
    peers = (SIBLING, CROSS)
    copies = 5
    owns = 1

    @staticmethod
    def shape(value):
        return (4,) + value.shape

    @staticmethod
    def scratch(value):
        return []

    def __init__(self, place, wires, src, dst, spare):
        self.p, self.w, self.src, self.dst = place, wires, src, dst
        self.at = wires.take(self.copies)
        self.own = wires.take_own()

    def _copies(self):
        p, w, src, dst, at = self.p, self.w, self.src, self.dst, self.at
        other = 1 - p.core
        near = p.rank_at(p.core, 1 - p.low)
        skew = p.rank_at(other, 1 - p.low)
        sib = p.sibling()
        return [
            lambda: w.copy(src, dst.at[p.rank], sib, at, at),
            lambda: w.copy(src.at[p.core], dst.at[p.rank, p.core], p.cross(p.core), at + 1, at + 1),
            lambda: w.copy(src.at[other], dst.at[p.rank, other], p.cross(other), at + 2, at + 2),
            lambda: w.copy(dst.at[near, p.core], dst.at[near, p.core], sib, at + 3, at + 4),
            lambda: w.copy(dst.at[skew, p.core], dst.at[skew, p.core], sib, at + 4, at + 3),
        ]

    def start(self):
        made = self._copies()
        for copy in (made[1], made[2], made[0]):
            copy().start()
        self.w.local(self.src, self.dst.at[self.p.rank], self.own).start()

    def relay(self):
        made = self._copies()
        made[1]().wait_recv()
        made[3]().start()
        made[2]().wait_recv()
        made[4]().start()

    def relay_more(self):
        pass

    def finish(self):
        made = self._copies()
        for index in (0, 3, 4):
            made[index]().wait_recv()
        for copy in made:
            copy().wait_send()
        self.w.local(self.src, self.dst.at[self.p.rank], self.own).wait()


class Reduce:
    peers = (SIBLING, CROSS)
    copies = 3
    owns = 1

    @staticmethod
    def shape(value):
        return (3,) + value.shape[1:]

    @staticmethod
    def scratch(value):
        return [pltpu.VMEM(value.shape[1:], value.dtype)] * 2

    def __init__(self, place, wires, src, dst, spare):
        self.p, self.w, self.src, self.dst = place, wires, src, dst
        self.held, self.mixed = spare
        self.at = wires.take(self.copies)
        self.own = wires.take_own()

    def _copies(self):
        p, w, src, dst, at = self.p, self.w, self.src, self.dst, self.at
        other = 1 - p.core
        sib = p.sibling()
        return [
            lambda: w.copy(src.at[p.rank_at(other, p.low)], dst.at[1], sib, at, at),
            lambda: w.copy(src.at[p.rank_at(other, 1 - p.low)], self.held, sib, at + 1, at + 1),
            lambda: w.copy(self.mixed, dst.at[2], p.cross(p.core), at + 2, at + 2),
        ]

    def start(self):
        made = self._copies()
        made[1]().start()
        made[0]().start()
        self.w.local(self.src.at[self.p.rank], self.dst.at[0], self.own).start()

    def relay(self):
        made = self._copies()
        made[1]().wait_recv()
        add_rows(self.mixed, self.held, self.src.at[self.p.rank_at(self.p.core, 1 - self.p.low)])
        made[2]().start()

    def relay_more(self):
        pass

    def finish(self):
        made = self._copies()
        made[0]().wait_recv()
        made[2]().wait_recv()
        for copy in made:
            copy().wait_send()
        self.w.local(self.src.at[self.p.rank], self.dst.at[0], self.own).wait()


class Pairing:
    peers = (SIBLING, FAR)
    copies = 3
    owns = 1

    @staticmethod
    def shape(value):
        return (2,) + value.shape

    @staticmethod
    def scratch(value):
        return []

    def __init__(self, place, wires, src, dst, spare):
        self.p, self.w, self.src, self.dst = place, wires, src, dst
        self.at = wires.take(self.copies)
        self.own = wires.take_own()

    def _near(self):
        p, at = self.p, self.at
        return self.w.copy(self.src, self.dst.at[p.core], p.sibling(), at, at)

    def _far(self, recv):
        p, at = self.p, self.at
        return self.w.copy(self.src, self.dst.at[p.core], p.far(p.pair), at + 1, recv)

    def start(self):
        p = self.p
        self._far(self.at + 1 + p.core).start()

        @pl.when(p.native)
        def _():
            self.w.local(self.src, self.dst.at[p.core], self.own).start()

        @pl.when(jnp.logical_not(p.native))
        def _():
            self._near().start()

    def settle(self):
        p = self.p

        @pl.when(p.native)
        def _():
            self._near().wait_recv()
            self.w.local(self.src, self.dst.at[p.core], self.own).wait()

        @pl.when(jnp.logical_not(p.native))
        def _():
            self._far(self.at + 1).wait_recv()
            self._far(self.at + 2).wait_recv()

    def sent(self):
        p = self.p
        self._far(self.at + 1).wait_send()

        @pl.when(jnp.logical_not(p.native))
        def _():
            self._near().wait_send()

    def relay(self):
        pass

    def relay_more(self):
        pass

    def finish(self):
        self.settle()
        self.sent()


class Spread:
    peers = (BESIDE, ABOVE)
    copies = 4
    owns = 1

    @staticmethod
    def shape(value):
        return (4,) + value.shape

    @staticmethod
    def scratch(value):
        return []

    def __init__(self, place, wires, src, dst, spare):
        self.p, self.w, self.src, self.dst = place, wires, src, dst
        self.at = wires.take(self.copies)
        self.own = wires.take_own()

    def _copies(self):
        p, w, src, dst, at = self.p, self.w, self.src, self.dst, self.at
        row, column = p.block_at(0, 1), p.block_at(1, 0)
        return [
            lambda: w.copy(src, dst.at[p.block], p.beside(), at, at),
            lambda: w.copy(src, dst.at[p.block], p.above(), at + 1, at + 1),
            lambda: w.copy(dst.at[row, 0], dst.at[row, 0], p.above(), at + 2, at + 2),
            lambda: w.copy(dst.at[column, 1], dst.at[column, 1], p.beside(), at + 3, at + 3),
        ]

    def start(self):
        made = self._copies()
        made[0]().start()
        made[1]().start()
        self.w.local(self.src, self.dst.at[self.p.block], self.own).start()

    def relay(self):
        pass

    def relay_more(self):
        made = self._copies()
        made[0]().wait_recv()
        made[2]().start()
        made[1]().wait_recv()
        made[3]().start()

    def finish(self):
        made = self._copies()
        made[2]().wait_recv()
        made[3]().wait_recv()
        for copy in made:
            copy().wait_send()
        self.w.local(self.src, self.dst.at[self.p.block], self.own).wait()


class Fetch:
    peers = (SIBLING, FAR, BESIDE, ABOVE)
    copies = 7
    owns = 2

    @staticmethod
    def shape(value):
        return (4, 2) + value.shape

    @staticmethod
    def scratch(value):
        return [pltpu.VMEM((2,) + value.shape, value.dtype)]

    def __init__(self, place, wires, src, dst, spare):
        self.one = Pairing(place, wires, src, spare[0], [])
        self.two = Spread(place, wires, spare[0], dst, [])

    def start(self):
        self.one.start()

    def relay(self):
        self.one.settle()
        self.two.start()

    def relay_more(self):
        self.two.relay_more()

    def finish(self):
        self.one.sent()
        self.two.finish()


class Total:
    peers = (BESIDE, ABOVE)
    copies = 6
    owns = 0

    @staticmethod
    def shape(value):
        return value.shape[1:]

    @staticmethod
    def scratch(value):
        one = pltpu.VMEM(value.shape[2:], value.dtype)
        two = pltpu.VMEM(value.shape[1:], value.dtype)
        return [two, two, two, one, one]

    def __init__(self, place, wires, src, dst, spare):
        self.p, self.w, self.src, self.dst = place, wires, src, dst
        self.from_x, self.from_y, self.last, self.to_y, self.to_x = spare
        self.at = wires.take(self.copies)

    def _copies(self):
        p, w, src, at = self.p, self.w, self.src, self.at
        here_x, here_y, skew = p.block_at(0, 1), p.block_at(1, 0), p.block_at(1, 1)
        return [
            lambda: w.copy(src.at[here_x, 0], self.from_x.at[0], p.beside(), at, at),
            lambda: w.copy(src.at[skew, 0], self.from_x.at[1], p.beside(), at + 1, at + 1),
            lambda: w.copy(src.at[here_y, 1], self.from_y.at[0], p.above(), at + 2, at + 2),
            lambda: w.copy(src.at[skew, 1], self.from_y.at[1], p.above(), at + 3, at + 3),
            lambda: w.copy(self.to_y, self.last.at[0], p.above(), at + 4, at + 4),
            lambda: w.copy(self.to_x, self.last.at[1], p.beside(), at + 5, at + 5),
        ]

    def start(self):
        made = self._copies()
        for index in (1, 3, 0, 2):
            made[index]().start()

    def relay(self):
        pass

    def relay_more(self):
        made = self._copies()
        p = self.p
        made[1]().wait_recv()
        add_rows(self.to_y, self.src.at[p.block_at(1, 0), 0], self.from_x.at[1])
        made[4]().start()
        made[3]().wait_recv()
        add_rows(self.to_x, self.src.at[p.block_at(0, 1), 1], self.from_y.at[1])
        made[5]().start()

    def finish(self):
        made = self._copies()
        p = self.p
        for index in (0, 2, 4, 5):
            made[index]().wait_recv()
        add_rows(self.dst.at[0], self.src.at[p.block, 0], self.from_x.at[0], self.last.at[0])
        add_rows(self.dst.at[1], self.src.at[p.block, 1], self.from_y.at[0], self.last.at[1])
        for copy in made:
            copy().wait_send()


class Deliver:
    peers = (SIBLING, FAR)
    copies = 4
    owns = 1

    @staticmethod
    def shape(value):
        return value.shape

    @staticmethod
    def scratch(value):
        return []

    def __init__(self, place, wires, src, dst, spare):
        self.p, self.w, self.src, self.dst = place, wires, src, dst
        self.at = wires.take(self.copies)
        self.own = wires.take_own()

    def _near(self):
        p, at = self.p, self.at
        return self.w.copy(self.src.at[1 - p.core], self.dst.at[0], p.sibling(), at, at)

    def _far(self, core):
        p, at = self.p, self.at
        return self.w.copy(
            self.src.at[core], self.dst.at[1], p.far(jnp.int32(core)), at + 1 + core, at + 1
        )

    def start(self):
        p = self.p

        @pl.when(p.native)
        def _():
            self._near().start()
            self.w.local(self.src.at[p.core], self.dst.at[0], self.own).start()

        @pl.when(jnp.logical_not(p.native))
        def _():
            self._far(0).start()
            self._far(1).start()

    def relay(self):
        pass

    def relay_more(self):
        pass

    def finish(self):
        p = self.p
        self._far(0).wait_recv()

        @pl.when(p.native)
        def _():
            self._near().wait_send()
            self.w.local(self.src.at[p.core], self.dst.at[0], self.own).wait()

        @pl.when(jnp.logical_not(p.native))
        def _():
            self._near().wait_recv()
            self._far(0).wait_send()
            self._far(1).wait_send()


class Swap:
    peers = (FAR,)
    copies = 1
    owns = 1

    @staticmethod
    def shape(value):
        return value.shape

    @staticmethod
    def scratch(value):
        return []

    def __init__(self, place, wires, src, dst, spare):
        self.p, self.w, self.src, self.dst = place, wires, src, dst
        self.at = wires.take(self.copies)
        self.own = wires.take_own()

    def _copy(self):
        p, at = self.p, self.at
        return self.w.copy(self.src, self.dst, p.far(1 - p.core), at, at)

    def start(self):
        @pl.when(self.p.native)
        def _():
            self.w.local(self.src, self.dst, self.own).start()

        @pl.when(jnp.logical_not(self.p.native))
        def _():
            self._copy().start()

    def relay(self):
        pass

    def relay_more(self):
        pass

    def finish(self):
        @pl.when(self.p.native)
        def _():
            self.w.local(self.src, self.dst, self.own).wait()

        @pl.when(jnp.logical_not(self.p.native))
        def _():
            self._copy().wait()


class Small:
    peers = (BESIDE, ABOVE, LINE)
    copies = 20
    owns = 1

    @staticmethod
    def shape(value):
        return (8,) + value.shape[2:]

    @staticmethod
    def scratch(value):
        return Total.scratch(value) + [pltpu.VMEM(value.shape[1:], value.dtype)]

    def __init__(self, place, wires, src, dst, spare):
        self.sums = spare[-1]
        self.total = Total(place, wires, src, self.sums, spare[:-1])
        self.p, self.w, self.dst = place, wires, dst
        self.at = wires.take(14)
        self.own = wires.take_own()

    def _ends(self, offset):
        p, at = self.p, self.at
        me = 2 * p.z + p.core
        to = lax.rem(me + offset, 8)
        return self.w.copy(
            self.sums.at[lax.rem(to, 2)], self.dst.at[me], p.in_line(to), at + offset - 1, at + 6 + offset
        )

    def _mine(self):
        p = self.p
        return self.w.local(self.sums.at[p.core], self.dst.at[2 * p.z + p.core], self.own)

    def start(self):
        self.total.start()

    def relay(self):
        pass

    def relay_more(self):
        self.total.relay_more()
        self.total.finish()
        for offset in range(1, 8):
            self._ends(offset).start()
        self._mine().start()

    def finish(self):
        self._mine().wait()
        for offset in range(1, 8):
            self._ends(offset).wait()


def greet(place, kinds):
    p = place
    devices = []
    if SIBLING in kinds or LINE in kinds:
        devices.append(p.sibling())
    if CROSS in kinds or LINE in kinds:
        devices += [p.cross(jnp.int32(0)), p.cross(jnp.int32(1))]
    if FAR in kinds or LINE in kinds:
        devices += [p.far(jnp.int32(0)), p.far(jnp.int32(1))]
    if LINE in kinds:
        last = 3 - p.z
        devices += [{"dp": p.base, "tensor": last}, {"dp": p.base + 1, "tensor": last}]
    if BESIDE in kinds:
        devices.append(p.beside())
    if ABOVE in kinds:
        devices.append(p.above())
    barrier = pltpu.get_barrier_semaphore()
    for device in devices:
        pl.semaphore_signal(barrier, inc=1, device_id=device, device_id_type=MESH)
    pl.semaphore_wait(barrier, len(devices))


def round_kernel(kinds, *refs):
    count = len(kinds)
    ins, outs = refs[:count], refs[count : 2 * count]
    wires = Wires(*refs[2 * count : 2 * count + 3])
    spare = list(refs[2 * count + 3 :])
    place = Place()
    greet(place, {peer for kind, _ in kinds for peer in kind.peers})
    jobs = []
    for (kind, held), src, dst in zip(kinds, ins, outs):
        jobs.append(kind(place, wires, src, dst, spare[:held]))
        del spare[:held]
    for job in jobs:
        job.start()
    for job in jobs:
        job.relay()
    for job in jobs:
        job.relay_more()
    for job in jobs:
        job.finish()


def make_rounds():
    calls = [0]

    def rounds(*items):
        kinds, shapes, scratch = [], [], []
        copies = owns = sent = 0
        for kind, value in items:
            held = kind.scratch(value)
            kinds.append((kind, len(held)))
            scratch += held
            shapes.append(jax.ShapeDtypeStruct(kind.shape(value), value.dtype))
            copies += kind.copies
            owns += kind.owns
            sent += math.prod(kind.shape(value)) * value.dtype.itemsize
        collective_id = calls[0]
        calls[0] += 1
        return pl.pallas_call(
            lambda *refs: round_kernel(tuple(kinds), *refs),
            out_shape=tuple(shapes),
            in_specs=[pl.BlockSpec(memory_space=pltpu.VMEM)] * len(kinds),
            out_specs=tuple([pl.BlockSpec(memory_space=pltpu.VMEM)] * len(kinds)),
            scratch_shapes=[
                pltpu.SemaphoreType.DMA((copies,)),
                pltpu.SemaphoreType.DMA((copies,)),
                pltpu.SemaphoreType.DMA((max(owns, 1),)),
                *scratch,
            ],
            compiler_params=pltpu.CompilerParams(
                collective_id=collective_id,
                has_side_effects=True,
                vmem_limit_bytes=48 * 1024 * 1024,
            ),
            cost_estimate=pl.CostEstimate(flops=0, bytes_accessed=sent, transcendentals=0),
            name=f"round_{collective_id}",
        )(*[value for _, value in items])

    return rounds


def masked_scores(queries, key_vecs, segments, score_scale):
    positions = jnp.arange(key_vecs.shape[0], dtype=jnp.int32)
    allowed = (segments[:, None] == segments[None, :]) & (
        positions[None, :] <= positions[:, None]
    )
    scores = (
        jnp.einsum("qhd,khd->hqk", queries, key_vecs, preferred_element_type=jnp.float32)
        * score_scale
    )
    return jnp.where(allowed[None], scores, -jnp.inf)


def attend(queries, key_vecs, val_vecs, segments, score_scale):
    scores = masked_scores(queries, key_vecs, segments, score_scale)
    row_max = jnp.max(scores, axis=-1, keepdims=True)
    log_total = row_max + jnp.log(jnp.sum(jnp.exp(scores - row_max), axis=-1, keepdims=True))
    probs_half = jnp.exp(scores - log_total).astype(jnp.bfloat16)
    attended = jnp.einsum("hqk,khd->qhd", probs_half, val_vecs, preferred_element_type=jnp.float32)
    return (attended.astype(jnp.bfloat16).reshape(queries.shape[0], -1), log_total)


def attend_back(queries, key_vecs, val_vecs, grad_attended, log_total, segments, score_scale):
    scores = masked_scores(queries, key_vecs, segments, score_scale)
    soft_probs = jnp.exp(scores - log_total)
    probs_half = soft_probs.astype(jnp.bfloat16)
    grad_probs = jnp.einsum(
        "qhd,khd->hqk", grad_attended, val_vecs, preferred_element_type=jnp.float32
    )
    val_grad = jnp.einsum(
        "hqk,qhd->khd", probs_half, grad_attended, preferred_element_type=jnp.float32
    )
    row_dot = jnp.sum(grad_probs * soft_probs, axis=-1, keepdims=True)
    score_grad = (soft_probs * (grad_probs - row_dot) * score_scale).astype(jnp.bfloat16)
    query_grad = jnp.einsum(
        "hqk,khd->qhd", score_grad, key_vecs, preferred_element_type=jnp.float32
    )
    key_grad = jnp.einsum("hqk,qhd->khd", score_grad, queries, preferred_element_type=jnp.float32)
    return (query_grad, key_grad, val_grad)


def pack(pieces, width, tile):
    flat = jnp.concatenate([piece.reshape(-1) for piece in pieces])
    unit = width * tile
    return jnp.pad(flat, (0, -flat.shape[0] % unit)).reshape(-1, width)


def unpack(packed, shapes):
    flat = packed.reshape(packed.shape[0], -1)
    pieces = []
    at = 0
    for shape in shapes:
        length = math.prod(shape)
        pieces.append(flat[:, at : at + length].reshape((packed.shape[0],) + shape))
        at += length
    return pieces


def shards(x_in, d_out, seq_lengths, w_qkv, b_qv, w_o, w_1, b_ffn, w_2, norm_gains, vec_biases):
    exchange = make_exchange()
    own_rows, width = x_in.shape
    tensor_size = lax.axis_size("tensor")
    dp_size = lax.axis_size("dp")
    group_rows = own_rows * tensor_size
    layer_count = w_qkv.shape[0]
    local_width = w_qkv.shape[3]
    local_heads = local_width // HEAD_DIM
    qkv_width = 3 * local_width
    score_scale = 1.0 / math.sqrt(HEAD_DIM)
    segments = segment_ids(seq_lengths[0], group_rows)
    half = jnp.bfloat16

    def shard_of(name, layer_index):
        if name == "qkv":
            return w_qkv[layer_index].reshape(w_qkv.shape[1], qkv_width)
        if name == "out":
            return w_o[layer_index].T
        if name == "up":
            return w_1[layer_index]
        return w_2[layer_index].T

    weights = {}

    def step(tensor_items, fetched=(), sums=()):
        items = [("tensor", kind, value) for kind, value in tensor_items]
        items += [("dp", "paired", shard_of(*key)) for key in fetched]
        items += [("dp", "swap", value) for value in sums]
        results = list(exchange(*items))
        for position, key in enumerate(fetched):
            piece = results[len(tensor_items) + position]
            weights[key] = piece.reshape(dp_size * piece.shape[1], piece.shape[2])
        gathered = [
            piece.reshape(group_rows, width) if kind == "gather" else piece.astype(jnp.float32).sum(0)
            for (kind, _), piece in zip(tensor_items, results)
        ]
        totals = [
            piece.astype(jnp.float32).sum(0) for piece in results[len(items) - len(sums) :]
        ]
        return gathered, totals

    def to_owners(partial):
        return ("swap", partial.astype(half).reshape(tensor_size, own_rows, width))

    def by_owner(gradient):
        return gradient.astype(half).reshape(dp_size, -1, gradient.shape[-1])

    small_shapes = [b_qv.shape, b_ffn.shape, norm_gains.shape, vec_biases.shape]
    small = pack([b_qv, b_ffn, norm_gains, vec_biases], 128, 16)
    first = exchange(
        ("tensor", "gather", d_out.astype(half)),
        ("dp", "paired", small),
        ("dp", "paired", shard_of("qkv", 0)),
    )
    last_grad_half = first[0].reshape(group_rows, width)
    weights["qkv", 0] = first[2].reshape(width, qkv_width)
    qv_all, ffn_all, gain_all, bias_all = [
        jnp.moveaxis(piece, 0, -2).reshape(piece.shape[1:-1] + (-1,)).astype(jnp.float32)
        for piece in unpack(first[1], small_shapes)
    ]

    caches = []
    hidden_in = x_in
    for layer_index in range(layer_count):
        last = layer_index == layer_count - 1
        following = layer_index + 1
        gain_rows = gain_all[layer_index]
        bias_rows = bias_all[layer_index]
        normed_own, unit_one, inv_one = layer_norm(hidden_in, gain_rows[0], bias_rows[0])
        fetched = [("out", 0), ("up", 0)] if layer_index == 0 else [("down", layer_index)]
        (normed_one,), _ = step([("gather", normed_own.astype(half))], fetched)
        projected = jnp.dot(
            normed_one, weights["qkv", layer_index], preferred_element_type=jnp.float32
        ).reshape(group_rows, 3, local_width)
        qv_bias = qv_all[layer_index]
        heads = (group_rows, local_heads, HEAD_DIM)
        queries = (projected[:, 0] + qv_bias[0]).astype(half).reshape(heads)
        key_vecs = projected[:, 1].astype(half).reshape(heads)
        val_vecs = (projected[:, 2] + qv_bias[1]).astype(half).reshape(heads)
        attended, log_total = attend(queries, key_vecs, val_vecs, segments, score_scale)
        fetched = [("down", 0)] if layer_index == 0 else []
        (summed,), _ = step(
            [to_owners(contract_last(attended, weights["out", layer_index]))], fetched
        )
        residual_mid = hidden_in + summed + bias_rows[2]
        normed_own_two, unit_two, inv_two = layer_norm(residual_mid, gain_rows[1], bias_rows[1])
        fetched = [] if last else [("qkv", following), ("out", following)]
        (normed_two,), _ = step([("gather", normed_own_two.astype(half))], fetched)
        pre_act = (
            jnp.dot(normed_two, weights["up", layer_index], preferred_element_type=jnp.float32)
            + ffn_all[layer_index]
        )
        gelu_value, gelu_slope = gelu_pair(pre_act)
        activated = gelu_value.astype(half)
        ffn_partial = to_owners(contract_last(activated, weights["down", layer_index]))
        if not last:
            (summed,), _ = step([ffn_partial], [("up", following)])
            hidden_in = residual_mid + summed + bias_rows[3]
        caches.append(
            (
                unit_one,
                inv_one,
                normed_one,
                queries,
                key_vecs,
                val_vecs,
                attended,
                log_total,
                unit_two,
                inv_two,
                normed_two,
                activated,
                gelu_slope,
            )
        )
    back = d_out
    grads = {}
    small_terms = [None] * layer_count
    output = None
    for layer_index in reversed(range(layer_count)):
        last = layer_index == layer_count - 1
        gain_rows = gain_all[layer_index]
        (
            unit_one,
            inv_one,
            normed_one,
            queries,
            key_vecs,
            val_vecs,
            attended,
            log_total,
            unit_two,
            inv_two,
            normed_two,
            activated,
            gelu_slope,
        ) = caches[layer_index]
        if last:
            grad_half = last_grad_half
        else:
            (grad_half,), (grads["qkv", layer_index + 1],) = step(
                [("gather", back.astype(half))], sums=[waiting]
            )
        grad_down = by_owner(contract_first(grad_half, activated))
        grad_pre = (
            jnp.dot(grad_half, weights["down", layer_index], preferred_element_type=jnp.float32)
            * gelu_slope
        )
        grad_pre_half = grad_pre.astype(half)
        grad_up = by_owner(contract_first(normed_two, grad_pre_half))
        partial = to_owners(contract_last(grad_pre_half, weights["up", layer_index]))
        if last:
            cut = grad_up.shape[2] // 2
            (grad_normed_two, summed), (grads["down", layer_index], up_left) = step(
                [partial, ffn_partial], sums=[grad_down, grad_up[:, :, :cut]]
            )
            output = residual_mid + summed + bias_all[layer_index][3]
        else:
            (grad_normed_two,), (grads["down", layer_index],) = step([partial], sums=[grad_down])
        grad_mid = back + norm_back(grad_normed_two, unit_two, inv_two, gain_rows[1])
        (grad_mid_half,), (up_part,) = step(
            [("gather", grad_mid.astype(half))], sums=[grad_up[:, :, cut:] if last else grad_up]
        )
        grads["up", layer_index] = (
            jnp.concatenate([up_left, up_part], axis=1) if last else up_part
        )
        grad_out = by_owner(contract_first(grad_mid_half, attended))
        grad_attended = jnp.dot(
            grad_mid_half, weights["out", layer_index], preferred_element_type=jnp.float32
        )
        grad_attended = grad_attended.astype(half).reshape(group_rows, local_heads, HEAD_DIM)
        query_grad, key_grad, val_grad = attend_back(
            queries, key_vecs, val_vecs, grad_attended, log_total, segments, score_scale
        )
        flat = (group_rows, local_width)
        grad_qkv = jnp.concatenate(
            [part.astype(half).reshape(flat) for part in (query_grad, key_grad, val_grad)], axis=1
        )
        grad_qkv_weight = by_owner(contract_first(normed_one, grad_qkv))
        (grad_normed_one,), sent_now = step(
            [to_owners(contract_last(grad_qkv, weights["qkv", layer_index]))],
            sums=[grad_out] if layer_index else [grad_out, grad_qkv_weight],
        )
        grads["out", layer_index] = sent_now[0]
        if layer_index:
            waiting = grad_qkv_weight
        else:
            grads["qkv", layer_index] = sent_now[1]
        small_terms[layer_index] = (
            jnp.stack(
                [
                    jnp.sum(query_grad, axis=0).reshape(local_width),
                    jnp.sum(val_grad, axis=0).reshape(local_width),
                ]
            ),
            jnp.sum(grad_pre, axis=0),
            jnp.stack(
                [
                    jnp.sum(grad_normed_one * unit_one, axis=0),
                    jnp.sum(grad_normed_two * unit_two, axis=0),
                ]
            ),
            jnp.stack(
                [
                    jnp.sum(grad_normed_one, axis=0),
                    jnp.sum(grad_normed_two, axis=0),
                    jnp.sum(grad_mid, axis=0),
                    jnp.sum(back, axis=0),
                ]
            ),
        )
        back = grad_mid + norm_back(grad_normed_one, unit_one, inv_one, gain_rows[0])

    def split_owner(piece):
        return jnp.moveaxis(
            piece.reshape(piece.shape[:-1] + (dp_size, -1)), -2, 0
        ).reshape(dp_size, -1)

    stacked = [
        split_owner(jnp.stack([small_terms[index][member] for index in range(layer_count)]))
        for member in (2, 3, 0, 1)
    ]
    flat = jnp.concatenate(stacked, axis=1)
    flat = jnp.pad(flat, ((0, 0), (0, -flat.shape[1] % 1024)))
    (parts,) = exchange(("dp", "swap", flat.reshape(dp_size, -1, 128)))
    total = parts.sum(0)
    (shared,) = exchange(("tensor", "gather", total))
    everyone = shared.sum(0).reshape(-1)
    gain_size, bias_size = norm_gains.size, vec_biases.size
    mine = total.reshape(-1)[gain_size + bias_size :]

    def stack_layers(name, shape, transposed):
        parts = [grads[name, index] for index in range(layer_count)]
        return jnp.stack([part.T if transposed else part for part in parts]).reshape(shape)

    return (
        output,
        back,
        stack_layers("qkv", w_qkv.shape, False),
        mine[: b_qv.size].reshape(b_qv.shape),
        stack_layers("out", w_o.shape, True),
        stack_layers("up", w_1.shape, False),
        mine[b_qv.size : b_qv.size + b_ffn.size].reshape(b_ffn.shape),
        stack_layers("down", w_2.shape, True),
        everyone[:gain_size].reshape(norm_gains.shape),
        everyone[gain_size : gain_size + bias_size].reshape(vec_biases.shape),
    )


def dot_nn(left, right):
    return jnp.dot(left, right, preferred_element_type=jnp.float32)


class GatherHere(Gather):
    def __init__(self, place, wires, dst):
        super().__init__(place, wires, dst.at[place.rank], dst, [])

    def start(self):
        made = self._copies()
        for index in (1, 2, 0):
            made[index]().start()

    def wait_sibling(self):
        self._copies()[0]().wait_recv()

    def finish(self):
        made = self._copies()
        for index in (3, 4):
            made[index]().wait_recv()
        for copy in made:
            copy().wait_send()


class ReduceHere(Reduce):
    def __init__(self, place, wires, src, dst, spare):
        super().__init__(place, wires, src, dst, spare)

    def _copies(self):
        p, w, src, dst, at = self.p, self.w, self.src, self.dst, self.at
        other = 1 - p.core
        sib = p.sibling()
        return [
            lambda: w.copy(src.at[p.rank_at(other, p.low)], dst.at[0], sib, at, at),
            lambda: w.copy(src.at[p.rank_at(other, 1 - p.low)], self.held, sib, at + 1, at + 1),
            lambda: w.copy(self.mixed, dst.at[1], p.cross(p.core), at + 2, at + 2),
        ]

    def start_cross(self):
        self._copies()[1]().start()

    def start_near(self):
        self._copies()[0]().start()

    def finish(self):
        made = self._copies()
        made[0]().wait_recv()
        made[2]().wait_recv()
        for copy in made:
            copy().wait_send()

    def total(self, rows):
        first = self.src[self.p.rank, rows].astype(jnp.float32)
        return first + self.dst[0, rows].astype(jnp.float32) + self.dst[1, rows].astype(jnp.float32)


class Env:
    pass


class Mover:
    def __init__(self, wires):
        self.wires = wires
        self.open = {}

    def start(self, src, dst, name):
        slot = self.wires.take_own()
        self.open[name] = (src, dst, slot)
        self.wires.local(src, dst, slot).start()

    def wait(self, *names):
        for name in names or list(self.open):
            self.wires.local(*self.open.pop(name)).wait()


def make_fused():
    calls = [32]

    def fused(body, ins, outs, scratch, kinds, hbm=()):
        names_in, names_out, names_spare = list(ins), list(outs), list(scratch)

        def kernel(*refs):
            k = Env()
            refs = list(refs)
            for name in names_in + names_out:
                setattr(k, name, refs.pop(0))
            k.wires = Wires(*refs[:3])
            for name, ref in zip(names_spare, refs[3:]):
                setattr(k, name, ref)
            k.place = Place()
            greet(k.place, kinds)
            body(k)
            assert k.wires.used <= 320 and k.wires.own_used <= 192

        collective_id = calls[0]
        calls[0] += 1
        results = pl.pallas_call(
            kernel,
            out_shape=tuple(jax.ShapeDtypeStruct(*outs[name]) for name in names_out),
            in_specs=[
                pl.BlockSpec(memory_space=pltpu.HBM if name in hbm else pltpu.VMEM)
                for name in names_in
            ],
            out_specs=tuple(
                pl.BlockSpec(memory_space=pltpu.HBM if name in hbm else pltpu.VMEM)
                for name in names_out
            ),
            scratch_shapes=[
                pltpu.SemaphoreType.DMA((320,)),
                pltpu.SemaphoreType.DMA((320,)),
                pltpu.SemaphoreType.DMA((192,)),
                *[pltpu.VMEM(*scratch[name]) for name in names_spare],
            ],
            compiler_params=pltpu.CompilerParams(
                collective_id=collective_id,
                has_side_effects=True,
                vmem_limit_bytes=60 * 1024 * 1024,
            ),
            cost_estimate=pl.CostEstimate(
                flops=0, bytes_accessed=16 * 1024 * 1024, transcendentals=0
            ),
            name=f"fused_{collective_id}",
        )(*[ins[name] for name in names_in])
        made = Env()
        made.__dict__.update(zip(names_out, results))
        return made

    return fused


def chips(place):
    other = 1 - place.core
    return (
        (place.rank, place.rank_at(other, place.low)),
        (place.rank_at(place.core, 1 - place.low), place.rank_at(other, 1 - place.low)),
    )


def two(ref, ranks, lanes=slice(None)):
    parts = [ref[rank, ..., lanes] for rank in ranks]
    return jnp.concatenate([part.reshape(-1, part.shape[-1]) for part in parts], axis=0)


def whole(ref, lanes=slice(None)):
    part = ref[..., lanes]
    return part.reshape(-1, part.shape[-1])


def put_two(ref, ranks, value, lanes=slice(None)):
    rows = value.shape[0] // 2
    ref[ranks[0], :, lanes] = value[:rows].astype(ref.dtype)
    ref[ranks[1], :, lanes] = value[rows:].astype(ref.dtype)


def lanes_at(index, size=256):
    return pl.ds(pl.multiple_of(index * size, size), size)


def loop(count, body):
    def step(index, carry):
        body(index)
        return carry

    lax.fori_loop(0, count, step, 0)


def columns_of(ref, block):
    return jnp.concatenate([ref[block, 0], ref[block, 1]], axis=1)


def all_columns(ref, rows):
    return jnp.concatenate([ref[block, core, rows] for block in range(4) for core in range(2)], axis=1)


ROWS = 32


def visible(k, block):
    shape = (128, (block + 1) * 128)
    end = k.lengths[0:1, 0:1].astype(jnp.int32)
    at_query = lax.broadcasted_iota(jnp.int32, shape, 0) + block * 128
    at_key = lax.broadcasted_iota(jnp.int32, shape, 1)
    late_query = jnp.where(at_query >= end, 1, 0)
    late_key = jnp.where(at_key >= end, 1, 0)
    return (late_query == late_key) & (at_key <= at_query)


def attention_forward(k, on_sent, on_gathered, on_middle, on_attended):
    p = k.place
    here, there = chips(p)
    for at in range(4):
        rows = pl.ds(at * ROWS, ROWS)
        normed, _, _ = layer_norm(k.hidden[rows], k.vecs[0:1], k.vecs[2:3])
        k.n1[p.rank, at // 2, pl.ds(at % 2 * ROWS, ROWS)] = normed.astype(jnp.bfloat16)
    gather = GatherHere(p, k.wires, k.n1)
    gather.start()
    on_sent()

    def project(ranks):
        rows = two(k.n1, ranks)
        for index, (dst, bias) in enumerate(((k.q, 0), (k.key, None), (k.val, 1))):
            weight = k.w_qkv[:, :, index * 128 : index * 128 + 128].reshape(1024, 256)
            made = dot_nn(rows, weight)
            if bias is not None:
                made = made + k.qv_bias[bias : bias + 1]
            put_two(dst, ranks, made)

    gather.wait_sibling()
    gather.relay()
    on_gathered()
    project(here)
    gather.finish()
    project(there)
    scale = 1.0 / math.sqrt(HEAD_DIM)
    for block in range(4):
        if block in (1, 3):
            on_middle(block)
        seen = visible(k, block)
        count = (block + 1) * 128
        for head in range(4):
            lanes = slice(head * HEAD_DIM, head * HEAD_DIM + HEAD_DIM)
            keys = k.key[: block + 1, :, lanes].reshape(count, HEAD_DIM)
            vals = k.val[: block + 1, :, lanes].reshape(count, HEAD_DIM)
            scores = contract_last(k.q[block, :, lanes], keys) * scale
            scores = jnp.where(seen, scores, -jnp.inf)
            raised = jnp.exp(scores - jnp.max(scores, axis=-1, keepdims=True))
            probs = raised * (1.0 / jnp.sum(raised, axis=-1, keepdims=True))
            probs = probs.astype(jnp.bfloat16)
            k.probs[head, pl.ds(block * 128, 128), :count] = probs
            k.att[block, :, lanes] = dot_nn(probs, vals).astype(jnp.bfloat16)
    on_attended()

    def out(ranks):
        rows = two(k.att, ranks)

        def column(block):
            put_two(k.part_a, ranks, dot_nn(rows, columns_of(k.w_out, block)), lanes_at(block))

        loop(4, column)

    reduce = ReduceHere(p, k.wires, k.part_a, k.got_a, (k.held_a, k.mixed_a))
    out(there)
    reduce.start_cross()
    out(here)
    reduce.start_near()
    reduce.relay()
    return reduce


def feed_forward(k, reduce, on_sent, on_gathered, on_raised, part):
    p = k.place
    here, there = chips(p)
    reduce.finish()
    for at in range(4):
        rows = pl.ds(at * ROWS, ROWS)
        mid = k.hidden[rows] + reduce.total(rows) + k.vecs[4:5]
        k.mid[rows] = mid
        normed, _, _ = layer_norm(mid, k.vecs[1:2], k.vecs[3:4])
        k.n2[p.rank, at // 2, pl.ds(at % 2 * ROWS, ROWS)] = normed.astype(jnp.bfloat16)
    gather = GatherHere(p, k.wires, k.n2)
    gather.start()
    on_sent()

    def up(ranks):
        def column(index):
            lanes = lanes_at(index)
            rows = two(k.n2, ranks)
            weight = k.w_up[:, :, :, lanes].reshape(1024, 256)
            pre_act = dot_nn(rows, weight) + k.ffn_bias[0:1, lanes]
            value, slope = gelu_pair(pre_act)
            put_two(k.act, ranks, value, lanes)
            put_two(k.slope, ranks, slope, lanes)

        loop(4, column)

    gather.wait_sibling()
    gather.relay()
    on_gathered()
    up(here)
    gather.finish()
    up(there)
    on_raised()

    def down(ranks):
        def column(block):
            rows = two(k.act, ranks)
            put_two(part, ranks, dot_nn(rows, columns_of(k.w_down, block)), lanes_at(block))

        loop(4, column)

    return down, here, there


def unpack_small(small_all, views):
    parts = [small_all[block, core].astype(jnp.float32) for block in range(4) for core in range(2)]

    def row(index):
        return jnp.concatenate([part[index : index + 1] for part in parts], axis=1)

    for layer, k in enumerate(views):
        for index in range(2):
            k.vecs[index : index + 1] = row(3 + 2 * layer + index)
            at = 64 * layer + 32 * index
            k.qv_bias[index : index + 1] = jnp.concatenate(
                [part[0:1, at : at + 32] for part in parts], axis=1
            )
        for index in range(4):
            k.vecs[2 + index : 3 + index] = row(7 + 4 * layer + index)
        k.ffn_bias[0:1] = row(1 + layer)


def pack_small(flat, layers):
    flat[...] = jnp.zeros(flat.shape, flat.dtype)
    for shard in range(8):
        block, core = shard // 2, shard % 2
        lanes = slice(shard * 128, shard * 128 + 128)
        quarter = slice(shard * 32, shard * 32 + 32)
        pieces = []
        for layer, (col, col_qv, col_ffn) in enumerate(layers):
            flat[block, core, 2 * layer : 2 * layer + 2] = col[0:2, lanes]
            flat[block, core, 4 + 4 * layer : 8 + 4 * layer] = col[2:6, lanes]
            flat[block, core, 13 + layer : 14 + layer] = col_ffn[0:1, lanes]
            pieces += [col_qv[0:1, quarter], col_qv[1:2, quarter]]
        flat[block, core, 12:13] = jnp.concatenate(pieces, axis=1)


def feed_forward_back(k, gather, on_gathered, on_grad_down):
    p = k.place
    here, there = chips(p)

    def pre(ranks, first):
        def rows_of(index):
            lanes = lanes_at(index)
            weight = all_columns(k.w_down, lanes)
            grad = contract_last(two(k.gh, ranks), weight) * two(k.slope, ranks, lanes).astype(
                jnp.float32
            )
            put_two(k.gp, ranks, grad, lanes)
            summed = jnp.sum(grad, axis=0, keepdims=True)
            k.col_ffn[0:1, lanes] = summed if first else k.col_ffn[0:1, lanes] + summed

        loop(4, rows_of)

    if gather is not None:
        gather.wait_sibling()
        gather.relay()
    on_gathered()
    pre(here, True)
    if gather is not None:
        gather.finish()

    def turn(index):
        lanes = lanes_at(index)
        k.turned[lanes] = whole(k.act, lanes).T

    loop(4, turn)

    def grad_down(block):
        made = dot_nn(k.turned[...], whole(k.gh, lanes_at(block)))
        k.g_down[block, 0] = made[:, :128].astype(jnp.bfloat16)
        k.g_down[block, 1] = made[:, 128:].astype(jnp.bfloat16)

    loop(4, grad_down)
    on_grad_down()
    pre(there, False)

    def term(ranks):
        def column(block):
            rows = two(k.gp, ranks)
            weight = k.w_up[block].reshape(256, 1024)
            put_two(k.part_a, ranks, contract_last(rows, weight), lanes_at(block))

        loop(4, column)

    reduce = ReduceHere(p, k.wires, k.part_a, k.got_a, (k.held_a, k.mixed_a))
    term(there)
    reduce.start_cross()
    term(here)
    reduce.start_near()
    reduce.relay()
    return reduce


def grad_up(k):
    def rows_of(block):
        turned = whole(k.n2, lanes_at(block)).T
        made = dot_nn(turned, whole(k.gp))
        k.g_up[block] = made.astype(jnp.bfloat16).reshape(2, 128, 1024)

    loop(4, rows_of)


def through_norm(k, reduce, hidden, back, sums, gain, dst, put):
    totals = None
    for at in range(4):
        rows = pl.ds(at * ROWS, ROWS)
        grad = reduce.total(rows)
        _, unit, inv = layer_norm(hidden[rows], 1.0, 0.0)
        was = back[rows]
        now = was + norm_back(grad, unit, inv, k.vecs[gain : gain + 1])
        dst[rows] = now
        put(at, now)
        terms = [grad * unit, grad, now, was]
        terms = [jnp.sum(term, axis=0, keepdims=True) for term in terms]
        totals = terms if totals is None else [a + b for a, b in zip(totals, terms)]
    for row, total in zip(sums, totals):
        if row is not None:
            k.col[row : row + 1] = total


def grad_qkv_thirds(k, third):
    def turn(index):
        lanes = lanes_at(index)
        k.turned[lanes] = whole(k.n1, lanes).T

    loop(4, turn)
    for index in range(3):
        rows = pl.ds(index * 128, 128)

        def grad_qkv(block):
            made = dot_nn(k.turned[lanes_at(block)], whole(k.gq.at[index]))
            k.g_qkv[block, :, rows] = made.astype(jnp.bfloat16).reshape(2, 128, 256)

        loop(4, grad_qkv)
        third(index)

def attention_back(k, reduce, background, third, weights_first):
    p = k.place
    here, there = chips(p)
    grad_up(k)
    background(AT_UP)
    reduce.finish()
    background(AT_SUMMED)

    def put(at, now):
        k.gm[p.rank, at // 2, pl.ds(at % 2 * ROWS, ROWS)] = now.astype(jnp.bfloat16)

    through_norm(k, reduce, k.mid, k.back, (1, 3, 4, 5), 1, k.grad_mid, put)
    gather = GatherHere(p, k.wires, k.gm)
    gather.start()

    def attended(ranks):
        weight = all_columns(k.w_out, slice(None))
        put_two(k.ga, ranks, contract_last(two(k.gm, ranks), weight))

    gather.wait_sibling()
    gather.relay()
    attended(here)
    gather.finish()
    attended(there)

    def grad_out(block):
        made = dot_nn(whole(k.att).T, whole(k.gm, lanes_at(block)))
        k.g_out[block, 0] = made[:, :128].astype(jnp.bfloat16)
        k.g_out[block, 1] = made[:, 128:].astype(jnp.bfloat16)

    loop(4, grad_out)
    background(AT_OUT)
    scale = 1.0 / math.sqrt(HEAD_DIM)
    for head in range(4):
        lanes = slice(head * HEAD_DIM, head * HEAD_DIM + HEAD_DIM)
        for block in range(4):
            rows = pl.ds(block * 128, 128)
            count = (block + 1) * 128
            keys = k.key[: block + 1, :, lanes].reshape(count, HEAD_DIM)
            vals = k.val[: block + 1, :, lanes].reshape(count, HEAD_DIM)
            probs = k.probs[head, rows, :count].astype(jnp.float32)
            grad_probs = contract_last(k.ga[block, :, lanes], vals)
            row_dot = jnp.sum(grad_probs * probs, axis=-1, keepdims=True)
            score_grad = (probs * (grad_probs - row_dot) * scale).astype(jnp.bfloat16)
            k.ds[head % 2, rows, :count] = score_grad
            query_grad = dot_nn(score_grad, keys)
            k.gq[0, block, :, lanes] = query_grad.astype(jnp.bfloat16)
            summed = jnp.sum(query_grad, axis=0, keepdims=True)
            k.col_qv[0:1, lanes] = summed if block == 0 else k.col_qv[0:1, lanes] + summed
        if head in (0, 2):
            background(AT_LATE if head else AT_HEADS)
        for block in range(4):
            below = pl.ds(block * 128, 512 - block * 128)
            cols = slice(block * 128, block * 128 + 128)
            count = 512 - block * 128
            queries = k.q[block:, :, lanes].reshape(count, HEAD_DIM)
            grads = k.ga[block:, :, lanes].reshape(count, HEAD_DIM)
            key_grad = contract_first(k.ds[head % 2, below, cols], queries)
            val_grad = contract_first(k.probs[head, below, cols], grads)
            k.gq[1, block, :, lanes] = key_grad.astype(jnp.bfloat16)
            k.gq[2, block, :, lanes] = val_grad.astype(jnp.bfloat16)
            summed = jnp.sum(val_grad, axis=0, keepdims=True)
            k.col_qv[1:2, lanes] = summed if block == 0 else k.col_qv[1:2, lanes] + summed
    background(AT_ATTENDED)

    if weights_first:
        grad_qkv_thirds(k, third)

    def term(ranks):
        rows = [two(k.gq.at[index], ranks) for index in range(3)]

        def column(block):
            made = None
            for index in range(3):
                weight = k.w_qkv[block, :, index * 128 : index * 128 + 128].reshape(256, 256)
                one = contract_last(rows[index], weight)
                made = one if made is None else made + one
            put_two(k.part_b, ranks, made, lanes_at(block))

        loop(4, column)

    reduce = ReduceHere(p, k.wires, k.part_b, k.got_b, (k.held_b, k.mixed_b))
    term(there)
    reduce.start_cross()
    term(here)
    reduce.start_near()
    reduce.relay()

    if not weights_first:
        grad_qkv_thirds(k, third)
    background(AT_QKV)
    reduce.finish()
    through_norm(
        k, reduce, k.hidden, k.grad_mid, (0, 2, None, None), 0, k.back_out, lambda at, now: None
    )


def total_scratch(name, rows, cols, half=jnp.bfloat16):
    one, two = ((rows, cols), half), ((2, rows, cols), half)
    return {f"{name}_t{index}": value for index, value in enumerate((two, two, two, one, one))}


def paired_shards(
    x_in, d_out, seq_lengths, w_qkv, b_qv, w_o, w_1, b_ffn, w_2, norm_gains, vec_biases
):
    fused = make_fused()
    own_rows, width = x_in.shape
    layer_count = w_qkv.shape[0]
    half, full = jnp.bfloat16, jnp.float32
    z = lax.axis_index("tensor")
    qkv_turned = jnp.transpose(w_qkv, (0, 2, 1, 3)).reshape(layer_count, 384, 256)
    shapes = {QKV: (384, 256), OUT: (256, 128), UP: (128, 1024), DOWN: (1024, 128)}
    def pair_spec(name):
        return ((2,) + shapes[name], half)

    def full_spec(name):
        return ((4, 2) + shapes[name], half)

    def added(parts):
        return parts[0].astype(full) + parts[1].astype(full)

    small_shapes = [b_qv.shape, b_ffn.shape, norm_gains.shape, vec_biases.shape]
    small = pack([b_qv, b_ffn, norm_gains, vec_biases], 128, 16)
    lengths = jnp.pad(seq_lengths.astype(full), ((0, 7), (0, 126)))

    rows_spec = ((4, 2, own_rows // 2, width), half)
    heads_spec = ((4, own_rows, 256), half)
    wide_spec = ((4, own_rows, width), half)
    own_half = ((own_rows, width), half)
    own_full = ((own_rows, width), full)
    two_half = ((2, own_rows, width), half)
    reduce_a = dict(part_a=wide_spec, got_a=two_half, held_a=own_half, mixed_a=own_half)
    reduce_b = dict(part_b=wide_spec, got_b=two_half, held_b=own_half, mixed_b=own_half)
    saved_specs = dict(
        hidden=own_full,
        vecs=((8, width), full),
        n1=rows_spec,
        q=heads_spec,
        key=heads_spec,
        val=heads_spec,
        probs=((4, 512, 512), half),
        att=heads_spec,
        mid=own_full,
        n2=rows_spec,
        act=wide_spec,
        slope=wide_spec,
        w_qkv=full_spec(QKV),
        w_out=full_spec(OUT),
        w_up=full_spec(UP),
        w_down=full_spec(DOWN),
    )
    own_specs = dict(
        reduce_a,
        qv_bias=((8, 256), full),
        ffn_bias=((8, width), full),
        pair_qkv=pair_spec(QKV),
        pair_out=pair_spec(OUT),
        pair_up=pair_spec(UP),
        pair_down=pair_spec(DOWN),
    )

    group_a, group_b, group_c = ("w_down", "slope"), ("w_up", "act", "n2"), ("mid", "att", "w_out")
    group_d, group_e = ("probs", "key", "val", "q", "w_qkv", "n1"), ("hidden",)

    def of_layers(specs):
        return {f"{name}_{layer}": spec for name, spec in specs.items() for layer in range(2)}

    def view(k, layer):
        made = Env()
        for name, ref in k.__dict__.items():
            if name.endswith(f"_{layer}"):
                setattr(made, name[:-2], ref)
        made.place, made.wires = k.place, k.wires
        return made

    def forward(k):
        p, w = k.place, k.wires
        k0, k1 = view(k, 0), view(k, 1)
        small_job = Fetch(p, w, k.small, k.small_all, [k.small_pair])
        length_job = Swap(p, w, k.lengths_in, k.lengths, [])
        swap_x = Swap(p, w, k.x_half, k.x_got, [])
        swap_d = Swap(p, w, k.d_half, k.d_got, [])
        k0.lengths = k1.lengths = k.lengths

        def relay_native(*jobs):
            @pl.when(p.native)
            def _():
                for job in jobs:
                    job.relay()

        def relay_foreign(*jobs):
            @pl.when(jnp.logical_not(p.native))
            def _():
                for job in jobs:
                    job.relay()

        def fetch_qkv(layer, v):
            jobs = []
            for index in range(3):
                rows = pl.ds(index * 128, 128)
                dst, pair = v.w_qkv.at[:, :, rows], v.pair_qkv.at[:, rows]
                jobs.append(Fetch(p, w, k.s_qkv.at[layer, rows], dst, [pair]))
            return jobs

        def fetch_rest(layer, v):
            return (
                Fetch(p, w, k.s_out.at[layer], v.w_out, [v.pair_out]),
                Fetch(p, w, k.s_up.at[layer], v.w_up, [v.pair_up]),
                Fetch(p, w, k.s_down.at[layer], v.w_down, [v.pair_down]),
            )

        qkv_0, qkv_1 = fetch_qkv(0, k0), fetch_qkv(1, k1)
        out_0, up_0, down_0 = fetch_rest(0, k0)
        out_1, up_1, down_1 = fetch_rest(1, k1)
        for at in range(4):
            rows = pl.ds(at * ROWS, ROWS)
            k.x_half[rows] = k.x_in[rows].astype(half)
        mover = Mover(w)

        small_job.start()
        length_job.start()
        swap_x.start()
        small_job.relay()
        small_job.relay_more()
        for job in qkv_0:
            job.start()

        @pl.when(p.native)
        def _():
            for job in qkv_0:
                job.relay()

        small_job.finish()
        unpack_small(k.small_all, (k0, k1))
        length_job.finish()
        swap_x.finish()
        for at in range(4):
            rows = pl.ds(at * ROWS, ROWS)
            k0.hidden[rows] = jnp.where(p.native, k.x_in[rows], k.x_got[rows].astype(full))
            k.d_half[rows] = k.d_in[rows].astype(half)

        def first_sent():
            @pl.when(jnp.logical_not(p.native))
            def _():
                for job in qkv_0:
                    job.relay()

        def first_gathered():
            out_0.start()
            up_0.start()
            for job in qkv_0:
                job.relay_more()
            relay_native(out_0, up_0)
            for job in qkv_0:
                job.finish()

        def first_middle(block):
            if block == 1:
                relay_foreign(out_0)
            else:
                out_0.relay_more()

        def first_attended():
            relay_foreign(up_0)
            down_0.start()
            out_0.finish()

        reduce = attention_forward(k0, first_sent, first_gathered, first_middle, first_attended)
        relay_native(down_0)

        def first_sent_two():
            up_0.relay_more()
            relay_foreign(down_0)

        def first_gathered_two():
            for job in qkv_1:
                job.start()
            out_1.start()
            up_0.finish()

        def first_raised():
            down_0.relay_more()
            relay_native(*qkv_1, out_1)
            up_1.start()
            down_0.finish()
            relay_foreign(*qkv_1, out_1)

        column, here, there = feed_forward(
            k0, reduce, first_sent_two, first_gathered_two, first_raised, k.part_b
        )
        second = ReduceHere(p, w, k.part_b, k.got_b, (k.held_b, k.mixed_b))
        column(there)
        second.start_cross()
        column(here)
        second.start_near()
        second.relay()
        for job in qkv_1:
            job.relay_more()
        out_1.relay_more()
        relay_native(up_1)
        for name in group_a + group_b + group_c + group_d + group_e:
            mover.start(getattr(k0, name), getattr(k, f"h_{name}"), name)
        second.finish()
        for at in range(4):
            rows = pl.ds(at * ROWS, ROWS)
            k1.hidden[rows] = k0.mid[rows] + second.total(rows) + k0.vecs[5:6]
        grads = GatherHere(p, w, k.gh)

        def last_sent():
            relay_foreign(up_1)

        def last_gathered():
            down_1.start()
            swap_d.start()
            for job in qkv_1:
                job.finish()
            out_1.finish()

        def last_middle(block):
            if block == 1:
                relay_native(down_1)
            else:
                up_1.relay_more()

        reduce = attention_forward(k1, last_sent, last_gathered, last_middle, lambda: None)
        relay_foreign(down_1)

        def last_gathered_two():
            up_1.finish()
            down_1.relay_more()
            swap_d.finish()
            for at in range(4):
                rows = pl.ds(at * ROWS, ROWS)
                k.back[rows] = jnp.where(p.native, k.d_in[rows], k.d_got[rows].astype(full))
                k.gh[p.rank, at // 2, pl.ds(at % 2 * ROWS, ROWS)] = k.back[rows].astype(half)
            grads.start()

        def raised():
            grads.wait_sibling()
            grads.relay()
            down_1.finish()

        column, here, there = feed_forward(
            k1, reduce, lambda: None, last_gathered_two, raised, k.ffn_part
        )
        column(there)
        column(here)
        grads.finish()
        mover.wait()

    totals = dict(shapes)
    spare = dict(
        of_layers(own_specs),
        **of_layers(saved_specs),
        **reduce_b,
        back=own_full,
        gh=rows_spec,
        ffn_part=wide_spec,
        lengths=((8, 128), full),
        small_pair=((2, 16, 128), half),
        small_all=((4, 2, 16, 128), half),
        x_half=own_half,
        x_got=own_half,
        d_half=own_half,
        d_got=own_half,
        turned=((1024, 512), half),
        ds=((2, 512, 512), half),
        gq=((3, 4, own_rows, 256), half),
        out_half=own_half,
        back_half=own_half,
        made=own_full,
        back_out=own_full,
        out_sent=own_half,
        back_sent=own_half,
        flat=((4, 2, 16, 128), full),
        small_sums=((2, 16, 128), full),
        g_last=full_spec(QKV),
        **total_scratch("small", 16, 128, full),
        **total_scratch("last", *shapes[QKV]),
    )
    for name, shape in shapes.items():
        spare.update(total_scratch(name, *shape))
    spare.update(
        of_layers(dict(col=((8, width), full), col_qv=((8, 256), full), col_ffn=((8, width), full)))
    )

    def backward(k):
        p, w = k.place, k.wires
        mover = Mover(w)
        first, last = view(k, 0), view(k, 1)
        for name in saved_specs:
            setattr(k, name, getattr(last, name))
        for name in shapes:
            setattr(k, f"g_{name}", getattr(first, f"w_{name}"))
        k.gm, k.gp, k.ga, k.grad_mid = first.n1, first.act, first.att, first.mid
        k.part_a, k.got_a, k.held_a, k.mixed_a = first.part_a, first.got_a, first.held_a, first.mixed_a
        k0, k1 = Env(), Env()
        for v, layer in ((k0, first), (k1, last)):
            v.__dict__.update(k.__dict__)
            v.vecs, v.col, v.col_qv, v.col_ffn = layer.vecs, layer.col, layer.col_qv, layer.col_ffn
        k1.back_out = k0.back = first.hidden
        k1.g_qkv = k.g_last

        def load(names):
            for name in names:
                mover.start(getattr(k, f"h_{name}"), getattr(k, name), name)

        def job_total(name, layer):
            spare = [getattr(k, f"{name}_t{at}") for at in range(5)]
            return Total(p, w, getattr(k, f"g_{name}"), getattr(k, f"pair_{name}_{layer}"), spare)

        def job_deliver(name, layer):
            src, dst = getattr(k, f"pair_{name}_{layer}"), getattr(k, f"done_{name}_{layer}")
            return Deliver(p, w, src, dst, [])

        def thirds(layer, v, name):
            made = []
            for index in range(3):
                rows = pl.ds(index * 128, 128)
                spare = [getattr(k, f"{name}_t{at}") for at in range(5)]
                spare = [ref.at[:, rows] for ref in spare[:3]] + [ref.at[rows] for ref in spare[3:]]
                dst = getattr(k, f"pair_{QKV}_{layer}").at[:, rows]
                done = getattr(k, f"done_{QKV}_{layer}").at[:, rows]
                made.append(
                    (
                        Total(p, w, v.g_qkv.at[:, :, rows], dst, spare),
                        Deliver(p, w, dst, done, []),
                    )
                )
            return made

        ffn = ReduceHere(p, w, k.ffn_part, last.got_a, (last.held_a, last.mixed_a))
        swap = Swap(p, w, k.out_half, k.out_sent, [])
        swap_back = Swap(p, w, k.back_half, k.back_sent, [])
        qkv_1, qkv_0 = thirds(1, k1, "last"), thirds(0, k0, QKV)
        down_1, up_1, out_1 = [job_total(name, 1) for name in (DOWN, UP, OUT)]
        down_0, up_0, out_0 = [job_total(name, 0) for name in (DOWN, UP, OUT)]
        to_down_1, to_up_1, to_out_1 = [job_deliver(name, 1) for name in (DOWN, UP, OUT)]
        to_down_0, to_up_0, to_out_0 = [job_deliver(name, 0) for name in (DOWN, UP, OUT)]
        small_job = Small(
            p, w, k.flat, k.small_parts, [getattr(k, f"small_t{at}") for at in range(5)] + [k.small_sums]
        )
        reduce = feed_forward_back(k1, None, lambda: None, down_1.start)
        def last_background(point):
            if point == AT_UP:
                load(group_a + group_b)
                up_1.start()
            if point == AT_SUMMED:
                down_1.relay_more()
            if point == AT_OUT:
                ffn.start_cross()
                ffn.start_near()
                out_1.start()
            if point == AT_HEADS:
                ffn.relay()
                down_1.finish()
                to_down_1.start()
            if point == AT_LATE:
                up_1.relay_more()
                out_1.relay_more()
                ffn.finish()
                for at in range(4):
                    rows = pl.ds(at * ROWS, ROWS)
                    made = k.mid[rows] + ffn.total(rows) + k1.vecs[5:6]
                    k.made[rows] = made
                    k.out_half[rows] = made.astype(half)
                load(group_c)
            if point == AT_QKV:
                load(group_d)
                up_1.finish()
                out_1.finish()

        attention_back(k1, reduce, last_background, lambda index: qkv_1[index][0].start(), False)
        load(group_e)
        for at in range(4):
            rows = pl.ds(at * ROWS, ROWS)
            k.gh[p.rank, at // 2, pl.ds(at % 2 * ROWS, ROWS)] = k0.back[rows].astype(half)
        gather = GatherHere(p, w, k.gh)
        gather.start()
        mover.wait(*group_a, *group_b)

        def first_started():
            to_up_1.start()
            for job, _ in qkv_1:
                job.relay_more()

        def first_grad_down():
            for job, _ in qkv_1:
                job.finish()
            down_0.start()

        reduce = feed_forward_back(k0, gather, first_started, first_grad_down)
        mover.wait(*group_c, *group_d, *group_e)

        for _, job in qkv_1:
            job.start()
        to_out_1.start()

        def first_background(point):
            if point == AT_UP:
                up_0.start()
            if point == AT_SUMMED:
                down_0.relay_more()
            if point == AT_OUT:
                swap.start()
                out_0.start()
            if point == AT_HEADS:
                down_0.finish()
                to_down_0.start()
            if point == AT_LATE:
                up_0.relay_more()
                out_0.relay_more()
            if point == AT_QKV:
                up_0.finish()
                to_up_0.start()
                out_0.finish()
                to_out_0.start()
                qkv_0[0][0].relay_more()
                qkv_0[1][0].relay_more()

        attention_back(k0, reduce, first_background, lambda index: qkv_0[index][0].start(), True)
        pack_small(k.flat, [(v.col, v.col_qv, v.col_ffn) for v in (k0, k1)])
        small_job.start()
        for at in range(4):
            rows = pl.ds(at * ROWS, ROWS)
            k.back_half[rows] = k.back_out[rows].astype(half)
        qkv_0[0][0].finish()
        qkv_0[2][0].relay_more()
        small_job.relay_more()
        swap_back.start()
        qkv_0[0][1].start()
        for job, then in qkv_0[1:]:
            job.finish()
            then.start()
        small_job.finish()
        swap.finish()
        swap_back.finish()
        for at in range(4):
            rows = pl.ds(at * ROWS, ROWS)
            k.output[rows] = jnp.where(p.native, k.made[rows], k.out_sent[rows].astype(full))
            k.grad_x[rows] = jnp.where(p.native, k.back_out[rows], k.back_sent[rows].astype(full))
        for job in (to_down_1, to_up_1, to_out_1, to_down_0, to_up_0, to_out_0):
            job.finish()
        for _, job in qkv_1 + qkv_0:
            job.finish()
        mover.wait()

    done_specs = {
        f"done_{name}_{layer}": pair_spec(name) for name in totals for layer in range(2)
    }
    def both(k):
        forward(k)
        backward(k)

    spilled = {f"h_{name}": spec for name, spec in saved_specs.items()}
    last = fused(
        both,
        dict(
            x_in=x_in,
            d_in=d_out,
            lengths_in=lengths,
            small=small,
            s_qkv=qkv_turned,
            s_out=w_o,
            s_up=w_1,
            s_down=w_2,
        ),
        dict(
            done_specs,
            **spilled,
            output=own_full,
            grad_x=own_full,
            small_parts=((8, 16, 128), full),
        ),
        spare,
        (SIBLING, CROSS, FAR, BESIDE, ABOVE, LINE),
        hbm=[f"s_{name}" for name in shapes] + list(spilled) + list(done_specs),
    )
    small_parts = last.small_parts
    small_parts = small_parts.reshape(8, -1)
    gain_size, bias_size = norm_gains.size, vec_biases.size
    everyone = small_parts.sum(0)
    sources = jnp.arange(8, dtype=jnp.int32)
    pair = z // 2
    mine_from = (sources == 2 * z + pair) | (sources == 2 * (z + 2 - 4 * pair) + pair)
    mine = jnp.where(mine_from[:, None], small_parts, 0.0).sum(0)[gain_size + bias_size :]

    def stacked_layers(name):
        return jnp.stack([added(getattr(last, f"done_{name}_{layer}")) for layer in range(2)])

    grad_qkv = stacked_layers(QKV)
    grad_qkv = jnp.transpose(grad_qkv.reshape(layer_count, 3, 128, 256), (0, 2, 1, 3))
    return (
        last.output,
        last.grad_x,
        grad_qkv,
        mine[: b_qv.size].reshape(b_qv.shape),
        stacked_layers(OUT),
        stacked_layers(UP),
        mine[b_qv.size : b_qv.size + b_ffn.size].reshape(b_ffn.shape),
        stacked_layers(DOWN),
        everyone[:gain_size].reshape(norm_gains.shape),
        everyone[gain_size : gain_size + bias_size].reshape(vec_biases.shape),
    )


def solution(mesh):
    in_specs = (
        P(("dp", "tensor"), None),
        P(("dp", "tensor"), None),
        P("dp", None),
        P(None, "dp", None, "tensor"),
        P(None, None, ("tensor", "dp")),
        P(None, "tensor", "dp"),
        P(None, "dp", "tensor"),
        P(None, ("tensor", "dp")),
        P(None, "tensor", "dp"),
        P(None, None, "dp"),
        P(None, None, "dp"),
    )
    out_specs = (
        P(("dp", "tensor"), None),
        P(("dp", "tensor"), None),
        P(None, "dp", None, "tensor"),
        P(None, None, ("tensor", "dp")),
        P(None, "tensor", "dp"),
        P(None, "dp", "tensor"),
        P(None, ("tensor", "dp")),
        P(None, "tensor", "dp"),
        P(None, None, "dp"),
        P(None, None, "dp"),
    )
    paired = mesh.shape["dp"] == 8 and mesh.shape["tensor"] == 4
    body = paired_shards if paired else shards
    return jax.shard_map(body, mesh=mesh, in_specs=in_specs, out_specs=out_specs, check_vma=False)
```
